32 devices in a mesh: seq: 4 (over x, core), fsdp: 8 (over z, y).
Axes of the slice: x: 2, y: 2, z: 4, core: 2. Of those that a mesh axis runs over, the one named last changes fastest.
Arguments:
- inputs: bfloat16 [16, 2048, 768], P('fsdp', 'seq'), may hold values from -6 to 6
- segment_ids: int32 [16, 1024], P('fsdp'), may hold values from 0 to 15, as said below
- block_ids: int32 [16, 1024], P('fsdp'), may hold values from 0 to 31, as said below
- attn_gain: bfloat16 [768], P('fsdp'), may hold values from 0.099609375 to 1.8984375
- attn_shift: bfloat16 [768], P('fsdp'), may hold values from -3 to 3
- proj_in: bfloat16 [768, 2304], P('fsdp'), may hold values from -0.21875 to 0.21875
- bias_in: bfloat16 [2304], P('fsdp'), may hold values from -2 to 2
- proj_out: bfloat16 [768, 768], P('fsdp'), may hold values from -0.875 to 0.875
- bias_out: bfloat16 [768], P('fsdp'), may hold values from -2 to 2
- mlp_gain: bfloat16 [768], P('fsdp'), may hold values from 0.099609375 to 1.8984375
- mlp_shift: bfloat16 [768], P('fsdp'), may hold values from -3 to 3
- weight_up: bfloat16 [768, 3072], P('fsdp'), may hold values from -0.21875 to 0.21875
- bias_up: bfloat16 [3072], P('fsdp'), may hold values from -3 to 3
- weight_down: bfloat16 [3072, 768], P('fsdp'), may hold values from -0.109375 to 0.109375
- bias_down: bfloat16 [768], P('fsdp'), may hold values from -2 to 2
- cotangent: bfloat16 [16, 2048, 768], P('fsdp', 'seq'), may hold values from -6 to 6
Outputs:
- out_rows: bfloat16 [16, 2048, 768], P('fsdp', 'seq')
- grad_input: float32 [16, 2048, 768], P('fsdp', 'seq')
- grad_attn_gain: float32 [768], P('fsdp')
- grad_attn_shift: float32 [768], P('fsdp')
- grad_proj_in: float32 [768, 2304], P('fsdp')
- grad_bias_in: float32 [2304], P('fsdp')
- grad_proj_out: float32 [768, 768], P('fsdp')
- grad_bias_out: float32 [768], P('fsdp')
- grad_mlp_gain: float32 [768], P('fsdp')
- grad_mlp_shift: float32 [768], P('fsdp')
- grad_weight_up: float32 [768, 3072], P('fsdp')
- grad_bias_up: float32 [3072], P('fsdp')
- grad_weight_down: float32 [3072, 768], P('fsdp')
- grad_bias_down: float32 [768], P('fsdp')
The draws below stay inside these ranges and needn't reach their ends.
Inputs may be any that keep to these rules, and one draw needn't show every extreme that they name: `segment_ids`: along each sequence the ids start at 0, never fall, and end at 15; equal ids mark one document. One document has exactly 512 tokens and begins between 128 and 384; all others are shorter. `block_ids`: A token's block is the number of whole 16-token blocks between its document's first token and it: 0 at a document's first token, rising by one every 16 tokens of the document.
All inputs are finite; a program needn't handle non-finite values.
Results may differ from the reference program's by a relative error of at most 0.015.
Values may be sent and summed in bfloat16 or wider, within the bound.
A program may use at most 104 MiB of HBM per device.

```python
import jax
import jax.numpy as jnp
from jax import lax

D = 768
H = 12
HD = 64
FF = 3072
BLK = 16
LEN = 1024
SEQS = 16
ROWS = 2048


def doc_layout(key):
    folded = jax.random.fold_in(key, 11)
    start_key, front_key, back_key = jax.random.split(folded, 3)
    long_start = jax.random.randint(start_key, (SEQS, 1), LEN // 8, 3 * LEN // 8 + 1).astype(jnp.int32)
    long_end = (long_start + LEN // 2).astype(jnp.int32)
    front_raw = jax.random.randint(front_key, (SEQS, 6), 0, 1 << 20).astype(jnp.int32)
    front_cuts = (front_raw % (long_start - 1) + 1).astype(jnp.int32)
    back_raw = jax.random.randint(back_key, (SEQS, 7), 0, 1 << 20).astype(jnp.int32)
    back_cuts = (back_raw % (LEN - long_end - 1) + long_end + 1).astype(jnp.int32)
    cuts = jnp.concatenate([front_cuts, long_start, long_end, back_cuts], axis=1).astype(jnp.int32)
    places = jnp.arange(LEN, dtype=jnp.int32)
    passed = cuts[:, None, :] <= places[None, :, None]
    segment = jnp.sum(passed.astype(jnp.int32), axis=2).astype(jnp.int32)
    first_token = jnp.max(jnp.where(passed, cuts[:, None, :], 0), axis=2).astype(jnp.int32)
    blocks = ((places[None, :] - first_token) // BLK).astype(jnp.int32)
    return (segment, blocks)


def draw_segment_ids(key, part):
    return doc_layout(key)[0]


def draw_block_ids(key, part):
    return doc_layout(key)[1]


def shard_levels(stream_key, shape, pieces, smallest, high):
    loudness, own = 1.0, jax.random.fold_in(stream_key, 6)
    for axis_at, blocks in pieces:
        steps = jnp.exp(jax.random.uniform(jax.random.fold_in(own, axis_at), (blocks,), jnp.float32, smallest / len(pieces), high / len(pieces)))
        loudness = loudness * jnp.repeat(steps, shape[axis_at] // blocks).reshape([-1 if axis == axis_at else 1 for axis in range(len(shape))])
    return loudness


def scatter_about(own_key, dims, spread, most, cuts=(), kind=jnp.bfloat16):
    values = spread * jax.random.normal(own_key, dims, jnp.float32)
    if cuts:
        values = values * shard_levels(own_key, dims, cuts, -0.22, 0.18)
    return jnp.clip(values, -most, most).astype(kind)


def setup_inputs(seed: int = 0) -> dict:
    seeds = jax.random.split(jax.random.key(seed), 17)
    return {
        "inputs": scatter_about(seeds[0], (SEQS, ROWS, D), 1.0, 6.0, ((0, 8), (1, 4))),
        "segment_ids": draw_segment_ids(jax.random.fold_in(seeds[16], 71), 0),
        "block_ids": draw_block_ids(jax.random.fold_in(seeds[16], 71), 0),
        "attn_gain": jnp.clip(1.0 + 0.18 * jax.random.normal(seeds[3], (D,), jnp.float32), 0.099609375, 1.8984375).astype(jnp.bfloat16),
        "attn_shift": scatter_about(seeds[4], (D,), 0.5, 3.0, ((0, 8),)),
        "proj_in": scatter_about(seeds[5], (D, 3 * D), D ** -0.5, 0.21875, ((0, 8),)),
        "bias_in": scatter_about(seeds[6], (3 * D,), 0.3, 2.0, ((0, 8),)),
        "proj_out": scatter_about(seeds[7], (D, D), (D // 16) ** -0.5, 0.875, ((0, 8),)),
        "bias_out": scatter_about(seeds[8], (D,), 0.3, 2.0, ((0, 8),)),
        "mlp_gain": jnp.clip(1.0 + 0.18 * jax.random.normal(seeds[9], (D,), jnp.float32), 0.099609375, 1.8984375).astype(jnp.bfloat16),
        "mlp_shift": scatter_about(seeds[10], (D,), 0.5, 3.0, ((0, 8),)),
        "weight_up": scatter_about(seeds[11], (D, FF), D ** -0.5, 0.21875, ((0, 8),)),
        "bias_up": scatter_about(seeds[12], (FF,), 0.5, 3.0, ((0, 8),)),
        "weight_down": scatter_about(seeds[13], (FF, D), FF ** -0.5, 0.109375, ((0, 8),)),
        "bias_down": scatter_about(seeds[14], (D,), 0.3, 2.0, ((0, 8),)),
        "cotangent": scatter_about(seeds[15], (SEQS, ROWS, D), 1.0, 6.0, ((0, 8), (1, 4))),
    }


@jax.custom_vjp
def low(v):
    return lax.optimization_barrier(v.astype(jnp.bfloat16)).astype(jnp.float32)

@jax.custom_vjp
def low_back(v):
    return v

def low_keep(v):
    return (low(v), None)

def low_pass(kept, grad):
    return (grad,)

def back_keep(v):
    return (v, None)

def back_low(kept, grad):
    return (low(grad),)
low.defvjp(low_keep, low_pass)
low_back.defvjp(back_keep, back_low)
norm_eps = 1e-05

def row_norm(value, gain, shift):
    center = lax.optimization_barrier(jnp.mean(value, axis=-1, keepdims=True))
    centered = value - center
    inverse = lax.rsqrt(lax.optimization_barrier(jnp.mean(centered * centered, axis=-1, keepdims=True)) + norm_eps)
    return centered * inverse * gain + shift

def angles(positions, half):
    freqs = 10000.0 ** (-(jnp.arange(half, dtype=jnp.float32) / half))
    turned = positions.astype(jnp.float32)[:, None] * freqs[None, :]
    return (jnp.cos(turned)[:, None, :], jnp.sin(turned)[:, None, :])

def rotate(value, cosine, sine):
    half = value.shape[-1] // 2
    first = value[..., :half]
    second = value[..., half:]
    return jnp.concatenate([first * cosine - second * sine, second * cosine + first * sine], axis=-1)

def allowed(seg_q, blk_q, copy_q, seg_k, blk_k, copy_k):
    same_doc = seg_q[:, None] == seg_k[None, :]
    noisy_q = (copy_q == 0)[:, None]
    noisy_k = (copy_k == 0)[None, :]
    from_noisy = noisy_k & (blk_k[None, :] == blk_q[:, None]) | ~noisy_k & (blk_k[None, :] < blk_q[:, None])
    from_clean = ~noisy_k & (blk_k[None, :] <= blk_q[:, None])
    return same_doc & jnp.where(noisy_q, from_noisy, from_clean)

def seq_layer(rows_in, segments, blocks, params):
    gain_one, shift_one, w_in, b_in, w_out, b_out, gain_two, shift_two, w_up, b_up, w_down, b_down = params
    highest = lax.Precision.HIGHEST
    total = rows_in.shape[0]
    length = total // 2
    a_one = low(row_norm(rows_in, gain_one, shift_one))
    qkv = low_back(jnp.dot(a_one, w_in, precision=highest) + b_in)
    positions = jnp.arange(total, dtype=jnp.int32) % length
    cosine, sine = angles(positions, HD // 2)
    parts = qkv.reshape(total, 3, H, HD)
    queries = low_back(low(rotate(parts[:, 0], cosine, sine)))
    keys_all = low_back(low(rotate(parts[:, 1], cosine, sine)))
    values = low_back(low(parts[:, 2]))
    seg_all = jnp.concatenate([segments, segments]).astype(jnp.int32)
    blk_all = jnp.concatenate([blocks, blocks]).astype(jnp.int32)
    copy_all = (jnp.arange(total, dtype=jnp.int32) // length).astype(jnp.int32)
    block_rows = min(512, total)
    count = total // block_rows
    scale = HD ** (-0.5)

    def attend(index):
        begin = (index * block_rows).astype(jnp.int32)
        q_blk = lax.dynamic_slice_in_dim(queries, begin, block_rows, 0)
        mask = allowed(lax.dynamic_slice_in_dim(seg_all, begin, block_rows, 0), lax.dynamic_slice_in_dim(blk_all, begin, block_rows, 0), lax.dynamic_slice_in_dim(copy_all, begin, block_rows, 0), seg_all, blk_all, copy_all)
        scores = jnp.einsum('qhd,khd->hqk', q_blk, keys_all, precision=highest) * scale
        scores = low_back(scores)
        scores = jnp.where(mask[None], scores, -1e+30)
        probs = low(jax.nn.softmax(scores, axis=-1))
        return jnp.einsum('hqk,khd->qhd', probs, values, precision=highest)
    heads_out = lax.map(jax.checkpoint(attend), jnp.arange(count, dtype=jnp.int32))
    attn = low_back(low(heads_out.reshape(total, D)))
    proj = low_back(jnp.dot(attn, w_out, precision=highest) + b_out)
    mid = rows_in + proj
    a_two = low(row_norm(mid, gain_two, shift_two))
    upper = low_back(jnp.dot(a_two, w_up, precision=highest) + b_up)
    gated = low(jax.nn.gelu(upper, approximate=True))
    return mid + jnp.dot(gated, w_down, precision=highest) + b_down

def reference(inputs, segment_ids, block_ids, attn_gain, attn_shift, proj_in, bias_in, proj_out, bias_out, mlp_gain, mlp_shift, weight_up, bias_up, weight_down, bias_down, cotangent):
    params = tuple((p.astype(jnp.float32) for p in (attn_gain, attn_shift, proj_in, bias_in, proj_out, bias_out, mlp_gain, mlp_shift, weight_up, bias_up, weight_down, bias_down)))
    rows_f = inputs.astype(jnp.float32)

    def whole(rows_all, params_all):

        def one_seq(carry, item):
            rows_one, segments, blocks = item
            return (carry, seq_layer(rows_one, segments, blocks, params_all))
        _, outs = lax.scan(jax.checkpoint(one_seq), jnp.zeros((), jnp.float32), (rows_all, segment_ids, block_ids))
        return outs
    outs, pull = jax.vjp(whole, rows_f, params)
    grad_rows, grad_params = pull(cotangent.astype(jnp.float32))
    return (outs.astype(jnp.bfloat16), grad_rows) + tuple(grad_params)
```

```python
import functools

import jax
import jax.numpy as jnp
from jax import lax
from jax.experimental import pallas as pl
from jax.experimental.pallas import tpu as pltpu
from jax.sharding import PartitionSpec as P

HD = 64
QUAD = 4
TILE = 128
HALO = 16
NEAR = TILE + 2 * HALO
EPS = 1e-05
MASKED = -1e30
SEG_STEP = 4096
F32 = jnp.float32
BF16 = jnp.bfloat16
VMEM_BYTES = 60 * 1024 * 1024


def dot(a, b):
    return jnp.dot(a, b, preferred_element_type=F32)


def dot_nt(a, b):
    return lax.dot_general(a, b, (((1,), (1,)), ((), ())), preferred_element_type=F32)


def dot_tn(a, b):
    return lax.dot_general(a, b, (((0,), (0,)), ((), ())), preferred_element_type=F32)


def norm_stats(x):
    center = jnp.mean(x, axis=-1, keepdims=True)
    centered = x - center
    inverse = lax.rsqrt(jnp.mean(centered * centered, axis=-1, keepdims=True) + EPS)
    return centered * inverse, inverse


def norm_back(grad, normed, inverse, gain):
    scaled = grad * gain
    first = jnp.mean(scaled, axis=-1, keepdims=True)
    second = jnp.mean(scaled * normed, axis=-1, keepdims=True)
    return inverse * (scaled - first - normed * second)


def partner(u):
    lane = lax.broadcasted_iota(jnp.int32, u.shape, 1)
    half = HD // 2
    return jnp.where(
        lane % HD < half, pltpu.roll(u, u.shape[1] - half, 1), pltpu.roll(u, half, 1)
    )


def whole(shape):
    return pl.BlockSpec(shape, lambda *_: (0,) * len(shape), pipeline_mode=pl.Buffered(1))


def call(kernel, grid, in_specs, out_specs, out_shape, scratch, flops, nbytes, name):
    return pl.pallas_call(
        kernel,
        grid=grid,
        in_specs=in_specs,
        out_specs=out_specs,
        out_shape=out_shape,
        scratch_shapes=scratch,
        compiler_params=pltpu.CompilerParams(vmem_limit_bytes=VMEM_BYTES),
        cost_estimate=pl.CostEstimate(flops=flops, bytes_accessed=nbytes, transcendentals=0),
        name=name,
    )


def like(shape, dtype):
    return jax.ShapeDtypeStruct(shape, dtype)


SMEM = functools.partial(pl.BlockSpec, memory_space=pltpu.SMEM)


def layout(rows, length):
    win = rows - length // 8
    noisy = win + rows + HALO
    return dict(rows=rows, win=win, length=length, noisy=noisy, keys=noisy + rows + 2 * HALO)


def places(lay, role):
    noisy = role[0] == 0
    second = role[1] == 1
    own_at = jnp.where(noisy, lay["noisy"] + HALO, lay["win"])
    halo_at = jnp.where(
        second,
        lay["noisy"],
        jnp.where(noisy, lay["noisy"] + HALO + lay["rows"], lay["win"] + lay["rows"]),
    )
    return noisy, second, pl.multiple_of(own_at, HALO), pl.multiple_of(halo_at, HALO)


def qkv_kernel(lay, role, x, xb, xc, w, b, gain, shift, cos, sin, q_out, k_out, v_out, a_out):
    width = x.shape[2]
    rows, win = lay["rows"], lay["win"]
    noisy, second, own_at, halo_at = places(lay, role)

    def norm(v):
        normed, _ = norm_stats(v.astype(F32))
        return (normed * gain[...] + shift[...]).astype(BF16)

    def zeros(at, count):
        k_out[0, at : at + count, :] = jnp.zeros((count, width), BF16)
        v_out[0, at : at + count, :] = jnp.zeros((count, width), BF16)

    def section(a, parts, table, want_q):
        def put(ref, col, value):
            for begin, count, at in parts:
                ref[0, pl.ds(at, count), col : col + value.shape[1]] = value[begin : begin + count]

        put(a_out, 0, a)
        c = cos[table : table + a.shape[0], :]
        s = sin[table : table + a.shape[0], :]
        first = 0 if want_q else width
        for col in range(first, 3 * width, 256):
            part = dot(a, w[:, col : col + 256]) + b[:, col : col + 256]
            for piece in range(2):
                u = part[:, piece * 128 : piece * 128 + 128]
                at_col = col + piece * 128
                if at_col < 2 * width:
                    u = u * c + partner(u) * s
                if at_col < width:
                    q_out[0, :, at_col : at_col + 128] = (u[:rows] * (HD**-0.5)).astype(BF16)
                elif at_col < 2 * width:
                    put(k_out, at_col - width, u.astype(BF16))
                else:
                    put(v_out, at_col - 2 * width, u.astype(BF16))

    zeros(win + rows, 2 * HALO)
    zeros(lay["keys"] - HALO, HALO)
    own = jnp.concatenate([norm(x[0]), norm(xc[0, win:, :])], axis=0)
    section(own, ((0, rows, own_at), (rows, HALO, halo_at)), win, True)

    @pl.when(noisy)
    def _():
        section(norm(xb[0]), ((0, rows, win),), win, False)

    @pl.when(jnp.logical_not(noisy))
    def _():
        zeros(lay["noisy"] + HALO, rows)

    @pl.when(second)
    def _():
        section(norm(xc[0, :win, :]), ((0, win, 0),), 0, False)

    @pl.when(jnp.logical_not(second))
    def _():
        zeros(0, win)


def windows(lay):
    rows, win, length = lay["rows"], lay["win"], lay["length"]
    longest, earliest, latest = length // 2, length // 8, 3 * length // 8
    found = []
    for at in range(0, rows, TILE):
        begin = win + rows
        for origin in range(0, length, rows):
            pos = origin + at
            low = max(pos - longest, 0)
            if origin > 0:
                low = max(low, earliest)
            if pos >= latest + longest:
                low = max(low, earliest + longest)
            begin = min(begin, low - origin + win)
        found.append((begin // TILE * TILE, win + at + TILE + HALO))
    return found


def make_bias(lay, codes, queries, biases):
    for t, (lo, hi) in enumerate(windows(lay)):
        here = slice(t * TILE, t * TILE + TILE)
        low, high, same = (queries[0, n : n + 1, here] for n in range(3))
        kc = codes[0, lo:hi, :]
        ok = (kc >= low) & (kc <= high)
        biases[t][: hi - lo, :] = jnp.where(ok, 0.0, MASKED)
        near = lay["noisy"] + t * TILE
        kn = codes[0, near : near + NEAR, :]
        biases[t][hi - lo :, :] = jnp.where(kn == same, 0.0, MASKED)


def stacked(tile):
    lane = lax.broadcasted_iota(jnp.int32, tile.shape, 1)
    zero = jnp.zeros_like(tile)
    return jnp.concatenate(
        [jnp.where(lane // HD == h, tile, zero) for h in range(QUAD)], axis=0
    )


def own_heads(wide):
    return jnp.concatenate(
        [wide[h * HD : h * HD + HD, h * TILE : h * TILE + TILE] for h in range(QUAD)], axis=0
    )


def keys_of(ref, lay, t, lo, hi):
    near = lay["noisy"] + t * TILE
    return jnp.concatenate([ref[0, lo:hi, :], ref[0, near : near + NEAR, :]], axis=0)


def attend_kernel(lay, codes, queries, q, k, v, o_out, lse_out, *biases):
    @pl.when(pl.program_id(1) == 0)
    def _():
        make_bias(lay, codes, queries, biases)

    for t, (lo, hi) in enumerate(windows(lay)):
        qm = stacked(q[0, t * TILE : t * TILE + TILE, :])
        kk = keys_of(k, lay, t, lo, hi)
        vv = keys_of(v, lay, t, lo, hi)
        s = dot_nt(kk, qm) + jnp.concatenate([biases[t][...]] * QUAD, axis=1)
        peak = jnp.max(s, axis=0, keepdims=True)
        p = jnp.exp(s - peak)
        total = jnp.sum(p, axis=0, keepdims=True)
        wide = dot_tn(vv, p.astype(BF16)) * (1.0 / total)
        o_out[0, t * TILE : t * TILE + TILE, :] = jnp.transpose(own_heads(wide)).astype(BF16)
        lse_out[0, 0, t : t + 1, :] = peak + jnp.log(total)


def attend_back_kernel(
    lay, codes, queries, q, k, v, o, do, lse, cos, sin, dq_out, dk_out, dv_out, dk_acc, dv_acc, *biases
):
    rows, win = lay["rows"], lay["win"]

    @pl.when(pl.program_id(1) == 0)
    def _():
        make_bias(lay, codes, queries, biases)

    dk_acc[...] = jnp.zeros_like(dk_acc)
    dv_acc[...] = jnp.zeros_like(dv_acc)
    for t, (lo, hi) in enumerate(windows(lay)):
        here = slice(t * TILE, t * TILE + TILE)
        size = hi - lo
        near = slice(lay["noisy"] + t * TILE, lay["noisy"] + t * TILE + NEAR)
        qm = stacked(q[0, here, :])
        dom = stacked(do[0, here, :])
        kk = keys_of(k, lay, t, lo, hi)
        vv = keys_of(v, lay, t, lo, hi)
        both = jnp.transpose(do[0, here, :].astype(F32) * o[0, here, :].astype(F32))
        delta = jnp.concatenate(
            [jnp.sum(both[h * HD : h * HD + HD, :], axis=0, keepdims=True) for h in range(QUAD)],
            axis=1,
        )
        s = dot_nt(kk, qm) + jnp.concatenate([biases[t][...]] * QUAD, axis=1)
        p = jnp.exp(s - lse[0, 0, t : t + 1, :])
        dp = dot_nt(vv, dom)
        ds = (p * (dp - delta)).astype(BF16)
        pb = p.astype(BF16)
        dv = dot(pb, dom)
        dk = dot(ds, qm)
        dv_acc[lo:hi, :] += dv[:size]
        dk_acc[lo:hi, :] += dk[:size]
        dv_acc[near, :] += dv[size:]
        dk_acc[near, :] += dk[size:]
        wide = dot_tn(kk, ds)
        dq = jnp.transpose(own_heads(wide)) * (HD**-0.5)
        c = cos[win + t * TILE : win + t * TILE + TILE, :]
        sn = sin[win + t * TILE : win + t * TILE + TILE, :]
        for piece in range(2):
            u = dq[:, piece * 128 : piece * 128 + 128]
            dq_out[0, here, piece * 128 : piece * 128 + 128] = (u * c - partner(u) * sn).astype(BF16)
    dv_out[0] = dv_acc[...].astype(BF16)
    half = (cos[win + rows :, :], sin[win + rows :, :])
    own = (cos[win : win + rows, :], sin[win : win + rows, :])
    tables = (
        (0, (cos[: win + rows, :], sin[: win + rows, :])),
        (win + rows, half),
        (lay["noisy"], half),
        (lay["noisy"] + HALO, own),
        (lay["keys"] - HALO, half),
    )
    for at, (c, sn) in tables:
        here = slice(at, at + c.shape[0])
        for piece in range(2):
            cols = slice(piece * 128, piece * 128 + 128)
            u = dk_acc[here, cols]
            dk_out[0, here, cols] = (u * c - partner(u) * sn).astype(BF16)


def mlp_kernel(
    o, x, dy, w_out, b_out, gain, shift, w_up, b_up, w_down, b_down,
    out_rows, dx2_out, do_out, g_w_out, g_w_up, g_b_up, g_w_down, g_vec,
    mid, a2, a2t, inv, acc_out, acc_da,
):
    step = pl.program_id(0)
    last = pl.num_programs(0) - 1

    @pl.when(step == 0)
    def _():
        value = x[...].astype(F32) + dot(o[...], w_out[...]) + b_out[...]
        mid[...] = value
        normed, inverse = norm_stats(value)
        inv[...] = inverse
        a = (normed * gain[...] + shift[...]).astype(BF16)
        a2[...] = a
        a2t[...] = jnp.transpose(a)
        acc_out[...] = jnp.zeros_like(acc_out)
        acc_da[...] = jnp.zeros_like(acc_da)

    u = dot(a2[...], w_up[...]) + b_up[...]
    scale = 0.7978845608028654
    square = u * u
    inner = scale * u * (1.0 + 0.044715 * square)
    th = jnp.tanh(inner)
    plus = 0.5 * (1.0 + th)
    g = (u * plus).astype(BF16)
    slope = plus + 0.5 * u * (1.0 - th * th) * (scale * (1.0 + 3 * 0.044715 * square))
    acc_out[...] += dot(g, w_down[...])
    du32 = dot_nt(dy[...], w_down[...]) * slope
    du = du32.astype(BF16)
    g_b_up[...] = jnp.broadcast_to(jnp.sum(du.astype(F32), axis=0, keepdims=True), g_b_up.shape)
    acc_da[...] += dot_nt(du, w_up[...])
    g_w_down[...] = dot_tn(g, dy[...]).astype(BF16)
    g_w_up[...] = dot(a2t[...], du).astype(BF16)

    @pl.when(step == last)
    def _():
        dyf = dy[...].astype(F32)
        out_rows[...] = (mid[...] + acc_out[...] + b_down[...]).astype(BF16)
        inverse = inv[...]
        value = mid[...]
        normed = (value - jnp.mean(value, axis=-1, keepdims=True)) * inverse
        da = acc_da[...]
        dx2 = dyf + norm_back(da, normed, inverse, gain[...])
        dx2_out[...] = dx2
        dp = dx2.astype(BF16)
        do_out[...] = dot_nt(dp, w_out[...]).astype(BF16)
        g_w_out[...] = dot_tn(o[...], dp).astype(BF16)
        g_vec[...] = jnp.concatenate(
            [
                jnp.sum(dyf, axis=0, keepdims=True),
                jnp.sum(da * normed, axis=0, keepdims=True),
                jnp.sum(da, axis=0, keepdims=True),
                jnp.sum(dp.astype(F32), axis=0, keepdims=True),
                jnp.zeros((4, dyf.shape[1]), F32),
            ],
            axis=0,
        )


def qkv_back_kernel(lay, role, a, dq, dk, dv, w, da_own, da_main, da_win, g_w, g_b, g_acc):
    width = dq.shape[2]
    rows, win = lay["rows"], lay["win"]
    noisy, second, own_at, halo_at = places(lay, role)

    @pl.when(pl.program_id(0) == 0)
    def _():
        g_acc[...] = jnp.zeros_like(g_acc)
        g_b[...] = jnp.zeros_like(g_b)

    def column_sums(col, value):
        g_b[0:1, col : col + width] += jnp.sum(value.astype(F32), axis=0, keepdims=True)

    def section(parts, query):
        def take(ref):
            return jnp.concatenate([ref[0, pl.ds(at, count), :] for at, count in parts], axis=0)

        at_t = jnp.transpose(take(a))
        key = take(dk)
        value = take(dv)
        g_acc[:, width : 2 * width] += dot(at_t, key)
        g_acc[:, 2 * width :] += dot(at_t, value)
        column_sums(width, key)
        column_sums(2 * width, value)
        total = dot_nt(key, w[:, width : 2 * width]) + dot_nt(value, w[:, 2 * width :])
        if query is not None:
            g_acc[:, :width] += dot(at_t[:, : query.shape[0]], query)
            column_sums(0, query)
            first = total[: query.shape[0]] + dot_nt(query, w[:, :width])
            return first, total[query.shape[0] :]
        return total

    own, near = section(((own_at, rows), (halo_at, HALO)), dq[0])
    da_own[0] = own
    da_win[0, win:, :] = near.astype(BF16)

    @pl.when(noisy)
    def _():
        da_main[0] = section(((win, rows),), None).astype(BF16)

    @pl.when(second)
    def _():
        da_win[0, :win, :] = section(((0, win),), None).astype(BF16)

    @pl.when(pl.program_id(0) == pl.num_programs(0) - 1)
    def _():
        g_w[...] = g_acc[...].astype(BF16)


def final_kernel(x, da, extra, dx2, gain, grad_in, g_vec):
    value = x[...].astype(F32)
    normed, inverse = norm_stats(value)
    grad = da[...] + extra[...].astype(F32)
    grad_in[...] = dx2[...] + norm_back(grad, normed, inverse, gain[...])

    @pl.when(pl.program_id(0) == 0)
    def _():
        g_vec[...] = jnp.zeros_like(g_vec)

    g_vec[0:1, :] += jnp.sum(grad * normed, axis=0, keepdims=True)
    g_vec[1:2, :] += jnp.sum(grad, axis=0, keepdims=True)


def per_device(
    inputs, segment_ids, block_ids, attn_gain, attn_shift, proj_in, bias_in, proj_out, bias_out,
    mlp_gain, mlp_shift, weight_up, bias_up, weight_down, bias_down, cotangent,
):
    micro, rows, width = inputs.shape
    length = segment_ids.shape[1]
    hidden = weight_up.shape[1]
    seq_n = lax.axis_size("seq")
    fsdp_n = lax.axis_size("fsdp")
    assert seq_n == 4 and seq_n * rows == 2 * length
    lay = layout(rows, length)
    win, keys = lay["win"], lay["keys"]
    me = lax.axis_index("seq")
    clean = me // 2
    half = me % 2
    role = jnp.stack([clean, half]).astype(jnp.int32)
    pairs = [(0, 1), (1, 0), (2, 3), (3, 2)]

    xb = lax.ppermute(inputs, "seq", [(2, 0), (3, 1)])
    xmain = jnp.where(clean == 1, inputs, xb)
    edge = jnp.where(half == 0, inputs[:, rows - HALO :], inputs[:, :HALO])
    xc = lax.ppermute(jnp.concatenate([xmain[:, rows - win :], edge], axis=1), "seq", pairs)

    start = half * rows
    edge_at = jnp.where(half == 0, rows, -HALO)
    positions = start + jnp.concatenate([jnp.arange(-win, rows), edge_at + jnp.arange(HALO)])
    freqs = 10000.0 ** (-(jnp.arange(HD // 2, dtype=F32) / (HD // 2)))
    turned = positions.astype(F32)[:, None] * freqs[None, :]
    cosine, sine = jnp.cos(turned), jnp.sin(turned)
    cos = jnp.concatenate([cosine] * 4, axis=1)
    sin = jnp.concatenate([-sine, sine] * 2, axis=1)

    code = segment_ids * SEG_STEP + block_ids
    padded = jnp.pad(code, ((0, 0), (win, 0)), constant_values=-1)
    key_codes = lax.dynamic_slice_in_dim(padded, start, win + rows, 1)
    own_code = lax.dynamic_slice_in_dim(code, start, rows, 1)
    own_seg = lax.dynamic_slice_in_dim(segment_ids, start, rows, 1)
    before, after = code[:, rows - HALO : rows], code[:, rows : rows + HALO]
    codes = jnp.concatenate(
        [
            key_codes,
            jnp.where((clean == 1) & (half == 0), after, -1),
            jnp.where((clean == 0) & (half == 1), before, -2),
            jnp.where(clean == 0, own_code, -2),
            jnp.where((clean == 0) & (half == 0), after, -2),
        ],
        axis=1,
    )[:, :, None]
    queries = jnp.stack([own_seg * SEG_STEP, own_code - (1 - clean), own_code], axis=1)
    queries = jnp.concatenate([queries, jnp.zeros((micro, 5, rows), jnp.int32)], axis=1)

    small = (attn_gain, attn_shift, bias_in, bias_out, mlp_gain, mlp_shift, bias_up, bias_down)
    sizes = [p.shape[0] for p in small]
    packed = lax.all_gather(jnp.concatenate(small)[None], "fsdp", axis=0, tiled=True)
    vectors, at = [], 0
    for size in sizes:
        vectors.append(packed[:, at : at + size].reshape(1, -1).astype(F32))
        at += size
    gain1, shift1, b_in, b_out, gain2, shift2, b_up, b_down = vectors
    w_in, w_out, w_up, w_down = (
        lax.all_gather(p, "fsdp", axis=0, tiled=True)
        for p in (proj_in, proj_out, weight_up, weight_down)
    )

    quads = width // (QUAD * HD)
    qw = QUAD * HD
    spans = [hi - lo + NEAR for lo, hi in windows(lay)]
    bias_scratch = [pltpu.VMEM((n, TILE), F32) for n in spans]
    per_seq = lambda n, d: pl.BlockSpec((1, n, d), lambda s: (s, 0, 0))
    role_spec = SMEM()

    q, k, v, a = call(
        functools.partial(qkv_kernel, lay), (micro,),
        [role_spec, per_seq(rows, width), per_seq(rows, width), per_seq(win + HALO, width),
         whole((width, 3 * width)), whole((1, 3 * width)), whole((1, width)), whole((1, width)),
         whole((win + rows + HALO, 128)), whole((win + rows + HALO, 128))],
        [per_seq(rows, width), per_seq(keys, width), per_seq(keys, width), per_seq(keys, width)],
        [like((micro, rows, width), BF16)] + [like((micro, keys, width), BF16)] * 3,
        [], 2 * micro * rows * width * 3 * width * 2, 20 << 20, "qkv",
    )(role, inputs, xb, xc, w_in, b_in, gain1, shift1, cos, sin)

    quad_block = lambda n: pl.BlockSpec((1, n, qw), lambda s, h: (s, 0, h))
    code_spec = pl.BlockSpec((1, keys, 1), lambda s, h: (s, 0, 0))
    query_spec = pl.BlockSpec((1, 8, rows), lambda s, h: (s, 0, 0))
    lse_spec = pl.BlockSpec((1, 1, rows // TILE, QUAD * TILE), lambda s, h: (s, h, 0, 0))
    attn_flops = micro * quads * sum(spans) * QUAD * TILE * qw * 2
    o, lse = call(
        functools.partial(attend_kernel, lay), (micro, quads),
        [code_spec, query_spec, quad_block(rows), quad_block(keys), quad_block(keys)],
        [quad_block(rows), lse_spec],
        [like((micro, rows, width), BF16), like((micro, quads, rows // TILE, QUAD * TILE), F32)],
        bias_scratch, 2 * attn_flops, 12 << 20, "attend",
    )(codes, queries, q, k, v)

    total = micro * rows
    flat = lambda z: z.reshape(total, width)
    chunk = min(512, hidden)
    vec = whole((1, width))
    rows_spec = whole((total, width))
    out_rows, dx2, do, g_w_out, g_w_up, g_b_up, g_w_down, g_mlp = call(
        mlp_kernel, (hidden // chunk,),
        [rows_spec, rows_spec, rows_spec, whole((width, width)), vec, vec, vec,
         pl.BlockSpec((width, chunk), lambda j: (0, j)), pl.BlockSpec((1, chunk), lambda j: (0, j)),
         pl.BlockSpec((chunk, width), lambda j: (j, 0)), vec],
        [rows_spec, rows_spec, rows_spec, whole((width, width)),
         pl.BlockSpec((width, chunk), lambda j: (0, j)), pl.BlockSpec((8, chunk), lambda j: (0, j)),
         pl.BlockSpec((chunk, width), lambda j: (j, 0)), whole((8, width))],
        [like((total, width), BF16), like((total, width), F32), like((total, width), BF16),
         like((width, width), BF16), like((width, hidden), BF16), like((8, hidden), F32),
         like((hidden, width), BF16), like((8, width), F32)],
        [pltpu.VMEM((total, width), F32), pltpu.VMEM((total, width), BF16), pltpu.VMEM((width, total), BF16),
         pltpu.VMEM((total, 1), F32), pltpu.VMEM((total, width), F32), pltpu.VMEM((total, width), F32)],
        2 * total * width * (6 * hidden + 3 * width), 40 << 20, "mlp",
    )(flat(o), flat(inputs), flat(cotangent), w_out, b_out, gain2, shift2, w_up, b_up, w_down, b_down)

    seqs = lambda z: z.reshape(micro, rows, width)
    table = pl.BlockSpec((win + rows + HALO, 128), lambda s, h: (0, 0), pipeline_mode=pl.Buffered(1))
    dq, dk, dv = call(
        functools.partial(attend_back_kernel, lay), (micro, quads),
        [code_spec, query_spec, quad_block(rows), quad_block(keys), quad_block(keys),
         quad_block(rows), quad_block(rows), lse_spec, table, table],
        [quad_block(rows), quad_block(keys), quad_block(keys)],
        [like((micro, rows, width), BF16), like((micro, keys, width), BF16), like((micro, keys, width), BF16)],
        [pltpu.VMEM((keys, qw), F32), pltpu.VMEM((keys, qw), F32)] + bias_scratch,
        5 * attn_flops, 24 << 20, "attend_back",
    )(codes, queries, q, k, v, o, seqs(do), lse, cos, sin)

    da_own, da_main, da_win, g_w_in, g_b_in = call(
        functools.partial(qkv_back_kernel, lay), (micro,),
        [role_spec, per_seq(keys, width), per_seq(rows, width), per_seq(keys, width), per_seq(keys, width),
         whole((width, 3 * width))],
        [per_seq(rows, width), per_seq(rows, width), per_seq(win + HALO, width),
         whole((width, 3 * width)), whole((8, 3 * width))],
        [like((micro, rows, width), F32), like((micro, rows, width), BF16), like((micro, win + HALO, width), BF16),
         like((width, 3 * width), BF16), like((8, 3 * width), F32)],
        [pltpu.VMEM((width, 3 * width), F32)], 2 * 2 * micro * rows * width * 3 * width * 2, 40 << 20, "qkv_back",
    )(role, a, dq, dk, dv, w_in)

    from_pair = lax.ppermute(da_win, "seq", pairs).astype(F32)
    from_second = jnp.where(half == 0, from_pair[:, :win], 0.0)
    edge = from_pair[:, win:]
    gap = jnp.zeros((micro, rows - HALO, width), F32)
    edges = jnp.where(
        half == 0, jnp.concatenate([gap, edge], axis=1), jnp.concatenate([edge, gap], axis=1)
    )
    added = jnp.pad(from_second, ((0, 0), (rows - win, 0), (0, 0)))
    to_clean = (jnp.where(clean == 0, da_main.astype(F32), 0.0) + added).astype(BF16)
    from_noisy = lax.ppermute(to_clean, "seq", [(0, 2), (1, 3)])
    extra = jnp.where(clean == 1, from_noisy.astype(F32) + added, 0.0) + edges

    grad_in, g_attn = call(
        final_kernel, (2,),
        [pl.BlockSpec((total // 2, width), lambda i: (i, 0))] * 4 + [vec],
        [pl.BlockSpec((total // 2, width), lambda i: (i, 0)), whole((8, width))],
        [like((total, width), F32), like((8, width), F32)], [], 0, 16 << 20, "norm_back",
    )(flat(inputs), flat(da_own), flat(extra), dx2, gain1)

    def scatter(g):
        return lax.psum(lax.psum_scatter(g, "fsdp", scatter_dimension=0, tiled=True), "seq")

    big = [scatter(g).astype(F32) for g in (g_w_in, g_w_out, g_w_up, g_w_down)]
    smalls = [g_attn[0], g_attn[1], g_b_in[0], g_mlp[3], g_mlp[1], g_mlp[2], g_b_up[0], g_mlp[0]]
    pack = jnp.concatenate([g.reshape(fsdp_n, -1) for g in smalls], axis=1)
    pack = lax.psum(pack, ("seq", "fsdp"))
    mine = lax.dynamic_slice_in_dim(pack, lax.axis_index("fsdp"), 1, 0)[0]
    outs, at = [], 0
    for size in sizes:
        outs.append(mine[at : at + size])
        at += size
    g_gain1, g_shift1, g_bin, g_bout, g_gain2, g_shift2, g_bup, g_bdown = outs
    return (
        seqs(out_rows), seqs(grad_in), g_gain1, g_shift1, big[0], g_bin, big[1], g_bout,
        g_gain2, g_shift2, big[2], g_bup, big[3], g_bdown,
    )


def solution(mesh):
    rows = P("fsdp", "seq", None)
    one, two = P("fsdp"), P("fsdp", None)
    params = (one, one, two, one, two, one, one, one, two, one, two, one)
    return jax.shard_map(
        per_device,
        mesh=mesh,
        in_specs=(rows, two, two) + params + (rows,),
        out_specs=(rows, rows) + params,
        check_vma=False,
    )
```

```python
import functools
import math

import jax
import jax.numpy as jnp
import numpy as np
from jax import lax
from jax.experimental import pallas as pl
from jax.experimental.pallas import tpu as pltpu
from jax.sharding import PartitionSpec as P

HD = 64
QUAD = 4
TILE = 128
HALO = 16
NEAR = TILE + 2 * HALO
EPS = 1e-05
MASKED = -1e30
SEG_STEP = 4096
F32 = jnp.float32
BF16 = jnp.bfloat16
VMEM_BYTES = 62 * 1024 * 1024
MESH = pl.DeviceIdType.MESH
ANY = pl.BlockSpec(memory_space=pl.ANY)
VMEM = pl.BlockSpec(memory_space=pltpu.VMEM)


def dot(a, b):
    return jnp.dot(a, b, preferred_element_type=F32)


def dot_nt(a, b):
    return lax.dot_general(a, b, (((1,), (1,)), ((), ())), preferred_element_type=F32)


def dot_tn(a, b):
    return lax.dot_general(a, b, (((0,), (0,)), ((), ())), preferred_element_type=F32)


def norm_stats(x):
    center = jnp.mean(x, axis=-1, keepdims=True)
    centered = x - center
    inverse = lax.rsqrt(jnp.mean(centered * centered, axis=-1, keepdims=True) + EPS)
    return centered * inverse, inverse


def norm_back(grad, normed, inverse, gain):
    scaled = grad * gain
    first = jnp.mean(scaled, axis=-1, keepdims=True)
    second = jnp.mean(scaled * normed, axis=-1, keepdims=True)
    return inverse * (scaled - first - normed * second)


def partner(u):
    lane = lax.broadcasted_iota(jnp.int32, u.shape, 1)
    half = HD // 2
    return jnp.where(
        lane % HD < half, pltpu.roll(u, u.shape[1] - half, 1), pltpu.roll(u, half, 1)
    )


def whole(shape):
    return pl.BlockSpec(shape, lambda *_: (0,) * len(shape), pipeline_mode=pl.Buffered(1))


def call(kernel, grid, in_specs, out_specs, out_shape, scratch, flops, nbytes, name):
    return pl.pallas_call(
        kernel,
        grid=grid,
        in_specs=in_specs,
        out_specs=out_specs,
        out_shape=out_shape,
        scratch_shapes=scratch,
        compiler_params=pltpu.CompilerParams(vmem_limit_bytes=VMEM_BYTES),
        cost_estimate=pl.CostEstimate(flops=flops, bytes_accessed=nbytes, transcendentals=0),
        name=name,
    )


def like(shape, dtype):
    return jax.ShapeDtypeStruct(shape, dtype)


SMEM = functools.partial(pl.BlockSpec, memory_space=pltpu.SMEM)


def layout(rows, length):
    win = rows - length // 8
    noisy = win + rows + HALO
    return dict(rows=rows, win=win, length=length, noisy=noisy, keys=noisy + rows + 2 * HALO)


def places(lay, role):
    noisy = role[0] == 0
    second = role[1] == 1
    own_at = jnp.where(noisy, lay["noisy"] + HALO, lay["win"])
    halo_at = jnp.where(
        second,
        lay["noisy"],
        jnp.where(noisy, lay["noisy"] + HALO + lay["rows"], lay["win"] + lay["rows"]),
    )
    return noisy, second, pl.multiple_of(own_at, HALO), pl.multiple_of(halo_at, HALO)


def qkv_rows(lay, where_am, n, x, xb, xc, w, b, gain, shift, cos, sin, q_out, k_out, v_out, a_out):
    width = x.shape[2]
    rows, win = lay["rows"], lay["win"]
    noisy, second, own_at, halo_at = where_am

    def norm(v):
        normed, _ = norm_stats(v.astype(F32))
        return (normed * gain + shift).astype(BF16)

    def zeros(at, count):
        k_out[n, at : at + count, :] = jnp.zeros((count, width), BF16)
        v_out[n, at : at + count, :] = jnp.zeros((count, width), BF16)

    def section(a, parts, table, want_q):
        def put(ref, col, value):
            for begin, count, at in parts:
                ref[n, pl.ds(at, count), col : col + value.shape[1]] = value[begin : begin + count]

        put(a_out, 0, a)
        c = cos[table : table + a.shape[0], :]
        s = sin[table : table + a.shape[0], :]
        first = 0 if want_q else width
        for col in range(first, 3 * width, 256):
            part = dot(a, w[:, col : col + 256]) + b[:, col : col + 256]
            for piece in range(2):
                u = part[:, piece * 128 : piece * 128 + 128]
                at_col = col + piece * 128
                if at_col < 2 * width:
                    u = u * c + partner(u) * s
                if at_col < width:
                    q_out[n, :, at_col : at_col + 128] = (u[:rows] * (HD**-0.5)).astype(BF16)
                elif at_col < 2 * width:
                    put(k_out, at_col - width, u.astype(BF16))
                else:
                    put(v_out, at_col - 2 * width, u.astype(BF16))

    zeros(win + rows, 2 * HALO)
    zeros(lay["keys"] - HALO, HALO)
    own = jnp.concatenate([norm(x[n]), norm(xc[n, win:, :])], axis=0)
    section(own, ((0, rows, own_at), (rows, HALO, halo_at)), win, True)

    @pl.when(noisy)
    def _():
        section(norm(xb[n]), ((0, rows, win),), win, False)

    @pl.when(jnp.logical_not(noisy))
    def _():
        zeros(lay["noisy"] + HALO, rows)

    @pl.when(second)
    def _():
        section(norm(xc[n, :win, :]), ((0, win, 0),), 0, False)

    @pl.when(jnp.logical_not(second))
    def _():
        zeros(0, win)


def qkv_kernel(lay, role, x, xb, xc, w, vec, cos, sin, *outs):
    width = x.shape[2]
    gain, shift, b = vec[0:1, :width], vec[1:2, :width], vec[2:3, : 3 * width]
    qkv_rows(lay, places(lay, role), 0, x, xb, xc, w, b, gain, shift, cos, sin, *outs)


def windows(lay):
    rows, win, length = lay["rows"], lay["win"], lay["length"]
    longest, earliest, latest = length // 2, length // 8, 3 * length // 8
    found = []
    for at in range(0, rows, TILE):
        begin = win + rows
        for origin in range(0, length, rows):
            pos = origin + at
            low = max(pos - longest, 0)
            if origin > 0:
                low = max(low, earliest)
            if pos >= latest + longest:
                low = max(low, earliest + longest)
            begin = min(begin, low - origin + win)
        found.append((begin // TILE * TILE, win + at + TILE + HALO))
    return found


def make_bias(lay, n, codes, queries, biases):
    for t, (lo, hi) in enumerate(windows(lay)):
        here = slice(t * TILE, t * TILE + TILE)
        low, high, same = (queries[n, r : r + 1, here] for r in range(3))
        kc = codes[n, lo:hi, :]
        ok = (kc >= low) & (kc <= high)
        biases[t][: hi - lo, :] = jnp.where(ok, 0.0, MASKED)
        near = lay["noisy"] + t * TILE
        kn = codes[n, near : near + NEAR, :]
        biases[t][hi - lo :, :] = jnp.where(kn == same, 0.0, MASKED)


def stacked(tile):
    lane = lax.broadcasted_iota(jnp.int32, tile.shape, 1)
    zero = jnp.zeros_like(tile)
    return jnp.concatenate(
        [jnp.where(lane // HD == h, tile, zero) for h in range(QUAD)], axis=0
    )


def own_heads(wide):
    return jnp.concatenate(
        [wide[h * HD : h * HD + HD, h * TILE : h * TILE + TILE] for h in range(QUAD)], axis=0
    )


def keys_of(ref, lay, n, cols, t, lo, hi):
    near = lay["noisy"] + t * TILE
    return jnp.concatenate([ref[n, lo:hi, cols], ref[n, near : near + NEAR, cols]], axis=0)


def attend(lay, n, cols, q, k, v, o_out, lse_out, lse_at, biases):
    for t, (lo, hi) in enumerate(windows(lay)):
        here = slice(t * TILE, t * TILE + TILE)
        qm = stacked(q[n, here, cols])
        kk = keys_of(k, lay, n, cols, t, lo, hi)
        vv = keys_of(v, lay, n, cols, t, lo, hi)
        s = dot_nt(kk, qm) + jnp.concatenate([biases[t][...]] * QUAD, axis=1)
        peak = jnp.max(s, axis=0, keepdims=True)
        p = jnp.exp(s - peak)
        total = jnp.sum(p, axis=0, keepdims=True)
        wide = dot_tn(vv, p.astype(BF16)) * (1.0 / total)
        o_out[n, here, cols] = jnp.transpose(own_heads(wide)).astype(BF16)
        lse_out[lse_at, t : t + 1, :] = peak + jnp.log(total)


def attend_kernel(lay, codes, queries, q, k, v, o_out, lse_out, *biases):
    @pl.when(pl.program_id(1) == 0)
    def _():
        make_bias(lay, 0, codes, queries, biases)

    attend(lay, 0, slice(None), q, k, v, o_out, lse_out, 0, biases)


def attend_back_kernel(
    lay, codes, queries, q, k, v, o, do, lse, cos, sin, dq_out, dk_out, dv_out, dk_acc, dv_acc, *biases
):
    rows, win = lay["rows"], lay["win"]

    @pl.when(pl.program_id(1) == 0)
    def _():
        make_bias(lay, 0, codes, queries, biases)

    dk_acc[...] = jnp.zeros_like(dk_acc)
    dv_acc[...] = jnp.zeros_like(dv_acc)
    for t, (lo, hi) in enumerate(windows(lay)):
        here = slice(t * TILE, t * TILE + TILE)
        size = hi - lo
        near = slice(lay["noisy"] + t * TILE, lay["noisy"] + t * TILE + NEAR)
        qm = stacked(q[0, here, :])
        dom = stacked(do[0, here, :])
        kk = keys_of(k, lay, 0, slice(None), t, lo, hi)
        vv = keys_of(v, lay, 0, slice(None), t, lo, hi)
        both = jnp.transpose(do[0, here, :].astype(F32) * o[0, here, :].astype(F32))
        delta = jnp.concatenate(
            [jnp.sum(both[h * HD : h * HD + HD, :], axis=0, keepdims=True) for h in range(QUAD)],
            axis=1,
        )
        s = dot_nt(kk, qm) + jnp.concatenate([biases[t][...]] * QUAD, axis=1)
        p = jnp.exp(s - lse[0, t : t + 1, :])
        dp = dot_nt(vv, dom)
        ds = (p * (dp - delta)).astype(BF16)
        pb = p.astype(BF16)
        dv = dot(pb, dom)
        dk = dot(ds, qm)
        dv_acc[lo:hi, :] += dv[:size]
        dk_acc[lo:hi, :] += dk[:size]
        dv_acc[near, :] += dv[size:]
        dk_acc[near, :] += dk[size:]
        wide = dot_tn(kk, ds)
        dq = jnp.transpose(own_heads(wide)) * (HD**-0.5)
        c = cos[win + t * TILE : win + t * TILE + TILE, :]
        sn = sin[win + t * TILE : win + t * TILE + TILE, :]
        for piece in range(2):
            u = dq[:, piece * 128 : piece * 128 + 128]
            dq_out[0, here, piece * 128 : piece * 128 + 128] = (u * c - partner(u) * sn).astype(BF16)
    dv_out[0] = dv_acc[...].astype(BF16)
    half = (cos[win + rows :, :], sin[win + rows :, :])
    own = (cos[win : win + rows, :], sin[win : win + rows, :])
    tables = (
        (0, (cos[: win + rows, :], sin[: win + rows, :])),
        (win + rows, half),
        (lay["noisy"], half),
        (lay["noisy"] + HALO, own),
        (lay["keys"] - HALO, half),
    )
    for at, (c, sn) in tables:
        here = slice(at, at + c.shape[0])
        for piece in range(2):
            cols = slice(piece * 128, piece * 128 + 128)
            u = dk_acc[here, cols]
            dk_out[0, here, cols] = (u * c - partner(u) * sn).astype(BF16)


def bit_of(index, b):
    return (index // (1 << b)) % 2


def other(index, b):
    return index + (1 << b) * (1 - 2 * bit_of(index, b))


class Net:
    def __init__(self, bits, send, recv, sems):
        self.me, self.f, self.bits = lax.axis_index("seq"), lax.axis_index("fsdp"), bits
        self.core, self.x = self.me % 2, self.me // 2
        self.send, self.recv, self.sems = send, recv, sems
        self.used, self.local_used = 0, 0
        self.started = []

    def partners(self):
        return [{"seq": other(self.me, 0)}, {"seq": other(self.me, 1)}] + [
            {"fsdp": other(self.f, b)} for b in range(self.bits)
        ]

    def barrier(self):
        barrier = pltpu.get_barrier_semaphore()
        for device in self.partners():
            pl.semaphore_signal(barrier, inc=1, device_id=device, device_id_type=MESH)
        pl.semaphore_wait(barrier, 2 + self.bits)

    def copy(self, src, dst, device):
        n = self.used
        self.used += 1
        return pltpu.make_async_remote_copy(
            src_ref=src, dst_ref=dst, send_sem=self.send.at[n], recv_sem=self.recv.at[n],
            device_id=device, device_id_type=MESH,
        )

    def local(self, src, dst):
        n = self.local_used
        self.local_used += 1
        return pltpu.make_async_copy(src, dst, self.sems.at[n])

    def fsdp_index(self, b):
        return (slice(None),) * (self.bits - 1 - b) + tuple(
            bit_of(self.f, low) for low in range(b, -1, -1)
        )


class Gather:
    def __init__(self, net, own, full, tail, tail_x=None, tail_core=None):
        self.net, self.at = net, 0
        mine = net.fsdp_index(net.bits - 1)
        self.own = net.local(own.at[tail], full.at[mine + tail])
        self.stages = []
        for b in range(net.bits - 1, -1, -1):
            here = full.at[net.fsdp_index(b) + tail]
            src = own.at[tail] if b == net.bits - 1 else here
            self.stages.append(net.copy(src, here, {"fsdp": other(net.f, b)}))
        everything = (slice(None),) * net.bits
        for region, b in ((tail_x, 1), (tail_core, 0)):
            if region is not None:
                here = full.at[everything + region]
                self.stages.append(net.copy(here, here, {"seq": other(net.me, b)}))

    def advance(self):
        if self.at == 0:
            self.own.start()
        else:
            self.stages[self.at - 1].wait_recv()
        if self.at == 1:
            self.own.wait()
        if self.at < len(self.stages):
            self.stages[self.at].start()
        self.at += 1

    def finish(self):
        for stage in self.stages:
            stage.wait_send()


def front_kernel(
    lay, bits, sizes, x, seg, blk, pack, freqs, w_in_s, w_out_s, w_up_s, w_down_s,
    w_in, w_out, w_up, w_down, q_out, k_out, v_out, a_out, o_out, lse_out, vec, cos, sin, codes, queries,
    xb, xc, w_vm, q, k, v, a, o, lse, packs, send, recv, sems, *biases,
):
    rows, win, length = lay["rows"], lay["win"], lay["length"]
    width = x.shape[2]
    hidden = w_up_s.shape[1]
    micro = x.shape[0]
    net = Net(bits, send, recv, sems)
    role = (net.x, net.core)
    where_am = noisy, second, _, _ = places(lay, role)
    first = jnp.logical_not(second)
    clean = jnp.logical_not(noisy)
    net.barrier()

    pair, across = {"seq": other(net.me, 0)}, {"seq": other(net.me, 1)}
    rows_across = [net.copy(x.at[n], xb.at[n], across) for n in range(micro)]
    window = (pl.ds(rows - win, win), slice(None))
    target = (pl.ds(0, win), slice(None))
    rows_pair, rows_pair_b = [], []
    for n in range(micro):
        at = net.used
        rows_pair.append(net.copy(x.at[(n,) + window], xc.at[(n,) + target], pair))
        net.used = at
        rows_pair_b.append(net.copy(xb.at[(n,) + window], xc.at[(n,) + target], pair))
    edge_at = pl.multiple_of((1 - net.core) * (rows - HALO), HALO)
    edge = net.copy(x.at[:, pl.ds(edge_at, HALO), :], xc.at[:, pl.ds(win, HALO), :], pair)

    def columns(begin, size):
        return (slice(None), pl.ds(pl.multiple_of(begin, 128), size))

    small = Gather(net, pack, packs, (slice(None), slice(None)))
    half_in, half_out, half_up = 3 * width // 2, width // 2, hidden // 2
    third = half_in // 3
    ins = [
        Gather(net, w_in_s, w_in, columns(net.core * half_in + n * third, third), None,
               columns(net.core * half_in + n * third, third))
        for n in range(3)
    ]
    out = Gather(net, w_out_s, w_out, columns(net.core * half_out, half_out), None,
                 columns(net.core * half_out, half_out))
    quarter = half_up // 2
    up = Gather(net, w_up_s, w_up, columns(net.core * half_up + net.x * quarter, quarter),
                columns(net.core * half_up + net.x * quarter, quarter),
                columns(net.core * half_up, half_up))
    slab = w_down_s.shape[0]
    downs = []
    for n in range(2):
        region = (pl.ds(pl.multiple_of(net.core * (slab // 2) + n * (slab // 4), HALO), slab // 4), slice(None))
        downs.append(Gather(net, w_down_s, w_down, region, None, region))
    down0, down1 = downs

    ins[0].advance()
    small.advance()

    @pl.when(clean)
    def _():
        rows_across[0].start()

    edge.start()
    ins[1].advance()
    ins[2].advance()

    position = lax.broadcasted_iota(jnp.int32, (win + rows + HALO, 128), 0)
    shifted = jnp.where(
        position < win + rows, position - win, position - win - rows + jnp.where(second, -HALO, rows)
    )
    turned = (shifted + jnp.where(second, rows, 0)).astype(F32) * freqs[...]
    lane = lax.broadcasted_iota(jnp.int32, (win + rows + HALO, 128), 1)
    cos[...] = jnp.cos(turned)
    sine = jnp.sin(turned)
    sin[...] = jnp.where(lane % HD < HD // 2, -sine, sine)
    code = (seg[...] * SEG_STEP + blk[...]).astype(F32)
    base = (seg[...] * SEG_STEP).astype(F32)
    turned_code = jnp.transpose(jnp.concatenate([code, jnp.zeros((8 - micro, length), F32)], axis=0))
    lay_noisy = lay["noisy"]
    for n in range(micro):
        col = turned_code[:, n : n + 1]
        none = lambda count, value: jnp.full((count, 1), value, F32)
        codes[n, :win, :] = jnp.where(second, col[rows - win : rows], -1.0)
        codes[n, win : win + rows, :] = jnp.where(second, col[rows:], col[:rows])
        after, before = col[rows : rows + HALO], col[rows - HALO : rows]
        codes[n, win + rows : lay_noisy, :] = jnp.where(jnp.logical_and(clean, first), after, -1.0)
        codes[n, lay_noisy : lay_noisy + HALO, :] = jnp.where(jnp.logical_and(noisy, second), before, -2.0)
        codes[n, lay_noisy + HALO : lay_noisy + HALO + rows, :] = jnp.where(
            noisy, jnp.where(second, col[rows:], col[:rows]), -2.0
        )
        codes[n, lay["keys"] - HALO :, :] = jnp.where(jnp.logical_and(noisy, first), after, -2.0)
        own_code = jnp.where(second, code[n : n + 1, rows:], code[n : n + 1, :rows])
        own_base = jnp.where(second, base[n : n + 1, rows:], base[n : n + 1, :rows])
        high = own_code - jnp.where(noisy, 1.0, 0.0)
        queries[n] = jnp.concatenate([own_base, high, own_code, jnp.zeros((5, rows), F32)], axis=0)

    small.advance()
    ins[0].advance()
    ins[1].advance()
    small.advance()
    ins[0].advance()
    ins[2].advance()
    small.advance()

    count = 1 << bits
    long_in, long_up = sizes[2] * count, sizes[6] * count
    spread = {}
    for size in sorted(set(sizes)):
        total = jnp.zeros((8, size * count), F32)
        for n in range(count):
            at = tuple((n >> b) & 1 for b in range(bits - 1, -1, -1))
            piece = packs[at]
            wide = size * count - piece.shape[1]
            if wide > 0:
                piece = jnp.concatenate([piece, jnp.zeros((8, wide), F32)], axis=1)
            lanes = lax.broadcasted_iota(jnp.int32, piece.shape, 1)
            piece = jnp.where(lanes < size, piece, 0.0)
            total += pltpu.roll(piece, n * size, 1) if n else piece
        spread[size] = total
    for r, size in enumerate(sizes):
        vec[r : r + 1, : size * count] = spread[size][r : r + 1]
        if size * count < vec.shape[1]:
            vec[r : r + 1, size * count :] = jnp.zeros((1, vec.shape[1] - size * count), F32)

    ins[1].advance()
    up.advance()
    ins[0].advance()
    ins[2].advance()

    def pass_on(n):
        @pl.when(noisy)
        def _():
            rows_across[n].wait_recv()

        @pl.when(jnp.logical_and(first, noisy))
        def _():
            rows_pair_b[n].start()

        @pl.when(jnp.logical_and(first, clean))
        def _():
            rows_pair[n].start()

    @pl.when(clean)
    def _():
        rows_across[1].start()

    pass_on(0)
    ins[1].advance()
    up.advance()
    out.advance()
    ins[2].advance()
    for n in range(3):
        ins[n].advance()
    loads = []
    for n in range(count):
        at = tuple((n >> b) & 1 for b in range(bits - 1, -1, -1))
        loads.append(net.local(w_in.at[at], w_vm.at[pl.ds(n * w_in_s.shape[0], w_in_s.shape[0]), :]))
    for load in loads:
        load.start()
    edge.wait_recv()
    up.advance()
    out.advance()
    down0.advance()
    for load in loads:
        load.wait()

    gain, shift, b_in = vec[0:1, :width], vec[1:2, :width], vec[2:3, : 3 * width]

    def qkv(n):
        @pl.when(second)
        def _():
            rows_pair[n].wait_recv()

        qkv_rows(lay, where_am, n, x, xb, xc, w_vm, b_in, gain, shift, cos, sin, q, k, v, a)
        stores = [
            net.local(here.at[n], there.at[n])
            for here, there in ((q, q_out), (k, k_out), (v, v_out), (a, a_out))
        ]
        for store in stores:
            store.start()
        return stores

    stores = qkv(0)
    down0.advance()
    out.advance()
    pass_on(1)
    down1.advance()
    stores += qkv(1)

    quads = width // (QUAD * HD)
    plan = ((up, down0, out), (down1,), (down0, down1), (up,), (out, down0, down1), (up,))
    assert micro * quads == len(plan)

    def step(index, carry):
        n, h = index // quads, index % quads

        @pl.when(h == 0)
        def _():
            make_bias(lay, n, codes, queries, biases)

        cols = pl.ds(pl.multiple_of(h * QUAD * HD, QUAD * HD), QUAD * HD)
        attend(lay, n, cols, q, k, v, o, lse, index, biases)
        for at, chunks in enumerate(plan):

            @pl.when(index == at)
            def _():
                for chunk in chunks:
                    chunk.advance()

        return carry

    lax.fori_loop(0, micro * quads, step, 0)
    last = [net.local(o, o_out), net.local(lse, lse_out)]
    for store in last:
        store.start()
    chunks = [small, out, up, down0, down1] + ins
    for chunk in chunks:
        while chunk.at <= len(chunk.stages):
            chunk.advance()
    for chunk in chunks:
        chunk.finish()
    for store in stores + last:
        store.wait()
    edge.wait_send()

    @pl.when(clean)
    def _():
        for n in range(micro):
            rows_across[n].wait_send()

    @pl.when(first)
    def _():
        for n in range(micro):
            rows_pair[n].wait_send()


def mlp_kernel(
    o, x, dy, w_out, vec, w_up, b_up, w_down,
    out_rows, dx2_out, do_out, g_w_out, g_w_up, g_b_up, g_w_down, g_vec,
    mid, a2, a2t, inv, acc_out, acc_da,
):
    step = pl.program_id(0)
    last = pl.num_programs(0) - 1
    width = x.shape[1]
    b_out, gain, shift, b_down = (vec[r : r + 1, :width] for r in (3, 4, 5, 7))

    @pl.when(step == 0)
    def _():
        value = x[...].astype(F32) + dot(o[...], w_out[...]) + b_out
        mid[...] = value
        normed, inverse = norm_stats(value)
        inv[...] = inverse
        a = (normed * gain + shift).astype(BF16)
        a2[...] = a
        a2t[...] = jnp.transpose(a)
        acc_out[...] = jnp.zeros_like(acc_out)
        acc_da[...] = jnp.zeros_like(acc_da)

    u = dot(a2[...], w_up[...]) + b_up[6:7, :]
    scale = 0.7978845608028654
    square = u * u
    inner = scale * u * (1.0 + 0.044715 * square)
    th = jnp.tanh(inner)
    plus = 0.5 * (1.0 + th)
    g = (u * plus).astype(BF16)
    slope = plus + 0.5 * u * (1.0 - th * th) * (scale * (1.0 + 3 * 0.044715 * square))
    acc_out[...] += dot(g, w_down[...])
    du32 = dot_nt(dy[...], w_down[...]) * slope
    du = du32.astype(BF16)
    g_b_up[...] = jnp.broadcast_to(jnp.sum(du.astype(F32), axis=0, keepdims=True), g_b_up.shape)
    acc_da[...] += dot_nt(du, w_up[...])
    g_w_down[...] = dot_tn(g, dy[...]).astype(BF16)
    g_w_up[...] = dot(a2t[...], du).astype(BF16)

    @pl.when(step == last)
    def _():
        dyf = dy[...].astype(F32)
        out_rows[...] = (mid[...] + acc_out[...] + b_down).astype(BF16)
        inverse = inv[...]
        value = mid[...]
        normed = (value - jnp.mean(value, axis=-1, keepdims=True)) * inverse
        da = acc_da[...]
        dx2 = dyf + norm_back(da, normed, inverse, gain)
        dx2_out[...] = dx2
        dp = dx2.astype(BF16)
        do_out[...] = dot_nt(dp, w_out[...]).astype(BF16)
        g_w_out[...] = dot_tn(o[...], dp).astype(BF16)
        g_vec[...] = jnp.concatenate(
            [
                jnp.sum(dyf, axis=0, keepdims=True),
                jnp.sum(da * normed, axis=0, keepdims=True),
                jnp.sum(da, axis=0, keepdims=True),
                jnp.sum(dp.astype(F32), axis=0, keepdims=True),
                jnp.zeros((4, dyf.shape[1]), F32),
            ],
            axis=0,
        )


def qkv_back_kernel(lay, role, a, dq, dk, dv, w, da_own, da_main, da_win, g_w, g_b, g_acc):
    width = dq.shape[2]
    rows, win = lay["rows"], lay["win"]
    noisy, second, own_at, halo_at = places(lay, role)

    @pl.when(pl.program_id(0) == 0)
    def _():
        g_acc[...] = jnp.zeros_like(g_acc)
        g_b[...] = jnp.zeros_like(g_b)

    def column_sums(col, value):
        g_b[0:1, col : col + width] += jnp.sum(value.astype(F32), axis=0, keepdims=True)

    def section(parts, query):
        def take(ref):
            return jnp.concatenate([ref[0, pl.ds(at, count), :] for at, count in parts], axis=0)

        at_t = jnp.transpose(take(a))
        key = take(dk)
        value = take(dv)
        g_acc[:, width : 2 * width] += dot(at_t, key)
        g_acc[:, 2 * width :] += dot(at_t, value)
        column_sums(width, key)
        column_sums(2 * width, value)
        total = dot_nt(key, w[:, width : 2 * width]) + dot_nt(value, w[:, 2 * width :])
        if query is not None:
            g_acc[:, :width] += dot(at_t[:, : query.shape[0]], query)
            column_sums(0, query)
            first = total[: query.shape[0]] + dot_nt(query, w[:, :width])
            return first, total[query.shape[0] :]
        return total

    own, near = section(((own_at, rows), (halo_at, HALO)), dq[0])
    da_own[0] = own
    da_win[0, win:, :] = near.astype(BF16)

    @pl.when(noisy)
    def _():
        da_main[0] = section(((win, rows),), None).astype(BF16)

    @pl.when(second)
    def _():
        da_win[0, :win, :] = section(((0, win),), None).astype(BF16)

    @pl.when(pl.program_id(0) == pl.num_programs(0) - 1)
    def _():
        g_w[...] = g_acc[...].astype(BF16)


def final_kernel(x, da, extra, dx2, gain, grad_in, g_vec):
    value = x[...].astype(F32)
    normed, inverse = norm_stats(value)
    grad = da[...] + extra[...].astype(F32)
    grad_in[...] = dx2[...] + norm_back(grad, normed, inverse, gain[...])

    @pl.when(pl.program_id(0) == 0)
    def _():
        g_vec[...] = jnp.zeros_like(g_vec)

    g_vec[0:1, :] += jnp.sum(grad * normed, axis=0, keepdims=True)
    g_vec[1:2, :] += jnp.sum(grad, axis=0, keepdims=True)


def front_remote(
    lay, role, sizes, inputs, segment_ids, block_ids, small, weights, freqs, lse_shape, bias_scratch, spans, attn_flops
):
    micro, rows, width = inputs.shape
    keys, win = lay["keys"], lay["win"]
    bits = lax.axis_size("fsdp").bit_length() - 1
    lanes = -(-max(sizes) // 128) * 128
    pack = jnp.stack([jnp.pad(p.astype(F32), (0, lanes - p.shape[0])) for p in small])
    full = [like((2,) * bits + p.shape, BF16) for p in weights]
    longest = max(sizes) << bits
    table_rows = win + rows + HALO
    shapes = full + [
        like((micro, rows, width), BF16), like((micro, keys, width), BF16), like((micro, keys, width), BF16),
        like((micro, keys, width), BF16), like((micro, rows, width), BF16), like(lse_shape, F32),
        like((8, longest), F32), like((table_rows, 128), F32), like((table_rows, 128), F32),
        like((micro, keys, 1), F32), like((micro, 8, rows), F32),
    ]
    remote = 3 * micro + 1 + bits * 8 + 10
    outs = pl.pallas_call(
        functools.partial(front_kernel, lay, bits, sizes),
        in_specs=[VMEM] * 9,
        out_specs=[ANY] * 10 + [VMEM] * 5,
        out_shape=shapes,
        scratch_shapes=[
            pltpu.VMEM((micro, rows, width), BF16), pltpu.VMEM((micro, win + HALO, width), BF16),
            pltpu.VMEM((width, 3 * width), BF16), pltpu.VMEM((micro, rows, width), BF16),
            pltpu.VMEM((micro, keys, width), BF16), pltpu.VMEM((micro, keys, width), BF16),
            pltpu.VMEM((micro, keys, width), BF16), pltpu.VMEM((micro, rows, width), BF16),
            pltpu.VMEM(lse_shape, F32), pltpu.VMEM((2,) * bits + (8, lanes), F32),
            pltpu.SemaphoreType.DMA((remote,)), pltpu.SemaphoreType.DMA((remote,)),
            pltpu.SemaphoreType.DMA((32,)),
        ] + bias_scratch,
        compiler_params=pltpu.CompilerParams(
            vmem_limit_bytes=VMEM_BYTES, collective_id=0, has_side_effects=True
        ),
        cost_estimate=pl.CostEstimate(flops=2 * attn_flops, bytes_accessed=40 << 20, transcendentals=0),
        name="front",
    )(inputs, segment_ids, block_ids, pack, freqs, *weights)
    joined = [w.reshape((-1, w.shape[-1])) for w in outs[:4]]
    return tuple(joined) + tuple(outs[4:])


def front_native(
    lay, role, sizes, inputs, segment_ids, block_ids, small, weights, freqs, lse_shape, bias_scratch, spans, attn_flops
):
    micro, rows, width = inputs.shape
    keys, win, length = lay["keys"], lay["win"], lay["length"]
    clean, half = role[0], role[1]
    pairs = [(0, 1), (1, 0), (2, 3), (3, 2)]
    xb = lax.ppermute(inputs, "seq", [(2, 0), (3, 1)])
    xmain = jnp.where(clean == 1, inputs, xb)
    edge = jnp.where(half == 0, inputs[:, rows - HALO :], inputs[:, :HALO])
    xc = lax.ppermute(jnp.concatenate([xmain[:, rows - win :], edge], axis=1), "seq", pairs)
    start = half * rows
    edge_at = jnp.where(half == 0, rows, -HALO)
    positions = start + jnp.concatenate([jnp.arange(-win, rows), edge_at + jnp.arange(HALO)])
    turned = positions.astype(F32)[:, None] * freqs
    sine = jnp.sin(turned)
    cos = jnp.cos(turned)
    sin = jnp.where(jnp.arange(128)[None] % HD < HD // 2, -sine, sine)
    code = segment_ids * SEG_STEP + block_ids
    padded = jnp.pad(code, ((0, 0), (win, 0)), constant_values=-1)
    key_codes = lax.dynamic_slice_in_dim(padded, start, win + rows, 1)
    own_code = lax.dynamic_slice_in_dim(code, start, rows, 1)
    own_seg = lax.dynamic_slice_in_dim(segment_ids, start, rows, 1)
    before, after = code[:, rows - HALO : rows], code[:, rows : rows + HALO]
    codes = jnp.concatenate(
        [
            key_codes,
            jnp.where((clean == 1) & (half == 0), after, -1),
            jnp.where((clean == 0) & (half == 1), before, -2),
            jnp.where(clean == 0, own_code, -2),
            jnp.where((clean == 0) & (half == 0), after, -2),
        ],
        axis=1,
    )[:, :, None].astype(F32)
    queries = jnp.stack([own_seg * SEG_STEP, own_code - (1 - clean), own_code], axis=1)
    queries = jnp.concatenate([queries, jnp.zeros((micro, 5, rows), jnp.int32)], axis=1).astype(F32)
    packed = lax.all_gather(jnp.concatenate(small)[None], "fsdp", axis=0, tiled=True)
    vectors, at = [], 0
    longest = max(sizes) * packed.shape[0]
    for size in sizes:
        one = packed[:, at : at + size].reshape(-1).astype(F32)
        vectors.append(jnp.pad(one, (0, longest - one.shape[0])))
        at += size
    vec = jnp.stack(vectors)
    w_in, w_out, w_up, w_down = (lax.all_gather(p, "fsdp", axis=0, tiled=True) for p in weights)
    per_seq = lambda n, d: pl.BlockSpec((1, n, d), lambda s: (s, 0, 0))
    table_rows = win + rows + HALO
    q, k, v, a = call(
        functools.partial(qkv_kernel, lay), (micro,),
        [SMEM(), per_seq(rows, width), per_seq(rows, width), per_seq(win + HALO, width),
         whole((width, 3 * width)), whole(vec.shape), whole((table_rows, 128)), whole((table_rows, 128))],
        [per_seq(rows, width), per_seq(keys, width), per_seq(keys, width), per_seq(keys, width)],
        [like((micro, rows, width), BF16)] + [like((micro, keys, width), BF16)] * 3,
        [], 2 * micro * rows * width * 3 * width * 2, 20 << 20, "qkv",
    )(role, inputs, xb, xc, w_in, vec, cos, sin)
    qw = QUAD * HD
    quads = width // qw
    quad_block = lambda n: pl.BlockSpec((1, n, qw), lambda s, h: (s, 0, h))
    o, lse = call(
        functools.partial(attend_kernel, lay), (micro, quads),
        [pl.BlockSpec((1, keys, 1), lambda s, h: (s, 0, 0)), pl.BlockSpec((1, 8, rows), lambda s, h: (s, 0, 0)),
         quad_block(rows), quad_block(keys), quad_block(keys)],
        [quad_block(rows), pl.BlockSpec((1,) + lse_shape[1:], lambda s, h: (s * quads + h, 0, 0))],
        [like((micro, rows, width), BF16), like(lse_shape, F32)],
        bias_scratch, 2 * attn_flops, 12 << 20, "attend",
    )(codes, queries, q, k, v)
    return w_in, w_out, w_up, w_down, q, k, v, a, o, lse, vec, cos, sin, codes, queries


def per_device(
    inputs, segment_ids, block_ids, attn_gain, attn_shift, proj_in, bias_in, proj_out, bias_out,
    mlp_gain, mlp_shift, weight_up, bias_up, weight_down, bias_down, cotangent,
):
    micro, rows, width = inputs.shape
    length = segment_ids.shape[1]
    hidden = weight_up.shape[1]
    seq_n = lax.axis_size("seq")
    fsdp_n = lax.axis_size("fsdp")
    assert seq_n == 4 and seq_n * rows == 2 * length
    lay = layout(rows, length)
    win, keys = lay["win"], lay["keys"]
    me = lax.axis_index("seq")
    clean = me // 2
    half = me % 2
    role = jnp.stack([clean, half]).astype(jnp.int32)
    pairs = [(0, 1), (1, 0), (2, 3), (3, 2)]
    small = (attn_gain, attn_shift, bias_in, bias_out, mlp_gain, mlp_shift, bias_up, bias_down)
    sizes = [p.shape[0] for p in small]
    weights = (proj_in, proj_out, weight_up, weight_down)
    half_dim = HD // 2
    freqs = (10000.0 ** (-(np.arange(half_dim, dtype=np.float32) / half_dim))).astype(np.float32)
    freqs = np.tile(freqs, 4)[None]
    quads = width // (QUAD * HD)
    qw = QUAD * HD
    spans = [hi - lo + NEAR for lo, hi in windows(lay)]
    bias_scratch = [pltpu.VMEM((n, TILE), F32) for n in spans]
    per_seq = lambda n, d: pl.BlockSpec((1, n, d), lambda s: (s, 0, 0))
    role_spec = SMEM()
    attn_flops = micro * quads * sum(spans) * QUAD * TILE * qw * 2
    lse_shape = (micro * quads, rows // TILE, QUAD * TILE)
    table_rows = win + rows + HALO
    aligned = fsdp_n & (fsdp_n - 1) == 0 and all(p.shape[0] % (4 * HALO) in (0, 32) for p in weights)
    front = front_remote if aligned else front_native
    (w_in, w_out, w_up, w_down, q, k, v, a, o, lse, vec, cos, sin, codes, queries) = front(
        lay, role, sizes, inputs, segment_ids, block_ids, small, weights, freqs,
        lse_shape, bias_scratch, spans, attn_flops,
    )
    quad_block = lambda n: pl.BlockSpec((1, n, qw), lambda s, h: (s, 0, h))
    code_spec = pl.BlockSpec((1, keys, 1), lambda s, h: (s, 0, 0))
    query_spec = pl.BlockSpec((1, 8, rows), lambda s, h: (s, 0, 0))
    lse_spec = pl.BlockSpec((1,) + lse_shape[1:], lambda s, h: (s * quads + h, 0, 0))

    total = micro * rows
    flat = lambda z: z.reshape(total, width)
    chunk = min(512, hidden)
    rows_spec = whole((total, width))
    out_rows, dx2, do, g_w_out, g_w_up, g_b_up, g_w_down, g_mlp = call(
        mlp_kernel, (hidden // chunk,),
        [rows_spec, rows_spec, rows_spec, whole((width, width)), whole(vec.shape),
         pl.BlockSpec((width, chunk), lambda j: (0, j)), pl.BlockSpec((8, chunk), lambda j: (0, j)),
         pl.BlockSpec((chunk, width), lambda j: (j, 0))],
        [rows_spec, rows_spec, rows_spec, whole((width, width)),
         pl.BlockSpec((width, chunk), lambda j: (0, j)), pl.BlockSpec((8, chunk), lambda j: (0, j)),
         pl.BlockSpec((chunk, width), lambda j: (j, 0)), whole((8, width))],
        [like((total, width), BF16), like((total, width), F32), like((total, width), BF16),
         like((width, width), BF16), like((width, hidden), BF16), like((8, hidden), F32),
         like((hidden, width), BF16), like((8, width), F32)],
        [pltpu.VMEM((total, width), F32), pltpu.VMEM((total, width), BF16), pltpu.VMEM((width, total), BF16),
         pltpu.VMEM((total, 1), F32), pltpu.VMEM((total, width), F32), pltpu.VMEM((total, width), F32)],
        2 * total * width * (6 * hidden + 3 * width), 40 << 20, "mlp",
    )(flat(o), flat(inputs), flat(cotangent), w_out, vec, w_up, vec, w_down)

    seqs = lambda z: z.reshape(micro, rows, width)
    table = pl.BlockSpec((table_rows, 128), lambda s, h: (0, 0), pipeline_mode=pl.Buffered(1))
    dq, dk, dv = call(
        functools.partial(attend_back_kernel, lay), (micro, quads),
        [code_spec, query_spec, quad_block(rows), quad_block(keys), quad_block(keys),
         quad_block(rows), quad_block(rows), lse_spec, table, table],
        [quad_block(rows), quad_block(keys), quad_block(keys)],
        [like((micro, rows, width), BF16), like((micro, keys, width), BF16), like((micro, keys, width), BF16)],
        [pltpu.VMEM((keys, qw), F32), pltpu.VMEM((keys, qw), F32)] + bias_scratch,
        5 * attn_flops, 24 << 20, "attend_back",
    )(codes, queries, q, k, v, o, seqs(do), lse, cos, sin)

    da_own, da_main, da_win, g_w_in, g_b_in = call(
        functools.partial(qkv_back_kernel, lay), (micro,),
        [role_spec, per_seq(keys, width), per_seq(rows, width), per_seq(keys, width), per_seq(keys, width),
         whole((width, 3 * width))],
        [per_seq(rows, width), per_seq(rows, width), per_seq(win + HALO, width),
         whole((width, 3 * width)), whole((8, 3 * width))],
        [like((micro, rows, width), F32), like((micro, rows, width), BF16), like((micro, win + HALO, width), BF16),
         like((width, 3 * width), BF16), like((8, 3 * width), F32)],
        [pltpu.VMEM((width, 3 * width), F32)], 2 * 2 * micro * rows * width * 3 * width * 2, 40 << 20, "qkv_back",
    )(role, a, dq, dk, dv, w_in)

    from_pair = lax.ppermute(da_win, "seq", pairs).astype(F32)
    from_second = jnp.where(half == 0, from_pair[:, :win], 0.0)
    edge = from_pair[:, win:]
    gap = jnp.zeros((micro, rows - HALO, width), F32)
    edges = jnp.where(
        half == 0, jnp.concatenate([gap, edge], axis=1), jnp.concatenate([edge, gap], axis=1)
    )
    added = jnp.pad(from_second, ((0, 0), (rows - win, 0), (0, 0)))
    to_clean = (jnp.where(clean == 0, da_main.astype(F32), 0.0) + added).astype(BF16)
    from_noisy = lax.ppermute(to_clean, "seq", [(0, 2), (1, 3)])
    extra = jnp.where(clean == 1, from_noisy.astype(F32) + added, 0.0) + edges

    grad_in, g_attn = call(
        final_kernel, (2,),
        [pl.BlockSpec((total // 2, width), lambda i: (i, 0))] * 4 + [whole((1, width))],
        [pl.BlockSpec((total // 2, width), lambda i: (i, 0)), whole((8, width))],
        [like((total, width), F32), like((8, width), F32)], [], 0, 16 << 20, "norm_back",
    )(flat(inputs), flat(da_own), flat(extra), dx2, vec[0:1, :width])

    def scatter(g):
        return lax.psum(lax.psum_scatter(g, "fsdp", scatter_dimension=0, tiled=True), "seq")

    big = [scatter(g).astype(F32) for g in (g_w_in, g_w_out, g_w_up, g_w_down)]
    smalls = [g_attn[0], g_attn[1], g_b_in[0], g_mlp[3], g_mlp[1], g_mlp[2], g_b_up[0], g_mlp[0]]
    pack = jnp.concatenate([g.reshape(fsdp_n, -1) for g in smalls], axis=1)
    pack = lax.psum(pack, ("seq", "fsdp"))
    mine = lax.dynamic_slice_in_dim(pack, lax.axis_index("fsdp"), 1, 0)[0]
    outs, at = [], 0
    for size in sizes:
        outs.append(mine[at : at + size])
        at += size
    g_gain1, g_shift1, g_bin, g_bout, g_gain2, g_shift2, g_bup, g_bdown = outs
    return (
        seqs(out_rows), seqs(grad_in), g_gain1, g_shift1, big[0], g_bin, big[1], g_bout,
        g_gain2, g_shift2, big[2], g_bup, big[3], g_bdown,
    )


def solution(mesh):
    rows = P("fsdp", "seq", None)
    one, two = P("fsdp"), P("fsdp", None)
    params = (one, one, two, one, two, one, one, one, two, one, two, one)
    return jax.shard_map(
        per_device,
        mesh=mesh,
        in_specs=(rows, two, two) + params + (rows,),
        out_specs=(rows, rows) + params,
        check_vma=False,
    )
```

```python
import functools
import itertools

import jax
import jax.numpy as jnp
import numpy as np
from jax import lax
from jax.experimental import pallas as pl
from jax.experimental.pallas import tpu as pltpu
from jax.sharding import PartitionSpec as P

HD = 64
QUAD = 4
TILE = 128
HALO = 16
NEAR = TILE + 2 * HALO
EPS = 1e-05
MASKED = -1e30
SEG_STEP = 4096
F32 = jnp.float32
BF16 = jnp.bfloat16
VMEM_BYTES = 62 * 1024 * 1024
MESH = pl.DeviceIdType.MESH
ANY = pl.BlockSpec(memory_space=pl.ANY)
VMEM = pl.BlockSpec(memory_space=pltpu.VMEM)


def dot(a, b):
    return jnp.dot(a, b, preferred_element_type=F32)


def dot_nt(a, b):
    return lax.dot_general(a, b, (((1,), (1,)), ((), ())), preferred_element_type=F32)


def dot_tn(a, b):
    return lax.dot_general(a, b, (((0,), (0,)), ((), ())), preferred_element_type=F32)


def norm_stats(x):
    center = jnp.mean(x, axis=-1, keepdims=True)
    centered = x - center
    inverse = lax.rsqrt(jnp.mean(centered * centered, axis=-1, keepdims=True) + EPS)
    return centered * inverse, inverse


def norm_back(grad, normed, inverse, gain):
    scaled = grad * gain
    first = jnp.mean(scaled, axis=-1, keepdims=True)
    second = jnp.mean(scaled * normed, axis=-1, keepdims=True)
    return inverse * (scaled - first - normed * second)


def partner(u):
    lane = lax.broadcasted_iota(jnp.int32, u.shape, 1)
    half = HD // 2
    return jnp.where(
        lane % HD < half, pltpu.roll(u, u.shape[1] - half, 1), pltpu.roll(u, half, 1)
    )


def whole(shape):
    return pl.BlockSpec(shape, lambda *_: (0,) * len(shape), pipeline_mode=pl.Buffered(1))


def call(kernel, grid, in_specs, out_specs, out_shape, scratch, flops, nbytes, name):
    return pl.pallas_call(
        kernel,
        grid=grid,
        in_specs=in_specs,
        out_specs=out_specs,
        out_shape=out_shape,
        scratch_shapes=scratch,
        compiler_params=pltpu.CompilerParams(vmem_limit_bytes=VMEM_BYTES),
        cost_estimate=pl.CostEstimate(flops=flops, bytes_accessed=nbytes, transcendentals=0),
        name=name,
    )


def like(shape, dtype):
    return jax.ShapeDtypeStruct(shape, dtype)


SMEM = functools.partial(pl.BlockSpec, memory_space=pltpu.SMEM)


def layout(rows, length):
    win = rows - length // 8
    noisy = win + rows + HALO
    used = noisy + rows + 2 * HALO
    return dict(rows=rows, win=win, length=length, noisy=noisy, used=used, keys=-(-used // 256) * 256)


def places(lay, role):
    noisy = role[0] == 0
    second = role[1] == 1
    own_at = jnp.where(noisy, lay["noisy"] + HALO, lay["win"])
    halo_at = jnp.where(
        second,
        lay["noisy"],
        jnp.where(noisy, lay["noisy"] + HALO + lay["rows"], lay["win"] + lay["rows"]),
    )
    return noisy, second, pl.multiple_of(own_at, HALO), pl.multiple_of(halo_at, HALO)


def qkv_rows(lay, where_am, n, x, xb, xc, w, b, gain, shift, cos, sin, q_out, k_out, v_out, a_out):
    width = x.shape[2]
    rows, win = lay["rows"], lay["win"]
    noisy, second, own_at, halo_at = where_am

    def norm(v):
        normed, _ = norm_stats(v.astype(F32))
        return (normed * gain + shift).astype(BF16)

    def zeros(at, count):
        for ref in (k_out, v_out, a_out):
            ref[n, at : at + count, :] = jnp.zeros((count, width), BF16)

    def section(a, parts, table, want_q):
        def put(ref, col, value):
            for begin, count, at in parts:
                ref[n, pl.ds(at, count), col : col + value.shape[1]] = value[begin : begin + count]

        put(a_out, 0, a)
        c = cos[table : table + a.shape[0], :]
        s = sin[table : table + a.shape[0], :]
        first = 0 if want_q else width
        for col in range(first, 3 * width, 256):
            part = dot(a, w[:, col : col + 256]) + b[:, col : col + 256]
            for piece in range(2):
                u = part[:, piece * 128 : piece * 128 + 128]
                at_col = col + piece * 128
                if at_col < 2 * width:
                    u = u * c + partner(u) * s
                if at_col < width:
                    q_out[n, :, at_col : at_col + 128] = (u[:rows] * (HD**-0.5)).astype(BF16)
                elif at_col < 2 * width:
                    put(k_out, at_col - width, u.astype(BF16))
                else:
                    put(v_out, at_col - 2 * width, u.astype(BF16))

    zeros(win + rows, 2 * HALO)
    zeros(lay["used"] - HALO, lay["keys"] - lay["used"] + HALO)
    own = jnp.concatenate([norm(x[n]), norm(xc[n, win:, :])], axis=0)
    section(own, ((0, rows, own_at), (rows, HALO, halo_at)), win, True)

    @pl.when(noisy)
    def _():
        section(norm(xb[n]), ((0, rows, win),), win, False)

    @pl.when(jnp.logical_not(noisy))
    def _():
        zeros(lay["noisy"] + HALO, rows)

    @pl.when(second)
    def _():
        section(norm(xc[n, :win, :]), ((0, win, 0),), 0, False)

    @pl.when(jnp.logical_not(second))
    def _():
        zeros(0, win)


def qkv_kernel(lay, role, x, xb, xc, w, vec, cos, sin, *outs):
    width = x.shape[2]
    gain, shift, b = vec[0:1, :width], vec[1:2, :width], vec[2:3, : 3 * width]
    qkv_rows(lay, places(lay, role), 0, x, xb, xc, w, b, gain, shift, cos, sin, *outs)


def windows(lay):
    rows, win, length = lay["rows"], lay["win"], lay["length"]
    longest, earliest, latest = length // 2, length // 8, 3 * length // 8
    found = []
    for at in range(0, rows, TILE):
        begin = win + rows
        for origin in range(0, length, rows):
            pos = origin + at
            low = max(pos - longest, 0)
            if origin > 0:
                low = max(low, earliest)
            if pos >= latest + longest:
                low = max(low, earliest + longest)
            begin = min(begin, low - origin + win)
        found.append((begin // TILE * TILE, win + at + TILE + HALO))
    return found


def make_bias(lay, n, codes, queries, biases):
    for t, (lo, hi) in enumerate(windows(lay)):
        here = slice(t * TILE, t * TILE + TILE)
        low, high, same = (queries[n, r : r + 1, here] for r in range(3))
        kc = codes[n, lo:hi, :]
        ok = (kc >= low) & (kc <= high)
        biases[t][: hi - lo, :] = jnp.where(ok, 0.0, MASKED)
        near = lay["noisy"] + t * TILE
        kn = codes[n, near : near + NEAR, :]
        biases[t][hi - lo :, :] = jnp.where(kn == same, 0.0, MASKED)


def stacked(tile):
    lane = lax.broadcasted_iota(jnp.int32, tile.shape, 1)
    zero = jnp.zeros_like(tile)
    return jnp.concatenate(
        [jnp.where(lane // HD == h, tile, zero) for h in range(QUAD)], axis=0
    )


def own_heads(wide):
    return jnp.concatenate(
        [wide[h * HD : h * HD + HD, h * TILE : h * TILE + TILE] for h in range(QUAD)], axis=0
    )


def keys_of(ref, lay, n, cols, t, lo, hi):
    near = lay["noisy"] + t * TILE
    return jnp.concatenate([ref[n, lo:hi, cols], ref[n, near : near + NEAR, cols]], axis=0)


def attend(lay, n, cols, q, k, v, o_out, lse_out, lse_at, biases):
    for t, (lo, hi) in enumerate(windows(lay)):
        here = slice(t * TILE, t * TILE + TILE)
        qm = stacked(q[n, here, cols])
        kk = keys_of(k, lay, n, cols, t, lo, hi)
        vv = keys_of(v, lay, n, cols, t, lo, hi)
        s = dot_nt(kk, qm) + jnp.concatenate([biases[t][...]] * QUAD, axis=1)
        peak = jnp.max(s, axis=0, keepdims=True)
        p = jnp.exp(s - peak)
        total = jnp.sum(p, axis=0, keepdims=True)
        wide = dot_tn(vv, p.astype(BF16)) * (1.0 / total)
        o_out[n, here, cols] = jnp.transpose(own_heads(wide)).astype(BF16)
        lse_out[lse_at, t : t + 1, :] = peak + jnp.log(total)


def attend_kernel(lay, codes, queries, q, k, v, o_out, lse_out, *biases):
    @pl.when(pl.program_id(1) == 0)
    def _():
        make_bias(lay, 0, codes, queries, biases)

    attend(lay, 0, slice(None), q, k, v, o_out, lse_out, 0, biases)


def attend_back(
    lay, n, cols, q, k, v, o, do, lse, lse_at, cos, sin, to, col, dq_out, dk_out, dv_out, dk_acc, dv_acc, biases
):
    rows, win = lay["rows"], lay["win"]
    qw = QUAD * HD

    def lanes(piece):
        return pl.ds(pl.multiple_of(col + piece * 128, 128), 128)

    dk_acc[...] = jnp.zeros_like(dk_acc)
    dv_acc[...] = jnp.zeros_like(dv_acc)
    for t, (lo, hi) in enumerate(windows(lay)):
        here = slice(t * TILE, t * TILE + TILE)
        size = hi - lo
        near = slice(lay["noisy"] + t * TILE, lay["noisy"] + t * TILE + NEAR)
        qm = stacked(q[n, here, cols])
        dom = stacked(do[n, here, cols])
        kk = keys_of(k, lay, n, cols, t, lo, hi)
        vv = keys_of(v, lay, n, cols, t, lo, hi)
        both = jnp.transpose(do[n, here, cols].astype(F32) * o[n, here, cols].astype(F32))
        delta = jnp.concatenate(
            [jnp.sum(both[h * HD : h * HD + HD, :], axis=0, keepdims=True) for h in range(QUAD)],
            axis=1,
        )
        s = dot_nt(kk, qm) + jnp.concatenate([biases[t][...]] * QUAD, axis=1)
        p = jnp.exp(s - lse[lse_at, t : t + 1, :])
        dp = dot_nt(vv, dom)
        ds = (p * (dp - delta)).astype(BF16)
        pb = p.astype(BF16)
        dv = dot(pb, dom)
        dk = dot(ds, qm)
        dv_acc[lo:hi, :] += dv[:size]
        dk_acc[lo:hi, :] += dk[:size]
        dv_acc[near, :] += dv[size:]
        dk_acc[near, :] += dk[size:]
        wide = dot_tn(kk, ds)
        dq = jnp.transpose(own_heads(wide)) * (HD**-0.5)
        c = cos[win + t * TILE : win + t * TILE + TILE, :]
        sn = sin[win + t * TILE : win + t * TILE + TILE, :]
        for piece in range(2):
            u = dq[:, piece * 128 : piece * 128 + 128]
            dq_out[to, here, lanes(piece)] = (u * c - partner(u) * sn).astype(BF16)
    for piece in range(2):
        dv_out[to, :, lanes(piece)] = dv_acc[:, piece * 128 : piece * 128 + 128].astype(BF16)
    half = (cos[win + rows :, :], sin[win + rows :, :])
    own = (cos[win : win + rows, :], sin[win : win + rows, :])
    tables = (
        (0, (cos[: win + rows, :], sin[: win + rows, :])),
        (win + rows, half),
        (lay["noisy"], half),
        (lay["noisy"] + HALO, own),
        (lay["used"] - HALO, half),
    )
    for at, (c, sn) in tables:
        here = slice(at, at + c.shape[0])
        for piece in range(2):
            u = dk_acc[here, piece * 128 : piece * 128 + 128]
            dk_out[to, here, lanes(piece)] = (u * c - partner(u) * sn).astype(BF16)
    spare = lay["keys"] - lay["used"]
    for piece in range(2):
        dk_out[to, lay["used"] :, lanes(piece)] = jnp.zeros((spare, 128), BF16)


def attend_back_kernel(
    lay, codes, queries, q, k, v, o, do, lse, cos, sin, dq_out, dk_out, dv_out, dk_acc, dv_acc, *biases
):
    @pl.when(pl.program_id(1) == 0)
    def _():
        make_bias(lay, 0, codes, queries, biases)

    attend_back(
        lay, 0, slice(None), q, k, v, o, do, lse, 0, cos, sin, 0, 0, dq_out, dk_out, dv_out, dk_acc, dv_acc, biases
    )


def bit_of(index, b):
    return (index // (1 << b)) % 2


def other(index, b):
    return index + (1 << b) * (1 - 2 * bit_of(index, b))


class Net:
    def __init__(self, bits, send, recv, sems):
        self.me, self.f, self.bits = lax.axis_index("seq"), lax.axis_index("fsdp"), bits
        self.core, self.x = self.me % 2, self.me // 2
        self.send, self.recv, self.sems = send, recv, sems
        self.used, self.local_used = 0, 0
        self.started = []

    def partners(self):
        return [{"seq": other(self.me, 0)}, {"seq": other(self.me, 1)}] + [
            {"fsdp": other(self.f, b)} for b in range(self.bits)
        ]

    def barrier(self):
        barrier = pltpu.get_barrier_semaphore()
        for device in self.partners():
            pl.semaphore_signal(barrier, inc=1, device_id=device, device_id_type=MESH)
        pl.semaphore_wait(barrier, 2 + self.bits)

    def copy(self, src, dst, device):
        n = self.used
        self.used += 1
        return pltpu.make_async_remote_copy(
            src_ref=src, dst_ref=dst, send_sem=self.send.at[n], recv_sem=self.recv.at[n],
            device_id=device, device_id_type=MESH,
        )

    def local(self, src, dst):
        n = self.local_used
        self.local_used += 1
        return pltpu.make_async_copy(src, dst, self.sems.at[n])

    def fsdp_index(self, b):
        return (slice(None),) * (self.bits - 1 - b) + tuple(
            bit_of(self.f, low) for low in range(b, -1, -1)
        )


class Gather:
    def __init__(self, net, own, full, tail, tail_x=None, tail_core=None):
        self.net, self.at = net, 0
        mine = net.fsdp_index(net.bits - 1)
        self.own = net.local(own.at[tail], full.at[mine + tail])
        self.stages = []
        for b in range(net.bits - 1, -1, -1):
            here = full.at[net.fsdp_index(b) + tail]
            src = own.at[tail] if b == net.bits - 1 else here
            self.stages.append(net.copy(src, here, {"fsdp": other(net.f, b)}))
        everything = (slice(None),) * net.bits
        for region, b in ((tail_x, 1), (tail_core, 0)):
            if region is not None:
                here = full.at[everything + region]
                self.stages.append(net.copy(here, here, {"seq": other(net.me, b)}))

    def advance(self):
        if self.at == 0:
            self.own.start()
        else:
            self.stages[self.at - 1].wait_recv()
        if self.at == 1:
            self.own.wait()
        if self.at < len(self.stages):
            self.stages[self.at].start()
        self.at += 1

    def finish(self):
        for stage in self.stages:
            stage.wait_send()


def front_kernel(
    lay, bits, sizes, x, seg, blk, pack, freqs, w_in_s, w_out_s, w_up_s, w_down_s,
    w_in, w_out, w_up, w_down, q_out, k_out, v_out, a_out, o_out, lse_out, vec, cos, sin, codes, queries,
    xb, xc, w_vm, q, k, v, a, o, lse, packs, send, recv, sems, *biases,
):
    rows, win, length = lay["rows"], lay["win"], lay["length"]
    width = x.shape[2]
    hidden = w_up_s.shape[1]
    micro = x.shape[0]
    net = Net(bits, send, recv, sems)
    role = (net.x, net.core)
    where_am = noisy, second, _, _ = places(lay, role)
    first = jnp.logical_not(second)
    clean = jnp.logical_not(noisy)
    net.barrier()

    pair, across = {"seq": other(net.me, 0)}, {"seq": other(net.me, 1)}
    rows_across = [net.copy(x.at[n], xb.at[n], across) for n in range(micro)]
    window = (pl.ds(rows - win, win), slice(None))
    target = (pl.ds(0, win), slice(None))
    rows_pair, rows_pair_b = [], []
    for n in range(micro):
        at = net.used
        rows_pair.append(net.copy(x.at[(n,) + window], xc.at[(n,) + target], pair))
        net.used = at
        rows_pair_b.append(net.copy(xb.at[(n,) + window], xc.at[(n,) + target], pair))
    edge_at = pl.multiple_of((1 - net.core) * (rows - HALO), HALO)
    edge = net.copy(x.at[:, pl.ds(edge_at, HALO), :], xc.at[:, pl.ds(win, HALO), :], pair)

    def columns(begin, size):
        return (slice(None), pl.ds(pl.multiple_of(begin, 128), size))

    small = Gather(net, pack, packs, (slice(None), slice(None)))
    half_in, half_out, half_up = 3 * width // 2, width // 2, hidden // 2
    third = half_in // 3
    ins = [
        Gather(net, w_in_s, w_in, columns(net.core * half_in + n * third, third), None,
               columns(net.core * half_in + n * third, third))
        for n in range(3)
    ]
    out = Gather(net, w_out_s, w_out, columns(net.core * half_out, half_out), None,
                 columns(net.core * half_out, half_out))
    quarter = half_up // 2
    up = Gather(net, w_up_s, w_up, columns(net.core * half_up + net.x * quarter, quarter),
                columns(net.core * half_up + net.x * quarter, quarter),
                columns(net.core * half_up, half_up))
    slab = w_down_s.shape[0]
    downs = []
    for n in range(2):
        region = (pl.ds(pl.multiple_of(net.core * (slab // 2) + n * (slab // 4), HALO), slab // 4), slice(None))
        downs.append(Gather(net, w_down_s, w_down, region, None, region))
    down0, down1 = downs

    ins[0].advance()
    small.advance()

    @pl.when(clean)
    def _():
        rows_across[0].start()

    edge.start()
    ins[1].advance()
    ins[2].advance()

    position = lax.broadcasted_iota(jnp.int32, (win + rows + HALO, 128), 0)
    shifted = jnp.where(
        position < win + rows, position - win, position - win - rows + jnp.where(second, -HALO, rows)
    )
    turned = (shifted + jnp.where(second, rows, 0)).astype(F32) * freqs[...]
    lane = lax.broadcasted_iota(jnp.int32, (win + rows + HALO, 128), 1)
    cos[...] = jnp.cos(turned)
    sine = jnp.sin(turned)
    sin[...] = jnp.where(lane % HD < HD // 2, -sine, sine)
    code = (seg[...] * SEG_STEP + blk[...]).astype(F32)
    base = (seg[...] * SEG_STEP).astype(F32)
    turned_code = jnp.transpose(jnp.concatenate([code, jnp.zeros((8 - micro, length), F32)], axis=0))
    lay_noisy = lay["noisy"]
    for n in range(micro):
        col = turned_code[:, n : n + 1]
        none = lambda count, value: jnp.full((count, 1), value, F32)
        codes[n, :win, :] = jnp.where(second, col[rows - win : rows], -1.0)
        codes[n, win : win + rows, :] = jnp.where(second, col[rows:], col[:rows])
        after, before = col[rows : rows + HALO], col[rows - HALO : rows]
        codes[n, win + rows : lay_noisy, :] = jnp.where(jnp.logical_and(clean, first), after, -1.0)
        codes[n, lay_noisy : lay_noisy + HALO, :] = jnp.where(jnp.logical_and(noisy, second), before, -2.0)
        codes[n, lay_noisy + HALO : lay_noisy + HALO + rows, :] = jnp.where(
            noisy, jnp.where(second, col[rows:], col[:rows]), -2.0
        )
        codes[n, lay["used"] - HALO : lay["used"], :] = jnp.where(jnp.logical_and(noisy, first), after, -2.0)
        codes[n, lay["used"] :, :] = none(lay["keys"] - lay["used"], -2.0)
        own_code = jnp.where(second, code[n : n + 1, rows:], code[n : n + 1, :rows])
        own_base = jnp.where(second, base[n : n + 1, rows:], base[n : n + 1, :rows])
        high = own_code - jnp.where(noisy, 1.0, 0.0)
        queries[n] = jnp.concatenate([own_base, high, own_code, jnp.zeros((5, rows), F32)], axis=0)

    small.advance()
    ins[0].advance()
    ins[1].advance()
    small.advance()
    ins[0].advance()
    ins[2].advance()
    small.advance()

    count = 1 << bits
    long_in, long_up = sizes[2] * count, sizes[6] * count
    spread = {}
    for size in sorted(set(sizes)):
        total = jnp.zeros((8, size * count), F32)
        for n in range(count):
            at = tuple((n >> b) & 1 for b in range(bits - 1, -1, -1))
            piece = packs[at]
            wide = size * count - piece.shape[1]
            if wide > 0:
                piece = jnp.concatenate([piece, jnp.zeros((8, wide), F32)], axis=1)
            lanes = lax.broadcasted_iota(jnp.int32, piece.shape, 1)
            piece = jnp.where(lanes < size, piece, 0.0)
            total += pltpu.roll(piece, n * size, 1) if n else piece
        spread[size] = total
    for r, size in enumerate(sizes):
        vec[r : r + 1, : size * count] = spread[size][r : r + 1]
        if size * count < vec.shape[1]:
            vec[r : r + 1, size * count :] = jnp.zeros((1, vec.shape[1] - size * count), F32)

    ins[1].advance()
    up.advance()
    ins[0].advance()
    ins[2].advance()

    def pass_on(n):
        @pl.when(noisy)
        def _():
            rows_across[n].wait_recv()

        @pl.when(jnp.logical_and(first, noisy))
        def _():
            rows_pair_b[n].start()

        @pl.when(jnp.logical_and(first, clean))
        def _():
            rows_pair[n].start()

    @pl.when(clean)
    def _():
        rows_across[1].start()

    pass_on(0)
    ins[1].advance()
    up.advance()
    out.advance()
    ins[2].advance()
    for n in range(3):
        ins[n].advance()
    loads = []
    for n in range(count):
        at = tuple((n >> b) & 1 for b in range(bits - 1, -1, -1))
        loads.append(net.local(w_in.at[at], w_vm.at[pl.ds(n * w_in_s.shape[0], w_in_s.shape[0]), :]))
    for load in loads:
        load.start()
    edge.wait_recv()
    up.advance()
    out.advance()
    down0.advance()
    for load in loads:
        load.wait()

    gain, shift, b_in = vec[0:1, :width], vec[1:2, :width], vec[2:3, : 3 * width]

    def qkv(n):
        @pl.when(second)
        def _():
            rows_pair[n].wait_recv()

        qkv_rows(lay, where_am, n, x, xb, xc, w_vm, b_in, gain, shift, cos, sin, q, k, v, a)
        stores = [
            net.local(here.at[n], there.at[n])
            for here, there in ((q, q_out), (k, k_out), (v, v_out), (a, a_out))
        ]
        for store in stores:
            store.start()
        return stores

    stores = qkv(0)
    down0.advance()
    out.advance()
    pass_on(1)
    down1.advance()
    stores += qkv(1)

    quads = width // (QUAD * HD)
    plan = ((up, down0, out), (down1,), (down0, down1), (up,), (out, down0, down1), (up,))
    assert micro * quads == len(plan)

    def step(index, carry):
        n, h = index // quads, index % quads

        @pl.when(h == 0)
        def _():
            make_bias(lay, n, codes, queries, biases)

        cols = pl.ds(pl.multiple_of(h * QUAD * HD, QUAD * HD), QUAD * HD)
        attend(lay, n, cols, q, k, v, o, lse, index, biases)
        for at, chunks in enumerate(plan):

            @pl.when(index == at)
            def _():
                for chunk in chunks:
                    chunk.advance()

        return carry

    lax.fori_loop(0, micro * quads, step, 0)
    last = [net.local(o, o_out), net.local(lse, lse_out)]
    for store in last:
        store.start()
    chunks = [small, out, up, down0, down1] + ins
    for chunk in chunks:
        while chunk.at <= len(chunk.stages):
            chunk.advance()
    for chunk in chunks:
        chunk.finish()
    for store in stores + last:
        store.wait()
    edge.wait_send()

    @pl.when(clean)
    def _():
        for n in range(micro):
            rows_across[n].wait_send()

    @pl.when(first)
    def _():
        for n in range(micro):
            rows_pair[n].wait_send()


def mlp_kernel(
    o, x, dy, w_out, vec, w_up, b_up, w_down,
    out_rows, dx2_out, do_out, g_w_out, g_w_up, g_b_up, g_w_down, g_vec,
    mid, a2, a2t, inv, acc_out, acc_da,
):
    step = pl.program_id(0)
    last = pl.num_programs(0) - 1
    width = x.shape[1]
    b_out, gain, shift, b_down = (vec[r : r + 1, :width] for r in (3, 4, 5, 7))

    @pl.when(step == 0)
    def _():
        value = x[...].astype(F32) + dot(o[...], w_out[...]) + b_out
        mid[...] = value
        normed, inverse = norm_stats(value)
        inv[...] = inverse
        a = (normed * gain + shift).astype(BF16)
        a2[...] = a
        a2t[...] = jnp.transpose(a)
        acc_out[...] = jnp.zeros_like(acc_out)
        acc_da[...] = jnp.zeros_like(acc_da)

    u = dot(a2[...], w_up[...]) + b_up[6:7, :]
    scale = 0.7978845608028654
    square = u * u
    inner = scale * u * (1.0 + 0.044715 * square)
    th = jnp.tanh(inner)
    plus = 0.5 * (1.0 + th)
    g = (u * plus).astype(BF16)
    slope = plus + 0.5 * u * (1.0 - th * th) * (scale * (1.0 + 3 * 0.044715 * square))
    acc_out[...] += dot(g, w_down[...])
    du32 = dot_nt(dy[...], w_down[...]) * slope
    du = du32.astype(BF16)
    g_b_up[...] = jnp.broadcast_to(jnp.sum(du.astype(F32), axis=0, keepdims=True), g_b_up.shape)
    acc_da[...] += dot_nt(du, w_up[...])
    g_w_down[...] = dot_tn(g, dy[...]).astype(BF16)
    g_w_up[...] = dot(a2t[...], du).astype(BF16)

    @pl.when(step == last)
    def _():
        dyf = dy[...].astype(F32)
        out_rows[...] = (mid[...] + acc_out[...] + b_down).astype(BF16)
        inverse = inv[...]
        value = mid[...]
        normed = (value - jnp.mean(value, axis=-1, keepdims=True)) * inverse
        da = acc_da[...]
        dx2 = dyf + norm_back(da, normed, inverse, gain)
        dx2_out[...] = dx2
        dp = dx2.astype(BF16)
        do_out[...] = dot_nt(dp, w_out[...]).astype(BF16)
        g_w_out[...] = dot_tn(o[...], dp).astype(BF16)
        g_vec[...] = jnp.concatenate(
            [
                jnp.sum(dyf, axis=0, keepdims=True),
                jnp.sum(da * normed, axis=0, keepdims=True),
                jnp.sum(da, axis=0, keepdims=True),
                jnp.sum(dp.astype(F32), axis=0, keepdims=True),
                jnp.zeros((4, dyf.shape[1]), F32),
            ],
            axis=0,
        )


def qkv_back_kernel(lay, role, a, dq, dk, dv, w, da_own, da_main, da_win, g_w, g_b, g_acc):
    width = dq.shape[2]
    rows, win = lay["rows"], lay["win"]
    noisy, second, own_at, halo_at = places(lay, role)

    @pl.when(pl.program_id(0) == 0)
    def _():
        g_acc[...] = jnp.zeros_like(g_acc)
        g_b[...] = jnp.zeros_like(g_b)

    def column_sums(col, value):
        g_b[0:1, col : col + width] += jnp.sum(value.astype(F32), axis=0, keepdims=True)

    def section(parts, query):
        def take(ref):
            return jnp.concatenate([ref[0, pl.ds(at, count), :] for at, count in parts], axis=0)

        at_t = jnp.transpose(take(a))
        key = take(dk)
        value = take(dv)
        g_acc[:, width : 2 * width] += dot(at_t, key)
        g_acc[:, 2 * width :] += dot(at_t, value)
        column_sums(width, key)
        column_sums(2 * width, value)
        total = dot_nt(key, w[:, width : 2 * width]) + dot_nt(value, w[:, 2 * width :])
        if query is not None:
            g_acc[:, :width] += dot(at_t[:, : query.shape[0]], query)
            column_sums(0, query)
            first = total[: query.shape[0]] + dot_nt(query, w[:, :width])
            return first, total[query.shape[0] :]
        return total

    own, near = section(((own_at, rows), (halo_at, HALO)), dq[0])
    da_own[0] = own
    da_win[0, win:, :] = near.astype(BF16)

    @pl.when(noisy)
    def _():
        da_main[0] = section(((win, rows),), None).astype(BF16)

    @pl.when(second)
    def _():
        da_win[0, :win, :] = section(((0, win),), None).astype(BF16)

    @pl.when(pl.program_id(0) == pl.num_programs(0) - 1)
    def _():
        g_w[...] = g_acc[...].astype(BF16)


def final_kernel(x, da, extra, dx2, gain, grad_in, g_vec):
    value = x[...].astype(F32)
    normed, inverse = norm_stats(value)
    grad = da[...] + extra[...].astype(F32)
    grad_in[...] = dx2[...] + norm_back(grad, normed, inverse, gain[...])

    @pl.when(pl.program_id(0) == 0)
    def _():
        g_vec[...] = jnp.zeros_like(g_vec)

    g_vec[0:1, :] += jnp.sum(grad * normed, axis=0, keepdims=True)
    g_vec[1:2, :] += jnp.sum(grad, axis=0, keepdims=True)


def add_to(ref, at, value):
    ref[at] = (ref[at].astype(F32) + value.astype(F32)).astype(BF16)


class Reduce:
    def __init__(self, net, theirs, mine, acc, recvs, out, tail, x_cols=None, tail_half=None):
        bits, self.net, self.at = net.bits, net, 0
        pair, across = {"seq": other(net.me, 0)}, {"seq": other(net.me, 1)}
        recvs = list(recvs)
        every = list(itertools.product(range(2), repeat=bits))
        cols = (slice(None), slice(None))
        self.steps = [(net.copy(theirs, acc, pair), mine)]
        if x_cols is not None:
            cols = (slice(None), pl.ds(pl.multiple_of(net.x * x_cols, 128), x_cols))
            away = (slice(None), pl.ds(pl.multiple_of((1 - net.x) * x_cols, 128), x_cols))
            over_x = recvs.pop(0)

            def add_x():
                for at in every:
                    add_to(acc, at + cols, over_x[at])

            self.steps.append((net.copy(acc.at[(slice(None),) * bits + away], over_x, across), add_x))
        for b in range(bits):
            low = tuple(bit_of(net.f, n) for n in range(b - 1, -1, -1))
            lead = (slice(None),) * (bits - 1 - b)
            got = recvs.pop(0)

            def add_bit(got=got, b=b, low=low):
                for at in itertools.product(range(2), repeat=bits - 1 - b):
                    add_to(acc, at + (bit_of(net.f, b),) + low + cols, got[at])

            src = acc.at[lead + (1 - bit_of(net.f, b),) + low + cols]
            self.steps.append((net.copy(src, got, {"fsdp": other(net.f, b)}), add_bit))
        own = tuple(bit_of(net.f, n) for n in range(bits - 1, -1, -1))
        if x_cols is None:
            over_x = recvs.pop(0)

            def last():
                out[tail] = (acc[own].astype(F32) + over_x[...].astype(F32)).astype(BF16)

            self.steps.append((net.copy(acc.at[own], over_x, across), last))
            tail_half = tail
        else:
            before = self.steps[-1][1]

            def keep():
                before()
                out[tail] = acc[own + cols]

            self.steps[-1] = (self.steps[-1][0], keep)
            self.steps.append((net.copy(out.at[tail], out.at[tail], across), lambda: None))
        self.steps.append((net.copy(out.at[tail_half], out.at[tail_half], pair), lambda: None))

    def advance(self):
        if self.at > len(self.steps):
            return
        if self.at > 0:
            copy, then = self.steps[self.at - 1]
            copy.wait_recv()
            then()
        if self.at < len(self.steps):
            self.steps[self.at][0].start()
        self.at += 1

    def finish(self):
        while self.at <= len(self.steps):
            self.advance()
        for copy, _ in self.steps:
            copy.wait_send()


class SumAll:
    def __init__(self, net, value, recvs):
        self.value, self.recvs, self.at = value, recvs, 0
        devices = [{"seq": other(net.me, b)} for b in range(2)]
        devices += [{"fsdp": other(net.f, b)} for b in range(net.bits)]
        self.copies = []
        for n, device in enumerate(devices):
            src = value if n == 0 else recvs.at[len(devices) + n - 1]
            self.copies.append(net.copy(src, recvs.at[n], device))

    def advance(self):
        count = len(self.copies)
        if self.at > count:
            return
        if self.at > 0:
            n = self.at - 1
            self.copies[n].wait_recv()
            held = self.value[...] if n == 0 else self.recvs[count + n - 1]
            self.recvs[count + n] = held + self.recvs[n]
        if self.at < count:
            self.copies[self.at].start()
        self.at += 1

    def finish(self):
        while self.at <= len(self.copies):
            self.advance()
        for copy in self.copies:
            copy.wait_send()
        return self.recvs[2 * len(self.copies) - 1]


def back_kernel(
    lay, bits, codes, queries, lse, cos, sin, vec, b_up_sums, mlp_sums,
    q, k, v, o, do, a, w_in, g_out, g_up, g_down, x, dx2,
    grad_in, f_in_out, f_out_out, f_up_out, f_down_out, sums_out, late_out,
    dq, dk, dv, w_vm, gin, parts, recv_parts, dwin, rwin,
    acc_in, acc_out, acc_up, acc_down, r_in, r_out, r_up, r_down, f_in, f_out, f_up, f_down,
    sums, sums_recv, late, late_recv, send, recv, sems, *biases,
):
    rows, win, keys = lay["rows"], lay["win"], lay["keys"]
    micro, width = dq.shape[0], dq.shape[2]
    hidden = vec.shape[1]
    qw = QUAD * HD
    quads = width // qw
    net = Net(bits, send, recv, sems)
    where_am = noisy, second, own_at, halo_at = places(lay, (net.x, net.core))
    first, clean = jnp.logical_not(second), jnp.logical_not(noisy)
    gain = vec[0:1, :width]
    net.barrier()
    every = list(itertools.product(range(2), repeat=bits))
    pair, across = {"seq": other(net.me, 0)}, {"seq": other(net.me, 1)}

    load_w = net.local(w_in, w_vm)
    load_w.start()

    whole_index = (slice(None),) * bits

    def columns(begin, size):
        return (slice(None), pl.ds(pl.multiple_of(begin, 128), size))

    half_out, half_up = width // 2, hidden // 2
    slab = g_down.shape[bits]
    here, there = net.core, 1 - net.core
    up = Reduce(
        net, g_up.at[whole_index + columns(there * half_up, half_up)],
        None, acc_up, r_up, f_up,
        columns(here * half_up + net.x * (half_up // 2), half_up // 2), half_up // 2,
        columns(here * half_up, half_up),
    )

    def part(core, n):
        begin = pl.multiple_of(core * (slab // 2) + n * (slab // 4), HALO)
        return (pl.ds(begin, slab // 4), slice(None))

    downs = [
        Reduce(
            net, g_down.at[whole_index + part(there, n)],
            None, acc_down[n], r_down[n], f_down, part(here, n),
        )
        for n in range(2)
    ]
    out = Reduce(
        net, g_out.at[whole_index + columns(there * half_out, half_out)],
        None, acc_out, r_out, f_out,
        columns(here * half_out, half_out),
    )
    p1 = [net.copy(dwin.at[n], rwin.at[n], pair) for n in range(micro)]
    p2 = [net.copy(parts.at[n], recv_parts.at[n], across) for n in range(micro)]
    own_up, own_out = columns(here * half_up, half_up), columns(here * half_out, half_out)
    own_down = [part(here, n) for n in range(2)]
    third = 3 * width // 6
    slab_in = width // len(every)
    ins = []
    for j in range(3):

        def mine(j=j):
            for at in every:
                add_to(acc_in[j], at, gin[(j, net.core) + at])

        region = (slice(None), pl.ds(pl.multiple_of(net.core * 3 * third + j * third, 128), third))
        ins.append(Reduce(net, gin.at[j, 1 - net.core], mine, acc_in[j], r_in[j], f_in, region))
    early = SumAll(net, sums, sums_recv)
    final = SumAll(net, late, late_recv)
    edge_at = pl.multiple_of((1 - net.core) * (rows - HALO), HALO)

    def pass_on(n):
        p1[n].wait_recv()

        @pl.when(noisy)
        def _():
            @pl.when(first)
            def _():
                add_to(parts, (n, slice(rows - win, rows), slice(None)), rwin[n, :win, :])

            p2[n].start()

    def phase_one(qb, kb, vb, ob, dob, dk_acc, dv_acc, piece_down, piece_up, piece_out, load_sems, piece_sems):
        blocks = ((q, qb), (k, kb), (v, vb), (o, ob), (do, dob))

        def loads(index):
            n, h = index // quads, index % quads
            cols = pl.ds(pl.multiple_of(h * qw, qw), qw)
            slot = index % 2
            return [
                pltpu.make_async_copy(src.at[n, :, cols], dst.at[slot], load_sems.at[slot, m])
                for m, (src, dst) in enumerate(blocks)
            ]

        for load in loads(0):
            load.start()

        def from_hbm(g, region, acc, piece):
            def run():
                copies = [
                    pltpu.make_async_copy(g.at[at + region], piece.at[m % 2], piece_sems.at[m % 2])
                    for m, at in enumerate(every)
                ]
                copies[0].start()
                for m, at in enumerate(every):
                    if m + 1 < len(every):
                        copies[m + 1].start()
                    copies[m].wait()
                    add_to(acc, at, piece[m % 2])

            return run

        up.advance()
        downs[0].advance()
        downs[1].advance()
        out.advance()
        load_w.wait()
        up.steps[0] = (up.steps[0][0], from_hbm(g_up, own_up, acc_up, piece_up))
        out.steps[0] = (out.steps[0][0], from_hbm(g_out, own_out, acc_out, piece_out))
        for n in range(2):
            downs[n].steps[0] = (downs[n].steps[0][0], from_hbm(g_down, own_down[n], acc_down[n], piece_down))

        @pl.when(noisy)
        def _():
            recv_parts[...] = jnp.zeros_like(recv_parts)

        def partial(n):
            key = jnp.concatenate([dk[n, :win, :], dk[n, pl.ds(halo_at, HALO), :]], axis=0)
            value = jnp.concatenate([dv[n, :win, :], dv[n, pl.ds(halo_at, HALO), :]], axis=0)
            w_key, w_value = w_vm[:, width : 2 * width], w_vm[:, 2 * width :]
            dwin[n] = (dot_nt(key, w_key) + dot_nt(value, w_value)).astype(BF16)
            p1[n].start()

            @pl.when(noisy)
            def _():
                main = slice(win, win + rows)
                parts[n] = (dot_nt(dk[n, main, :], w_key) + dot_nt(dv[n, main, :], w_value)).astype(BF16)

        plan = ((up, downs[0]), (downs[1], out), (), (downs[0],), (up, downs[1], downs[0]), (out, downs[0]))

        def step(index, carry):
            n, h = index // quads, index % quads
            slot = index % 2

            @pl.when(index + 1 < micro * quads)
            def _():
                for load in loads(index + 1):
                    load.start()

            @pl.when(h == 0)
            def _():
                make_bias(lay, n, codes, queries, biases)

            for load in loads(index):
                load.wait()
            attend_back(
                lay, slot, slice(None), qb, kb, vb, ob, dob, lse, index, cos, sin,
                n, h * qw, dq, dk, dv, dk_acc, dv_acc, biases,
            )
            for at, chunks in enumerate(plan):

                @pl.when(index == at)
                def _():
                    for chunk in chunks:
                        chunk.advance()
                    for m in range(micro):
                        if at == m * quads + quads - 1:
                            partial(m)
                        if at == m * quads + quads:
                            pass_on(m)

            return carry

        lax.fori_loop(0, micro * quads, step, 0)

    pl.run_scoped(
        phase_one,
        pltpu.VMEM((2, rows, qw), BF16), pltpu.VMEM((2, keys, qw), BF16), pltpu.VMEM((2, keys, qw), BF16),
        pltpu.VMEM((2, rows, qw), BF16), pltpu.VMEM((2, rows, qw), BF16),
        pltpu.VMEM((keys, qw), F32), pltpu.VMEM((keys, qw), F32),
        pltpu.VMEM((2,) + acc_down[0].shape[bits:], BF16), pltpu.VMEM((2,) + acc_up.shape[bits:], BF16),
        pltpu.VMEM((2,) + acc_out.shape[bits:], BF16),
        pltpu.SemaphoreType.DMA((2, 5)), pltpu.SemaphoreType.DMA((2,)),
    )
    def phase_two(av, at_all, at_own, xv, dxv, sem_a, sem_x):
        load_a = [pltpu.make_async_copy(a.at[n], av.at[n % 1], sem_a.at[n]) for n in range(micro)]
        load_x = [pltpu.make_async_copy(x, xv, sem_x.at[0]), pltpu.make_async_copy(dx2, dxv, sem_x.at[1])]
        load_a[0].start()
        for load in load_x:
            load.start()
        for n in range(micro):
            load_a[n].wait()
            at_all[n] = jnp.transpose(av[0])
            at_own[n] = jnp.transpose(av[0, pl.ds(own_at, rows), :])
            if n + 1 < micro:
                load_a[n + 1].start()
        pass_on(micro - 1)
        sums[...] = jnp.zeros_like(sums)
        sums[6:7, :] = b_up_sums[0:1, :]
        for r, row in ((3, 3), (4, 1), (5, 2), (7, 0)):
            sums[r : r + 1, :width] = mlp_sums[row : row + 1, :]
        follow = ((downs[1], up, out), (downs[0], downs[1], up), (downs[1], out, up))
        for j in range(3):
            for block in range(2):
                col = block * 3 * third + j * third
                source, lhs = ((dq, at_own), (dk, at_all), (dv, at_all))[col // width]
                inside = slice(col % width, col % width + third)
                total = jnp.zeros((width, third), F32)
                count = jnp.zeros((8, third), F32)
                for n in range(micro):
                    rhs = source[n, :, inside]
                    total += dot(lhs[n], rhs)
                    count += dot(jnp.ones((8, rhs.shape[0]), BF16), rhs)
                for m, at in enumerate(every):
                    gin[(j, block) + at] = total[m * slab_in : m * slab_in + slab_in].astype(BF16)
                sums[2:3, col : col + third] = count[0:1]
            ins[j].advance()
            for chunk in follow[j]:
                chunk.advance()
            if j > 0:
                ins[j - 1].advance()
        early.advance()
        ins[2].advance()

        def settle(n):
            @pl.when(clean)
            def _():
                p2[n].wait_recv()

                @pl.when(first)
                def _():
                    add_to(recv_parts, (n, slice(rows - win, rows), slice(None)), rwin[n, :win, :])

            add_to(recv_parts, (n, pl.ds(edge_at, HALO), slice(None)), rwin[n, win:, :])

        for load in load_x:
            load.wait()
        late[...] = jnp.zeros_like(late)
        block = rows // 2
        stores = []
        after = ((ins[0], early), (ins[1], downs[1]), (ins[0], early, ins[2]), (ins[1], early))
        for n in range(micro):
            settle(n)
            for part in range(2):
                here = slice(part * block, part * block + block)
                mine_rows = pl.ds(pl.multiple_of(own_at + part * block, HALO), block)
                da = dot_nt(dq[n, here, :], w_vm[:, :width])
                da += dot_nt(dk[n, mine_rows, :], w_vm[:, width : 2 * width])
                da += dot_nt(dv[n, mine_rows, :], w_vm[:, 2 * width :])
                da += recv_parts[n, here, :].astype(F32)
                normed, inverse = norm_stats(xv[n, here, :].astype(F32))
                dxv[n, here, :] += norm_back(da, normed, inverse, gain)
                late[0:1, :] += jnp.sum(da * normed, axis=0, keepdims=True)
                late[1:2, :] += jnp.sum(da, axis=0, keepdims=True)
                for chunk in after[2 * n + part]:
                    chunk.advance()
            store = pltpu.make_async_copy(dxv.at[n], grad_in.at[n], sem_x.at[2 + n])
            store.start()
            stores.append(store)
        chunks = [final, early] + ins + [up, out] + downs
        while any(c.at <= len(c.steps if isinstance(c, Reduce) else c.copies) for c in chunks):
            for chunk in chunks:
                chunk.advance()
        late_out[...] = final.finish()
        sums_out[...] = early.finish()
        for chunk in ins + [up, out] + downs:
            chunk.finish()
        puts = [
            net.local(src, dst)
            for src, dst in ((f_in, f_in_out), (f_out, f_out_out), (f_up, f_up_out), (f_down, f_down_out))
        ]
        for put in puts:
            put.start()
        for put in puts + stores:
            put.wait()
        for copy in p1:
            copy.wait_send()

        @pl.when(noisy)
        def _():
            for copy in p2:
                copy.wait_send()

    pl.run_scoped(
        phase_two,
        pltpu.VMEM((1, keys, width), BF16), pltpu.VMEM((micro, width, keys), BF16),
        pltpu.VMEM((micro, width, rows), BF16), pltpu.VMEM((micro, rows, width), BF16),
        pltpu.VMEM((micro, rows, width), F32),
        pltpu.SemaphoreType.DMA((micro,)), pltpu.SemaphoreType.DMA((4,)),
    )


def front_remote(
    lay, role, sizes, inputs, segment_ids, block_ids, small, weights, freqs, lse_shape, bias_scratch, spans, attn_flops
):
    micro, rows, width = inputs.shape
    keys, win = lay["keys"], lay["win"]
    bits = lax.axis_size("fsdp").bit_length() - 1
    lanes = -(-max(sizes) // 128) * 128
    pack = jnp.stack([jnp.pad(p.astype(F32), (0, lanes - p.shape[0])) for p in small])
    full = [like((2,) * bits + p.shape, BF16) for p in weights]
    longest = max(sizes) << bits
    table_rows = win + rows + HALO
    shapes = full + [
        like((micro, rows, width), BF16), like((micro, keys, width), BF16), like((micro, keys, width), BF16),
        like((micro, keys, width), BF16), like((micro, rows, width), BF16), like(lse_shape, F32),
        like((8, longest), F32), like((table_rows, 128), F32), like((table_rows, 128), F32),
        like((micro, keys, 1), F32), like((micro, 8, rows), F32),
    ]
    remote = 3 * micro + 1 + bits * 8 + 10
    outs = pl.pallas_call(
        functools.partial(front_kernel, lay, bits, sizes),
        in_specs=[VMEM] * 9,
        out_specs=[ANY] * 10 + [VMEM] * 5,
        out_shape=shapes,
        scratch_shapes=[
            pltpu.VMEM((micro, rows, width), BF16), pltpu.VMEM((micro, win + HALO, width), BF16),
            pltpu.VMEM((width, 3 * width), BF16), pltpu.VMEM((micro, rows, width), BF16),
            pltpu.VMEM((micro, keys, width), BF16), pltpu.VMEM((micro, keys, width), BF16),
            pltpu.VMEM((micro, keys, width), BF16), pltpu.VMEM((micro, rows, width), BF16),
            pltpu.VMEM(lse_shape, F32), pltpu.VMEM((2,) * bits + (8, lanes), F32),
            pltpu.SemaphoreType.DMA((remote,)), pltpu.SemaphoreType.DMA((remote,)),
            pltpu.SemaphoreType.DMA((32,)),
        ] + bias_scratch,
        compiler_params=pltpu.CompilerParams(
            vmem_limit_bytes=VMEM_BYTES, collective_id=0, has_side_effects=True
        ),
        cost_estimate=pl.CostEstimate(flops=2 * attn_flops, bytes_accessed=40 << 20, transcendentals=0),
        name="front",
    )(inputs, segment_ids, block_ids, pack, freqs, *weights)
    joined = [w.reshape((-1, w.shape[-1])) for w in outs[:4]]
    return tuple(joined) + tuple(outs[4:])


def front_native(
    lay, role, sizes, inputs, segment_ids, block_ids, small, weights, freqs, lse_shape, bias_scratch, spans, attn_flops
):
    micro, rows, width = inputs.shape
    keys, win, length = lay["keys"], lay["win"], lay["length"]
    clean, half = role[0], role[1]
    pairs = [(0, 1), (1, 0), (2, 3), (3, 2)]
    xb = lax.ppermute(inputs, "seq", [(2, 0), (3, 1)])
    xmain = jnp.where(clean == 1, inputs, xb)
    edge = jnp.where(half == 0, inputs[:, rows - HALO :], inputs[:, :HALO])
    xc = lax.ppermute(jnp.concatenate([xmain[:, rows - win :], edge], axis=1), "seq", pairs)
    start = half * rows
    edge_at = jnp.where(half == 0, rows, -HALO)
    positions = start + jnp.concatenate([jnp.arange(-win, rows), edge_at + jnp.arange(HALO)])
    turned = positions.astype(F32)[:, None] * freqs
    sine = jnp.sin(turned)
    cos = jnp.cos(turned)
    sin = jnp.where(jnp.arange(128)[None] % HD < HD // 2, -sine, sine)
    code = segment_ids * SEG_STEP + block_ids
    padded = jnp.pad(code, ((0, 0), (win, 0)), constant_values=-1)
    key_codes = lax.dynamic_slice_in_dim(padded, start, win + rows, 1)
    own_code = lax.dynamic_slice_in_dim(code, start, rows, 1)
    own_seg = lax.dynamic_slice_in_dim(segment_ids, start, rows, 1)
    before, after = code[:, rows - HALO : rows], code[:, rows : rows + HALO]
    codes = jnp.concatenate(
        [
            key_codes,
            jnp.where((clean == 1) & (half == 0), after, -1),
            jnp.where((clean == 0) & (half == 1), before, -2),
            jnp.where(clean == 0, own_code, -2),
            jnp.where((clean == 0) & (half == 0), after, -2),
            jnp.full((micro, keys - lay["used"]), -2, jnp.int32),
        ],
        axis=1,
    )[:, :, None].astype(F32)
    queries = jnp.stack([own_seg * SEG_STEP, own_code - (1 - clean), own_code], axis=1)
    queries = jnp.concatenate([queries, jnp.zeros((micro, 5, rows), jnp.int32)], axis=1).astype(F32)
    packed = lax.all_gather(jnp.concatenate(small)[None], "fsdp", axis=0, tiled=True)
    vectors, at = [], 0
    longest = max(sizes) * packed.shape[0]
    for size in sizes:
        one = packed[:, at : at + size].reshape(-1).astype(F32)
        vectors.append(jnp.pad(one, (0, longest - one.shape[0])))
        at += size
    vec = jnp.stack(vectors)
    w_in, w_out, w_up, w_down = (lax.all_gather(p, "fsdp", axis=0, tiled=True) for p in weights)
    per_seq = lambda n, d: pl.BlockSpec((1, n, d), lambda s: (s, 0, 0))
    table_rows = win + rows + HALO
    q, k, v, a = call(
        functools.partial(qkv_kernel, lay), (micro,),
        [SMEM(), per_seq(rows, width), per_seq(rows, width), per_seq(win + HALO, width),
         whole((width, 3 * width)), whole(vec.shape), whole((table_rows, 128)), whole((table_rows, 128))],
        [per_seq(rows, width), per_seq(keys, width), per_seq(keys, width), per_seq(keys, width)],
        [like((micro, rows, width), BF16)] + [like((micro, keys, width), BF16)] * 3,
        [], 2 * micro * rows * width * 3 * width * 2, 20 << 20, "qkv",
    )(role, inputs, xb, xc, w_in, vec, cos, sin)
    qw = QUAD * HD
    quads = width // qw
    quad_block = lambda n: pl.BlockSpec((1, n, qw), lambda s, h: (s, 0, h))
    o, lse = call(
        functools.partial(attend_kernel, lay), (micro, quads),
        [pl.BlockSpec((1, keys, 1), lambda s, h: (s, 0, 0)), pl.BlockSpec((1, 8, rows), lambda s, h: (s, 0, 0)),
         quad_block(rows), quad_block(keys), quad_block(keys)],
        [quad_block(rows), pl.BlockSpec((1,) + lse_shape[1:], lambda s, h: (s * quads + h, 0, 0))],
        [like((micro, rows, width), BF16), like(lse_shape, F32)],
        bias_scratch, 2 * attn_flops, 12 << 20, "attend",
    )(codes, queries, q, k, v)
    return w_in, w_out, w_up, w_down, q, k, v, a, o, lse, vec, cos, sin, codes, queries


def back_remote(
    lay, role, sizes, inputs, codes, queries, lse, cos, sin, vec, g_b_up, g_mlp,
    q, k, v, o, do, a, w_in, grads, dx2, bias_scratch, attn_flops,
):
    micro, rows, width = inputs.shape
    keys, win = lay["keys"], lay["win"]
    bits = lax.axis_size("fsdp").bit_length() - 1
    lead = (2,) * bits
    g_out, g_up, g_down = (g.reshape(lead + (g.shape[0] >> bits, g.shape[1])) for g in grads)
    slab, hidden, slab_down = g_up.shape[bits], g_up.shape[-1], g_down.shape[bits]
    third = width // 2

    def bank(r, c, x_cols=None):
        full = pltpu.VMEM(lead + (r, c), BF16)
        cols = c if x_cols is None else x_cols
        over = [pltpu.VMEM(lead[: bits - 1 - b] + (r, cols), BF16) for b in range(bits)]
        if x_cols is None:
            return full, over + [pltpu.VMEM((r, c), BF16)]
        return full, [pltpu.VMEM(lead + (r, cols), BF16)] + over

    acc_in, r_in = zip(*[bank(slab, third) for _ in range(3)])
    acc_out, r_out = bank(slab, width // 2)
    acc_up, r_up = bank(slab, hidden // 2, hidden // 4)
    acc_down, r_down = zip(*[bank(slab_down // 4, width) for _ in range(2)])
    stages = 2 + bits
    remote = 7 * (bits + 3) + 2 * stages + 4 * micro
    scratch = [
        pltpu.VMEM((micro, rows, width), BF16), pltpu.VMEM((micro, keys, width), BF16),
        pltpu.VMEM((micro, keys, width), BF16), pltpu.VMEM((width, 3 * width), BF16),
        pltpu.VMEM((3, 2) + lead + (slab, third), BF16),
        pltpu.VMEM((micro, rows, width), BF16), pltpu.VMEM((micro, rows, width), BF16),
        pltpu.VMEM((micro, win + HALO, width), BF16), pltpu.VMEM((micro, win + HALO, width), BF16),
        tuple(acc_in), acc_out, acc_up, tuple(acc_down),
        tuple(tuple(r) for r in r_in), tuple(r_out), tuple(r_up), tuple(tuple(r) for r in r_down),
        pltpu.VMEM((slab, 3 * width), BF16), pltpu.VMEM((slab, width), BF16), pltpu.VMEM((slab, hidden), BF16),
        pltpu.VMEM((slab_down, width), BF16),
        pltpu.VMEM((8, hidden), F32), pltpu.VMEM((2 * stages, 8, hidden), F32),
        pltpu.VMEM((8, width), F32), pltpu.VMEM((2 * stages, 8, width), F32),
        pltpu.SemaphoreType.DMA((remote,)), pltpu.SemaphoreType.DMA((remote,)),
        pltpu.SemaphoreType.DMA((16,)),
    ] + bias_scratch
    grad_in, f_in, f_out, f_up, f_down, sums, late = pl.pallas_call(
        functools.partial(back_kernel, lay, bits),
        in_specs=[VMEM] * 8 + [ANY] * 12,
        out_specs=[ANY] * 5 + [VMEM] * 2,
        out_shape=[
            like((micro, rows, width), F32), like((slab, 3 * width), BF16), like((slab, width), BF16),
            like((slab, hidden), BF16), like((slab_down, width), BF16), like((8, hidden), F32), like((8, width), F32),
        ],
        scratch_shapes=scratch,
        compiler_params=pltpu.CompilerParams(
            vmem_limit_bytes=67043328, collective_id=1, has_side_effects=True
        ),
        cost_estimate=pl.CostEstimate(flops=6 * attn_flops, bytes_accessed=60 << 20, transcendentals=0),
        name="back",
    )(codes, queries, lse, cos, sin, vec, g_b_up, g_mlp, q, k, v, o, do, a, w_in, g_out, g_up, g_down, inputs, dx2)
    f = lax.axis_index("fsdp")
    vectors = []
    for r, size in enumerate(sizes):
        source = late if r < 2 else sums
        vectors.append(lax.dynamic_slice(source, (r, f * size), (1, size))[0])
    return grad_in, [g.astype(F32) for g in (f_in, f_out, f_up, f_down)], vectors


def back_native(
    lay, role, sizes, inputs, codes, queries, lse, cos, sin, vec, g_b_up, g_mlp,
    q, k, v, o, do, a, w_in, grads, dx2, bias_scratch, attn_flops,
):
    micro, rows, width = inputs.shape
    keys, win = lay["keys"], lay["win"]
    clean, half = role[0], role[1]
    pairs = [(0, 1), (1, 0), (2, 3), (3, 2)]
    fsdp_n = lax.axis_size("fsdp")
    g_w_out, g_w_up, g_w_down = grads
    qw = QUAD * HD
    quads = width // qw
    total = micro * rows
    flat = lambda z: z.reshape(total, width)
    per_seq = lambda n, d: pl.BlockSpec((1, n, d), lambda s: (s, 0, 0))
    role_spec = SMEM()
    quad_block = lambda n: pl.BlockSpec((1, n, qw), lambda s, h: (s, 0, h))
    code_spec = pl.BlockSpec((1, keys, 1), lambda s, h: (s, 0, 0))
    query_spec = pl.BlockSpec((1, 8, rows), lambda s, h: (s, 0, 0))
    lse_spec = pl.BlockSpec((1,) + lse.shape[1:], lambda s, h: (s * quads + h, 0, 0))
    table = pl.BlockSpec((win + rows + HALO, 128), lambda s, h: (0, 0), pipeline_mode=pl.Buffered(1))
    dq, dk, dv = call(
        functools.partial(attend_back_kernel, lay), (micro, quads),
        [code_spec, query_spec, quad_block(rows), quad_block(keys), quad_block(keys),
         quad_block(rows), quad_block(rows), lse_spec, table, table],
        [quad_block(rows), quad_block(keys), quad_block(keys)],
        [like((micro, rows, width), BF16), like((micro, keys, width), BF16), like((micro, keys, width), BF16)],
        [pltpu.VMEM((keys, qw), F32), pltpu.VMEM((keys, qw), F32)] + bias_scratch,
        5 * attn_flops, 24 << 20, "attend_back",
    )(codes, queries, q, k, v, o, do, lse, cos, sin)

    da_own, da_main, da_win, g_w_in, g_b_in = call(
        functools.partial(qkv_back_kernel, lay), (micro,),
        [role_spec, per_seq(keys, width), per_seq(rows, width), per_seq(keys, width), per_seq(keys, width),
         whole((width, 3 * width))],
        [per_seq(rows, width), per_seq(rows, width), per_seq(win + HALO, width),
         whole((width, 3 * width)), whole((8, 3 * width))],
        [like((micro, rows, width), F32), like((micro, rows, width), BF16), like((micro, win + HALO, width), BF16),
         like((width, 3 * width), BF16), like((8, 3 * width), F32)],
        [pltpu.VMEM((width, 3 * width), F32)], 2 * 2 * micro * rows * width * 3 * width * 2, 40 << 20, "qkv_back",
    )(role, a, dq, dk, dv, w_in)

    from_pair = lax.ppermute(da_win, "seq", pairs).astype(F32)
    from_second = jnp.where(half == 0, from_pair[:, :win], 0.0)
    edge = from_pair[:, win:]
    gap = jnp.zeros((micro, rows - HALO, width), F32)
    edges = jnp.where(
        half == 0, jnp.concatenate([gap, edge], axis=1), jnp.concatenate([edge, gap], axis=1)
    )
    added = jnp.pad(from_second, ((0, 0), (rows - win, 0), (0, 0)))
    to_clean = (jnp.where(clean == 0, da_main.astype(F32), 0.0) + added).astype(BF16)
    from_noisy = lax.ppermute(to_clean, "seq", [(0, 2), (1, 3)])
    extra = jnp.where(clean == 1, from_noisy.astype(F32) + added, 0.0) + edges

    grad_in, g_attn = call(
        final_kernel, (2,),
        [pl.BlockSpec((total // 2, width), lambda i: (i, 0))] * 4 + [whole((1, width))],
        [pl.BlockSpec((total // 2, width), lambda i: (i, 0)), whole((8, width))],
        [like((total, width), F32), like((8, width), F32)], [], 0, 16 << 20, "norm_back",
    )(flat(inputs), flat(da_own), flat(extra), flat(dx2), vec[0:1, :width])

    def scatter(g):
        return lax.psum(lax.psum_scatter(g, "fsdp", scatter_dimension=0, tiled=True), "seq")

    big = [scatter(g).astype(F32) for g in (g_w_in, g_w_out, g_w_up, g_w_down)]
    smalls = [g_attn[0], g_attn[1], g_b_in[0], g_mlp[3], g_mlp[1], g_mlp[2], g_b_up[0], g_mlp[0]]
    pack = jnp.concatenate([g.reshape(fsdp_n, -1) for g in smalls], axis=1)
    pack = lax.psum(pack, ("seq", "fsdp"))
    mine = lax.dynamic_slice_in_dim(pack, lax.axis_index("fsdp"), 1, 0)[0]
    outs, at = [], 0
    for size in sizes:
        outs.append(mine[at : at + size])
        at += size
    return grad_in.reshape(micro, rows, width), big, outs


def per_device(
    inputs, segment_ids, block_ids, attn_gain, attn_shift, proj_in, bias_in, proj_out, bias_out,
    mlp_gain, mlp_shift, weight_up, bias_up, weight_down, bias_down, cotangent,
):
    micro, rows, width = inputs.shape
    length = segment_ids.shape[1]
    hidden = weight_up.shape[1]
    seq_n = lax.axis_size("seq")
    fsdp_n = lax.axis_size("fsdp")
    assert seq_n == 4 and seq_n * rows == 2 * length
    lay = layout(rows, length)
    win, keys = lay["win"], lay["keys"]
    me = lax.axis_index("seq")
    clean = me // 2
    half = me % 2
    role = jnp.stack([clean, half]).astype(jnp.int32)
    pairs = [(0, 1), (1, 0), (2, 3), (3, 2)]
    small = (attn_gain, attn_shift, bias_in, bias_out, mlp_gain, mlp_shift, bias_up, bias_down)
    sizes = [p.shape[0] for p in small]
    weights = (proj_in, proj_out, weight_up, weight_down)
    half_dim = HD // 2
    freqs = (10000.0 ** (-(np.arange(half_dim, dtype=np.float32) / half_dim))).astype(np.float32)
    freqs = np.tile(freqs, 4)[None]
    quads = width // (QUAD * HD)
    qw = QUAD * HD
    spans = [hi - lo + NEAR for lo, hi in windows(lay)]
    bias_scratch = [pltpu.VMEM((n, TILE), F32) for n in spans]
    per_seq = lambda n, d: pl.BlockSpec((1, n, d), lambda s: (s, 0, 0))
    role_spec = SMEM()
    attn_flops = micro * quads * sum(spans) * QUAD * TILE * qw * 2
    lse_shape = (micro * quads, rows // TILE, QUAD * TILE)
    table_rows = win + rows + HALO
    aligned = fsdp_n & (fsdp_n - 1) == 0 and all(p.shape[0] % (4 * HALO) in (0, 32) for p in weights)
    front = front_remote if aligned else front_native
    (w_in, w_out, w_up, w_down, q, k, v, a, o, lse, vec, cos, sin, codes, queries) = front(
        lay, role, sizes, inputs, segment_ids, block_ids, small, weights, freqs,
        lse_shape, bias_scratch, spans, attn_flops,
    )
    total = micro * rows
    flat = lambda z: z.reshape(total, width)
    chunk = min(512, hidden)
    rows_spec = whole((total, width))
    out_rows, dx2, do, g_w_out, g_w_up, g_b_up, g_w_down, g_mlp = call(
        mlp_kernel, (hidden // chunk,),
        [rows_spec, rows_spec, rows_spec, whole((width, width)), whole(vec.shape),
         pl.BlockSpec((width, chunk), lambda j: (0, j)), pl.BlockSpec((8, chunk), lambda j: (0, j)),
         pl.BlockSpec((chunk, width), lambda j: (j, 0))],
        [rows_spec, rows_spec, rows_spec, whole((width, width)),
         pl.BlockSpec((width, chunk), lambda j: (0, j)), pl.BlockSpec((8, chunk), lambda j: (0, j)),
         pl.BlockSpec((chunk, width), lambda j: (j, 0)), whole((8, width))],
        [like((total, width), BF16), like((total, width), F32), like((total, width), BF16),
         like((width, width), BF16), like((width, hidden), BF16), like((8, hidden), F32),
         like((hidden, width), BF16), like((8, width), F32)],
        [pltpu.VMEM((total, width), F32), pltpu.VMEM((total, width), BF16), pltpu.VMEM((width, total), BF16),
         pltpu.VMEM((total, 1), F32), pltpu.VMEM((total, width), F32), pltpu.VMEM((total, width), F32)],
        2 * total * width * (6 * hidden + 3 * width), 40 << 20, "mlp",
    )(flat(o), flat(inputs), flat(cotangent), w_out, vec, w_up, vec, w_down)

    back = back_remote if aligned else back_native
    grad_in, big, vectors = back(
        lay, role, sizes, inputs, codes, queries, lse, cos, sin, vec, g_b_up, g_mlp,
        q, k, v, o, do.reshape(micro, rows, width), a, w_in, (g_w_out, g_w_up, g_w_down), dx2.reshape(micro, rows, width),
        bias_scratch, attn_flops,
    )
    g_gain1, g_shift1, g_bin, g_bout, g_gain2, g_shift2, g_bup, g_bdown = vectors
    return (
        out_rows.reshape(micro, rows, width), grad_in, g_gain1, g_shift1, big[0], g_bin, big[1], g_bout,
        g_gain2, g_shift2, big[2], g_bup, big[3], g_bdown,
    )


def solution(mesh):
    rows = P("fsdp", "seq", None)
    one, two = P("fsdp"), P("fsdp", None)
    params = (one, one, two, one, two, one, one, one, two, one, two, one)
    return jax.shard_map(
        per_device,
        mesh=mesh,
        in_specs=(rows, two, two) + params + (rows,),
        out_specs=(rows, rows) + params,
        check_vma=False,
    )
```

```python
import functools
import itertools

import jax
import jax.numpy as jnp
import numpy as np
from jax import lax
from jax.experimental import pallas as pl
from jax.experimental.pallas import tpu as pltpu
from jax.sharding import PartitionSpec as P

HD = 64
QUAD = 4
TILE = 128
HALO = 16
NEAR = TILE + 2 * HALO
EPS = 1e-05
MASKED = -1e30
SEG_STEP = 4096
F32 = jnp.float32
BF16 = jnp.bfloat16
VMEM_BYTES = 62 * 1024 * 1024
MESH = pl.DeviceIdType.MESH
ANY = pl.BlockSpec(memory_space=pl.ANY)
VMEM = pl.BlockSpec(memory_space=pltpu.VMEM)


def dot(a, b):
    return jnp.dot(a, b, preferred_element_type=F32)


def dot_nt(a, b):
    return lax.dot_general(a, b, (((1,), (1,)), ((), ())), preferred_element_type=F32)


def dot_tn(a, b):
    return lax.dot_general(a, b, (((0,), (0,)), ((), ())), preferred_element_type=F32)


def norm_stats(x):
    center = jnp.mean(x, axis=-1, keepdims=True)
    centered = x - center
    inverse = lax.rsqrt(jnp.mean(centered * centered, axis=-1, keepdims=True) + EPS)
    return centered * inverse, inverse


def norm_back(grad, normed, inverse, gain):
    scaled = grad * gain
    first = jnp.mean(scaled, axis=-1, keepdims=True)
    second = jnp.mean(scaled * normed, axis=-1, keepdims=True)
    return inverse * (scaled - first - normed * second)


def partner(u):
    lane = lax.broadcasted_iota(jnp.int32, u.shape, 1)
    half = HD // 2
    return jnp.where(
        lane % HD < half, pltpu.roll(u, u.shape[1] - half, 1), pltpu.roll(u, half, 1)
    )


def whole(shape):
    return pl.BlockSpec(shape, lambda *_: (0,) * len(shape), pipeline_mode=pl.Buffered(1))


def call(kernel, grid, in_specs, out_specs, out_shape, scratch, flops, nbytes, name):
    return pl.pallas_call(
        kernel,
        grid=grid,
        in_specs=in_specs,
        out_specs=out_specs,
        out_shape=out_shape,
        scratch_shapes=scratch,
        compiler_params=pltpu.CompilerParams(vmem_limit_bytes=VMEM_BYTES),
        cost_estimate=pl.CostEstimate(flops=flops, bytes_accessed=nbytes, transcendentals=0),
        name=name,
    )


def like(shape, dtype):
    return jax.ShapeDtypeStruct(shape, dtype)


SMEM = functools.partial(pl.BlockSpec, memory_space=pltpu.SMEM)


def layout(rows, length):
    win = rows - length // 8
    noisy = win + rows + HALO
    used = noisy + rows + 2 * HALO
    return dict(rows=rows, win=win, length=length, noisy=noisy, used=used, keys=-(-used // 256) * 256)


def places(lay, role):
    noisy = role[0] == 0
    second = role[1] == 1
    own_at = jnp.where(noisy, lay["noisy"] + HALO, lay["win"])
    halo_at = jnp.where(
        second,
        lay["noisy"],
        jnp.where(noisy, lay["noisy"] + HALO + lay["rows"], lay["win"] + lay["rows"]),
    )
    return noisy, second, pl.multiple_of(own_at, HALO), pl.multiple_of(halo_at, HALO)


def qkv_rows(lay, where_am, n, x, xb, xc, w, b, gain, shift, cos, sin, q_out, k_out, v_out, a_out):
    width = x.shape[2]
    rows, win = lay["rows"], lay["win"]
    noisy, second, own_at, halo_at = where_am

    def norm(v):
        normed, _ = norm_stats(v.astype(F32))
        return (normed * gain + shift).astype(BF16)

    def zeros(at, count):
        for ref in (k_out, v_out, a_out):
            ref[n, at : at + count, :] = jnp.zeros((count, width), BF16)

    def section(a, parts, table, want_q):
        def put(ref, col, value):
            for begin, count, at in parts:
                ref[n, pl.ds(at, count), col : col + value.shape[1]] = value[begin : begin + count]

        put(a_out, 0, a)
        c = cos[table : table + a.shape[0], :]
        s = sin[table : table + a.shape[0], :]
        first = 0 if want_q else width
        for col in range(first, 3 * width, 256):
            part = dot(a, w[:, col : col + 256]) + b[:, col : col + 256]
            for piece in range(2):
                u = part[:, piece * 128 : piece * 128 + 128]
                at_col = col + piece * 128
                if at_col < 2 * width:
                    u = u * c + partner(u) * s
                if at_col < width:
                    q_out[n, :, at_col : at_col + 128] = (u[:rows] * (HD**-0.5)).astype(BF16)
                elif at_col < 2 * width:
                    put(k_out, at_col - width, u.astype(BF16))
                else:
                    put(v_out, at_col - 2 * width, u.astype(BF16))

    zeros(win + rows, 2 * HALO)
    zeros(lay["used"] - HALO, lay["keys"] - lay["used"] + HALO)
    own = jnp.concatenate([norm(x[n]), norm(xc[n, win:, :])], axis=0)
    section(own, ((0, rows, own_at), (rows, HALO, halo_at)), win, True)

    @pl.when(noisy)
    def _():
        section(norm(xb[n]), ((0, rows, win),), win, False)

    @pl.when(jnp.logical_not(noisy))
    def _():
        zeros(lay["noisy"] + HALO, rows)

    @pl.when(second)
    def _():
        section(norm(xc[n, :win, :]), ((0, win, 0),), 0, False)

    @pl.when(jnp.logical_not(second))
    def _():
        zeros(0, win)


def qkv_kernel(lay, role, x, xb, xc, w, vec, cos, sin, *outs):
    width = x.shape[2]
    gain, shift, b = vec[0:1, :width], vec[1:2, :width], vec[2:3, : 3 * width]
    qkv_rows(lay, places(lay, role), 0, x, xb, xc, w, b, gain, shift, cos, sin, *outs)


def windows(lay):
    rows, win, length = lay["rows"], lay["win"], lay["length"]
    longest, earliest, latest = length // 2, length // 8, 3 * length // 8
    found = []
    for at in range(0, rows, TILE):
        begin = win + rows
        for origin in range(0, length, rows):
            pos = origin + at
            low = max(pos - longest, 0)
            if origin > 0:
                low = max(low, earliest)
            if pos >= latest + longest:
                low = max(low, earliest + longest)
            begin = min(begin, low - origin + win)
        found.append((begin // TILE * TILE, win + at + TILE + HALO))
    return found


def make_bias(lay, n, codes, queries, biases):
    for t, (lo, hi) in enumerate(windows(lay)):
        here = slice(t * TILE, t * TILE + TILE)
        low, high, same = (queries[n, r : r + 1, here] for r in range(3))
        kc = codes[n, lo:hi, :]
        ok = (kc >= low) & (kc <= high)
        biases[t][: hi - lo, :] = jnp.where(ok, 0.0, MASKED)
        near = lay["noisy"] + t * TILE
        kn = codes[n, near : near + NEAR, :]
        biases[t][hi - lo :, :] = jnp.where(kn == same, 0.0, MASKED)


def stacked(tile):
    lane = lax.broadcasted_iota(jnp.int32, tile.shape, 1)
    zero = jnp.zeros_like(tile)
    return jnp.concatenate(
        [jnp.where(lane // HD == h, tile, zero) for h in range(QUAD)], axis=0
    )


def own_heads(wide):
    return jnp.concatenate(
        [wide[h * HD : h * HD + HD, h * TILE : h * TILE + TILE] for h in range(QUAD)], axis=0
    )


def keys_of(ref, lay, n, cols, t, lo, hi):
    near = lay["noisy"] + t * TILE
    return jnp.concatenate([ref[n, lo:hi, cols], ref[n, near : near + NEAR, cols]], axis=0)


def attend(lay, n, cols, q, k, v, o_out, lse_out, lse_at, biases):
    for t, (lo, hi) in enumerate(windows(lay)):
        here = slice(t * TILE, t * TILE + TILE)
        qm = stacked(q[n, here, cols])
        kk = keys_of(k, lay, n, cols, t, lo, hi)
        vv = keys_of(v, lay, n, cols, t, lo, hi)
        s = dot_nt(kk, qm) + jnp.concatenate([biases[t][...]] * QUAD, axis=1)
        peak = jnp.max(s, axis=0, keepdims=True)
        p = jnp.exp(s - peak)
        total = jnp.sum(p, axis=0, keepdims=True)
        wide = dot_tn(vv, p.astype(BF16)) * (1.0 / total)
        o_out[n, here, cols] = jnp.transpose(own_heads(wide)).astype(BF16)
        lse_out[lse_at, t : t + 1, :] = peak + jnp.log(total)


def attend_kernel(lay, codes, queries, q, k, v, o_out, lse_out, *biases):
    @pl.when(pl.program_id(1) == 0)
    def _():
        make_bias(lay, 0, codes, queries, biases)

    attend(lay, 0, slice(None), q, k, v, o_out, lse_out, 0, biases)


def attend_back(
    lay, n, cols, q, k, v, m, cols_m, o, do, lse, lse_at, cos, sin, to, col, dq_out, dk_out, dv_out, dk_acc, dv_acc, biases
):
    rows, win = lay["rows"], lay["win"]
    qw = QUAD * HD

    def lanes(piece):
        return pl.ds(pl.multiple_of(col + piece * 128, 128), 128)

    dk_acc[...] = jnp.zeros_like(dk_acc)
    dv_acc[...] = jnp.zeros_like(dv_acc)
    for t, (lo, hi) in enumerate(windows(lay)):
        here = slice(t * TILE, t * TILE + TILE)
        size = hi - lo
        near = slice(lay["noisy"] + t * TILE, lay["noisy"] + t * TILE + NEAR)
        qm = stacked(q[n, here, cols])
        dom = stacked(do[m, here, cols_m])
        kk = keys_of(k, lay, n, cols, t, lo, hi)
        vv = keys_of(v, lay, n, cols, t, lo, hi)
        both = jnp.transpose(do[m, here, cols_m].astype(F32) * o[m, here, cols_m].astype(F32))
        delta = jnp.concatenate(
            [jnp.sum(both[h * HD : h * HD + HD, :], axis=0, keepdims=True) for h in range(QUAD)],
            axis=1,
        )
        s = dot_nt(kk, qm) + jnp.concatenate([biases[t][...]] * QUAD, axis=1)
        p = jnp.exp(s - lse[lse_at, t : t + 1, :])
        dp = dot_nt(vv, dom)
        ds = (p * (dp - delta)).astype(BF16)
        pb = p.astype(BF16)
        dv = dot(pb, dom)
        dk = dot(ds, qm)
        dv_acc[lo:hi, :] += dv[:size]
        dk_acc[lo:hi, :] += dk[:size]
        dv_acc[near, :] += dv[size:]
        dk_acc[near, :] += dk[size:]
        wide = dot_tn(kk, ds)
        dq = jnp.transpose(own_heads(wide)) * (HD**-0.5)
        c = cos[win + t * TILE : win + t * TILE + TILE, :]
        sn = sin[win + t * TILE : win + t * TILE + TILE, :]
        for piece in range(2):
            u = dq[:, piece * 128 : piece * 128 + 128]
            dq_out[to, here, lanes(piece)] = (u * c - partner(u) * sn).astype(BF16)
    for piece in range(2):
        dv_out[to, :, lanes(piece)] = dv_acc[:, piece * 128 : piece * 128 + 128].astype(BF16)
    half = (cos[win + rows :, :], sin[win + rows :, :])
    own = (cos[win : win + rows, :], sin[win : win + rows, :])
    tables = (
        (0, (cos[: win + rows, :], sin[: win + rows, :])),
        (win + rows, half),
        (lay["noisy"], half),
        (lay["noisy"] + HALO, own),
        (lay["used"] - HALO, half),
    )
    for at, (c, sn) in tables:
        here = slice(at, at + c.shape[0])
        for piece in range(2):
            u = dk_acc[here, piece * 128 : piece * 128 + 128]
            dk_out[to, here, lanes(piece)] = (u * c - partner(u) * sn).astype(BF16)
    spare = lay["keys"] - lay["used"]
    for piece in range(2):
        dk_out[to, lay["used"] :, lanes(piece)] = jnp.zeros((spare, 128), BF16)


def attend_back_kernel(
    lay, codes, queries, q, k, v, o, do, lse, cos, sin, dq_out, dk_out, dv_out, dk_acc, dv_acc, *biases
):
    @pl.when(pl.program_id(1) == 0)
    def _():
        make_bias(lay, 0, codes, queries, biases)

    attend_back(
        lay, 0, slice(None), q, k, v, 0, slice(None), o, do, lse, 0, cos, sin, 0, 0, dq_out, dk_out, dv_out, dk_acc, dv_acc, biases
    )


def bit_of(index, b):
    return (index // (1 << b)) % 2


def other(index, b):
    return index + (1 << b) * (1 - 2 * bit_of(index, b))


class Net:
    def __init__(self, bits, send, recv, sems):
        self.me, self.f, self.bits = lax.axis_index("seq"), lax.axis_index("fsdp"), bits
        self.core, self.x = self.me % 2, self.me // 2
        self.send, self.recv, self.sems = send, recv, sems
        self.used, self.local_used = 0, 0
        self.started = []

    def partners(self):
        return [{"seq": other(self.me, 0)}, {"seq": other(self.me, 1)}] + [
            {"fsdp": other(self.f, b)} for b in range(self.bits)
        ]

    def barrier(self):
        barrier = pltpu.get_barrier_semaphore()
        for device in self.partners():
            pl.semaphore_signal(barrier, inc=1, device_id=device, device_id_type=MESH)
        pl.semaphore_wait(barrier, 2 + self.bits)

    def copy(self, src, dst, device):
        n = self.used
        self.used += 1
        return pltpu.make_async_remote_copy(
            src_ref=src, dst_ref=dst, send_sem=self.send.at[n], recv_sem=self.recv.at[n],
            device_id=device, device_id_type=MESH,
        )

    def local(self, src, dst):
        n = self.local_used
        self.local_used += 1
        return pltpu.make_async_copy(src, dst, self.sems.at[n])

    def fsdp_index(self, done):
        return tuple(slice(None) if b in done else bit_of(self.f, b) for b in range(self.bits - 1, -1, -1))


FRONT_ORDER = (
    "s i0 i1 E",
    "T R0 s i2",
    "i0 i1 i2 i0",
    "s u0 i1 s",
    "u1 i2 R1 o",
    "u0 V P0 i1",
    "i0 i1 i2 u1",
    "i0 o u0 d0",
    "i2 L u1 W",
    "Q0 d0 u0 d1",
    "o P1 Q1 d1",
    "d0 A o u1",
    "A d1 A d0",
    "u0 A u1 A",
    "u0 d1 A d0",
    "o u1",
)
FRONT_BITS = {
    "i0": ((2, 0, 1), False),
    "i1": ((2, 1, 0), False),
    "i2": ((2, 1, 0), False),
    "o": ((2, 1, 0), False),
    "u0": ((2, 1, 0), True),
    "u1": ((2, 1, 0), True),
    "d0": ((2, 1, 0), False),
    "d1": ((0, 2, 1), False),
}


class Gather:
    def __init__(self, net, own, full, tail, tail_x=None, tail_core=None, order=None):
        self.net, self.at = net, 0
        mine = net.fsdp_index(())
        self.own = net.local(own.at[tail], full.at[mine + tail])
        self.stages = []
        done = []
        for b in order if order is not None and len(order) == net.bits else range(net.bits - 1, -1, -1):
            here = full.at[net.fsdp_index(done) + tail]
            src = here if done else own.at[tail]
            self.stages.append(net.copy(src, here, {"fsdp": other(net.f, b)}))
            done.append(b)
        everything = (slice(None),) * net.bits
        for region, b in ((tail_x, 1), (tail_core, 0)):
            if region is not None:
                here = full.at[everything + region]
                self.stages.append(net.copy(here, here, {"seq": other(net.me, b)}))

    def advance(self):
        if self.at > len(self.stages):
            return
        if self.at == 0:
            self.own.start()
        else:
            self.stages[self.at - 1].wait_recv()
        if self.at == 1:
            self.own.wait()
        if self.at < len(self.stages):
            self.stages[self.at].start()
        self.at += 1

    def finish(self):
        for stage in self.stages:
            stage.wait_send()


def front_kernel(
    lay, bits, sizes, x, seg, blk, pack, freqs, w_in_s, w_out_s, w_up_s, w_down_s,
    w_in, w_out, w_up, w_down, q_out, k_out, v_out, a_out, o_out, lse_out, vec, cos, sin, codes, queries,
    xb, xc, w_vm, q, k, v, a, o, lse, packs, send, recv, sems, *biases,
):
    rows, win, length = lay["rows"], lay["win"], lay["length"]
    width = x.shape[2]
    hidden = w_up_s.shape[1]
    micro = x.shape[0]
    net = Net(bits, send, recv, sems)
    role = (net.x, net.core)
    where_am = noisy, second, _, _ = places(lay, role)
    first = jnp.logical_not(second)
    clean = jnp.logical_not(noisy)
    net.barrier()

    pair, across = {"seq": other(net.me, 0)}, {"seq": other(net.me, 1)}
    rows_across = [net.copy(x.at[n], xb.at[n], across) for n in range(micro)]
    window = (pl.ds(rows - win, win), slice(None))
    target = (pl.ds(0, win), slice(None))
    rows_pair, rows_pair_b = [], []
    for n in range(micro):
        at = net.used
        rows_pair.append(net.copy(x.at[(n,) + window], xc.at[(n,) + target], pair))
        net.used = at
        rows_pair_b.append(net.copy(xb.at[(n,) + window], xc.at[(n,) + target], pair))
    edge_at = pl.multiple_of((1 - net.core) * (rows - HALO), HALO)
    edge = net.copy(x.at[:, pl.ds(edge_at, HALO), :], xc.at[:, pl.ds(win, HALO), :], pair)

    def columns(begin, size):
        return (slice(None), pl.ds(pl.multiple_of(begin, 128), size))

    chunks = {"s": Gather(net, pack, packs, (slice(None), slice(None)))}
    half_in, half_out, half_up = 3 * width // 2, width // 2, hidden // 2
    third = half_in // 3
    for n in range(3):
        region = columns(net.core * half_in + n * third, third)
        chunks["i%d" % n] = Gather(net, w_in_s, w_in, region, None, region, FRONT_BITS["i%d" % n][0])
    region = columns(net.core * half_out, half_out)
    chunks["o"] = Gather(net, w_out_s, w_out, region, None, region, FRONT_BITS["o"][0])
    quarter = half_up // 2
    slab = w_down_s.shape[0]
    for n in range(2):
        order, over_x = FRONT_BITS["u%d" % n]
        region = columns(net.core * half_up + n * quarter, quarter)
        part = columns(net.core * half_up + n * quarter + net.x * (quarter // 2), quarter // 2) if over_x else region
        chunks["u%d" % n] = Gather(net, w_up_s, w_up, part, part if over_x else None, region, order)
        order, over_x = FRONT_BITS["d%d" % n]
        begin = net.core * (slab // 2) + n * (slab // 4)
        region = (pl.ds(pl.multiple_of(begin, HALO), slab // 4), slice(None))
        half_region = (pl.ds(pl.multiple_of(begin + net.x * (slab // 8), HALO), slab // 8), slice(None))
        part = half_region if over_x else region
        chunks["d%d" % n] = Gather(net, w_down_s, w_down, part, part if over_x else None, region, order)

    def rows_start(n):
        @pl.when(clean)
        def _():
            rows_across[n].start()

    count = 1 << bits

    def tables():
        position = lax.broadcasted_iota(jnp.int32, (win + rows + HALO, 128), 0)
        shifted = jnp.where(
            position < win + rows, position - win, position - win - rows + jnp.where(second, -HALO, rows)
        )
        turned = (shifted + jnp.where(second, rows, 0)).astype(F32) * freqs[...]
        lane = lax.broadcasted_iota(jnp.int32, (win + rows + HALO, 128), 1)
        cos[...] = jnp.cos(turned)
        sine = jnp.sin(turned)
        sin[...] = jnp.where(lane % HD < HD // 2, -sine, sine)
        code = (seg[...] * SEG_STEP + blk[...]).astype(F32)
        base = (seg[...] * SEG_STEP).astype(F32)
        turned_code = jnp.transpose(jnp.concatenate([code, jnp.zeros((8 - micro, length), F32)], axis=0))
        lay_noisy = lay["noisy"]
        for n in range(micro):
            col = turned_code[:, n : n + 1]
            none = lambda count, value: jnp.full((count, 1), value, F32)
            codes[n, :win, :] = jnp.where(second, col[rows - win : rows], -1.0)
            codes[n, win : win + rows, :] = jnp.where(second, col[rows:], col[:rows])
            after, before = col[rows : rows + HALO], col[rows - HALO : rows]
            codes[n, win + rows : lay_noisy, :] = jnp.where(jnp.logical_and(clean, first), after, -1.0)
            codes[n, lay_noisy : lay_noisy + HALO, :] = jnp.where(jnp.logical_and(noisy, second), before, -2.0)
            codes[n, lay_noisy + HALO : lay_noisy + HALO + rows, :] = jnp.where(
                noisy, jnp.where(second, col[rows:], col[:rows]), -2.0
            )
            codes[n, lay["used"] - HALO : lay["used"], :] = jnp.where(jnp.logical_and(noisy, first), after, -2.0)
            codes[n, lay["used"] :, :] = none(lay["keys"] - lay["used"], -2.0)
            own_code = jnp.where(second, code[n : n + 1, rows:], code[n : n + 1, :rows])
            own_base = jnp.where(second, base[n : n + 1, rows:], base[n : n + 1, :rows])
            high = own_code - jnp.where(noisy, 1.0, 0.0)
            queries[n] = jnp.concatenate([own_base, high, own_code, jnp.zeros((5, rows), F32)], axis=0)

    def vectors():
        spread = {}
        for size in sorted(set(sizes)):
            total = jnp.zeros((8, size * count), F32)
            for n in range(count):
                at = tuple((n >> b) & 1 for b in range(bits - 1, -1, -1))
                piece = packs[at]
                wide = size * count - piece.shape[1]
                if wide > 0:
                    piece = jnp.concatenate([piece, jnp.zeros((8, wide), F32)], axis=1)
                lanes = lax.broadcasted_iota(jnp.int32, piece.shape, 1)
                piece = jnp.where(lanes < size, piece, 0.0)
                total += pltpu.roll(piece, n * size, 1) if n else piece
            spread[size] = total
        for r, size in enumerate(sizes):
            vec[r : r + 1, : size * count] = spread[size][r : r + 1]
            if size * count < vec.shape[1]:
                vec[r : r + 1, size * count :] = jnp.zeros((1, vec.shape[1] - size * count), F32)

    def pass_on(n):
        @pl.when(noisy)
        def _():
            rows_across[n].wait_recv()

        @pl.when(jnp.logical_and(first, noisy))
        def _():
            rows_pair_b[n].start()

        @pl.when(jnp.logical_and(first, clean))
        def _():
            rows_pair[n].start()

    def load_weights():
        loads = []
        for n in range(count):
            at = tuple((n >> b) & 1 for b in range(bits - 1, -1, -1))
            loads.append(net.local(w_in.at[at], w_vm.at[pl.ds(n * w_in_s.shape[0], w_in_s.shape[0]), :]))
        for load in loads:
            load.start()
        for load in loads:
            load.wait()

    stores = []

    def qkv(n):
        gain, shift, b_in = vec[0:1, :width], vec[1:2, :width], vec[2:3, : 3 * width]
        @pl.when(second)
        def _():
            rows_pair[n].wait_recv()

        qkv_rows(lay, where_am, n, x, xb, xc, w_vm, b_in, gain, shift, cos, sin, q, k, v, a)
        for here, there in ((q, q_out), (k, k_out), (v, v_out), (a, a_out)):
            stores.append(net.local(here.at[n], there.at[n]))
            stores[-1].start()

    def serve(token):
        if token in chunks:
            chunks[token].advance()
        elif token[0] in "RPQ":
            {"R": rows_start, "P": pass_on, "Q": qkv}[token[0]](int(token[1]))
        else:
            {"E": edge.start, "W": edge.wait_recv, "T": tables, "V": vectors, "L": load_weights}[token]()

    ahead, *after = [part.split() for part in " ".join(FRONT_ORDER).split("A")]
    for token in ahead:
        serve(token)

    quads = width // (QUAD * HD)
    assert micro * quads == len(after)

    def step(index, carry):
        n, h = index // quads, index % quads

        @pl.when(h == 0)
        def _():
            make_bias(lay, n, codes, queries, biases)

        cols = pl.ds(pl.multiple_of(h * QUAD * HD, QUAD * HD), QUAD * HD)
        attend(lay, n, cols, q, k, v, o, lse, index, biases)
        for at, tokens in enumerate(after):

            @pl.when(index == at)
            def _():
                for token in tokens:
                    serve(token)

        return carry

    lax.fori_loop(0, micro * quads, step, 0)
    last = [net.local(o, o_out), net.local(lse, lse_out)]
    for store in last:
        store.start()
    while any(chunk.at <= len(chunk.stages) for chunk in chunks.values()):
        for chunk in chunks.values():
            chunk.advance()
    for chunk in chunks.values():
        chunk.finish()
    for store in stores + last:
        store.wait()
    edge.wait_send()

    @pl.when(clean)
    def _():
        for n in range(micro):
            rows_across[n].wait_send()

    @pl.when(first)
    def _():
        for n in range(micro):
            rows_pair[n].wait_send()


def gelu_both(u):
    scale = 0.7978845608028654
    square = u * u
    inner = scale * u * (1.0 + 0.044715 * square)
    th = jnp.tanh(inner)
    plus = 0.5 * (1.0 + th)
    slope = plus + 0.5 * u * (1.0 - th * th) * (scale * (1.0 + 3 * 0.044715 * square))
    return (u * plus).astype(BF16), slope


def mlp_kernel(
    o, x, dy, w_out, vec, w_up, b_up, w_down,
    out_rows, dx2_out, do_out, g_w_out, g_w_up, g_b_up, g_w_down, g_vec,
    mid, a2, a2t, inv, acc_out, acc_da,
):
    step = pl.program_id(0)
    last = pl.num_programs(0) - 1
    width = x.shape[1]
    b_out, gain, shift, b_down = (vec[r : r + 1, :width] for r in (3, 4, 5, 7))

    @pl.when(step == 0)
    def _():
        value = x[...].astype(F32) + dot(o[...], w_out[...]) + b_out
        mid[...] = value
        normed, inverse = norm_stats(value)
        inv[...] = inverse
        a = (normed * gain + shift).astype(BF16)
        a2[...] = a
        a2t[...] = jnp.transpose(a)
        acc_out[...] = jnp.zeros_like(acc_out)
        acc_da[...] = jnp.zeros_like(acc_da)

    g, slope = gelu_both(dot(a2[...], w_up[...]) + b_up[6:7, :])
    acc_out[...] += dot(g, w_down[...])
    du32 = dot_nt(dy[...], w_down[...]) * slope
    du = du32.astype(BF16)
    g_b_up[...] = jnp.broadcast_to(jnp.sum(du.astype(F32), axis=0, keepdims=True), g_b_up.shape)
    acc_da[...] += dot_nt(du, w_up[...])
    g_w_down[...] = dot_tn(g, dy[...]).astype(BF16)
    g_w_up[...] = dot(a2t[...], du).astype(BF16)

    @pl.when(step == last)
    def _():
        dyf = dy[...].astype(F32)
        out_rows[...] = (mid[...] + acc_out[...] + b_down).astype(BF16)
        inverse = inv[...]
        value = mid[...]
        normed = (value - jnp.mean(value, axis=-1, keepdims=True)) * inverse
        da = acc_da[...]
        dx2 = dyf + norm_back(da, normed, inverse, gain)
        dx2_out[...] = dx2
        dp = dx2.astype(BF16)
        do_out[...] = dot_nt(dp, w_out[...]).astype(BF16)
        g_w_out[...] = dot_tn(o[...], dp).astype(BF16)
        g_vec[...] = jnp.concatenate(
            [
                jnp.sum(dyf, axis=0, keepdims=True),
                jnp.sum(da * normed, axis=0, keepdims=True),
                jnp.sum(da, axis=0, keepdims=True),
                jnp.sum(dp.astype(F32), axis=0, keepdims=True),
                jnp.zeros((4, dyf.shape[1]), F32),
            ],
            axis=0,
        )


def qkv_back_kernel(lay, role, a, dq, dk, dv, w, da_own, da_main, da_win, g_w, g_b, g_acc):
    width = dq.shape[2]
    rows, win = lay["rows"], lay["win"]
    noisy, second, own_at, halo_at = places(lay, role)

    @pl.when(pl.program_id(0) == 0)
    def _():
        g_acc[...] = jnp.zeros_like(g_acc)
        g_b[...] = jnp.zeros_like(g_b)

    def column_sums(col, value):
        g_b[0:1, col : col + width] += jnp.sum(value.astype(F32), axis=0, keepdims=True)

    def section(parts, query):
        def take(ref):
            return jnp.concatenate([ref[0, pl.ds(at, count), :] for at, count in parts], axis=0)

        at_t = jnp.transpose(take(a))
        key = take(dk)
        value = take(dv)
        g_acc[:, width : 2 * width] += dot(at_t, key)
        g_acc[:, 2 * width :] += dot(at_t, value)
        column_sums(width, key)
        column_sums(2 * width, value)
        total = dot_nt(key, w[:, width : 2 * width]) + dot_nt(value, w[:, 2 * width :])
        if query is not None:
            g_acc[:, :width] += dot(at_t[:, : query.shape[0]], query)
            column_sums(0, query)
            first = total[: query.shape[0]] + dot_nt(query, w[:, :width])
            return first, total[query.shape[0] :]
        return total

    own, near = section(((own_at, rows), (halo_at, HALO)), dq[0])
    da_own[0] = own
    da_win[0, win:, :] = near.astype(BF16)

    @pl.when(noisy)
    def _():
        da_main[0] = section(((win, rows),), None).astype(BF16)

    @pl.when(second)
    def _():
        da_win[0, :win, :] = section(((0, win),), None).astype(BF16)

    @pl.when(pl.program_id(0) == pl.num_programs(0) - 1)
    def _():
        g_w[...] = g_acc[...].astype(BF16)


def final_kernel(x, da, extra, dx2, gain, grad_in, g_vec):
    value = x[...].astype(F32)
    normed, inverse = norm_stats(value)
    grad = da[...] + extra[...].astype(F32)
    grad_in[...] = dx2[...] + norm_back(grad, normed, inverse, gain[...])

    @pl.when(pl.program_id(0) == 0)
    def _():
        g_vec[...] = jnp.zeros_like(g_vec)

    g_vec[0:1, :] += jnp.sum(grad * normed, axis=0, keepdims=True)
    g_vec[1:2, :] += jnp.sum(grad, axis=0, keepdims=True)


def add_to(ref, at, value):
    ref[at] = (ref[at].astype(F32) + value.astype(F32)).astype(BF16)


def for_all(bits, body):
    if bits == 0:
        body(())
        return

    def step(n, carry):
        body(tuple((n // (1 << b)) % 2 for b in range(bits - 1, -1, -1)))
        return carry

    lax.fori_loop(0, 1 << bits, step, 0)


BACK_ORDER = (
    "S S u0 d0",
    "S d0 u0 S",
    "u1 d1 S u1",
    "d1 S d2 d0",
    "u0 u2 E o",
    "u2 u1 d2 d1",
    "u0 d0 o X",
    "e A A e",
    "u2 A u0 d2",
    "A d1 P0 u2",
    "u1 A A o",
    "u1 u2 e d2",
    "T P1 G0 i0",
    "o G1 i1 Y0",
    "i0 G2 i2 i1",
    "e o d0 d2",
    "d1 N0 i0 i2",
    "N1 i1 e Y1",
    "N2 d2 N3 l",
    "i0 i2 l l",
)
BACK_BITS = {
    "u0": ((0, 1, 2), True),
    "u1": ((0, 1, 2), True),
    "u2": ((0, 1, 2), True),
    "d0": ((0, 1, 2), False),
    "d1": ((0, 1, 2), False),
    "d2": ((0, 1, 2), False),
    "o": ((0, 1, 2), False),
    "i0": ((1, 2, 0), False),
    "i1": ((0, 1, 2), False),
    "i2": ((0, 1, 2), False),
}


class Reduce:
    def __init__(self, net, acc, recvs, out, rows, cols, order, over_x):
        bits, self.net, self.at, self.sent = net.bits, net, 0, False
        pair, across = {"seq": other(net.me, 0)}, {"seq": other(net.me, 1)}
        recvs = list(recvs)
        part = (slice(None), slice(None))
        begin, size = rows
        tail = tail_half = (pl.ds(begin, size), cols)
        self.acc, self.steps = acc, [None]
        if over_x:
            piece = size // 2
            part = (pl.ds(pl.multiple_of(net.x * piece, HALO), piece), slice(None))
            away = (pl.ds(pl.multiple_of((1 - net.x) * piece, HALO), piece), slice(None))
            tail = (pl.ds(pl.multiple_of(begin + net.x * piece, HALO), piece), cols)
            got_x = recvs.pop(0)

            def add_x():
                for_all(bits, lambda at: add_to(acc, at + part, got_x[at]))

            self.steps.append((net.copy(acc.at[(slice(None),) * bits + away], got_x, across), add_x))
        done = []
        for b in order if len(order) == bits else range(bits):
            got = recvs.pop(0)

            def index(mine, rest, b=b, done=tuple(done)):
                rest = iter(rest)
                return tuple(
                    mine if p == b else bit_of(net.f, p) if p in done else next(rest) for p in range(bits - 1, -1, -1)
                )

            left = bits - 1 - len(done)

            def add_bit(got=got, b=b, index=index, left=left):
                for_all(left, lambda at: add_to(acc, index(bit_of(net.f, b), at) + part, got[at]))

            src = acc.at[index(1 - bit_of(net.f, b), (slice(None),) * left) + part]
            self.steps.append((net.copy(src, got, {"fsdp": other(net.f, b)}), add_bit))
            done.append(b)
        own = tuple(bit_of(net.f, n) for n in range(bits - 1, -1, -1))
        if over_x:
            before = self.steps[-1][1]

            def keep():
                before()
                out[tail] = acc[own + part]

            self.steps[-1] = (self.steps[-1][0], keep)
            self.steps.append((net.copy(out.at[tail], out.at[tail], across), lambda: None))
        else:
            got_last = recvs.pop(0)

            def last():
                out[tail] = (acc[own].astype(F32) + got_last[...].astype(F32)).astype(BF16)

            self.steps.append((net.copy(acc.at[own], got_last, across), last))
        self.steps.append((net.copy(out.at[tail_half], out.at[tail_half], pair), lambda: None))

    def feed(self, theirs, get):
        def mine():
            for_all(self.net.bits, lambda at: add_to(self.acc, at, get(at)))

        self.steps[0] = (self.net.copy(theirs, self.acc, {"seq": other(self.net.me, 0)}), mine)

    def open(self):
        return self.at <= len(self.steps)

    def advance(self):
        if not self.open():
            return
        if self.at > 0:
            copy, then = self.steps[self.at - 1]
            copy.wait_recv()
            then()
        if self.at < len(self.steps):
            self.steps[self.at][0].start()
        self.at += 1

    def finish(self):
        while self.open():
            self.advance()
        for copy, _ in self.steps[1 if self.sent else 0 :]:
            copy.wait_send()


class SumAll:
    def __init__(self, net, value, recvs):
        self.value, self.recvs, self.at = value, recvs, 0
        devices = [{"seq": other(net.me, b)} for b in range(2)]
        devices += [{"fsdp": other(net.f, b)} for b in range(net.bits)]
        self.copies = []
        for n, device in enumerate(devices):
            src = value if n == 0 else recvs.at[len(devices) + n - 1]
            self.copies.append(net.copy(src, recvs.at[n], device))

    def open(self):
        return self.at <= len(self.copies)

    def advance(self):
        count = len(self.copies)
        if not self.open():
            return
        if self.at > 0:
            n = self.at - 1
            self.copies[n].wait_recv()
            held = self.value[...] if n == 0 else self.recvs[count + n - 1]
            self.recvs[count + n] = held + self.recvs[n]
        if self.at < count:
            self.copies[self.at].start()
        self.at += 1

    def finish(self):
        while self.open():
            self.advance()
        for copy in self.copies:
            copy.wait_send()
        return self.recvs[2 * len(self.copies) - 1]


def back_kernel(
    lay, bits, codes, queries, lse, cos, sin, vec, x, o,
    dy, q, k, v, a, w_in, w_out, w_up, w_down,
    out_rows, grad_in, f_in_out, f_out_out, f_up_out, f_down_out, sums_out, late_out,
    do, recv_parts, rwin,
    acc_in, acc_out, acc_up, acc_down, r_in, r_out, r_up, r_down, f_in, f_out, f_up, f_down,
    sums, sums_recv, late, late_recv, send, recv, sems, *biases,
):
    rows, win, keys = lay["rows"], lay["win"], lay["keys"]
    micro, width = x.shape[0], x.shape[2]
    total = micro * rows
    hidden = vec.shape[1]
    qw = QUAD * HD
    quads = width // qw
    net = Net(bits, send, recv, sems)
    where_am = noisy, second, own_at, halo_at = places(lay, (net.x, net.core))
    first, clean = jnp.logical_not(second), jnp.logical_not(noisy)
    gain = vec[0:1, :width]
    net.barrier()
    every = list(itertools.product(range(2), repeat=bits))
    count = len(every)
    pair, across = {"seq": other(net.me, 0)}, {"seq": other(net.me, 1)}
    slab_down = f_down.shape[0]
    steps = slab_down // 128
    share = count // 2
    wide = share * 128
    whole_index = (slice(None),) * bits
    here, there = net.core, 1 - net.core

    def columns(begin, size):
        return (slice(None), pl.ds(pl.multiple_of(begin, 128), size))

    @pl.when(noisy)
    def _():
        recv_parts[...] = jnp.zeros_like(recv_parts)

    sums[...] = jnp.zeros_like(sums)

    def feed_forward(dyv, wu, wd, w_ov, mid, a2, a2t, inv, acc_y, acc_da, gv, duv, gd, gu, gu_out, sem_w, sem_m):
        block = total // 4

        def loads(index):
            j, h = index // 2, index % 2
            slot = index % 2
            copies = []
            for n in range(share):
                at = pl.multiple_of((h * share + n) * slab_down + j * 128, 128)
                part = pl.ds(n * 128, 128)
                copies.append(pltpu.make_async_copy(w_up.at[:, pl.ds(at, 128)], wu.at[slot, :, part], sem_w.at[slot, 2 * n]))
                copies.append(pltpu.make_async_copy(w_down.at[pl.ds(at, 128), :], wd.at[slot, part, :], sem_w.at[slot, 2 * n + 1]))
            return copies

        first_loads = [pltpu.make_async_copy(w_out, w_ov, sem_m.at[0]), pltpu.make_async_copy(dy, dyv, sem_m.at[1])]
        for load in first_loads + loads(0):
            load.start()
        flat = lambda ref: ref[...].reshape(total, width)
        b_out, gain2, shift2, b_down = (vec[r : r + 1, :width] for r in (3, 4, 5, 7))
        first_loads[0].wait()
        value = flat(x).astype(F32) + dot(flat(o), w_ov[...]) + b_out
        mid[...] = value
        normed, inverse = norm_stats(value)
        inv[...] = inverse
        act = (normed * gain2 + shift2).astype(BF16)
        a2[...] = act
        a2t[...] = jnp.transpose(act)
        acc_y[...] = jnp.zeros_like(acc_y)
        acc_da[...] = jnp.zeros_like(acc_da)
        first_loads[1].wait()

        away = columns(there * (width // 2), width // 2)
        near = columns(here * (width // 2), width // 2)
        for j in range(steps):
            chunks["u%d" % j].feed(gu.at[j, there], lambda at, j=j: gu[(j, here) + at])
            chunks["d%d" % j].feed(gd.at[(j,) + whole_index + away], lambda at, j=j: gd[(j,) + at + near])

        def step(index, carry):
            j, h = index // 2, index % 2
            slot = index % 2

            @pl.when(index + 1 < 2 * steps)
            def _():
                for load in loads(index + 1):
                    load.start()

            for load in loads(index):
                load.wait()
            at = [pl.ds(pl.multiple_of((h * share + n) * slab_down + j * 128, 128), 128) for n in range(share)]
            bias = jnp.concatenate([vec[6:7, here_at] for here_at in at], axis=1)
            w_u, w_d = wu[slot], wd[slot]
            row = jnp.zeros((1, wide), F32)
            for begin in range(0, total, block):
                span = slice(begin, begin + block)
                g, slope = gelu_both(dot(a2[span, :], w_u) + bias)
                gv[span, :] = g
                acc_y[span, :] += dot(g, w_d)
                du = (dot_nt(dyv[span, :], w_d) * slope).astype(BF16)
                duv[span, :] = du
                row += jnp.sum(du.astype(F32), axis=0, keepdims=True)
                acc_da[span, :] += dot_nt(du, w_u)
            for n in range(share):
                sums[6:7, at[n]] = row[:, n * 128 : n * 128 + 128]
            g_d = dot_tn(gv[...], dyv[...]).astype(BF16)
            for n in range(share):
                low = tuple((n >> b) & 1 for b in range(bits - 2, -1, -1))
                gd[(j, h) + low] = g_d[n * 128 : n * 128 + 128]
            g_u = dot(a2t[...], duv[...]).astype(BF16)
            slab = width // count
            for n, idx in enumerate(every):
                gu[(j, h) + idx] = g_u[n * slab : n * slab + slab]
            for when, tokens in enumerate(in_feed):

                @pl.when(index == when)
                def _():
                    for token in tokens:
                        chunks[token].advance()

            return carry

        lax.fori_loop(0, 2 * steps, step, 0)
        for begin in range(0, total, block):
            span = slice(begin, begin + block)
            dyf = dyv[span, :].astype(F32)
            value = mid[span, :]
            a2[span, :] = (value + acc_y[span, :] + b_down).astype(BF16)
            normed = (value - jnp.mean(value, axis=-1, keepdims=True)) * inv[span, :]
            da = acc_da[span, :]
            dx2 = dyf + norm_back(da, normed, inv[span, :], gain2)
            acc_da[span, :] = dx2
            dp = dx2.astype(BF16)
            dyv[span, :] = dp
            for r, part in ((7, dyf), (4, da * normed), (5, da), (3, dp.astype(F32))):
                sums[r : r + 1, :width] += jnp.sum(part, axis=0, keepdims=True)
        puts = []
        for n in range(micro):
            part = pl.ds(n * rows, rows)
            puts.append(pltpu.make_async_copy(acc_da.at[part, :], grad_in.at[n], sem_m.at[2 + 2 * n]))
            puts.append(pltpu.make_async_copy(a2.at[part, :], out_rows.at[n], sem_m.at[3 + 2 * n]))
        for put in puts:
            put.start()
        do[...] = dot_nt(dyv[...], w_ov[...]).astype(BF16).reshape(do.shape)
        g_o = dot_tn(flat(o), dyv[...]).astype(BF16)
        slab = width // count
        for n, idx in enumerate(every):
            for c in range(2):
                gu_out[(c,) + idx] = g_o[n * slab : n * slab + slab, c * (width // 2) : (c + 1) * (width // 2)]
        chunks["o"].feed(gu_out.at[there], lambda at: gu_out[(here,) + at])
        for token in after_feed:
            chunks[token].advance()
        for name, chunk in chunks.items():
            if name[0] in "udo":
                assert chunk.at >= 2
                chunk.steps[0][0].wait_send()
                chunk.sent = True
        for put in puts:
            put.wait()

    half_out = width // 2
    slab = width // count
    chunks = {}
    for j in range(steps):
        chunks["u%d" % j] = Reduce(net, acc_up[j], r_up[j], f_up.at[j], (0, slab),
                                   columns(here * wide, wide)[1], *BACK_BITS["u%d" % j])
        chunks["d%d" % j] = Reduce(net, acc_down[j], r_down[j], f_down, (j * 128, 128),
                                   columns(here * half_out, half_out)[1], *BACK_BITS["d%d" % j])
    chunks["o"] = Reduce(net, acc_out, r_out, f_out, (0, slab), columns(here * half_out, half_out)[1], *BACK_BITS["o"])
    chunks["e"] = SumAll(net, sums, sums_recv)
    chunks["l"] = SumAll(net, late, late_recv)
    edge_at = pl.multiple_of((1 - net.core) * (rows - HALO), HALO)
    tokens = " ".join(BACK_ORDER).split()
    feed_end, free, turn = tokens.index("E"), tokens.index("X"), tokens.index("T")
    in_feed = [part.split() for part in " ".join(tokens[:feed_end]).split("S")][1:]
    after_feed = tokens[feed_end + 1 : free]
    in_attention = [part.split() for part in " ".join(tokens[free + 1 : turn]).split("A")]
    after_attention = tokens[turn + 1 :]
    assert len(in_feed) == 2 * steps and len(in_attention) == 1 + micro * quads

    pl.run_scoped(
        feed_forward,
        pltpu.VMEM((total, width), BF16), pltpu.VMEM((2, width, wide), BF16), pltpu.VMEM((2, wide, width), BF16),
        pltpu.VMEM((width, width), BF16), pltpu.VMEM((total, width), F32), pltpu.VMEM((total, width), BF16),
        pltpu.VMEM((width, total), BF16), pltpu.VMEM((total, 1), F32), pltpu.VMEM((total, width), F32),
        pltpu.VMEM((total, width), F32), pltpu.VMEM((total, wide), BF16), pltpu.VMEM((total, wide), BF16),
        pltpu.VMEM((steps,) + (2,) * bits + (128, width), BF16),
        pltpu.VMEM((steps, 2) + (2,) * bits + (width // count, wide), BF16),
        pltpu.VMEM((2,) + (2,) * bits + (width // count, half_out), BF16),
        pltpu.SemaphoreType.DMA((2, 2 * share)), pltpu.SemaphoreType.DMA((2 + 2 * micro,)),
    )

    def backward(dq, dk, dv, w_vm, gin, parts, dwin, sem_l):
        load_w = pltpu.make_async_copy(w_in, w_vm, sem_l.at[0])
        load_w.start()
        p1 = [net.copy(dwin.at[n], rwin.at[n], pair) for n in range(micro)]
        p2 = [net.copy(parts.at[n], recv_parts.at[n], across) for n in range(micro)]
        third = 3 * width // 6
        slab_in = width // count
        for j in range(3):
            chunks["i%d" % j] = Reduce(net, acc_in[j], r_in[j], f_in, (0, slab_in),
                                       columns(here * 3 * third + j * third, third)[1], *BACK_BITS["i%d" % j])
            chunks["i%d" % j].feed(gin.at[j, there], lambda at, j=j: gin[(j, here) + at])

        def pass_on(n):
            p1[n].wait_recv()

            @pl.when(noisy)
            def _():
                @pl.when(first)
                def _():
                    add_to(parts, (n, slice(rows - win, rows), slice(None)), rwin[n, :win, :])

                p2[n].start()

        def attention(qb, kb, vb, dk_acc, dv_acc, load_sems):
            blocks = ((q, qb), (k, kb), (v, vb))

            def loads(index):
                n, h = index // quads, index % quads
                cols = pl.ds(pl.multiple_of(h * qw, qw), qw)
                slot = index % 2
                return [
                    pltpu.make_async_copy(src.at[n, :, cols], dst.at[slot], load_sems.at[slot, m])
                    for m, (src, dst) in enumerate(blocks)
                ]

            for load in loads(0):
                load.start()
            load_w.wait()

            def partial(n):
                key = jnp.concatenate([dk[n, :win, :], dk[n, pl.ds(halo_at, HALO), :]], axis=0)
                value = jnp.concatenate([dv[n, :win, :], dv[n, pl.ds(halo_at, HALO), :]], axis=0)
                w_key, w_value = w_vm[:, width : 2 * width], w_vm[:, 2 * width :]
                dwin[n] = (dot_nt(key, w_key) + dot_nt(value, w_value)).astype(BF16)
                p1[n].start()

                @pl.when(noisy)
                def _():
                    main = slice(win, win + rows)
                    parts[n] = (dot_nt(dk[n, main, :], w_key) + dot_nt(dv[n, main, :], w_value)).astype(BF16)

            def serve(token):
                if token[0] == "P":
                    pass_on(int(token[1]))
                else:
                    chunks[token].advance()

            for token in in_attention[0]:
                serve(token)

            def step(index, carry):
                n, h = index // quads, index % quads
                slot = index % 2

                @pl.when(index + 1 < micro * quads)
                def _():
                    for load in loads(index + 1):
                        load.start()

                @pl.when(h == 0)
                def _():
                    make_bias(lay, n, codes, queries, biases)

                for load in loads(index):
                    load.wait()
                cols = pl.ds(pl.multiple_of(h * qw, qw), qw)
                attend_back(
                    lay, slot, slice(None), qb, kb, vb, n, cols, o, do, lse, index, cos, sin,
                    n, h * qw, dq, dk, dv, dk_acc, dv_acc, biases,
                )
                for at, tokens in enumerate(in_attention[1:]):

                    @pl.when(index == at)
                    def _():
                        for m in range(micro):
                            if at == m * quads + quads - 1:
                                partial(m)
                        for token in tokens:
                            serve(token)

                return carry

            lax.fori_loop(0, micro * quads, step, 0)

        pl.run_scoped(
            attention,
            pltpu.VMEM((2, rows, qw), BF16), pltpu.VMEM((2, keys, qw), BF16), pltpu.VMEM((2, keys, qw), BF16),
            pltpu.VMEM((keys, qw), F32), pltpu.VMEM((keys, qw), F32),
            pltpu.SemaphoreType.DMA((2, 3)),
        )

        def projection(av, at_all, at_own, dxv, sem_a, sem_x):
            load_a = [pltpu.make_async_copy(a.at[n], av, sem_a.at[n]) for n in range(micro)]
            load_x = pltpu.make_async_copy(grad_in, dxv, sem_x.at[0])
            load_a[0].start()
            load_x.start()
            for n in range(micro):
                load_a[n].wait()
                at_all[n] = jnp.transpose(av[...])
                at_own[n] = jnp.transpose(av[pl.ds(own_at, rows), :])
                if n + 1 < micro:
                    load_a[n + 1].start()
            late[...] = jnp.zeros_like(late)
            stores = []

            def gradient(j):
                for block in range(2):
                    col = block * 3 * third + j * third
                    source, lhs = ((dq, at_own), (dk, at_all), (dv, at_all))[col // width]
                    inside = slice(col % width, col % width + third)
                    grad = jnp.zeros((width, third), F32)
                    ones = jnp.zeros((8, third), F32)
                    for n in range(micro):
                        rhs = source[n, :, inside]
                        grad += dot(lhs[n], rhs)
                        ones += dot(jnp.ones((8, rhs.shape[0]), BF16), rhs)
                    for m, at in enumerate(every):
                        gin[(j, block) + at] = grad[m * slab_in : m * slab_in + slab_in].astype(BF16)
                    row = 2 + col // width
                    late[row : row + 1, inside] = ones[0:1]

            def settle(n):
                @pl.when(clean)
                def _():
                    p2[n].wait_recv()

                    @pl.when(first)
                    def _():
                        add_to(recv_parts, (n, slice(rows - win, rows), slice(None)), rwin[n, :win, :])

                add_to(recv_parts, (n, pl.ds(edge_at, HALO), slice(None)), rwin[n, win:, :])

            def norm_part(m):
                n, part = m // 2, m % 2
                if not stores:
                    load_x.wait()
                size = rows // 2
                span = slice(part * size, part * size + size)
                mine_rows = pl.ds(pl.multiple_of(own_at + part * size, HALO), size)
                da = dot_nt(dq[n, span, :], w_vm[:, :width])
                da += dot_nt(dk[n, mine_rows, :], w_vm[:, width : 2 * width])
                da += dot_nt(dv[n, mine_rows, :], w_vm[:, 2 * width :])
                da += recv_parts[n, span, :].astype(F32)
                normed, inverse = norm_stats(x[n, span, :].astype(F32))
                dxv[n, span, :] += norm_back(da, normed, inverse, gain)
                late[0:1, :] += jnp.sum(da * normed, axis=0, keepdims=True)
                late[1:2, :] += jnp.sum(da, axis=0, keepdims=True)
                store = pltpu.make_async_copy(dxv.at[n, span, :], grad_in.at[n, span, :], sem_x.at[1 + m])
                store.start()
                stores.append(store)

            for token in after_attention:
                if token in chunks:
                    chunks[token].advance()
                else:
                    {"P": pass_on, "Y": settle, "G": gradient, "N": norm_part}[token[0]](int(token[1]))
            while any(chunk.open() for chunk in chunks.values()):
                for chunk in chunks.values():
                    chunk.advance()
            sums_out[...] = chunks["e"].finish()
            late_out[...] = chunks["l"].finish()
            for name, chunk in chunks.items():
                if name not in "el":
                    chunk.finish()
            puts = [net.local(src, dst) for src, dst in ((f_in, f_in_out), (f_out, f_out_out), (f_down, f_down_out))]
            for j in range(steps):
                for n in range(count):
                    puts.append(net.local(
                        f_up.at[j, :, pl.ds(n * 128, 128)], f_up_out.at[:, pl.ds(n * slab_down + j * 128, 128)]
                    ))
            for put in puts:
                put.start()
            for put in puts + stores:
                put.wait()
            for copy in p1:
                copy.wait_send()

            @pl.when(noisy)
            def _():
                for copy in p2:
                    copy.wait_send()

        pl.run_scoped(
            projection,
            pltpu.VMEM((keys, width), BF16), pltpu.VMEM((micro, width, keys), BF16),
            pltpu.VMEM((micro, width, rows), BF16), pltpu.VMEM((micro, rows, width), F32),
            pltpu.SemaphoreType.DMA((micro,)), pltpu.SemaphoreType.DMA((1 + 2 * micro,)),
        )

    third = 3 * width // 6
    pl.run_scoped(
        backward,
        pltpu.VMEM((micro, rows, width), BF16), pltpu.VMEM((micro, keys, width), BF16),
        pltpu.VMEM((micro, keys, width), BF16), pltpu.VMEM((width, 3 * width), BF16),
        pltpu.VMEM((3, 2) + (2,) * bits + (width // count, third), BF16),
        pltpu.VMEM((micro, rows, width), BF16), pltpu.VMEM((micro, win + HALO, width), BF16),
        pltpu.SemaphoreType.DMA((1,)),
    )


def front_remote(
    lay, role, sizes, inputs, segment_ids, block_ids, small, weights, freqs, lse_shape, bias_scratch, spans, attn_flops
):
    micro, rows, width = inputs.shape
    keys, win = lay["keys"], lay["win"]
    bits = lax.axis_size("fsdp").bit_length() - 1
    lanes = -(-max(sizes) // 128) * 128
    pack = jnp.stack([jnp.pad(p.astype(F32), (0, lanes - p.shape[0])) for p in small])
    full = [like((2,) * bits + p.shape, BF16) for p in weights]
    longest = max(sizes) << bits
    table_rows = win + rows + HALO
    shapes = full + [
        like((micro, rows, width), BF16), like((micro, keys, width), BF16), like((micro, keys, width), BF16),
        like((micro, keys, width), BF16), like((micro, rows, width), BF16), like(lse_shape, F32),
        like((8, longest), F32), like((table_rows, 128), F32), like((table_rows, 128), F32),
        like((micro, keys, 1), F32), like((micro, 8, rows), F32),
    ]
    remote = 3 * micro + 1 + (bits + 2) * 9
    outs = pl.pallas_call(
        functools.partial(front_kernel, lay, bits, sizes),
        in_specs=[VMEM] * 9,
        out_specs=[ANY] * 10 + [VMEM] * 5,
        out_shape=shapes,
        scratch_shapes=[
            pltpu.VMEM((micro, rows, width), BF16), pltpu.VMEM((micro, win + HALO, width), BF16),
            pltpu.VMEM((width, 3 * width), BF16), pltpu.VMEM((micro, rows, width), BF16),
            pltpu.VMEM((micro, keys, width), BF16), pltpu.VMEM((micro, keys, width), BF16),
            pltpu.VMEM((micro, keys, width), BF16), pltpu.VMEM((micro, rows, width), BF16),
            pltpu.VMEM(lse_shape, F32), pltpu.VMEM((2,) * bits + (8, lanes), F32),
            pltpu.SemaphoreType.DMA((remote,)), pltpu.SemaphoreType.DMA((remote,)),
            pltpu.SemaphoreType.DMA((32,)),
        ] + bias_scratch,
        compiler_params=pltpu.CompilerParams(
            vmem_limit_bytes=VMEM_BYTES, collective_id=0, has_side_effects=True
        ),
        cost_estimate=pl.CostEstimate(flops=2 * attn_flops, bytes_accessed=40 << 20, transcendentals=0),
        name="front",
    )(inputs, segment_ids, block_ids, pack, freqs, *weights)
    joined = [w.reshape((-1, w.shape[-1])) for w in outs[:4]]
    return tuple(joined) + tuple(outs[4:])


def front_native(
    lay, role, sizes, inputs, segment_ids, block_ids, small, weights, freqs, lse_shape, bias_scratch, spans, attn_flops
):
    micro, rows, width = inputs.shape
    keys, win, length = lay["keys"], lay["win"], lay["length"]
    clean, half = role[0], role[1]
    pairs = [(0, 1), (1, 0), (2, 3), (3, 2)]
    xb = lax.ppermute(inputs, "seq", [(2, 0), (3, 1)])
    xmain = jnp.where(clean == 1, inputs, xb)
    edge = jnp.where(half == 0, inputs[:, rows - HALO :], inputs[:, :HALO])
    xc = lax.ppermute(jnp.concatenate([xmain[:, rows - win :], edge], axis=1), "seq", pairs)
    start = half * rows
    edge_at = jnp.where(half == 0, rows, -HALO)
    positions = start + jnp.concatenate([jnp.arange(-win, rows), edge_at + jnp.arange(HALO)])
    turned = positions.astype(F32)[:, None] * freqs
    sine = jnp.sin(turned)
    cos = jnp.cos(turned)
    sin = jnp.where(jnp.arange(128)[None] % HD < HD // 2, -sine, sine)
    code = segment_ids * SEG_STEP + block_ids
    padded = jnp.pad(code, ((0, 0), (win, 0)), constant_values=-1)
    key_codes = lax.dynamic_slice_in_dim(padded, start, win + rows, 1)
    own_code = lax.dynamic_slice_in_dim(code, start, rows, 1)
    own_seg = lax.dynamic_slice_in_dim(segment_ids, start, rows, 1)
    before, after = code[:, rows - HALO : rows], code[:, rows : rows + HALO]
    codes = jnp.concatenate(
        [
            key_codes,
            jnp.where((clean == 1) & (half == 0), after, -1),
            jnp.where((clean == 0) & (half == 1), before, -2),
            jnp.where(clean == 0, own_code, -2),
            jnp.where((clean == 0) & (half == 0), after, -2),
            jnp.full((micro, keys - lay["used"]), -2, jnp.int32),
        ],
        axis=1,
    )[:, :, None].astype(F32)
    queries = jnp.stack([own_seg * SEG_STEP, own_code - (1 - clean), own_code], axis=1)
    queries = jnp.concatenate([queries, jnp.zeros((micro, 5, rows), jnp.int32)], axis=1).astype(F32)
    packed = lax.all_gather(jnp.concatenate(small)[None], "fsdp", axis=0, tiled=True)
    vectors, at = [], 0
    longest = max(sizes) * packed.shape[0]
    for size in sizes:
        one = packed[:, at : at + size].reshape(-1).astype(F32)
        vectors.append(jnp.pad(one, (0, longest - one.shape[0])))
        at += size
    vec = jnp.stack(vectors)
    w_in, w_out, w_up, w_down = (lax.all_gather(p, "fsdp", axis=0, tiled=True) for p in weights)
    per_seq = lambda n, d: pl.BlockSpec((1, n, d), lambda s: (s, 0, 0))
    table_rows = win + rows + HALO
    q, k, v, a = call(
        functools.partial(qkv_kernel, lay), (micro,),
        [SMEM(), per_seq(rows, width), per_seq(rows, width), per_seq(win + HALO, width),
         whole((width, 3 * width)), whole(vec.shape), whole((table_rows, 128)), whole((table_rows, 128))],
        [per_seq(rows, width), per_seq(keys, width), per_seq(keys, width), per_seq(keys, width)],
        [like((micro, rows, width), BF16)] + [like((micro, keys, width), BF16)] * 3,
        [], 2 * micro * rows * width * 3 * width * 2, 20 << 20, "qkv",
    )(role, inputs, xb, xc, w_in, vec, cos, sin)
    qw = QUAD * HD
    quads = width // qw
    quad_block = lambda n: pl.BlockSpec((1, n, qw), lambda s, h: (s, 0, h))
    o, lse = call(
        functools.partial(attend_kernel, lay), (micro, quads),
        [pl.BlockSpec((1, keys, 1), lambda s, h: (s, 0, 0)), pl.BlockSpec((1, 8, rows), lambda s, h: (s, 0, 0)),
         quad_block(rows), quad_block(keys), quad_block(keys)],
        [quad_block(rows), pl.BlockSpec((1,) + lse_shape[1:], lambda s, h: (s * quads + h, 0, 0))],
        [like((micro, rows, width), BF16), like(lse_shape, F32)],
        bias_scratch, 2 * attn_flops, 12 << 20, "attend",
    )(codes, queries, q, k, v)
    return w_in, w_out, w_up, w_down, q, k, v, a, o, lse, vec, cos, sin, codes, queries


def back_remote(
    lay, role, sizes, inputs, cotangent, codes, queries, lse, cos, sin, vec,
    q, k, v, o, a, w_in, w_out, w_up, w_down, bias_scratch, attn_flops,
):
    micro, rows, width = inputs.shape
    keys, win = lay["keys"], lay["win"]
    bits = lax.axis_size("fsdp").bit_length() - 1
    lead = (2,) * bits
    count = 1 << bits
    hidden = w_up.shape[1]
    slab, slab_down = width // count, hidden // count
    third = width // 2
    steps, wide = slab_down // 128, count // 2 * 128

    def bank(name, r, c):
        over_x = BACK_BITS[name][1]
        kept = r // 2 if over_x else r
        over = [pltpu.VMEM(lead[: bits - 1 - b] + (kept, c), BF16) for b in range(bits)]
        ends = [pltpu.VMEM(lead + (kept, c), BF16)] if over_x else []
        return pltpu.VMEM(lead + (r, c), BF16), tuple(ends + over + ([] if over_x else [pltpu.VMEM((r, c), BF16)]))

    acc_in, r_in = zip(*[bank("i%d" % j, slab, third) for j in range(3)])
    acc_out, r_out = bank("o", slab, width // 2)
    acc_up, r_up = zip(*[bank("u%d" % j, slab, wide) for j in range(steps)])
    acc_down, r_down = zip(*[bank("d%d" % j, 128, width // 2) for j in range(steps)])
    stages = 2 + bits
    remote = (7 + 2 * steps) * (bits + 5) + 2 * stages + 4 * micro
    scratch = [
        pltpu.VMEM((micro, rows, width), BF16), pltpu.VMEM((micro, rows, width), BF16),
        pltpu.VMEM((micro, win + HALO, width), BF16),
        acc_in, acc_out, acc_up, acc_down, r_in, r_out, r_up, r_down,
        pltpu.VMEM((slab, 3 * width), BF16), pltpu.VMEM((slab, width), BF16),
        pltpu.VMEM((steps, slab, count * 128), BF16), pltpu.VMEM((slab_down, width), BF16),
        pltpu.VMEM((8, hidden), F32), pltpu.VMEM((2 * stages, 8, hidden), F32),
        pltpu.VMEM((8, width), F32), pltpu.VMEM((2 * stages, 8, width), F32),
        pltpu.SemaphoreType.DMA((remote,)), pltpu.SemaphoreType.DMA((remote,)),
        pltpu.SemaphoreType.DMA((8 + steps * count,)),
    ] + bias_scratch
    out_rows, grad_in, f_in, f_out, f_up, f_down, sums, late = pl.pallas_call(
        functools.partial(back_kernel, lay, bits),
        in_specs=[VMEM] * 8 + [ANY] * 9,
        out_specs=[ANY] * 6 + [VMEM] * 2,
        out_shape=[
            like((micro, rows, width), BF16), like((micro, rows, width), F32), like((slab, 3 * width), BF16),
            like((slab, width), BF16), like((slab, hidden), BF16), like((slab_down, width), BF16),
            like((8, hidden), F32), like((8, width), F32),
        ],
        scratch_shapes=scratch,
        compiler_params=pltpu.CompilerParams(
            vmem_limit_bytes=67043328, collective_id=1, has_side_effects=True
        ),
        cost_estimate=pl.CostEstimate(flops=6 * attn_flops, bytes_accessed=60 << 20, transcendentals=0),
        name="back",
    )(codes, queries, lse, cos, sin, vec, inputs, o, cotangent.reshape(micro * rows, width),
      q, k, v, a, w_in, w_out, w_up, w_down)
    f = lax.axis_index("fsdp")
    vectors = []
    for r, size in enumerate(sizes):
        row = late[r] if r < 2 else late[2:5].reshape(-1) if r == 2 else sums[r]
        vectors.append(lax.dynamic_slice(row, (f * size,), (size,)))
    return out_rows, grad_in, [g.astype(F32) for g in (f_in, f_out, f_up, f_down)], vectors


def back_native(
    lay, role, sizes, inputs, cotangent, codes, queries, lse, cos, sin, vec,
    q, k, v, o, a, w_in, w_out, w_up, w_down, bias_scratch, attn_flops,
):
    micro, rows, width = inputs.shape
    keys, win = lay["keys"], lay["win"]
    clean, half = role[0], role[1]
    pairs = [(0, 1), (1, 0), (2, 3), (3, 2)]
    fsdp_n = lax.axis_size("fsdp")
    hidden = w_up.shape[1]
    qw = QUAD * HD
    quads = width // qw
    total = micro * rows
    flat = lambda z: z.reshape(total, width)
    chunk = min(512, hidden)
    rows_spec = whole((total, width))
    out_rows, dx2, do, g_w_out, g_w_up, g_b_up, g_w_down, g_mlp = call(
        mlp_kernel, (hidden // chunk,),
        [rows_spec, rows_spec, rows_spec, whole((width, width)), whole(vec.shape),
         pl.BlockSpec((width, chunk), lambda j: (0, j)), pl.BlockSpec((8, chunk), lambda j: (0, j)),
         pl.BlockSpec((chunk, width), lambda j: (j, 0))],
        [rows_spec, rows_spec, rows_spec, whole((width, width)),
         pl.BlockSpec((width, chunk), lambda j: (0, j)), pl.BlockSpec((8, chunk), lambda j: (0, j)),
         pl.BlockSpec((chunk, width), lambda j: (j, 0)), whole((8, width))],
        [like((total, width), BF16), like((total, width), F32), like((total, width), BF16),
         like((width, width), BF16), like((width, hidden), BF16), like((8, hidden), F32),
         like((hidden, width), BF16), like((8, width), F32)],
        [pltpu.VMEM((total, width), F32), pltpu.VMEM((total, width), BF16), pltpu.VMEM((width, total), BF16),
         pltpu.VMEM((total, 1), F32), pltpu.VMEM((total, width), F32), pltpu.VMEM((total, width), F32)],
        2 * total * width * (6 * hidden + 3 * width), 40 << 20, "mlp",
    )(flat(o), flat(inputs), flat(cotangent), w_out, vec, w_up, vec, w_down)

    do = do.reshape(micro, rows, width)
    per_seq = lambda n, d: pl.BlockSpec((1, n, d), lambda s: (s, 0, 0))
    role_spec = SMEM()
    quad_block = lambda n: pl.BlockSpec((1, n, qw), lambda s, h: (s, 0, h))
    code_spec = pl.BlockSpec((1, keys, 1), lambda s, h: (s, 0, 0))
    query_spec = pl.BlockSpec((1, 8, rows), lambda s, h: (s, 0, 0))
    lse_spec = pl.BlockSpec((1,) + lse.shape[1:], lambda s, h: (s * quads + h, 0, 0))
    table = pl.BlockSpec((win + rows + HALO, 128), lambda s, h: (0, 0), pipeline_mode=pl.Buffered(1))
    dq, dk, dv = call(
        functools.partial(attend_back_kernel, lay), (micro, quads),
        [code_spec, query_spec, quad_block(rows), quad_block(keys), quad_block(keys),
         quad_block(rows), quad_block(rows), lse_spec, table, table],
        [quad_block(rows), quad_block(keys), quad_block(keys)],
        [like((micro, rows, width), BF16), like((micro, keys, width), BF16), like((micro, keys, width), BF16)],
        [pltpu.VMEM((keys, qw), F32), pltpu.VMEM((keys, qw), F32)] + bias_scratch,
        5 * attn_flops, 24 << 20, "attend_back",
    )(codes, queries, q, k, v, o, do, lse, cos, sin)

    da_own, da_main, da_win, g_w_in, g_b_in = call(
        functools.partial(qkv_back_kernel, lay), (micro,),
        [role_spec, per_seq(keys, width), per_seq(rows, width), per_seq(keys, width), per_seq(keys, width),
         whole((width, 3 * width))],
        [per_seq(rows, width), per_seq(rows, width), per_seq(win + HALO, width),
         whole((width, 3 * width)), whole((8, 3 * width))],
        [like((micro, rows, width), F32), like((micro, rows, width), BF16), like((micro, win + HALO, width), BF16),
         like((width, 3 * width), BF16), like((8, 3 * width), F32)],
        [pltpu.VMEM((width, 3 * width), F32)], 2 * 2 * micro * rows * width * 3 * width * 2, 40 << 20, "qkv_back",
    )(role, a, dq, dk, dv, w_in)

    from_pair = lax.ppermute(da_win, "seq", pairs).astype(F32)
    from_second = jnp.where(half == 0, from_pair[:, :win], 0.0)
    edge = from_pair[:, win:]
    gap = jnp.zeros((micro, rows - HALO, width), F32)
    edges = jnp.where(
        half == 0, jnp.concatenate([gap, edge], axis=1), jnp.concatenate([edge, gap], axis=1)
    )
    added = jnp.pad(from_second, ((0, 0), (rows - win, 0), (0, 0)))
    to_clean = (jnp.where(clean == 0, da_main.astype(F32), 0.0) + added).astype(BF16)
    from_noisy = lax.ppermute(to_clean, "seq", [(0, 2), (1, 3)])
    extra = jnp.where(clean == 1, from_noisy.astype(F32) + added, 0.0) + edges

    grad_in, g_attn = call(
        final_kernel, (2,),
        [pl.BlockSpec((total // 2, width), lambda i: (i, 0))] * 4 + [whole((1, width))],
        [pl.BlockSpec((total // 2, width), lambda i: (i, 0)), whole((8, width))],
        [like((total, width), F32), like((8, width), F32)], [], 0, 16 << 20, "norm_back",
    )(flat(inputs), flat(da_own), flat(extra), flat(dx2), vec[0:1, :width])

    def scatter(g):
        return lax.psum(lax.psum_scatter(g, "fsdp", scatter_dimension=0, tiled=True), "seq")

    big = [scatter(g).astype(F32) for g in (g_w_in, g_w_out, g_w_up, g_w_down)]
    smalls = [g_attn[0], g_attn[1], g_b_in[0], g_mlp[3], g_mlp[1], g_mlp[2], g_b_up[0], g_mlp[0]]
    pack = jnp.concatenate([g.reshape(fsdp_n, -1) for g in smalls], axis=1)
    pack = lax.psum(pack, ("seq", "fsdp"))
    mine = lax.dynamic_slice_in_dim(pack, lax.axis_index("fsdp"), 1, 0)[0]
    outs, at = [], 0
    for size in sizes:
        outs.append(mine[at : at + size])
        at += size
    return out_rows.reshape(micro, rows, width), grad_in.reshape(micro, rows, width), big, outs


def per_device(
    inputs, segment_ids, block_ids, attn_gain, attn_shift, proj_in, bias_in, proj_out, bias_out,
    mlp_gain, mlp_shift, weight_up, bias_up, weight_down, bias_down, cotangent,
):
    micro, rows, width = inputs.shape
    length = segment_ids.shape[1]
    hidden = weight_up.shape[1]
    seq_n = lax.axis_size("seq")
    fsdp_n = lax.axis_size("fsdp")
    assert seq_n == 4 and seq_n * rows == 2 * length
    lay = layout(rows, length)
    win, keys = lay["win"], lay["keys"]
    me = lax.axis_index("seq")
    clean = me // 2
    half = me % 2
    role = jnp.stack([clean, half]).astype(jnp.int32)
    pairs = [(0, 1), (1, 0), (2, 3), (3, 2)]
    small = (attn_gain, attn_shift, bias_in, bias_out, mlp_gain, mlp_shift, bias_up, bias_down)
    sizes = [p.shape[0] for p in small]
    weights = (proj_in, proj_out, weight_up, weight_down)
    half_dim = HD // 2
    freqs = (10000.0 ** (-(np.arange(half_dim, dtype=np.float32) / half_dim))).astype(np.float32)
    freqs = np.tile(freqs, 4)[None]
    quads = width // (QUAD * HD)
    qw = QUAD * HD
    spans = [hi - lo + NEAR for lo, hi in windows(lay)]
    bias_scratch = [pltpu.VMEM((n, TILE), F32) for n in spans]
    per_seq = lambda n, d: pl.BlockSpec((1, n, d), lambda s: (s, 0, 0))
    role_spec = SMEM()
    attn_flops = micro * quads * sum(spans) * QUAD * TILE * qw * 2
    lse_shape = (micro * quads, rows // TILE, QUAD * TILE)
    table_rows = win + rows + HALO
    aligned = fsdp_n & (fsdp_n - 1) == 0 and all(p.shape[0] % (4 * HALO) in (0, 32) for p in weights)
    front = front_remote if aligned else front_native
    (w_in, w_out, w_up, w_down, q, k, v, a, o, lse, vec, cos, sin, codes, queries) = front(
        lay, role, sizes, inputs, segment_ids, block_ids, small, weights, freqs,
        lse_shape, bias_scratch, spans, attn_flops,
    )
    back = back_remote if aligned else back_native
    out_rows, grad_in, big, vectors = back(
        lay, role, sizes, inputs, cotangent, codes, queries, lse, cos, sin, vec,
        q, k, v, o, a, w_in, w_out, w_up, w_down, bias_scratch, attn_flops,
    )
    g_gain1, g_shift1, g_bin, g_bout, g_gain2, g_shift2, g_bup, g_bdown = vectors
    return (
        out_rows, grad_in, g_gain1, g_shift1, big[0], g_bin, big[1], g_bout,
        g_gain2, g_shift2, big[2], g_bup, big[3], g_bdown,
    )


def solution(mesh):
    rows = P("fsdp", "seq", None)
    one, two = P("fsdp"), P("fsdp", None)
    params = (one, one, two, one, two, one, one, one, two, one, two, one)
    return jax.shard_map(
        per_device,
        mesh=mesh,
        in_specs=(rows, two, two) + params + (rows,),
        out_specs=(rows, rows) + params,
        check_vma=False,
    )
```

```python
import functools
import itertools

import jax
import jax.numpy as jnp
import numpy as np
from jax import lax
from jax.experimental import pallas as pl
from jax.experimental.pallas import tpu as pltpu
from jax.sharding import PartitionSpec as P

HD = 64
QUAD = 4
TILE = 128
HALO = 16
NEAR = TILE + 2 * HALO
EPS = 1e-05
MASKED = -1e30
SEG_STEP = 4096
F32 = jnp.float32
BF16 = jnp.bfloat16
VMEM_BYTES = 62 * 1024 * 1024
MESH = pl.DeviceIdType.MESH
ANY = pl.BlockSpec(memory_space=pl.ANY)
VMEM = pl.BlockSpec(memory_space=pltpu.VMEM)


def dot(a, b):
    return jnp.dot(a, b, preferred_element_type=F32)


def dot_nt(a, b):
    return lax.dot_general(a, b, (((1,), (1,)), ((), ())), preferred_element_type=F32)


def dot_tn(a, b):
    return lax.dot_general(a, b, (((0,), (0,)), ((), ())), preferred_element_type=F32)


def norm_stats(x):
    center = jnp.mean(x, axis=-1, keepdims=True)
    centered = x - center
    inverse = lax.rsqrt(jnp.mean(centered * centered, axis=-1, keepdims=True) + EPS)
    return centered * inverse, inverse


def norm_back(grad, normed, inverse, gain):
    scaled = grad * gain
    first = jnp.mean(scaled, axis=-1, keepdims=True)
    second = jnp.mean(scaled * normed, axis=-1, keepdims=True)
    return inverse * (scaled - first - normed * second)


def partner(u):
    lane = lax.broadcasted_iota(jnp.int32, u.shape, 1)
    half = HD // 2
    return jnp.where(
        lane % HD < half, pltpu.roll(u, u.shape[1] - half, 1), pltpu.roll(u, half, 1)
    )


def whole(shape):
    return pl.BlockSpec(shape, lambda *_: (0,) * len(shape), pipeline_mode=pl.Buffered(1))


def call(kernel, grid, in_specs, out_specs, out_shape, scratch, flops, nbytes, name):
    return pl.pallas_call(
        kernel,
        grid=grid,
        in_specs=in_specs,
        out_specs=out_specs,
        out_shape=out_shape,
        scratch_shapes=scratch,
        compiler_params=pltpu.CompilerParams(vmem_limit_bytes=VMEM_BYTES),
        cost_estimate=pl.CostEstimate(flops=flops, bytes_accessed=nbytes, transcendentals=0),
        name=name,
    )


def like(shape, dtype):
    return jax.ShapeDtypeStruct(shape, dtype)


SMEM = functools.partial(pl.BlockSpec, memory_space=pltpu.SMEM)


def layout(rows, length):
    win = rows - length // 8
    noisy = win + rows + HALO
    used = noisy + rows + 2 * HALO
    return dict(rows=rows, win=win, length=length, noisy=noisy, used=used, keys=-(-used // 256) * 256)


def places(lay, role):
    noisy = role[0] == 0
    second = role[1] == 1
    own_at = jnp.where(noisy, lay["noisy"] + HALO, lay["win"])
    halo_at = jnp.where(
        second,
        lay["noisy"],
        jnp.where(noisy, lay["noisy"] + HALO + lay["rows"], lay["win"] + lay["rows"]),
    )
    return noisy, second, pl.multiple_of(own_at, HALO), pl.multiple_of(halo_at, HALO)


def qkv_rows(lay, where_am, n, x, xb, xc, w, b, gain, shift, cos, sin, q_out, k_out, v_out, a_out):
    width = x.shape[2]
    rows, win = lay["rows"], lay["win"]
    noisy, second, own_at, halo_at = where_am

    def norm(v):
        normed, _ = norm_stats(v.astype(F32))
        return (normed * gain + shift).astype(BF16)

    def zeros(at, count):
        for ref in (k_out, v_out, a_out):
            ref[n, at : at + count, :] = jnp.zeros((count, width), BF16)

    def section(a, parts, table, want_q):
        def put(ref, col, value):
            for begin, count, at in parts:
                ref[n, pl.ds(at, count), col : col + value.shape[1]] = value[begin : begin + count]

        put(a_out, 0, a)
        c = cos[table : table + a.shape[0], :]
        s = sin[table : table + a.shape[0], :]
        first = 0 if want_q else width
        for col in range(first, 3 * width, 256):
            part = dot(a, w[:, col : col + 256]) + b[:, col : col + 256]
            for piece in range(2):
                u = part[:, piece * 128 : piece * 128 + 128]
                at_col = col + piece * 128
                if at_col < 2 * width:
                    u = u * c + partner(u) * s
                if at_col < width:
                    q_out[n, :, at_col : at_col + 128] = (u[:rows] * (HD**-0.5)).astype(BF16)
                elif at_col < 2 * width:
                    put(k_out, at_col - width, u.astype(BF16))
                else:
                    put(v_out, at_col - 2 * width, u.astype(BF16))

    zeros(win + rows, 2 * HALO)
    zeros(lay["used"] - HALO, lay["keys"] - lay["used"] + HALO)
    own = jnp.concatenate([norm(x[n]), norm(xc[n, win:, :])], axis=0)
    section(own, ((0, rows, own_at), (rows, HALO, halo_at)), win, True)

    @pl.when(noisy)
    def _():
        section(norm(xb[n]), ((0, rows, win),), win, False)

    @pl.when(jnp.logical_not(noisy))
    def _():
        zeros(lay["noisy"] + HALO, rows)

    @pl.when(second)
    def _():
        section(norm(xc[n, :win, :]), ((0, win, 0),), 0, False)

    @pl.when(jnp.logical_not(second))
    def _():
        zeros(0, win)


def qkv_columns(lay, n, act, at_parts, table, col, count, w, b, cos, sin, q, k, v):
    width, rows = q.shape[2], lay["rows"]

    def put(ref, at_col, value):
        for begin, size, at in at_parts:
            ref[n, pl.ds(at, size), at_col : at_col + 128] = value[begin : begin + size].astype(BF16)

    c = cos[table : table + act.shape[0], :]
    s = sin[table : table + act.shape[0], :]
    part = dot(act, w[:, col : col + count]) + b[:, col : col + count]
    for at_col in range(col, col + count, 128):
        u = part[:, at_col - col : at_col - col + 128]
        if at_col < 2 * width:
            u = u * c + partner(u) * s
        if at_col < width:
            q[n, :, at_col : at_col + 128] = (u[:rows] * (HD**-0.5)).astype(BF16)
        elif at_col < 2 * width:
            put(k, at_col - width, u)
        else:
            put(v, at_col - 2 * width, u)


def qkv_kernel(lay, role, x, xb, xc, w, vec, cos, sin, *outs):
    width = x.shape[2]
    gain, shift, b = vec[0:1, :width], vec[1:2, :width], vec[2:3, : 3 * width]
    qkv_rows(lay, places(lay, role), 0, x, xb, xc, w, b, gain, shift, cos, sin, *outs)


def windows(lay):
    rows, win, length = lay["rows"], lay["win"], lay["length"]
    longest, earliest, latest = length // 2, length // 8, 3 * length // 8
    found = []
    for at in range(0, rows, TILE):
        begin = win + rows
        for origin in range(0, length, rows):
            pos = origin + at
            low = max(pos - longest, 0)
            if origin > 0:
                low = max(low, earliest)
            if pos >= latest + longest:
                low = max(low, earliest + longest)
            begin = min(begin, low - origin + win)
        found.append((begin // TILE * TILE, win + at + TILE + HALO))
    return found


def tile_loop(lay, body):
    for t, (lo, hi) in enumerate(windows(lay)):
        near = lay["noisy"] + t * TILE
        body(t, slice(t * TILE, t * TILE + TILE), slice(lo, hi), slice(near, near + NEAR), hi - lo)


def make_bias(lay, n, codes, queries, biases):
    (bias,) = biases
    groups = {}
    for t, (lo, hi) in enumerate(windows(lay)):
        groups.setdefault(hi - lo, []).append((t, lo))
    for size, tiles in groups.items():
        (t0, lo0), (t1, lo1), number = tiles[0], tiles[-1], len(tiles)
        apart = max(number - 1, 1)
        assert all(tile == (t0 + k * (t1 - t0) // apart, lo0 + k * (lo1 - lo0) // apart) for k, tile in enumerate(tiles))

        def step(k, carry, size=size, t0=t0, lo0=lo0, dt=(t1 - t0) // apart, dlo=(lo1 - lo0) // apart):
            t = t0 + k * dt
            here = pl.ds(pl.multiple_of(t * TILE, TILE), TILE)
            low, high, same = (queries[n, r : r + 1, here] for r in range(3))
            kc = codes[n, pl.ds(pl.multiple_of(lo0 + k * dlo, HALO), size), :]
            ok = jnp.logical_and(kc >= low, kc <= high)
            bias[t, :size, :] = jnp.where(ok, 0.0, MASKED)
            kn = codes[n, pl.ds(pl.multiple_of(lay["noisy"] + t * TILE, HALO), NEAR), :]
            bias[t, size : size + NEAR, :] = jnp.where(kn == same, 0.0, MASKED)
            return carry

        lax.fori_loop(0, number, step, 0)


def stacked(tile):
    lane = lax.broadcasted_iota(jnp.int32, tile.shape, 1)
    zero = jnp.zeros_like(tile)
    return jnp.concatenate(
        [jnp.where(lane // HD == h, tile, zero) for h in range(QUAD)], axis=0
    )


def own_heads(wide):
    return jnp.concatenate(
        [wide[h * HD : h * HD + HD, h * TILE : h * TILE + TILE] for h in range(QUAD)], axis=0
    )


def keys_of(ref, n, cols, lo, near):
    return jnp.concatenate([ref[n, lo, cols], ref[n, near, cols]], axis=0)


def attend(lay, n, cols, q, k, v, o_out, lse_out, lse_at, biases):
    (bias,) = biases

    def body(t, here, lo, near, size):
        qm = stacked(q[n, here, cols])
        kk = keys_of(k, n, cols, lo, near)
        vv = keys_of(v, n, cols, lo, near)
        s = dot_nt(kk, qm) + jnp.concatenate([bias[t, : size + NEAR, :]] * QUAD, axis=1)
        peak = jnp.max(s, axis=0, keepdims=True)
        p = jnp.exp(s - peak)
        total = jnp.sum(p, axis=0, keepdims=True)
        wide = dot_tn(vv, p.astype(BF16)) * (1.0 / total)
        o_out[n, here, cols] = jnp.transpose(own_heads(wide)).astype(BF16)
        lse_out[lse_at, t : t + 1, :] = peak + jnp.log(total)

    tile_loop(lay, body)


def attend_kernel(lay, codes, queries, q, k, v, o_out, lse_out, *biases):
    @pl.when(pl.program_id(1) == 0)
    def _():
        make_bias(lay, 0, codes, queries, biases)

    attend(lay, 0, slice(None), q, k, v, o_out, lse_out, 0, biases)


def attend_back(
    lay, n, cols, q, k, v, m, cols_m, o, do, lse, lse_at, cos, sin, to, col, dq_out, dk_out, dv_out, dk_acc, dv_acc, biases,
):
    rows, win = lay["rows"], lay["win"]
    qw = QUAD * HD

    def lanes(piece):
        return pl.ds(pl.multiple_of(col + piece * 128, 128), 128)

    dk_acc[...] = jnp.zeros_like(dk_acc)
    dv_acc[...] = jnp.zeros_like(dv_acc)
    (bias,) = biases

    def body(t, here, lo, near, size):
        qm = stacked(q[n, here, cols])
        dom = stacked(do[m, here, cols_m])
        kk = keys_of(k, n, cols, lo, near)
        vv = keys_of(v, n, cols, lo, near)
        both = jnp.transpose(do[m, here, cols_m].astype(F32) * o[m, here, cols_m].astype(F32))
        delta = jnp.concatenate(
            [jnp.sum(both[h * HD : h * HD + HD, :], axis=0, keepdims=True) for h in range(QUAD)],
            axis=1,
        )
        s = dot_nt(kk, qm) + jnp.concatenate([bias[t, : size + NEAR, :]] * QUAD, axis=1)
        p = jnp.exp(s - lse[lse_at, t : t + 1, :])
        dp = dot_nt(vv, dom)
        ds = (p * (dp - delta)).astype(BF16)
        pb = p.astype(BF16)
        dv = dot(pb, dom)
        dk = dot(ds, qm)
        dv_acc[lo, :] += dv[:size]
        dk_acc[lo, :] += dk[:size]
        dv_acc[near, :] += dv[size:]
        dk_acc[near, :] += dk[size:]
        wide = dot_tn(kk, ds)
        dq = jnp.transpose(own_heads(wide)) * (HD**-0.5)
        turn = slice(win + t * TILE, win + t * TILE + TILE)
        c, sn = cos[turn, :], sin[turn, :]
        for piece in range(2):
            u = dq[:, piece * 128 : piece * 128 + 128]
            dq_out[to, here, lanes(piece)] = (u * c - partner(u) * sn).astype(BF16)

    tile_loop(lay, body)
    for piece in range(2):
        dv_out[to, :, lanes(piece)] = dv_acc[:, piece * 128 : piece * 128 + 128].astype(BF16)
    half = (cos[win + rows :, :], sin[win + rows :, :])
    own = (cos[win : win + rows, :], sin[win : win + rows, :])
    tables = (
        (0, (cos[: win + rows, :], sin[: win + rows, :])),
        (win + rows, half),
        (lay["noisy"], half),
        (lay["noisy"] + HALO, own),
        (lay["used"] - HALO, half),
    )
    for at, (c, sn) in tables:
        here = slice(at, at + c.shape[0])
        for piece in range(2):
            u = dk_acc[here, piece * 128 : piece * 128 + 128]
            dk_out[to, here, lanes(piece)] = (u * c - partner(u) * sn).astype(BF16)
    spare = lay["keys"] - lay["used"]
    for piece in range(2):
        dk_out[to, lay["used"] :, lanes(piece)] = jnp.zeros((spare, 128), BF16)


def attend_back_kernel(
    lay, codes, queries, q, k, v, o, do, lse, cos, sin, dq_out, dk_out, dv_out, dk_acc, dv_acc, *biases
):
    @pl.when(pl.program_id(1) == 0)
    def _():
        make_bias(lay, 0, codes, queries, biases)

    attend_back(
        lay, 0, slice(None), q, k, v, 0, slice(None), o, do, lse, 0, cos, sin, 0, 0, dq_out, dk_out, dv_out, dk_acc, dv_acc, biases
    )


def bit_of(index, b):
    return (index // (1 << b)) % 2


def other(index, b):
    return index + (1 << b) * (1 - 2 * bit_of(index, b))


class Net:
    def __init__(self, bits, send, recv, sems):
        self.me, self.f, self.bits = lax.axis_index("seq"), lax.axis_index("fsdp"), bits
        self.core, self.x = self.me % 2, self.me // 2
        self.send, self.recv, self.sems = send, recv, sems
        self.used, self.local_used = 0, 0
        self.started = []

    def partners(self):
        return [{"seq": other(self.me, 0)}, {"seq": other(self.me, 1)}] + [
            {"fsdp": other(self.f, b)} for b in range(self.bits)
        ]

    def barrier(self):
        barrier = pltpu.get_barrier_semaphore()
        for device in self.partners():
            pl.semaphore_signal(barrier, inc=1, device_id=device, device_id_type=MESH)
        pl.semaphore_wait(barrier, 2 + self.bits)

    def copy(self, src, dst, device):
        n = self.used
        self.used += 1
        return pltpu.make_async_remote_copy(
            src_ref=src, dst_ref=dst, send_sem=self.send.at[n], recv_sem=self.recv.at[n],
            device_id=device, device_id_type=MESH,
        )

    def local(self, src, dst):
        n = self.local_used
        self.local_used += 1
        return pltpu.make_async_copy(src, dst, self.sems.at[n])

    def fsdp_index(self, done):
        return tuple(slice(None) if b in done else bit_of(self.f, b) for b in range(self.bits - 1, -1, -1))


FRONT_ORDER = (
    "E s i0 i1",
    "T s R0 i2",
    "i0 i1 i2 i0",
    "u0 s i1 s",
    "u1 i2 o i1",
    "V u0 i0 R1",
    "u1 i1 i2 i0",
    "o d0 P0 L0",
    "L1 W H i2",
    "u0 L2 u1 O0",
    "O1 O2 d1 u0",
    "o d0 A d1",
    "P1 d0 u1 A",
    "A d1 o u0",
    "A u0 d0 u1",
    "A d1 d0 A",
    "o u1",
)
FRONT_BITS = {
    "i0": ((2, 0, 1), False),
    "i1": ((2, 1, 0), False),
    "i2": ((2, 1, 0), False),
    "o": ((2, 1, 0), False),
    "u0": ((2, 1, 0), True),
    "u1": ((2, 0, 1), True),
    "d0": ((2, 1, 0), False),
    "d1": ((0, 2, 1), False),
}


class Gather:
    def __init__(self, net, own, full, tail, tail_x=None, tail_core=None, order=None):
        self.net, self.at = net, 0
        mine = net.fsdp_index(())
        self.own = net.local(own.at[tail], full.at[mine + tail])
        self.stages = []
        done = []
        for b in order if order is not None and len(order) == net.bits else range(net.bits - 1, -1, -1):
            here = full.at[net.fsdp_index(done) + tail]
            src = here if done else own.at[tail]
            self.stages.append(net.copy(src, here, {"fsdp": other(net.f, b)}))
            done.append(b)
        everything = (slice(None),) * net.bits
        for region, b in ((tail_x, 1), (tail_core, 0)):
            if region is not None:
                here = full.at[everything + region]
                self.stages.append(net.copy(here, here, {"seq": other(net.me, b)}))

    def advance(self):
        if self.at > len(self.stages):
            return
        if self.at == 0:
            self.own.start()
        else:
            self.stages[self.at - 1].wait_recv()
        if self.at == 1:
            self.own.wait()
        if self.at < len(self.stages):
            self.stages[self.at].start()
        self.at += 1

    def finish(self):
        for stage in self.stages:
            stage.wait_send()


def front_kernel(
    lay, bits, sizes, x, seg, blk, freqs, w_in_s, w_out_s, w_up_s, w_down_s,
    small0, small1, small2, small3, small4, small5, small6, small7,
    w_in, w_out, w_up, w_down, q_out, k_out, v_out, a_out, o_out, lse_out, vec, cos, sin, codes, queries,
    xb, xc, w_vm, q, k, v, a, o, lse, packs, pack, send, recv, sems, *biases,
):
    rows, win, length = lay["rows"], lay["win"], lay["length"]
    width = x.shape[2]
    hidden = w_up_s.shape[1]
    micro = x.shape[0]
    net = Net(bits, send, recv, sems)
    role = (net.x, net.core)
    noisy, second, own_at, halo_at = places(lay, role)
    first = jnp.logical_not(second)
    clean = jnp.logical_not(noisy)
    net.barrier()

    pair, across = {"seq": other(net.me, 0)}, {"seq": other(net.me, 1)}
    rows_across = [net.copy(x.at[n], xb.at[n], across) for n in range(micro)]
    window = (pl.ds(rows - win, win), slice(None))
    target = (pl.ds(0, win), slice(None))
    rows_pair, rows_pair_b = [], []
    for n in range(micro):
        at = net.used
        rows_pair.append(net.copy(x.at[(n,) + window], xc.at[(n,) + target], pair))
        net.used = at
        rows_pair_b.append(net.copy(xb.at[(n,) + window], xc.at[(n,) + target], pair))
    edge_at = pl.multiple_of((1 - net.core) * (rows - HALO), HALO)
    edge = net.copy(x.at[:, pl.ds(edge_at, HALO), :], xc.at[:, pl.ds(win, HALO), :], pair)

    def columns(begin, size):
        return (slice(None), pl.ds(pl.multiple_of(begin, 128), size))

    pack[...] = jnp.zeros_like(pack)
    smalls = (small0, small1, small2, small3, small4, small5, small6, small7)
    for r, (ref, size) in enumerate(zip(smalls, sizes)):
        pack[r : r + 1, :size] = ref[...].astype(F32).reshape(1, size)
    chunks = {"s": Gather(net, pack, packs, (slice(None), slice(None)))}
    half_in, half_out, half_up = 3 * width // 2, width // 2, hidden // 2
    third = half_in // 3
    for n in range(3):
        region = columns(net.core * half_in + n * third, third)
        chunks["i%d" % n] = Gather(net, w_in_s, w_in, region, None, region, FRONT_BITS["i%d" % n][0])
    region = columns(net.core * half_out, half_out)
    chunks["o"] = Gather(net, w_out_s, w_out, region, None, region, FRONT_BITS["o"][0])
    quarter = half_up // 2
    slab = w_down_s.shape[0]
    for n in range(2):
        order, over_x = FRONT_BITS["u%d" % n]
        region = columns(net.core * half_up + n * quarter, quarter)
        part = columns(net.core * half_up + n * quarter + net.x * (quarter // 2), quarter // 2) if over_x else region
        chunks["u%d" % n] = Gather(net, w_up_s, w_up, part, part if over_x else None, region, order)
        order, over_x = FRONT_BITS["d%d" % n]
        begin = net.core * (slab // 2) + n * (slab // 4)
        region = (pl.ds(pl.multiple_of(begin, HALO), slab // 4), slice(None))
        half_region = (pl.ds(pl.multiple_of(begin + net.x * (slab // 8), HALO), slab // 8), slice(None))
        part = half_region if over_x else region
        chunks["d%d" % n] = Gather(net, w_down_s, w_down, part, part if over_x else None, region, order)

    def rows_start(n):
        @pl.when(clean)
        def _():
            rows_across[n].start()

    count = 1 << bits

    def tables():
        block = 48
        assert (win + rows + HALO) % block == 0

        def table_step(n, carry):
            span = pl.ds(pl.multiple_of(n * block, HALO), block)
            position = lax.broadcasted_iota(jnp.int32, (block, 128), 0) + n * block
            shifted = jnp.where(
                position < win + rows, position - win, position - win - rows + jnp.where(second, -HALO, rows)
            )
            turned = (shifted + jnp.where(second, rows, 0)).astype(F32) * freqs[...]
            lane = lax.broadcasted_iota(jnp.int32, (block, 128), 1)
            cos[span, :] = jnp.cos(turned)
            sine = jnp.sin(turned)
            sin[span, :] = jnp.where(lane % HD < HD // 2, -sine, sine)
            return carry

        lax.fori_loop(0, (win + rows + HALO) // block, table_step, 0)
        code = (seg[...] * SEG_STEP + blk[...]).astype(F32)
        base = (seg[...] * SEG_STEP).astype(F32)
        turned_code = jnp.transpose(jnp.concatenate([code, jnp.zeros((8 - micro, length), F32)], axis=0))
        lay_noisy = lay["noisy"]
        for n in range(micro):
            col = turned_code[:, n : n + 1]
            none = lambda count, value: jnp.full((count, 1), value, F32)
            codes[n, :win, :] = jnp.where(second, col[rows - win : rows], -1.0)
            codes[n, win : win + rows, :] = jnp.where(second, col[rows:], col[:rows])
            after, before = col[rows : rows + HALO], col[rows - HALO : rows]
            codes[n, win + rows : lay_noisy, :] = jnp.where(jnp.logical_and(clean, first), after, -1.0)
            codes[n, lay_noisy : lay_noisy + HALO, :] = jnp.where(jnp.logical_and(noisy, second), before, -2.0)
            codes[n, lay_noisy + HALO : lay_noisy + HALO + rows, :] = jnp.where(
                noisy, jnp.where(second, col[rows:], col[:rows]), -2.0
            )
            codes[n, lay["used"] - HALO : lay["used"], :] = jnp.where(jnp.logical_and(noisy, first), after, -2.0)
            codes[n, lay["used"] :, :] = none(lay["keys"] - lay["used"], -2.0)
            own_code = jnp.where(second, code[n : n + 1, rows:], code[n : n + 1, :rows])
            own_base = jnp.where(second, base[n : n + 1, rows:], base[n : n + 1, :rows])
            high = own_code - jnp.where(noisy, 1.0, 0.0)
            queries[n] = jnp.concatenate([own_base, high, own_code, jnp.zeros((5, rows), F32)], axis=0)

    def vectors():
        kinds = sorted(set(sizes))

        def spread_step(n, totals):
            piece = packs[tuple((n // (1 << b)) % 2 for b in range(bits - 1, -1, -1))]
            added = []
            for size, total in zip(kinds, totals):
                wide = size * count - piece.shape[1]
                padded = jnp.concatenate([piece, jnp.zeros((8, wide), F32)], axis=1) if wide > 0 else piece
                lanes = lax.broadcasted_iota(jnp.int32, padded.shape, 1)
                added.append(total + pltpu.roll(jnp.where(lanes < size, padded, 0.0), n * size, 1))
            return tuple(added)

        zero = tuple(jnp.zeros((8, size * count), F32) for size in kinds)
        spread = dict(zip(kinds, lax.fori_loop(0, count, spread_step, zero)))
        for r, size in enumerate(sizes):
            vec[r : r + 1, : size * count] = spread[size][r : r + 1]
            if size * count < vec.shape[1]:
                vec[r : r + 1, size * count :] = jnp.zeros((1, vec.shape[1] - size * count), F32)

    def pass_on(n):
        @pl.when(noisy)
        def _():
            rows_across[n].wait_recv()

        @pl.when(jnp.logical_and(first, noisy))
        def _():
            rows_pair_b[n].start()

        @pl.when(jnp.logical_and(first, clean))
        def _():
            rows_pair[n].start()

    loads = {}

    def load_weights(j):
        slab_in = w_in_s.shape[0]
        for n in range(count):
            at = tuple((n >> b) & 1 for b in range(bits - 1, -1, -1))
            for block in range(2):
                cols = slice(block * half_in + j * third, block * half_in + (j + 1) * third)
                copy = net.local(w_in.at[at + (slice(None), cols)], w_vm.at[n * slab_in : (n + 1) * slab_in, cols])
                copy.start()
                loads.setdefault(j, []).append(copy)

    def norm(value):
        normed, _ = norm_stats(value.astype(F32))
        return (normed * vec[0:1, :width] + vec[1:2, :width]).astype(BF16)

    def zeros(n, at, size):
        for ref in (k, v, a):
            ref[n, at : at + size, :] = jnp.zeros((size, width), BF16)

    def norms():
        def step(n, carry):
            zeros(n, win + rows, 2 * HALO)
            zeros(n, lay["used"] - HALO, lay["keys"] - lay["used"] + HALO)

            @pl.when(clean)
            def _():
                zeros(n, lay["noisy"] + HALO, rows)

            @pl.when(first)
            def _():
                zeros(n, 0, win)

            a[n, pl.ds(own_at, rows), :] = norm(x[n])
            a[n, pl.ds(halo_at, HALO), :] = norm(xc[n, win:, :])
            return carry

        lax.fori_loop(0, micro, step, 0)

    def own_rows(j):
        for load in loads[j]:
            load.wait()

        def step(n, carry):
            act = jnp.concatenate([a[n, pl.ds(own_at, rows), :], a[n, pl.ds(halo_at, HALO), :]], axis=0)
            for block in range(2):
                qkv_columns(
                    lay, n, act, ((0, rows, own_at), (rows, HALO, halo_at)), win, block * half_in + j * third, third,
                    w_vm, vec[2:3, : 3 * width], cos, sin, q, k, v,
                )
            return carry

        lax.fori_loop(0, micro, step, 0)

    def key_rows(n):
        def section(value, at):
            a[n, at : at + value.shape[0], :] = act = norm(value)
            for col in range(width, 3 * width, 384):
                qkv_columns(
                    lay, n, act, ((0, value.shape[0], at),), at, col, 384, w_vm, vec[2:3, : 3 * width], cos, sin, q, k, v
                )

        @pl.when(noisy)
        def _():
            section(xb[n], win)

        @pl.when(second)
        def _():
            for m in range(micro):

                @pl.when(n == m)
                def _(m=m):
                    rows_pair[m].wait_recv()

            section(xc[n, :win, :], 0)

        for store in stores_of(n):
            store.start()

    first_store = net.local_used
    net.local_used += 4 * micro

    def stores_of(n):
        return [
            pltpu.make_async_copy(here.at[n], there.at[n], sems.at[first_store + 4 * n + m])
            for m, (here, there) in enumerate(((q, q_out), (k, k_out), (v, v_out), (a, a_out)))
        ]

    def serve(token):
        if token in chunks:
            chunks[token].advance()
        elif len(token) == 2:
            {"R": rows_start, "P": pass_on, "L": load_weights, "O": own_rows}[token[0]](int(token[1]))
        else:
            {"E": edge.start, "W": edge.wait_recv, "T": tables, "V": vectors, "H": norms}[token]()

    ahead, *after = [part.split() for part in " ".join(FRONT_ORDER).split("A")]
    for token in ahead:
        serve(token)

    quads = width // (QUAD * HD)
    assert micro * quads == len(after)

    def step(index, carry):
        n, h = index // quads, index % quads

        @pl.when(h == 0)
        def _():
            key_rows(n)
            make_bias(lay, n, codes, queries, biases)

        cols = pl.ds(pl.multiple_of(h * QUAD * HD, QUAD * HD), QUAD * HD)
        def serve_all():
            for at, tokens in enumerate(after):
                if tokens:

                    @pl.when(index == at)
                    def _(tokens=tokens):
                        for token in tokens:
                            serve(token)

        attend(lay, n, cols, q, k, v, o, lse, index, biases)
        serve_all()
        return carry

    lax.fori_loop(0, micro * quads, step, 0)
    last = [net.local(o, o_out), net.local(lse, lse_out)]
    for store in last:
        store.start()
    while any(chunk.at <= len(chunk.stages) for chunk in chunks.values()):
        for chunk in chunks.values():
            chunk.advance()
    for chunk in chunks.values():
        chunk.finish()
    for store in stores_of(0) + stores_of(1) + last:
        store.wait()
    edge.wait_send()

    @pl.when(clean)
    def _():
        for n in range(micro):
            rows_across[n].wait_send()

    @pl.when(first)
    def _():
        for n in range(micro):
            rows_pair[n].wait_send()


def gelu_both(u):
    scale = 0.7978845608028654
    square = u * u
    inner = scale * u * (1.0 + 0.044715 * square)
    th = jnp.tanh(inner)
    plus = 0.5 * (1.0 + th)
    slope = plus + 0.5 * u * (1.0 - th * th) * (scale * (1.0 + 3 * 0.044715 * square))
    return (u * plus).astype(BF16), slope


def mlp_kernel(
    o, x, dy, w_out, vec, w_up, b_up, w_down,
    out_rows, dx2_out, do_out, g_w_out, g_w_up, g_b_up, g_w_down, g_vec,
    mid, a2, a2t, inv, acc_out, acc_da,
):
    step = pl.program_id(0)
    last = pl.num_programs(0) - 1
    width = x.shape[1]
    b_out, gain, shift, b_down = (vec[r : r + 1, :width] for r in (3, 4, 5, 7))

    @pl.when(step == 0)
    def _():
        value = x[...].astype(F32) + dot(o[...], w_out[...]) + b_out
        mid[...] = value
        normed, inverse = norm_stats(value)
        inv[...] = inverse
        a = (normed * gain + shift).astype(BF16)
        a2[...] = a
        a2t[...] = jnp.transpose(a)
        acc_out[...] = jnp.zeros_like(acc_out)
        acc_da[...] = jnp.zeros_like(acc_da)

    g, slope = gelu_both(dot(a2[...], w_up[...]) + b_up[6:7, :])
    acc_out[...] += dot(g, w_down[...])
    du32 = dot_nt(dy[...], w_down[...]) * slope
    du = du32.astype(BF16)
    g_b_up[...] = jnp.broadcast_to(jnp.sum(du.astype(F32), axis=0, keepdims=True), g_b_up.shape)
    acc_da[...] += dot_nt(du, w_up[...])
    g_w_down[...] = dot_tn(g, dy[...]).astype(BF16)
    g_w_up[...] = dot(a2t[...], du).astype(BF16)

    @pl.when(step == last)
    def _():
        dyf = dy[...].astype(F32)
        out_rows[...] = (mid[...] + acc_out[...] + b_down).astype(BF16)
        inverse = inv[...]
        value = mid[...]
        normed = (value - jnp.mean(value, axis=-1, keepdims=True)) * inverse
        da = acc_da[...]
        dx2 = dyf + norm_back(da, normed, inverse, gain)
        dx2_out[...] = dx2
        dp = dx2.astype(BF16)
        do_out[...] = dot_nt(dp, w_out[...]).astype(BF16)
        g_w_out[...] = dot_tn(o[...], dp).astype(BF16)
        g_vec[...] = jnp.concatenate(
            [
                jnp.sum(dyf, axis=0, keepdims=True),
                jnp.sum(da * normed, axis=0, keepdims=True),
                jnp.sum(da, axis=0, keepdims=True),
                jnp.sum(dp.astype(F32), axis=0, keepdims=True),
                jnp.zeros((4, dyf.shape[1]), F32),
            ],
            axis=0,
        )


def qkv_back_kernel(lay, role, a, dq, dk, dv, w, da_own, da_main, da_win, g_w, g_b, g_acc):
    width = dq.shape[2]
    rows, win = lay["rows"], lay["win"]
    noisy, second, own_at, halo_at = places(lay, role)

    @pl.when(pl.program_id(0) == 0)
    def _():
        g_acc[...] = jnp.zeros_like(g_acc)
        g_b[...] = jnp.zeros_like(g_b)

    def column_sums(col, value):
        g_b[0:1, col : col + width] += jnp.sum(value.astype(F32), axis=0, keepdims=True)

    def section(parts, query):
        def take(ref):
            return jnp.concatenate([ref[0, pl.ds(at, count), :] for at, count in parts], axis=0)

        at_t = jnp.transpose(take(a))
        key = take(dk)
        value = take(dv)
        g_acc[:, width : 2 * width] += dot(at_t, key)
        g_acc[:, 2 * width :] += dot(at_t, value)
        column_sums(width, key)
        column_sums(2 * width, value)
        total = dot_nt(key, w[:, width : 2 * width]) + dot_nt(value, w[:, 2 * width :])
        if query is not None:
            g_acc[:, :width] += dot(at_t[:, : query.shape[0]], query)
            column_sums(0, query)
            first = total[: query.shape[0]] + dot_nt(query, w[:, :width])
            return first, total[query.shape[0] :]
        return total

    own, near = section(((own_at, rows), (halo_at, HALO)), dq[0])
    da_own[0] = own
    da_win[0, win:, :] = near.astype(BF16)

    @pl.when(noisy)
    def _():
        da_main[0] = section(((win, rows),), None).astype(BF16)

    @pl.when(second)
    def _():
        da_win[0, :win, :] = section(((0, win),), None).astype(BF16)

    @pl.when(pl.program_id(0) == pl.num_programs(0) - 1)
    def _():
        g_w[...] = g_acc[...].astype(BF16)


def final_kernel(x, da, extra, dx2, gain, grad_in, g_vec):
    value = x[...].astype(F32)
    normed, inverse = norm_stats(value)
    grad = da[...] + extra[...].astype(F32)
    grad_in[...] = dx2[...] + norm_back(grad, normed, inverse, gain[...])

    @pl.when(pl.program_id(0) == 0)
    def _():
        g_vec[...] = jnp.zeros_like(g_vec)

    g_vec[0:1, :] += jnp.sum(grad * normed, axis=0, keepdims=True)
    g_vec[1:2, :] += jnp.sum(grad, axis=0, keepdims=True)


def add_to(ref, at, value):
    ref[at] = (ref[at].astype(F32) + value.astype(F32)).astype(BF16)


def for_all(bits, body):
    if bits == 0:
        body(())
        return

    def step(n, carry):
        body(tuple((n // (1 << b)) % 2 for b in range(bits - 1, -1, -1)))
        return carry

    lax.fori_loop(0, 1 << bits, step, 0)


BACK_ORDER = (
    "S s S s",
    "u0 d0 S s",
    "d0 u0 S s",
    "u1 d1 S s",
    "u1 d1 S s",
    "d2 d0 u0 u2",
    "E o u2 u1",
    "d2 d1 u0 d0",
    "o X e A",
    "A e u2 A",
    "u0 d2 A d1",
    "P0 u2 u1 A",
    "A o u2 e",
    "d2 T P1 G0",
    "i0 o G1 i1",
    "Y0 i0 G2 i2",
    "i1 e o d0",
    "d2 d1 N i0",
    "i2 N i1 e",
    "Y1 N d2 N",
    "l i0 i2 l",
    "l",
)
BACK_BITS = {
    "u0": ((0, 1, 2), True),
    "u1": ((1, 2, 0), True),
    "u2": ((0, 1, 2), True),
    "d0": ((0, 1, 2), False),
    "d1": ((0, 1, 2), False),
    "d2": ((0, 1, 2), False),
    "o": ((0, 1, 2), False),
    "i0": ((1, 2, 0), False),
    "i1": ((0, 1, 2), False),
    "i2": ((0, 1, 2), False),
}


class Reduce:
    def __init__(self, net, acc, recvs, out, rows, cols, order, over_x):
        bits, self.net, self.at, self.sent = net.bits, net, 0, False
        pair, across = {"seq": other(net.me, 0)}, {"seq": other(net.me, 1)}
        recvs = list(recvs)
        part = (slice(None), slice(None))
        begin, size = rows
        tail = tail_half = (pl.ds(begin, size), cols)
        self.acc, self.steps = acc, [None]
        if over_x:
            piece = size // 2
            part = (pl.ds(pl.multiple_of(net.x * piece, HALO), piece), slice(None))
            away = (pl.ds(pl.multiple_of((1 - net.x) * piece, HALO), piece), slice(None))
            tail = (pl.ds(pl.multiple_of(begin + net.x * piece, HALO), piece), cols)
            got_x = recvs.pop(0)

            def add_x():
                for_all(bits, lambda at: add_to(acc, at + part, got_x[at]))

            self.steps.append((net.copy(acc.at[(slice(None),) * bits + away], got_x, across), add_x))
        done = []
        for b in order if len(order) == bits else range(bits):
            got = recvs.pop(0)

            def index(mine, rest, b=b, done=tuple(done)):
                rest = iter(rest)
                return tuple(
                    mine if p == b else bit_of(net.f, p) if p in done else next(rest) for p in range(bits - 1, -1, -1)
                )

            left = bits - 1 - len(done)

            def add_bit(got=got, b=b, index=index, left=left):
                for_all(left, lambda at: add_to(acc, index(bit_of(net.f, b), at) + part, got[at]))

            src = acc.at[index(1 - bit_of(net.f, b), (slice(None),) * left) + part]
            self.steps.append((net.copy(src, got, {"fsdp": other(net.f, b)}), add_bit))
            done.append(b)
        own = tuple(bit_of(net.f, n) for n in range(bits - 1, -1, -1))
        if over_x:
            before = self.steps[-1][1]

            def keep():
                before()
                out[tail] = acc[own + part]

            self.steps[-1] = (self.steps[-1][0], keep)
            self.steps.append((net.copy(out.at[tail], out.at[tail], across), lambda: None))
        else:
            got_last = recvs.pop(0)

            def last():
                out[tail] = (acc[own].astype(F32) + got_last[...].astype(F32)).astype(BF16)

            self.steps.append((net.copy(acc.at[own], got_last, across), last))
        self.steps.append((net.copy(out.at[tail_half], out.at[tail_half], pair), lambda: None))

    def feed(self, theirs, get):
        def mine():
            for_all(self.net.bits, lambda at: add_to(self.acc, at, get(at)))

        self.steps[0] = (self.net.copy(theirs, self.acc, {"seq": other(self.net.me, 0)}), mine)

    def open(self):
        return self.at <= len(self.steps)

    def advance(self):
        if not self.open():
            return
        if self.at > 0:
            copy, then = self.steps[self.at - 1]
            copy.wait_recv()
            then()
        if self.at < len(self.steps):
            self.steps[self.at][0].start()
        self.at += 1

    def finish(self):
        while self.open():
            self.advance()
        for copy, _ in self.steps[1 if self.sent else 0 :]:
            copy.wait_send()


class SumAll:
    def __init__(self, net, value, recvs):
        self.value, self.recvs, self.at = value, recvs, 0
        devices = [{"seq": other(net.me, b)} for b in range(2)]
        devices += [{"fsdp": other(net.f, b)} for b in range(net.bits)]
        self.copies = []
        for n, device in enumerate(devices):
            src = value if n == 0 else recvs.at[len(devices) + n - 1]
            self.copies.append(net.copy(src, recvs.at[n], device))

    def open(self):
        return self.at <= len(self.copies)

    def advance(self):
        count = len(self.copies)
        if not self.open():
            return
        if self.at > 0:
            n = self.at - 1
            self.copies[n].wait_recv()
            held = self.value[...] if n == 0 else self.recvs[count + n - 1]
            self.recvs[count + n] = held + self.recvs[n]
        if self.at < count:
            self.copies[self.at].start()
        self.at += 1

    def finish(self):
        while self.open():
            self.advance()
        for copy in self.copies:
            copy.wait_send()
        return self.recvs[2 * len(self.copies) - 1]


def back_kernel(
    lay, bits, codes, queries, lse, cos, sin, vec, x, o,
    dy, q, k, v, a, w_in, w_out, w_up, w_down,
    out_rows, grad_in, f_in_out, f_out_out, f_up_out, f_down_out, sums_out, late_out,
    do, recv_parts, rwin,
    acc_in, acc_out, acc_up, acc_down, r_in, r_out, r_up, r_down, f_in, f_out, f_up, f_down,
    sums, sums_recv, late, late_recv, send, recv, sems, *biases,
):
    rows, win, keys = lay["rows"], lay["win"], lay["keys"]
    micro, width = x.shape[0], x.shape[2]
    total = micro * rows
    hidden = vec.shape[1]
    qw = QUAD * HD
    quads = width // qw
    net = Net(bits, send, recv, sems)
    where_am = noisy, second, own_at, halo_at = places(lay, (net.x, net.core))
    first, clean = jnp.logical_not(second), jnp.logical_not(noisy)
    gain = vec[0:1, :width]
    net.barrier()
    every = list(itertools.product(range(2), repeat=bits))
    count = len(every)
    pair, across = {"seq": other(net.me, 0)}, {"seq": other(net.me, 1)}
    slab_down = f_down.shape[0]
    steps = slab_down // 128
    share = count // 2
    wide = share * 128
    whole_index = (slice(None),) * bits
    here, there = net.core, 1 - net.core

    def columns(begin, size):
        return (slice(None), pl.ds(pl.multiple_of(begin, 128), size))

    @pl.when(noisy)
    def _():
        recv_parts[...] = jnp.zeros_like(recv_parts)

    sums[...] = jnp.zeros_like(sums)

    def feed_forward(dyv, wu, wd, w_ov, mid, a2, a2t, inv, acc_y, acc_da, gv, duv, gd, gu, gu_out, sem_w, sem_m):
        block = total // 4

        def loads(index):
            j, h = index // 2, index % 2
            slot = index % 2
            copies = []
            for n in range(share):
                at = pl.multiple_of((h * share + n) * slab_down + j * 128, 128)
                part = pl.ds(n * 128, 128)
                copies.append(pltpu.make_async_copy(w_up.at[:, pl.ds(at, 128)], wu.at[slot, :, part], sem_w.at[slot, 2 * n]))
                copies.append(pltpu.make_async_copy(w_down.at[pl.ds(at, 128), :], wd.at[slot, part, :], sem_w.at[slot, 2 * n + 1]))
            return copies

        first_loads = [pltpu.make_async_copy(w_out, w_ov, sem_m.at[0]), pltpu.make_async_copy(dy, dyv, sem_m.at[1])]
        for load in first_loads + loads(0):
            load.start()
        flat = lambda ref: ref[...].reshape(total, width)
        b_out, gain2, shift2, b_down = (vec[r : r + 1, :width] for r in (3, 4, 5, 7))
        first_loads[0].wait()
        def part_rows(n):
            per = rows // block
            return n // per, pl.ds(pl.multiple_of((n % per) * block, block), block)

        def open_step(n, carry):
            span = pl.ds(pl.multiple_of(n * block, block), block)
            m, sub = part_rows(n)
            value = x[m, sub, :].astype(F32) + dot(o[m, sub, :], w_ov[...]) + b_out
            mid[span, :] = value
            normed, inverse = norm_stats(value)
            inv[span, :] = inverse
            act = (normed * gain2 + shift2).astype(BF16)
            a2[span, :] = act
            a2t[:, span] = jnp.transpose(act)
            return carry

        lax.fori_loop(0, total // block, open_step, 0)
        acc_y[...] = jnp.zeros_like(acc_y)
        acc_da[...] = jnp.zeros_like(acc_da)
        first_loads[1].wait()

        away = columns(there * (width // 2), width // 2)
        near = columns(here * (width // 2), width // 2)
        for j in range(steps):
            chunks["u%d" % j].feed(gu.at[j, there], lambda at, j=j: gu[(j, here) + at])
            chunks["d%d" % j].feed(gd.at[(j,) + whole_index + away], lambda at, j=j: gd[(j,) + at + near])

        def serve_all(index, part):
            for at, tokens in enumerate(in_feed):
                if tokens[part]:

                    @pl.when(index == at)
                    def _(tokens=tokens[part]):
                        for token in tokens:
                            chunks[token].advance()

        def step(index, carry):
            j, h = index // 2, index % 2
            slot = index % 2

            @pl.when(index + 1 < 2 * steps)
            def _():
                for load in loads(index + 1):
                    load.start()

            for load in loads(index):
                load.wait()
            at = [pl.ds(pl.multiple_of((h * share + n) * slab_down + j * 128, 128), 128) for n in range(share)]
            bias = jnp.concatenate([vec[6:7, here_at] for here_at in at], axis=1)
            w_u, w_d = wu[slot], wd[slot]

            def rows_step(r, row):
                for sub in range(2):
                    span = pl.ds(pl.multiple_of((2 * r + sub) * block, block), block)
                    g, slope = gelu_both(dot(a2[span, :], w_u) + bias)
                    gv[span, :] = g
                    acc_y[span, :] += dot(g, w_d)
                    du = (dot_nt(dyv[span, :], w_d) * slope).astype(BF16)
                    duv[span, :] = du
                    row += jnp.sum(du.astype(F32), axis=0, keepdims=True)
                    acc_da[span, :] += dot_nt(du, w_u)
                return row

            row = lax.fori_loop(0, total // (2 * block), rows_step, jnp.zeros((1, wide), F32))
            for n in range(share):
                sums[6:7, at[n]] = row[:, n * 128 : n * 128 + 128]
            serve_all(index, 0)
            g_d = dot_tn(gv[...], dyv[...]).astype(BF16)
            for n in range(share):
                low = tuple((n >> b) & 1 for b in range(bits - 2, -1, -1))
                gd[(j, h) + low] = g_d[n * 128 : n * 128 + 128]
            g_u = dot(a2t[...], duv[...]).astype(BF16)
            slab = width // count
            for n, idx in enumerate(every):
                gu[(j, h) + idx] = g_u[n * slab : n * slab + slab]
            serve_all(index, 1)
            return carry

        lax.fori_loop(0, 2 * steps, step, 0)
        def close_step(n, carry):
            span = pl.ds(pl.multiple_of(n * block, block), block)
            m, sub = part_rows(n)
            dyf = dyv[span, :].astype(F32)
            value = mid[span, :]
            a2[span, :] = (value + acc_y[span, :] + b_down).astype(BF16)
            normed = (value - jnp.mean(value, axis=-1, keepdims=True)) * inv[span, :]
            da = acc_da[span, :]
            dx2 = dyf + norm_back(da, normed, inv[span, :], gain2)
            acc_da[span, :] = dx2
            dp = dx2.astype(BF16)
            dyv[span, :] = dp
            do[m, sub, :] = dot_nt(dp, w_ov[...]).astype(BF16)
            for r, part in ((7, dyf), (4, da * normed), (5, da), (3, dp.astype(F32))):
                sums[r : r + 1, :width] += jnp.sum(part, axis=0, keepdims=True)
            return carry

        lax.fori_loop(0, total // block, close_step, 0)
        puts = []
        for n in range(micro):
            part = pl.ds(n * rows, rows)
            puts.append(pltpu.make_async_copy(acc_da.at[part, :], grad_in.at[n], sem_m.at[2 + 2 * n]))
            puts.append(pltpu.make_async_copy(a2.at[part, :], out_rows.at[n], sem_m.at[3 + 2 * n]))
        for put in puts:
            put.start()
        g_o = dot_tn(flat(o), dyv[...]).astype(BF16)
        slab = width // count
        for n, idx in enumerate(every):
            for c in range(2):
                gu_out[(c,) + idx] = g_o[n * slab : n * slab + slab, c * (width // 2) : (c + 1) * (width // 2)]
        chunks["o"].feed(gu_out.at[there], lambda at: gu_out[(here,) + at])
        for token in after_feed:
            chunks[token].advance()
        for name, chunk in chunks.items():
            if name[0] in "udo":
                assert chunk.at >= 2
                chunk.steps[0][0].wait_send()
                chunk.sent = True
        for put in puts:
            put.wait()

    half_out = width // 2
    slab = width // count
    chunks = {}
    for j in range(steps):
        chunks["u%d" % j] = Reduce(net, acc_up[j], r_up[j], f_up.at[j], (0, slab),
                                   columns(here * wide, wide)[1], *BACK_BITS["u%d" % j])
        chunks["d%d" % j] = Reduce(net, acc_down[j], r_down[j], f_down, (j * 128, 128),
                                   columns(here * half_out, half_out)[1], *BACK_BITS["d%d" % j])
    chunks["o"] = Reduce(net, acc_out, r_out, f_out, (0, slab), columns(here * half_out, half_out)[1], *BACK_BITS["o"])
    chunks["e"] = SumAll(net, sums, sums_recv)
    chunks["l"] = SumAll(net, late, late_recv)
    edge_at = pl.multiple_of((1 - net.core) * (rows - HALO), HALO)
    tokens = " ".join(BACK_ORDER).split()
    feed_end, free, turn = tokens.index("E"), tokens.index("X"), tokens.index("T")
    halves = lambda text, outer, inner: [[half.split() for half in part.split(inner)] for part in text.split(outer)]
    (_,), *in_feed = halves(" ".join(tokens[:feed_end]), "S", "s")
    after_feed = tokens[feed_end + 1 : free]
    early_tokens, *in_attention = [part.split() for part in " ".join(tokens[free + 1 : turn]).split("A")]
    after_attention = tokens[turn + 1 :]
    assert len(in_feed) == 2 * steps and len(in_attention) == micro * quads

    pl.run_scoped(
        feed_forward,
        pltpu.VMEM((total, width), BF16), pltpu.VMEM((2, width, wide), BF16), pltpu.VMEM((2, wide, width), BF16),
        pltpu.VMEM((width, width), BF16), pltpu.VMEM((total, width), F32), pltpu.VMEM((total, width), BF16),
        pltpu.VMEM((width, total), BF16), pltpu.VMEM((total, 1), F32), pltpu.VMEM((total, width), F32),
        pltpu.VMEM((total, width), F32), pltpu.VMEM((total, wide), BF16), pltpu.VMEM((total, wide), BF16),
        pltpu.VMEM((steps,) + (2,) * bits + (128, width), BF16),
        pltpu.VMEM((steps, 2) + (2,) * bits + (width // count, wide), BF16),
        pltpu.VMEM((2,) + (2,) * bits + (width // count, half_out), BF16),
        pltpu.SemaphoreType.DMA((2, 2 * share)), pltpu.SemaphoreType.DMA((2 + 2 * micro,)),
    )

    def backward(dq, dk, dv, w_vm, gin, parts, dwin, sem_l):
        load_w = pltpu.make_async_copy(w_in, w_vm, sem_l.at[0])
        load_w.start()
        p1 = [net.copy(dwin.at[n], rwin.at[n], pair) for n in range(micro)]
        p2 = [net.copy(parts.at[n], recv_parts.at[n], across) for n in range(micro)]
        third = 3 * width // 6
        slab_in = width // count
        for j in range(3):
            chunks["i%d" % j] = Reduce(net, acc_in[j], r_in[j], f_in, (0, slab_in),
                                       columns(here * 3 * third + j * third, third)[1], *BACK_BITS["i%d" % j])
            chunks["i%d" % j].feed(gin.at[j, there], lambda at, j=j: gin[(j, here) + at])

        def pass_on(n):
            p1[n].wait_recv()

            @pl.when(noisy)
            def _():
                @pl.when(first)
                def _():
                    add_to(parts, (n, slice(rows - win, rows), slice(None)), rwin[n, :win, :])

                p2[n].start()

        def attention(qb, kb, vb, dk_acc, dv_acc, load_sems):
            blocks = ((q, qb), (k, kb), (v, vb))

            def loads(index):
                n, h = index // quads, index % quads
                cols = pl.ds(pl.multiple_of(h * qw, qw), qw)
                slot = index % 2
                return [
                    pltpu.make_async_copy(src.at[n, :, cols], dst.at[slot], load_sems.at[slot, m])
                    for m, (src, dst) in enumerate(blocks)
                ]

            for load in loads(0):
                load.start()
            load_w.wait()

            def partial(n):
                key = jnp.concatenate([dk[n, :win, :], dk[n, pl.ds(halo_at, HALO), :]], axis=0)
                value = jnp.concatenate([dv[n, :win, :], dv[n, pl.ds(halo_at, HALO), :]], axis=0)
                w_key, w_value = w_vm[:, width : 2 * width], w_vm[:, 2 * width :]
                dwin[n] = (dot_nt(key, w_key) + dot_nt(value, w_value)).astype(BF16)
                for m in range(micro):

                    @pl.when(n == m)
                    def _(m=m):
                        p1[m].start()

                @pl.when(noisy)
                def _():
                    main = slice(win, win + rows)
                    parts[n] = (dot_nt(dk[n, main, :], w_key) + dot_nt(dv[n, main, :], w_value)).astype(BF16)

            def serve(token):
                if token[0] == "P":
                    pass_on(int(token[1]))
                else:
                    chunks[token].advance()

            for token in early_tokens:
                serve(token)

            def serve_all(index):
                for at, tokens in enumerate(in_attention):
                    if tokens:

                        @pl.when(index == at)
                        def _(tokens=tokens):
                            for token in tokens:
                                serve(token)

            def step(index, carry):
                n, h = index // quads, index % quads
                slot = index % 2

                @pl.when(index + 1 < micro * quads)
                def _():
                    for load in loads(index + 1):
                        load.start()

                @pl.when(h == 0)
                def _():
                    make_bias(lay, n, codes, queries, biases)

                for load in loads(index):
                    load.wait()
                cols = pl.ds(pl.multiple_of(h * qw, qw), qw)
                attend_back(
                    lay, slot, slice(None), qb, kb, vb, n, cols, o, do, lse, index, cos, sin,
                    n, h * qw, dq, dk, dv, dk_acc, dv_acc, biases,
                )
                @pl.when(h == quads - 1)
                def _():
                    partial(n)

                serve_all(index)
                return carry

            lax.fori_loop(0, micro * quads, step, 0)

        pl.run_scoped(
            attention,
            pltpu.VMEM((2, rows, qw), BF16), pltpu.VMEM((2, keys, qw), BF16), pltpu.VMEM((2, keys, qw), BF16),
            pltpu.VMEM((keys, qw), F32), pltpu.VMEM((keys, qw), F32),
            pltpu.SemaphoreType.DMA((2, 3)),
        )

        def projection(av, at_all, at_own, dxv, sem_a, sem_x):
            load_x = pltpu.make_async_copy(grad_in, dxv, sem_x.at[0])
            pltpu.make_async_copy(a.at[0], av, sem_a.at[0]).start()
            load_x.start()
            def turn_step(n, carry):
                pltpu.make_async_copy(a.at[n], av, sem_a.at[n]).wait()
                at_all[n] = jnp.transpose(av[...])
                at_own[n] = jnp.transpose(av[pl.ds(own_at, rows), :])

                @pl.when(n + 1 < micro)
                def _():
                    pltpu.make_async_copy(a.at[n + 1], av, sem_a.at[n + 1]).start()

                return carry

            lax.fori_loop(0, micro, turn_step, 0)
            late[...] = jnp.zeros_like(late)
            def gradient(j):
                for block in range(2):
                    col = block * 3 * third + j * third
                    source, lhs = ((dq, at_own), (dk, at_all), (dv, at_all))[col // width]
                    inside = slice(col % width, col % width + third)
                    part = width // 2

                    def rows_step(m, carry):
                        grad = jnp.zeros((part, third), F32)
                        for n in range(micro):
                            grad += dot(lhs[n, pl.ds(pl.multiple_of(m * part, 128), part), :], source[n, :, inside])
                        for low, at in enumerate(itertools.product(range(2), repeat=bits - 1)):
                            gin[(j, block, m) + at] = grad[low * slab_in : low * slab_in + slab_in].astype(BF16)
                        return carry

                    lax.fori_loop(0, 2, rows_step, 0)
                    ones = jnp.zeros((8, third), F32)
                    for n in range(micro):
                        rhs = source[n, :, inside]
                        ones += dot(jnp.ones((8, rhs.shape[0]), BF16), rhs)
                    row = 2 + col // width
                    late[row : row + 1, inside] = ones[0:1]

            def settle(n):
                @pl.when(clean)
                def _():
                    p2[n].wait_recv()

                    @pl.when(first)
                    def _():
                        add_to(recv_parts, (n, slice(rows - win, rows), slice(None)), rwin[n, :win, :])

                add_to(recv_parts, (n, pl.ds(edge_at, HALO), slice(None)), rwin[n, win:, :])

            def store(m):
                span = pl.ds(pl.multiple_of((m % 2) * (rows // 2), TILE), rows // 2)
                return pltpu.make_async_copy(dxv.at[m // 2, span, :], grad_in.at[m // 2, span, :], sem_x.at[1 + m])

            def norm_part(m):
                n, part = m // 2, m % 2
                size = rows // 2
                span = pl.ds(pl.multiple_of(part * size, TILE), size)
                mine_rows = pl.ds(pl.multiple_of(own_at + part * size, HALO), size)
                da = dot_nt(dq[n, span, :], w_vm[:, :width])
                da += dot_nt(dk[n, mine_rows, :], w_vm[:, width : 2 * width])
                da += dot_nt(dv[n, mine_rows, :], w_vm[:, 2 * width :])
                da += recv_parts[n, span, :].astype(F32)
                normed, inverse = norm_stats(x[n, span, :].astype(F32))
                dxv[n, span, :] += norm_back(da, normed, inverse, gain)
                late[0:1, :] += jnp.sum(da * normed, axis=0, keepdims=True)
                late[1:2, :] += jnp.sum(da, axis=0, keepdims=True)
                store(m).start()

            def serve(token):
                if token in chunks:
                    chunks[token].advance()
                else:
                    {"P": pass_on, "Y": settle, "G": gradient}[token[0]](int(token[1]))

            groups = [part.split() for part in " ".join(after_attention).split("N")]
            assert len(groups) == 1 + 2 * micro
            for token in groups[0]:
                serve(token)
            load_x.wait()

            def norm_step(m, carry):
                norm_part(m)
                for at, tokens in enumerate(groups[1:-1]):
                    if tokens:

                        @pl.when(m == at)
                        def _(tokens=tokens):
                            for token in tokens:
                                serve(token)

                return carry

            lax.fori_loop(0, 2 * micro, norm_step, 0)
            for token in groups[-1]:
                serve(token)
            while any(chunk.open() for chunk in chunks.values()):
                for chunk in chunks.values():
                    chunk.advance()
            sums_out[...] = chunks["e"].finish()
            late_out[...] = chunks["l"].finish()
            for name, chunk in chunks.items():
                if name not in "el":
                    chunk.finish()
            puts = [net.local(src, dst) for src, dst in ((f_in, f_in_out), (f_out, f_out_out), (f_down, f_down_out))]
            for j in range(steps):
                for n in range(count):
                    puts.append(net.local(
                        f_up.at[j, :, pl.ds(n * 128, 128)], f_up_out.at[:, pl.ds(n * slab_down + j * 128, 128)]
                    ))
            for put in puts:
                put.start()
            for put in puts:
                put.wait()
            for m in range(2 * micro):
                store(m).wait()
            for copy in p1:
                copy.wait_send()

            @pl.when(noisy)
            def _():
                for copy in p2:
                    copy.wait_send()

        pl.run_scoped(
            projection,
            pltpu.VMEM((keys, width), BF16), pltpu.VMEM((micro, width, keys), BF16),
            pltpu.VMEM((micro, width, rows), BF16), pltpu.VMEM((micro, rows, width), F32),
            pltpu.SemaphoreType.DMA((micro,)), pltpu.SemaphoreType.DMA((1 + 2 * micro,)),
        )

    third = 3 * width // 6
    pl.run_scoped(
        backward,
        pltpu.VMEM((micro, rows, width), BF16), pltpu.VMEM((micro, keys, width), BF16),
        pltpu.VMEM((micro, keys, width), BF16), pltpu.VMEM((width, 3 * width), BF16),
        pltpu.VMEM((3, 2) + (2,) * bits + (width // count, third), BF16),
        pltpu.VMEM((micro, rows, width), BF16), pltpu.VMEM((micro, win + HALO, width), BF16),
        pltpu.SemaphoreType.DMA((1,)),
    )


def finish_kernel(sizes, sums, late, g_in, g_out, g_up, g_down, o_in, o_out, o_up, o_down, *vectors):
    for src, dst in ((g_in, o_in), (g_out, o_out), (g_up, o_up), (g_down, o_down)):
        dst[...] = src[...].astype(F32)
    f = lax.axis_index("fsdp")
    width = late.shape[1]
    for r, (size, out) in enumerate(zip(sizes, vectors)):
        if r < 2:
            row = late[r : r + 1, :]
        elif r == 2:
            row = jnp.concatenate([late[m : m + 1, :] for m in range(2, 5)], axis=1)
        else:
            row = sums[r : r + 1, :] if sums.shape[1] == size * (width // sizes[0]) else sums[r : r + 1, :width]
        whole_size = row.shape[1]
        row = jnp.broadcast_to(row, (8, whole_size))
        turned = pltpu.roll(row, lax.rem(whole_size - f * size, whole_size), 1)
        out[...] = turned[0, :size]


def front_remote(
    lay, role, sizes, inputs, segment_ids, block_ids, small, weights, freqs, lse_shape, bias_scratch, spans, attn_flops
):
    micro, rows, width = inputs.shape
    keys, win = lay["keys"], lay["win"]
    bits = lax.axis_size("fsdp").bit_length() - 1
    lanes = -(-max(sizes) // 128) * 128
    full = [like((2,) * bits + p.shape, BF16) for p in weights]
    longest = max(sizes) << bits
    table_rows = win + rows + HALO
    shapes = full + [
        like((micro, rows, width), BF16), like((micro, keys, width), BF16), like((micro, keys, width), BF16),
        like((micro, keys, width), BF16), like((micro, rows, width), BF16), like(lse_shape, F32),
        like((8, longest), F32), like((table_rows, 128), F32), like((table_rows, 128), F32),
        like((micro, keys, 1), F32), like((micro, 8, rows), F32),
    ]
    remote = 3 * micro + 1 + (bits + 2) * 9
    outs = pl.pallas_call(
        functools.partial(front_kernel, lay, bits, sizes),
        in_specs=[VMEM] * 16,
        out_specs=[ANY] * 10 + [VMEM] * 5,
        out_shape=shapes,
        scratch_shapes=[
            pltpu.VMEM((micro, rows, width), BF16), pltpu.VMEM((micro, win + HALO, width), BF16),
            pltpu.VMEM((width, 3 * width), BF16), pltpu.VMEM((micro, rows, width), BF16),
            pltpu.VMEM((micro, keys, width), BF16), pltpu.VMEM((micro, keys, width), BF16),
            pltpu.VMEM((micro, keys, width), BF16), pltpu.VMEM((micro, rows, width), BF16),
            pltpu.VMEM(lse_shape, F32), pltpu.VMEM((2,) * bits + (8, lanes), F32), pltpu.VMEM((8, lanes), F32),
            pltpu.SemaphoreType.DMA((remote,)), pltpu.SemaphoreType.DMA((remote,)),
            pltpu.SemaphoreType.DMA((96,)),
        ] + bias_scratch,
        compiler_params=pltpu.CompilerParams(
            vmem_limit_bytes=VMEM_BYTES, collective_id=0, has_side_effects=True
        ),
        cost_estimate=pl.CostEstimate(flops=2 * attn_flops, bytes_accessed=40 << 20, transcendentals=0),
        name="front",
    )(inputs, segment_ids, block_ids, freqs, *weights, *small)
    joined = [w.reshape((-1, w.shape[-1])) for w in outs[:4]]
    return tuple(joined) + tuple(outs[4:])


def front_native(
    lay, role, sizes, inputs, segment_ids, block_ids, small, weights, freqs, lse_shape, bias_scratch, spans, attn_flops
):
    micro, rows, width = inputs.shape
    keys, win, length = lay["keys"], lay["win"], lay["length"]
    clean, half = role[0], role[1]
    pairs = [(0, 1), (1, 0), (2, 3), (3, 2)]
    xb = lax.ppermute(inputs, "seq", [(2, 0), (3, 1)])
    xmain = jnp.where(clean == 1, inputs, xb)
    edge = jnp.where(half == 0, inputs[:, rows - HALO :], inputs[:, :HALO])
    xc = lax.ppermute(jnp.concatenate([xmain[:, rows - win :], edge], axis=1), "seq", pairs)
    start = half * rows
    edge_at = jnp.where(half == 0, rows, -HALO)
    positions = start + jnp.concatenate([jnp.arange(-win, rows), edge_at + jnp.arange(HALO)])
    turned = positions.astype(F32)[:, None] * freqs
    sine = jnp.sin(turned)
    cos = jnp.cos(turned)
    sin = jnp.where(jnp.arange(128)[None] % HD < HD // 2, -sine, sine)
    code = segment_ids * SEG_STEP + block_ids
    padded = jnp.pad(code, ((0, 0), (win, 0)), constant_values=-1)
    key_codes = lax.dynamic_slice_in_dim(padded, start, win + rows, 1)
    own_code = lax.dynamic_slice_in_dim(code, start, rows, 1)
    own_seg = lax.dynamic_slice_in_dim(segment_ids, start, rows, 1)
    before, after = code[:, rows - HALO : rows], code[:, rows : rows + HALO]
    codes = jnp.concatenate(
        [
            key_codes,
            jnp.where((clean == 1) & (half == 0), after, -1),
            jnp.where((clean == 0) & (half == 1), before, -2),
            jnp.where(clean == 0, own_code, -2),
            jnp.where((clean == 0) & (half == 0), after, -2),
            jnp.full((micro, keys - lay["used"]), -2, jnp.int32),
        ],
        axis=1,
    )[:, :, None].astype(F32)
    queries = jnp.stack([own_seg * SEG_STEP, own_code - (1 - clean), own_code], axis=1)
    queries = jnp.concatenate([queries, jnp.zeros((micro, 5, rows), jnp.int32)], axis=1).astype(F32)
    packed = lax.all_gather(jnp.concatenate(small)[None], "fsdp", axis=0, tiled=True)
    vectors, at = [], 0
    longest = max(sizes) * packed.shape[0]
    for size in sizes:
        one = packed[:, at : at + size].reshape(-1).astype(F32)
        vectors.append(jnp.pad(one, (0, longest - one.shape[0])))
        at += size
    vec = jnp.stack(vectors)
    w_in, w_out, w_up, w_down = (lax.all_gather(p, "fsdp", axis=0, tiled=True) for p in weights)
    per_seq = lambda n, d: pl.BlockSpec((1, n, d), lambda s: (s, 0, 0))
    table_rows = win + rows + HALO
    q, k, v, a = call(
        functools.partial(qkv_kernel, lay), (micro,),
        [SMEM(), per_seq(rows, width), per_seq(rows, width), per_seq(win + HALO, width),
         whole((width, 3 * width)), whole(vec.shape), whole((table_rows, 128)), whole((table_rows, 128))],
        [per_seq(rows, width), per_seq(keys, width), per_seq(keys, width), per_seq(keys, width)],
        [like((micro, rows, width), BF16)] + [like((micro, keys, width), BF16)] * 3,
        [], 2 * micro * rows * width * 3 * width * 2, 20 << 20, "qkv",
    )(role, inputs, xb, xc, w_in, vec, cos, sin)
    qw = QUAD * HD
    quads = width // qw
    quad_block = lambda n: pl.BlockSpec((1, n, qw), lambda s, h: (s, 0, h))
    o, lse = call(
        functools.partial(attend_kernel, lay), (micro, quads),
        [pl.BlockSpec((1, keys, 1), lambda s, h: (s, 0, 0)), pl.BlockSpec((1, 8, rows), lambda s, h: (s, 0, 0)),
         quad_block(rows), quad_block(keys), quad_block(keys)],
        [quad_block(rows), pl.BlockSpec((1,) + lse_shape[1:], lambda s, h: (s * quads + h, 0, 0))],
        [like((micro, rows, width), BF16), like(lse_shape, F32)],
        bias_scratch, 2 * attn_flops, 12 << 20, "attend",
    )(codes, queries, q, k, v)
    return w_in, w_out, w_up, w_down, q, k, v, a, o, lse, vec, cos, sin, codes, queries


def back_remote(
    lay, role, sizes, inputs, cotangent, codes, queries, lse, cos, sin, vec,
    q, k, v, o, a, w_in, w_out, w_up, w_down, bias_scratch, attn_flops,
):
    micro, rows, width = inputs.shape
    keys, win = lay["keys"], lay["win"]
    bits = lax.axis_size("fsdp").bit_length() - 1
    lead = (2,) * bits
    count = 1 << bits
    hidden = w_up.shape[1]
    slab, slab_down = width // count, hidden // count
    third = width // 2
    steps, wide = slab_down // 128, count // 2 * 128

    def bank(name, r, c):
        over_x = BACK_BITS[name][1]
        kept = r // 2 if over_x else r
        over = [pltpu.VMEM(lead[: bits - 1 - b] + (kept, c), BF16) for b in range(bits)]
        ends = [pltpu.VMEM(lead + (kept, c), BF16)] if over_x else []
        return pltpu.VMEM(lead + (r, c), BF16), tuple(ends + over + ([] if over_x else [pltpu.VMEM((r, c), BF16)]))

    acc_in, r_in = zip(*[bank("i%d" % j, slab, third) for j in range(3)])
    acc_out, r_out = bank("o", slab, width // 2)
    acc_up, r_up = zip(*[bank("u%d" % j, slab, wide) for j in range(steps)])
    acc_down, r_down = zip(*[bank("d%d" % j, 128, width // 2) for j in range(steps)])
    stages = 2 + bits
    remote = (7 + 2 * steps) * (bits + 5) + 2 * stages + 4 * micro
    scratch = [
        pltpu.VMEM((micro, rows, width), BF16), pltpu.VMEM((micro, rows, width), BF16),
        pltpu.VMEM((micro, win + HALO, width), BF16),
        acc_in, acc_out, acc_up, acc_down, r_in, r_out, r_up, r_down,
        pltpu.VMEM((slab, 3 * width), BF16), pltpu.VMEM((slab, width), BF16),
        pltpu.VMEM((steps, slab, count * 128), BF16), pltpu.VMEM((slab_down, width), BF16),
        pltpu.VMEM((8, hidden), F32), pltpu.VMEM((2 * stages, 8, hidden), F32),
        pltpu.VMEM((8, width), F32), pltpu.VMEM((2 * stages, 8, width), F32),
        pltpu.SemaphoreType.DMA((remote,)), pltpu.SemaphoreType.DMA((remote,)),
        pltpu.SemaphoreType.DMA((8 + steps * count,)),
    ] + bias_scratch
    out_rows, grad_in, f_in, f_out, f_up, f_down, sums, late = pl.pallas_call(
        functools.partial(back_kernel, lay, bits),
        in_specs=[VMEM] * 8 + [ANY] * 9,
        out_specs=[ANY] * 6 + [VMEM] * 2,
        out_shape=[
            like((micro, rows, width), BF16), like((micro, rows, width), F32), like((slab, 3 * width), BF16),
            like((slab, width), BF16), like((slab, hidden), BF16), like((slab_down, width), BF16),
            like((8, hidden), F32), like((8, width), F32),
        ],
        scratch_shapes=scratch,
        compiler_params=pltpu.CompilerParams(
            vmem_limit_bytes=67043328, collective_id=1, has_side_effects=True
        ),
        cost_estimate=pl.CostEstimate(flops=6 * attn_flops, bytes_accessed=60 << 20, transcendentals=0),
        name="back",
    )(codes, queries, lse, cos, sin, vec, inputs, o, cotangent.reshape(micro * rows, width),
      q, k, v, a, w_in, w_out, w_up, w_down)
    big_shapes = [like(g.shape, F32) for g in (f_in, f_out, f_up, f_down)]
    done = pl.pallas_call(
        functools.partial(finish_kernel, sizes),
        in_specs=[VMEM] * 6,
        out_specs=[VMEM] * 12,
        out_shape=big_shapes + [like((size,), F32) for size in sizes],
        compiler_params=pltpu.CompilerParams(vmem_limit_bytes=VMEM_BYTES),
        cost_estimate=pl.CostEstimate(flops=0, bytes_accessed=6 << 20, transcendentals=0),
        name="finish",
    )(sums, late, f_in, f_out, f_up, f_down)
    return out_rows, grad_in, list(done[:4]), list(done[4:])


def back_native(
    lay, role, sizes, inputs, cotangent, codes, queries, lse, cos, sin, vec,
    q, k, v, o, a, w_in, w_out, w_up, w_down, bias_scratch, attn_flops,
):
    micro, rows, width = inputs.shape
    keys, win = lay["keys"], lay["win"]
    clean, half = role[0], role[1]
    pairs = [(0, 1), (1, 0), (2, 3), (3, 2)]
    fsdp_n = lax.axis_size("fsdp")
    hidden = w_up.shape[1]
    qw = QUAD * HD
    quads = width // qw
    total = micro * rows
    flat = lambda z: z.reshape(total, width)
    chunk = min(512, hidden)
    rows_spec = whole((total, width))
    out_rows, dx2, do, g_w_out, g_w_up, g_b_up, g_w_down, g_mlp = call(
        mlp_kernel, (hidden // chunk,),
        [rows_spec, rows_spec, rows_spec, whole((width, width)), whole(vec.shape),
         pl.BlockSpec((width, chunk), lambda j: (0, j)), pl.BlockSpec((8, chunk), lambda j: (0, j)),
         pl.BlockSpec((chunk, width), lambda j: (j, 0))],
        [rows_spec, rows_spec, rows_spec, whole((width, width)),
         pl.BlockSpec((width, chunk), lambda j: (0, j)), pl.BlockSpec((8, chunk), lambda j: (0, j)),
         pl.BlockSpec((chunk, width), lambda j: (j, 0)), whole((8, width))],
        [like((total, width), BF16), like((total, width), F32), like((total, width), BF16),
         like((width, width), BF16), like((width, hidden), BF16), like((8, hidden), F32),
         like((hidden, width), BF16), like((8, width), F32)],
        [pltpu.VMEM((total, width), F32), pltpu.VMEM((total, width), BF16), pltpu.VMEM((width, total), BF16),
         pltpu.VMEM((total, 1), F32), pltpu.VMEM((total, width), F32), pltpu.VMEM((total, width), F32)],
        2 * total * width * (6 * hidden + 3 * width), 40 << 20, "mlp",
    )(flat(o), flat(inputs), flat(cotangent), w_out, vec, w_up, vec, w_down)

    do = do.reshape(micro, rows, width)
    per_seq = lambda n, d: pl.BlockSpec((1, n, d), lambda s: (s, 0, 0))
    role_spec = SMEM()
    quad_block = lambda n: pl.BlockSpec((1, n, qw), lambda s, h: (s, 0, h))
    code_spec = pl.BlockSpec((1, keys, 1), lambda s, h: (s, 0, 0))
    query_spec = pl.BlockSpec((1, 8, rows), lambda s, h: (s, 0, 0))
    lse_spec = pl.BlockSpec((1,) + lse.shape[1:], lambda s, h: (s * quads + h, 0, 0))
    table = pl.BlockSpec((win + rows + HALO, 128), lambda s, h: (0, 0), pipeline_mode=pl.Buffered(1))
    dq, dk, dv = call(
        functools.partial(attend_back_kernel, lay), (micro, quads),
        [code_spec, query_spec, quad_block(rows), quad_block(keys), quad_block(keys),
         quad_block(rows), quad_block(rows), lse_spec, table, table],
        [quad_block(rows), quad_block(keys), quad_block(keys)],
        [like((micro, rows, width), BF16), like((micro, keys, width), BF16), like((micro, keys, width), BF16)],
        [pltpu.VMEM((keys, qw), F32), pltpu.VMEM((keys, qw), F32)] + bias_scratch,
        5 * attn_flops, 24 << 20, "attend_back",
    )(codes, queries, q, k, v, o, do, lse, cos, sin)

    da_own, da_main, da_win, g_w_in, g_b_in = call(
        functools.partial(qkv_back_kernel, lay), (micro,),
        [role_spec, per_seq(keys, width), per_seq(rows, width), per_seq(keys, width), per_seq(keys, width),
         whole((width, 3 * width))],
        [per_seq(rows, width), per_seq(rows, width), per_seq(win + HALO, width),
         whole((width, 3 * width)), whole((8, 3 * width))],
        [like((micro, rows, width), F32), like((micro, rows, width), BF16), like((micro, win + HALO, width), BF16),
         like((width, 3 * width), BF16), like((8, 3 * width), F32)],
        [pltpu.VMEM((width, 3 * width), F32)], 2 * 2 * micro * rows * width * 3 * width * 2, 40 << 20, "qkv_back",
    )(role, a, dq, dk, dv, w_in)

    from_pair = lax.ppermute(da_win, "seq", pairs).astype(F32)
    from_second = jnp.where(half == 0, from_pair[:, :win], 0.0)
    edge = from_pair[:, win:]
    gap = jnp.zeros((micro, rows - HALO, width), F32)
    edges = jnp.where(
        half == 0, jnp.concatenate([gap, edge], axis=1), jnp.concatenate([edge, gap], axis=1)
    )
    added = jnp.pad(from_second, ((0, 0), (rows - win, 0), (0, 0)))
    to_clean = (jnp.where(clean == 0, da_main.astype(F32), 0.0) + added).astype(BF16)
    from_noisy = lax.ppermute(to_clean, "seq", [(0, 2), (1, 3)])
    extra = jnp.where(clean == 1, from_noisy.astype(F32) + added, 0.0) + edges

    grad_in, g_attn = call(
        final_kernel, (2,),
        [pl.BlockSpec((total // 2, width), lambda i: (i, 0))] * 4 + [whole((1, width))],
        [pl.BlockSpec((total // 2, width), lambda i: (i, 0)), whole((8, width))],
        [like((total, width), F32), like((8, width), F32)], [], 0, 16 << 20, "norm_back",
    )(flat(inputs), flat(da_own), flat(extra), flat(dx2), vec[0:1, :width])

    def scatter(g):
        return lax.psum(lax.psum_scatter(g, "fsdp", scatter_dimension=0, tiled=True), "seq")

    big = [scatter(g).astype(F32) for g in (g_w_in, g_w_out, g_w_up, g_w_down)]
    smalls = [g_attn[0], g_attn[1], g_b_in[0], g_mlp[3], g_mlp[1], g_mlp[2], g_b_up[0], g_mlp[0]]
    pack = jnp.concatenate([g.reshape(fsdp_n, -1) for g in smalls], axis=1)
    pack = lax.psum(pack, ("seq", "fsdp"))
    mine = lax.dynamic_slice_in_dim(pack, lax.axis_index("fsdp"), 1, 0)[0]
    outs, at = [], 0
    for size in sizes:
        outs.append(mine[at : at + size])
        at += size
    return out_rows.reshape(micro, rows, width), grad_in.reshape(micro, rows, width), big, outs


def per_device(
    inputs, segment_ids, block_ids, attn_gain, attn_shift, proj_in, bias_in, proj_out, bias_out,
    mlp_gain, mlp_shift, weight_up, bias_up, weight_down, bias_down, cotangent,
):
    micro, rows, width = inputs.shape
    length = segment_ids.shape[1]
    hidden = weight_up.shape[1]
    seq_n = lax.axis_size("seq")
    fsdp_n = lax.axis_size("fsdp")
    assert seq_n == 4 and seq_n * rows == 2 * length
    lay = layout(rows, length)
    win, keys = lay["win"], lay["keys"]
    me = lax.axis_index("seq")
    clean = me // 2
    half = me % 2
    role = jnp.stack([clean, half]).astype(jnp.int32)
    pairs = [(0, 1), (1, 0), (2, 3), (3, 2)]
    small = (attn_gain, attn_shift, bias_in, bias_out, mlp_gain, mlp_shift, bias_up, bias_down)
    sizes = [p.shape[0] for p in small]
    weights = (proj_in, proj_out, weight_up, weight_down)
    half_dim = HD // 2
    freqs = (10000.0 ** (-(np.arange(half_dim, dtype=np.float32) / half_dim))).astype(np.float32)
    freqs = np.tile(freqs, 4)[None]
    quads = width // (QUAD * HD)
    qw = QUAD * HD
    spans = [hi - lo + NEAR for lo, hi in windows(lay)]
    bias_scratch = [pltpu.VMEM((rows // TILE, max(spans), TILE), F32)]
    per_seq = lambda n, d: pl.BlockSpec((1, n, d), lambda s: (s, 0, 0))
    role_spec = SMEM()
    attn_flops = micro * quads * sum(spans) * QUAD * TILE * qw * 2
    lse_shape = (micro * quads, rows // TILE, QUAD * TILE)
    table_rows = win + rows + HALO
    aligned = fsdp_n & (fsdp_n - 1) == 0 and all(p.shape[0] % (4 * HALO) in (0, 32) for p in weights)
    front = front_remote if aligned else front_native
    (w_in, w_out, w_up, w_down, q, k, v, a, o, lse, vec, cos, sin, codes, queries) = front(
        lay, role, sizes, inputs, segment_ids, block_ids, small, weights, freqs,
        lse_shape, bias_scratch, spans, attn_flops,
    )
    back = back_remote if aligned else back_native
    out_rows, grad_in, big, vectors = back(
        lay, role, sizes, inputs, cotangent, codes, queries, lse, cos, sin, vec,
        q, k, v, o, a, w_in, w_out, w_up, w_down, bias_scratch, attn_flops,
    )
    g_gain1, g_shift1, g_bin, g_bout, g_gain2, g_shift2, g_bup, g_bdown = vectors
    return (
        out_rows, grad_in, g_gain1, g_shift1, big[0], g_bin, big[1], g_bout,
        g_gain2, g_shift2, big[2], g_bup, big[3], g_bdown,
    )


def solution(mesh):
    rows = P("fsdp", "seq", None)
    one, two = P("fsdp"), P("fsdp", None)
    params = (one, one, two, one, two, one, one, one, two, one, two, one)
    return jax.shard_map(
        per_device,
        mesh=mesh,
        in_specs=(rows, two, two) + params + (rows,),
        out_specs=(rows, rows) + params,
        check_vma=False,
    )
```

```python
import functools
import itertools

import jax
import jax.numpy as jnp
import numpy as np
from jax import lax
from jax.experimental import pallas as pl
from jax.experimental.pallas import tpu as pltpu
from jax.sharding import PartitionSpec as P

HD = 64
QUAD = 4
TILE = 128
HALO = 16
NEAR = TILE + 2 * HALO
EPS = 1e-05
MASKED = -1e30
SEG_STEP = 4096
F32 = jnp.float32
BF16 = jnp.bfloat16
VMEM_BYTES = 62 * 1024 * 1024
MESH = pl.DeviceIdType.MESH
ANY = pl.BlockSpec(memory_space=pl.ANY)
VMEM = pl.BlockSpec(memory_space=pltpu.VMEM)


def dot(a, b):
    return jnp.dot(a, b, preferred_element_type=F32)


def dot_nt(a, b):
    return lax.dot_general(a, b, (((1,), (1,)), ((), ())), preferred_element_type=F32)


def dot_tn(a, b):
    return lax.dot_general(a, b, (((0,), (0,)), ((), ())), preferred_element_type=F32)


def norm_stats(x):
    center = jnp.mean(x, axis=-1, keepdims=True)
    centered = x - center
    inverse = lax.rsqrt(jnp.mean(centered * centered, axis=-1, keepdims=True) + EPS)
    return centered * inverse, inverse


def norm_back(grad, normed, inverse, gain):
    scaled = grad * gain
    first = jnp.mean(scaled, axis=-1, keepdims=True)
    second = jnp.mean(scaled * normed, axis=-1, keepdims=True)
    return inverse * (scaled - first - normed * second)


def partner(u):
    lane = lax.broadcasted_iota(jnp.int32, u.shape, 1)
    half = HD // 2
    return jnp.where(
        lane % HD < half, pltpu.roll(u, u.shape[1] - half, 1), pltpu.roll(u, half, 1)
    )


def whole(shape):
    return pl.BlockSpec(shape, lambda *_: (0,) * len(shape), pipeline_mode=pl.Buffered(1))


def call(kernel, grid, in_specs, out_specs, out_shape, scratch, flops, nbytes, name):
    return pl.pallas_call(
        kernel,
        grid=grid,
        in_specs=in_specs,
        out_specs=out_specs,
        out_shape=out_shape,
        scratch_shapes=scratch,
        compiler_params=pltpu.CompilerParams(vmem_limit_bytes=VMEM_BYTES),
        cost_estimate=pl.CostEstimate(flops=flops, bytes_accessed=nbytes, transcendentals=0),
        name=name,
    )


def like(shape, dtype):
    return jax.ShapeDtypeStruct(shape, dtype)


SMEM = functools.partial(pl.BlockSpec, memory_space=pltpu.SMEM)


def layout(rows, length):
    win = rows - length // 8
    noisy = win + rows + HALO
    used = noisy + rows + 2 * HALO
    return dict(rows=rows, win=win, length=length, noisy=noisy, used=used, keys=-(-used // 256) * 256)


def places(lay, role):
    noisy = role[0] == 0
    second = role[1] == 1
    own_at = jnp.where(noisy, lay["noisy"] + HALO, lay["win"])
    halo_at = jnp.where(
        second,
        lay["noisy"],
        jnp.where(noisy, lay["noisy"] + HALO + lay["rows"], lay["win"] + lay["rows"]),
    )
    return noisy, second, pl.multiple_of(own_at, HALO), pl.multiple_of(halo_at, HALO)


def qkv_rows(lay, where_am, n, x, xb, xc, w, b, gain, shift, cos, sin, q_out, k_out, v_out, a_out):
    width = x.shape[2]
    rows, win = lay["rows"], lay["win"]
    noisy, second, own_at, halo_at = where_am

    def norm(v):
        normed, _ = norm_stats(v.astype(F32))
        return (normed * gain + shift).astype(BF16)

    def zeros(at, count):
        for ref in (k_out, v_out, a_out):
            ref[n, at : at + count, :] = jnp.zeros((count, width), BF16)

    def section(a, parts, table, want_q):
        def put(ref, col, value):
            for begin, count, at in parts:
                ref[n, pl.ds(at, count), col : col + value.shape[1]] = value[begin : begin + count]

        put(a_out, 0, a)
        c = cos[table : table + a.shape[0], :]
        s = sin[table : table + a.shape[0], :]
        first = 0 if want_q else width
        for col in range(first, 3 * width, 256):
            part = dot(a, w[:, col : col + 256]) + b[:, col : col + 256]
            for piece in range(2):
                u = part[:, piece * 128 : piece * 128 + 128]
                at_col = col + piece * 128
                if at_col < 2 * width:
                    u = u * c + partner(u) * s
                if at_col < width:
                    q_out[n, :, at_col : at_col + 128] = (u[:rows] * (HD**-0.5)).astype(BF16)
                elif at_col < 2 * width:
                    put(k_out, at_col - width, u.astype(BF16))
                else:
                    put(v_out, at_col - 2 * width, u.astype(BF16))

    zeros(win + rows, 2 * HALO)
    zeros(lay["used"] - HALO, lay["keys"] - lay["used"] + HALO)
    own = jnp.concatenate([norm(x[n]), norm(xc[n, win:, :])], axis=0)
    section(own, ((0, rows, own_at), (rows, HALO, halo_at)), win, True)

    @pl.when(noisy)
    def _():
        section(norm(xb[n]), ((0, rows, win),), win, False)

    @pl.when(jnp.logical_not(noisy))
    def _():
        zeros(lay["noisy"] + HALO, rows)

    @pl.when(second)
    def _():
        section(norm(xc[n, :win, :]), ((0, win, 0),), 0, False)

    @pl.when(jnp.logical_not(second))
    def _():
        zeros(0, win)


def qkv_columns(lay, n, act, at_parts, table, col, count, w, b, cos, sin, q, k, v):
    width, rows = q.shape[2], lay["rows"]

    def put(ref, at_col, value):
        for begin, size, at in at_parts:
            ref[n, pl.ds(at, size), at_col : at_col + 128] = value[begin : begin + size].astype(BF16)

    c = cos[table : table + act.shape[0], :]
    s = sin[table : table + act.shape[0], :]
    part = dot(act, w[:, col : col + count]) + b[:, col : col + count]
    for at_col in range(col, col + count, 128):
        u = part[:, at_col - col : at_col - col + 128]
        if at_col < 2 * width:
            u = u * c + partner(u) * s
        if at_col < width:
            q[n, :, at_col : at_col + 128] = (u[:rows] * (HD**-0.5)).astype(BF16)
        elif at_col < 2 * width:
            put(k, at_col - width, u)
        else:
            put(v, at_col - 2 * width, u)


def qkv_kernel(lay, role, x, xb, xc, w, vec, cos, sin, *outs):
    width = x.shape[2]
    gain, shift, b = vec[0:1, :width], vec[1:2, :width], vec[2:3, : 3 * width]
    qkv_rows(lay, places(lay, role), 0, x, xb, xc, w, b, gain, shift, cos, sin, *outs)


def windows(lay):
    rows, win, length = lay["rows"], lay["win"], lay["length"]
    longest, earliest, latest = length // 2, length // 8, 3 * length // 8
    found = []
    for at in range(0, rows, TILE):
        begin = win + rows
        for origin in range(0, length, rows):
            pos = origin + at
            low = max(pos - longest, 0)
            if origin > 0:
                low = max(low, earliest)
            if pos >= latest + longest:
                low = max(low, earliest + longest)
            begin = min(begin, low - origin + win)
        found.append((begin // TILE * TILE, win + at + TILE + HALO))
    return found


def tile_loop(lay, body):
    for t, (lo, hi) in enumerate(windows(lay)):
        near = lay["noisy"] + t * TILE
        body(t, slice(t * TILE, t * TILE + TILE), slice(lo, hi), slice(near, near + NEAR), hi - lo)


def make_bias(lay, n, codes, queries, biases):
    (bias,) = biases
    groups = {}
    for t, (lo, hi) in enumerate(windows(lay)):
        groups.setdefault(hi - lo, []).append((t, lo))
    for size, tiles in groups.items():
        (t0, lo0), (t1, lo1), number = tiles[0], tiles[-1], len(tiles)
        apart = max(number - 1, 1)
        assert all(tile == (t0 + k * (t1 - t0) // apart, lo0 + k * (lo1 - lo0) // apart) for k, tile in enumerate(tiles))

        def step(k, carry, size=size, t0=t0, lo0=lo0, dt=(t1 - t0) // apart, dlo=(lo1 - lo0) // apart):
            t = t0 + k * dt
            here = pl.ds(pl.multiple_of(t * TILE, TILE), TILE)
            low, high, same = (queries[n, r : r + 1, here] for r in range(3))
            kc = codes[n, pl.ds(pl.multiple_of(lo0 + k * dlo, HALO), size), :]
            ok = jnp.logical_and(kc >= low, kc <= high)
            bias[t, :size, :] = jnp.where(ok, 0.0, MASKED)
            kn = codes[n, pl.ds(pl.multiple_of(lay["noisy"] + t * TILE, HALO), NEAR), :]
            bias[t, size : size + NEAR, :] = jnp.where(kn == same, 0.0, MASKED)
            return carry

        lax.fori_loop(0, number, step, 0)


def stacked(tile):
    lane = lax.broadcasted_iota(jnp.int32, tile.shape, 1)
    zero = jnp.zeros_like(tile)
    return jnp.concatenate(
        [jnp.where(lane // HD == h, tile, zero) for h in range(QUAD)], axis=0
    )


def own_heads(wide):
    return jnp.concatenate(
        [wide[h * HD : h * HD + HD, h * TILE : h * TILE + TILE] for h in range(QUAD)], axis=0
    )


def keys_of(ref, n, cols, lo, near):
    return jnp.concatenate([ref[n, lo, cols], ref[n, near, cols]], axis=0)


def attend(lay, n, cols, q, k, v, o_out, lse_out, lse_at, biases):
    (bias,) = biases

    def body(t, here, lo, near, size):
        qm = stacked(q[n, here, cols])
        kk = keys_of(k, n, cols, lo, near)
        vv = keys_of(v, n, cols, lo, near)
        s = dot_nt(kk, qm) + jnp.concatenate([bias[t, : size + NEAR, :]] * QUAD, axis=1)
        peak = jnp.max(s, axis=0, keepdims=True)
        p = jnp.exp(s - peak)
        total = jnp.sum(p, axis=0, keepdims=True)
        wide = dot_tn(vv, p.astype(BF16)) * (1.0 / total)
        o_out[n, here, cols] = jnp.transpose(own_heads(wide)).astype(BF16)
        lse_out[lse_at, t : t + 1, :] = peak + jnp.log(total)

    tile_loop(lay, body)


def attend_kernel(lay, codes, queries, q, k, v, o_out, lse_out, *biases):
    @pl.when(pl.program_id(1) == 0)
    def _():
        make_bias(lay, 0, codes, queries, biases)

    attend(lay, 0, slice(None), q, k, v, o_out, lse_out, 0, biases)


def attend_back(
    lay, n, cols, q, k, v, m, cols_m, o, do, lse, lse_at, cos, sin, to, col, dq_out, dk_out, dv_out, dk_acc, dv_acc, biases,
):
    rows, win = lay["rows"], lay["win"]
    qw = QUAD * HD

    def lanes(piece):
        return pl.ds(pl.multiple_of(col + piece * 128, 128), 128)

    dk_acc[...] = jnp.zeros_like(dk_acc)
    dv_acc[...] = jnp.zeros_like(dv_acc)
    (bias,) = biases

    def body(t, here, lo, near, size):
        qm = stacked(q[n, here, cols])
        dom = stacked(do[m, here, cols_m])
        kk = keys_of(k, n, cols, lo, near)
        vv = keys_of(v, n, cols, lo, near)
        both = jnp.transpose(do[m, here, cols_m].astype(F32) * o[m, here, cols_m].astype(F32))
        delta = jnp.concatenate(
            [jnp.sum(both[h * HD : h * HD + HD, :], axis=0, keepdims=True) for h in range(QUAD)],
            axis=1,
        )
        s = dot_nt(kk, qm) + jnp.concatenate([bias[t, : size + NEAR, :]] * QUAD, axis=1)
        p = jnp.exp(s - lse[lse_at, t : t + 1, :])
        dp = dot_nt(vv, dom)
        ds = (p * (dp - delta)).astype(BF16)
        pb = p.astype(BF16)
        dv = dot(pb, dom)
        dk = dot(ds, qm)
        dv_acc[lo, :] += dv[:size]
        dk_acc[lo, :] += dk[:size]
        dv_acc[near, :] += dv[size:]
        dk_acc[near, :] += dk[size:]
        wide = dot_tn(kk, ds)
        dq = jnp.transpose(own_heads(wide)) * (HD**-0.5)
        turn = slice(win + t * TILE, win + t * TILE + TILE)
        c, sn = cos[turn, :], sin[turn, :]
        for piece in range(2):
            u = dq[:, piece * 128 : piece * 128 + 128]
            dq_out[to, here, lanes(piece)] = (u * c - partner(u) * sn).astype(BF16)

    tile_loop(lay, body)
    for piece in range(2):
        dv_out[to, :, lanes(piece)] = dv_acc[:, piece * 128 : piece * 128 + 128].astype(BF16)
    half = (cos[win + rows :, :], sin[win + rows :, :])
    own = (cos[win : win + rows, :], sin[win : win + rows, :])
    tables = (
        (0, (cos[: win + rows, :], sin[: win + rows, :])),
        (win + rows, half),
        (lay["noisy"], half),
        (lay["noisy"] + HALO, own),
        (lay["used"] - HALO, half),
    )
    for at, (c, sn) in tables:
        here = slice(at, at + c.shape[0])
        for piece in range(2):
            u = dk_acc[here, piece * 128 : piece * 128 + 128]
            dk_out[to, here, lanes(piece)] = (u * c - partner(u) * sn).astype(BF16)
    spare = lay["keys"] - lay["used"]
    for piece in range(2):
        dk_out[to, lay["used"] :, lanes(piece)] = jnp.zeros((spare, 128), BF16)


def attend_back_kernel(
    lay, codes, queries, q, k, v, o, do, lse, cos, sin, dq_out, dk_out, dv_out, dk_acc, dv_acc, *biases
):
    @pl.when(pl.program_id(1) == 0)
    def _():
        make_bias(lay, 0, codes, queries, biases)

    attend_back(
        lay, 0, slice(None), q, k, v, 0, slice(None), o, do, lse, 0, cos, sin, 0, 0, dq_out, dk_out, dv_out, dk_acc, dv_acc, biases
    )


def bit_of(index, b):
    return (index // (1 << b)) % 2


def other(index, b):
    return index + (1 << b) * (1 - 2 * bit_of(index, b))


class Net:
    def __init__(self, bits, send, recv, sems):
        self.me, self.f, self.bits = lax.axis_index("seq"), lax.axis_index("fsdp"), bits
        self.core, self.x = self.me % 2, self.me // 2
        self.send, self.recv, self.sems = send, recv, sems
        self.used, self.local_used = 0, 0
        self.started = []

    def partners(self):
        return [{"seq": other(self.me, 0)}, {"seq": other(self.me, 1)}] + [
            {"fsdp": other(self.f, b)} for b in range(self.bits)
        ]

    def barrier(self):
        barrier = pltpu.get_barrier_semaphore()
        for device in self.partners():
            pl.semaphore_signal(barrier, inc=1, device_id=device, device_id_type=MESH)
        pl.semaphore_wait(barrier, 2 + self.bits)

    def copy(self, src, dst, device):
        n = self.used
        self.used += 1
        return pltpu.make_async_remote_copy(
            src_ref=src, dst_ref=dst, send_sem=self.send.at[n], recv_sem=self.recv.at[n],
            device_id=device, device_id_type=MESH,
        )

    def local(self, src, dst):
        n = self.local_used
        self.local_used += 1
        return pltpu.make_async_copy(src, dst, self.sems.at[n])

    def fsdp_index(self, done):
        return tuple(slice(None) if b in done else bit_of(self.f, b) for b in range(self.bits - 1, -1, -1))


FRONT_ORDER = (
    "E s i0 i1",
    "T s R0 i2",
    "i0 i1 i2 i0",
    "u0 s i1 s",
    "u1 i2 o i1",
    "V u0 i0 R1",
    "u1 i1 i2 i0",
    "o d0 P0 L0",
    "L1 W H i2",
    "u0 L2 u1 O0",
    "O1 O2 d1 u0",
    "o d0 A d1",
    "P1 d0 u1 A",
    "A d1 o u0",
    "A u0 d0 u1",
    "A d1 d0 A",
    "o u1",
)
FRONT_BITS = {
    "i0": ((2, 0, 1), False),
    "i1": ((2, 1, 0), False),
    "i2": ((2, 1, 0), False),
    "o": ((2, 1, 0), False),
    "u0": ((2, 1, 0), True),
    "u1": ((2, 0, 1), True),
    "d0": ((2, 1, 0), False),
    "d1": ((0, 2, 1), False),
}


class Gather:
    def __init__(self, net, own, full, tail, tail_x=None, tail_core=None, order=None):
        self.net, self.at = net, 0
        mine = net.fsdp_index(())
        self.own = net.local(own.at[tail], full.at[mine + tail])
        self.stages = []
        done = []
        for b in order if order is not None and len(order) == net.bits else range(net.bits - 1, -1, -1):
            here = full.at[net.fsdp_index(done) + tail]
            src = here if done else own.at[tail]
            self.stages.append(net.copy(src, here, {"fsdp": other(net.f, b)}))
            done.append(b)
        everything = (slice(None),) * net.bits
        for region, b in ((tail_x, 1), (tail_core, 0)):
            if region is not None:
                here = full.at[everything + region]
                self.stages.append(net.copy(here, here, {"seq": other(net.me, b)}))

    def advance(self):
        if self.at > len(self.stages):
            return
        if self.at == 0:
            self.own.start()
        else:
            self.stages[self.at - 1].wait_recv()
        if self.at == 1:
            self.own.wait()
        if self.at < len(self.stages):
            self.stages[self.at].start()
        self.at += 1

    def finish(self):
        for stage in self.stages:
            stage.wait_send()


def front_kernel(
    lay, bits, sizes, x, seg, blk, freqs, w_in_s, w_out_s, w_up_s, w_down_s,
    small0, small1, small2, small3, small4, small5, small6, small7,
    w_in, w_out, w_up, w_down, q_out, k_out, v_out, a_out, o_out, lse_out, vec, cos, sin, codes, queries,
    xb, xc, w_vm, q, k, v, a, o, lse, packs, pack, send, recv, sems, *biases,
):
    rows, win, length = lay["rows"], lay["win"], lay["length"]
    width = x.shape[2]
    hidden = w_up_s.shape[1]
    micro = x.shape[0]
    net = Net(bits, send, recv, sems)
    role = (net.x, net.core)
    noisy, second, own_at, halo_at = places(lay, role)
    first = jnp.logical_not(second)
    clean = jnp.logical_not(noisy)
    net.barrier()

    pair, across = {"seq": other(net.me, 0)}, {"seq": other(net.me, 1)}
    rows_across = [net.copy(x.at[n], xb.at[n], across) for n in range(micro)]
    window = (pl.ds(rows - win, win), slice(None))
    target = (pl.ds(0, win), slice(None))
    rows_pair, rows_pair_b = [], []
    for n in range(micro):
        at = net.used
        rows_pair.append(net.copy(x.at[(n,) + window], xc.at[(n,) + target], pair))
        net.used = at
        rows_pair_b.append(net.copy(xb.at[(n,) + window], xc.at[(n,) + target], pair))
    edge_at = pl.multiple_of((1 - net.core) * (rows - HALO), HALO)
    edge = net.copy(x.at[:, pl.ds(edge_at, HALO), :], xc.at[:, pl.ds(win, HALO), :], pair)

    def columns(begin, size):
        return (slice(None), pl.ds(pl.multiple_of(begin, 128), size))

    pack[...] = jnp.zeros_like(pack)
    smalls = (small0, small1, small2, small3, small4, small5, small6, small7)
    for r, (ref, size) in enumerate(zip(smalls, sizes)):
        pack[r : r + 1, :size] = ref[...].astype(F32).reshape(1, size)
    chunks = {"s": Gather(net, pack, packs, (slice(None), slice(None)))}
    half_in, half_out, half_up = 3 * width // 2, width // 2, hidden // 2
    third = half_in // 3
    for n in range(3):
        region = columns(net.core * half_in + n * third, third)
        chunks["i%d" % n] = Gather(net, w_in_s, w_in, region, None, region, FRONT_BITS["i%d" % n][0])
    region = columns(net.core * half_out, half_out)
    chunks["o"] = Gather(net, w_out_s, w_out, region, None, region, FRONT_BITS["o"][0])
    quarter = half_up // 2
    slab = w_down_s.shape[0]
    for n in range(2):
        order, over_x = FRONT_BITS["u%d" % n]
        region = columns(net.core * half_up + n * quarter, quarter)
        part = columns(net.core * half_up + n * quarter + net.x * (quarter // 2), quarter // 2) if over_x else region
        chunks["u%d" % n] = Gather(net, w_up_s, w_up, part, part if over_x else None, region, order)
        order, over_x = FRONT_BITS["d%d" % n]
        begin = net.core * (slab // 2) + n * (slab // 4)
        region = (pl.ds(pl.multiple_of(begin, HALO), slab // 4), slice(None))
        half_region = (pl.ds(pl.multiple_of(begin + net.x * (slab // 8), HALO), slab // 8), slice(None))
        part = half_region if over_x else region
        chunks["d%d" % n] = Gather(net, w_down_s, w_down, part, part if over_x else None, region, order)

    def rows_start(n):
        @pl.when(clean)
        def _():
            rows_across[n].start()

    count = 1 << bits

    def tables():
        block = 48
        assert (win + rows + HALO) % block == 0

        def table_step(n, carry):
            span = pl.ds(pl.multiple_of(n * block, HALO), block)
            position = lax.broadcasted_iota(jnp.int32, (block, 128), 0) + n * block
            shifted = jnp.where(
                position < win + rows, position - win, position - win - rows + jnp.where(second, -HALO, rows)
            )
            turned = (shifted + jnp.where(second, rows, 0)).astype(F32) * freqs[...]
            lane = lax.broadcasted_iota(jnp.int32, (block, 128), 1)
            cos[span, :] = jnp.cos(turned)
            sine = jnp.sin(turned)
            sin[span, :] = jnp.where(lane % HD < HD // 2, -sine, sine)
            return carry

        lax.fori_loop(0, (win + rows + HALO) // block, table_step, 0)
        code = (seg[...] * SEG_STEP + blk[...]).astype(F32)
        base = (seg[...] * SEG_STEP).astype(F32)
        turned_code = jnp.transpose(jnp.concatenate([code, jnp.zeros((8 - micro, length), F32)], axis=0))
        lay_noisy = lay["noisy"]
        for n in range(micro):
            col = turned_code[:, n : n + 1]
            none = lambda count, value: jnp.full((count, 1), value, F32)
            codes[n, :win, :] = jnp.where(second, col[rows - win : rows], -1.0)
            codes[n, win : win + rows, :] = jnp.where(second, col[rows:], col[:rows])
            after, before = col[rows : rows + HALO], col[rows - HALO : rows]
            codes[n, win + rows : lay_noisy, :] = jnp.where(jnp.logical_and(clean, first), after, -1.0)
            codes[n, lay_noisy : lay_noisy + HALO, :] = jnp.where(jnp.logical_and(noisy, second), before, -2.0)
            codes[n, lay_noisy + HALO : lay_noisy + HALO + rows, :] = jnp.where(
                noisy, jnp.where(second, col[rows:], col[:rows]), -2.0
            )
            codes[n, lay["used"] - HALO : lay["used"], :] = jnp.where(jnp.logical_and(noisy, first), after, -2.0)
            codes[n, lay["used"] :, :] = none(lay["keys"] - lay["used"], -2.0)
            own_code = jnp.where(second, code[n : n + 1, rows:], code[n : n + 1, :rows])
            own_base = jnp.where(second, base[n : n + 1, rows:], base[n : n + 1, :rows])
            high = own_code - jnp.where(noisy, 1.0, 0.0)
            queries[n] = jnp.concatenate([own_base, high, own_code, jnp.zeros((5, rows), F32)], axis=0)

    def vectors():
        kinds = sorted(set(sizes))

        def spread_step(n, totals):
            piece = packs[tuple((n // (1 << b)) % 2 for b in range(bits - 1, -1, -1))]
            added = []
            for size, total in zip(kinds, totals):
                wide = size * count - piece.shape[1]
                padded = jnp.concatenate([piece, jnp.zeros((8, wide), F32)], axis=1) if wide > 0 else piece
                lanes = lax.broadcasted_iota(jnp.int32, padded.shape, 1)
                added.append(total + pltpu.roll(jnp.where(lanes < size, padded, 0.0), n * size, 1))
            return tuple(added)

        zero = tuple(jnp.zeros((8, size * count), F32) for size in kinds)
        spread = dict(zip(kinds, lax.fori_loop(0, count, spread_step, zero)))
        for r, size in enumerate(sizes):
            vec[r : r + 1, : size * count] = spread[size][r : r + 1]
            if size * count < vec.shape[1]:
                vec[r : r + 1, size * count :] = jnp.zeros((1, vec.shape[1] - size * count), F32)

    def pass_on(n):
        @pl.when(noisy)
        def _():
            rows_across[n].wait_recv()

        @pl.when(jnp.logical_and(first, noisy))
        def _():
            rows_pair_b[n].start()

        @pl.when(jnp.logical_and(first, clean))
        def _():
            rows_pair[n].start()

    loads = {}

    def load_weights(j):
        slab_in = w_in_s.shape[0]
        for n in range(count):
            at = tuple((n >> b) & 1 for b in range(bits - 1, -1, -1))
            for block in range(2):
                cols = slice(block * half_in + j * third, block * half_in + (j + 1) * third)
                copy = net.local(w_in.at[at + (slice(None), cols)], w_vm.at[n * slab_in : (n + 1) * slab_in, cols])
                copy.start()
                loads.setdefault(j, []).append(copy)

    def norm(value):
        normed, _ = norm_stats(value.astype(F32))
        return (normed * vec[0:1, :width] + vec[1:2, :width]).astype(BF16)

    def zeros(n, at, size):
        for ref in (k, v, a):
            ref[n, at : at + size, :] = jnp.zeros((size, width), BF16)

    def norms():
        def step(n, carry):
            zeros(n, win + rows, 2 * HALO)
            zeros(n, lay["used"] - HALO, lay["keys"] - lay["used"] + HALO)

            @pl.when(clean)
            def _():
                zeros(n, lay["noisy"] + HALO, rows)

            @pl.when(first)
            def _():
                zeros(n, 0, win)

            a[n, pl.ds(own_at, rows), :] = norm(x[n])
            a[n, pl.ds(halo_at, HALO), :] = norm(xc[n, win:, :])
            return carry

        lax.fori_loop(0, micro, step, 0)

    def own_rows(j):
        for load in loads[j]:
            load.wait()

        def step(n, carry):
            act = jnp.concatenate([a[n, pl.ds(own_at, rows), :], a[n, pl.ds(halo_at, HALO), :]], axis=0)
            for block in range(2):
                qkv_columns(
                    lay, n, act, ((0, rows, own_at), (rows, HALO, halo_at)), win, block * half_in + j * third, third,
                    w_vm, vec[2:3, : 3 * width], cos, sin, q, k, v,
                )
            return carry

        lax.fori_loop(0, micro, step, 0)

    def key_rows(n):
        def section(value, at):
            a[n, at : at + value.shape[0], :] = act = norm(value)
            for col in range(width, 3 * width, 384):
                qkv_columns(
                    lay, n, act, ((0, value.shape[0], at),), at, col, 384, w_vm, vec[2:3, : 3 * width], cos, sin, q, k, v
                )

        @pl.when(noisy)
        def _():
            section(xb[n], win)

        @pl.when(second)
        def _():
            for m in range(micro):

                @pl.when(n == m)
                def _(m=m):
                    rows_pair[m].wait_recv()

            section(xc[n, :win, :], 0)

        for store in stores_of(n):
            store.start()

    first_store = net.local_used
    net.local_used += 4 * micro

    def stores_of(n):
        return [
            pltpu.make_async_copy(here.at[n], there.at[n], sems.at[first_store + 4 * n + m])
            for m, (here, there) in enumerate(((q, q_out), (k, k_out), (v, v_out), (a, a_out)))
        ]

    def serve(token):
        if token in chunks:
            chunks[token].advance()
        elif len(token) == 2:
            {"R": rows_start, "P": pass_on, "L": load_weights, "O": own_rows}[token[0]](int(token[1]))
        else:
            {"E": edge.start, "W": edge.wait_recv, "T": tables, "V": vectors, "H": norms}[token]()

    ahead, *after = [part.split() for part in " ".join(FRONT_ORDER).split("A")]
    for token in ahead:
        serve(token)

    quads = width // (QUAD * HD)
    assert micro * quads == len(after)

    def step(index, carry):
        n, h = index // quads, index % quads

        @pl.when(h == 0)
        def _():
            key_rows(n)
            make_bias(lay, n, codes, queries, biases)

        cols = pl.ds(pl.multiple_of(h * QUAD * HD, QUAD * HD), QUAD * HD)
        def serve_all():
            for at, tokens in enumerate(after):
                if tokens:

                    @pl.when(index == at)
                    def _(tokens=tokens):
                        for token in tokens:
                            serve(token)

        attend(lay, n, cols, q, k, v, o, lse, index, biases)
        serve_all()
        return carry

    lax.fori_loop(0, micro * quads, step, 0)
    last = [net.local(o, o_out), net.local(lse, lse_out)]
    for store in last:
        store.start()
    while any(chunk.at <= len(chunk.stages) for chunk in chunks.values()):
        for chunk in chunks.values():
            chunk.advance()
    for chunk in chunks.values():
        chunk.finish()
    for store in stores_of(0) + stores_of(1) + last:
        store.wait()
    edge.wait_send()

    @pl.when(clean)
    def _():
        for n in range(micro):
            rows_across[n].wait_send()

    @pl.when(first)
    def _():
        for n in range(micro):
            rows_pair[n].wait_send()


def gelu_both(u):
    scale = 0.7978845608028654
    square = u * u
    inner = scale * u * (1.0 + 0.044715 * square)
    th = jnp.tanh(inner)
    plus = 0.5 * (1.0 + th)
    slope = plus + 0.5 * u * (1.0 - th * th) * (scale * (1.0 + 3 * 0.044715 * square))
    return (u * plus).astype(BF16), slope


def mlp_kernel(
    o, x, dy, w_out, vec, w_up, b_up, w_down,
    out_rows, dx2_out, do_out, g_w_out, g_w_up, g_b_up, g_w_down, g_vec,
    mid, a2, a2t, inv, acc_out, acc_da,
):
    step = pl.program_id(0)
    last = pl.num_programs(0) - 1
    width = x.shape[1]
    b_out, gain, shift, b_down = (vec[r : r + 1, :width] for r in (3, 4, 5, 7))

    @pl.when(step == 0)
    def _():
        value = x[...].astype(F32) + dot(o[...], w_out[...]) + b_out
        mid[...] = value
        normed, inverse = norm_stats(value)
        inv[...] = inverse
        a = (normed * gain + shift).astype(BF16)
        a2[...] = a
        a2t[...] = jnp.transpose(a)
        acc_out[...] = jnp.zeros_like(acc_out)
        acc_da[...] = jnp.zeros_like(acc_da)

    g, slope = gelu_both(dot(a2[...], w_up[...]) + b_up[6:7, :])
    acc_out[...] += dot(g, w_down[...])
    du32 = dot_nt(dy[...], w_down[...]) * slope
    du = du32.astype(BF16)
    g_b_up[...] = jnp.broadcast_to(jnp.sum(du.astype(F32), axis=0, keepdims=True), g_b_up.shape)
    acc_da[...] += dot_nt(du, w_up[...])
    g_w_down[...] = dot_tn(g, dy[...]).astype(BF16)
    g_w_up[...] = dot(a2t[...], du).astype(BF16)

    @pl.when(step == last)
    def _():
        dyf = dy[...].astype(F32)
        out_rows[...] = (mid[...] + acc_out[...] + b_down).astype(BF16)
        inverse = inv[...]
        value = mid[...]
        normed = (value - jnp.mean(value, axis=-1, keepdims=True)) * inverse
        da = acc_da[...]
        dx2 = dyf + norm_back(da, normed, inverse, gain)
        dx2_out[...] = dx2
        dp = dx2.astype(BF16)
        do_out[...] = dot_nt(dp, w_out[...]).astype(BF16)
        g_w_out[...] = dot_tn(o[...], dp).astype(BF16)
        g_vec[...] = jnp.concatenate(
            [
                jnp.sum(dyf, axis=0, keepdims=True),
                jnp.sum(da * normed, axis=0, keepdims=True),
                jnp.sum(da, axis=0, keepdims=True),
                jnp.sum(dp.astype(F32), axis=0, keepdims=True),
                jnp.zeros((4, dyf.shape[1]), F32),
            ],
            axis=0,
        )


def qkv_back_kernel(lay, role, a, dq, dk, dv, w, da_own, da_main, da_win, g_w, g_b, g_acc):
    width = dq.shape[2]
    rows, win = lay["rows"], lay["win"]
    noisy, second, own_at, halo_at = places(lay, role)

    @pl.when(pl.program_id(0) == 0)
    def _():
        g_acc[...] = jnp.zeros_like(g_acc)
        g_b[...] = jnp.zeros_like(g_b)

    def column_sums(col, value):
        g_b[0:1, col : col + width] += jnp.sum(value.astype(F32), axis=0, keepdims=True)

    def section(parts, query):
        def take(ref):
            return jnp.concatenate([ref[0, pl.ds(at, count), :] for at, count in parts], axis=0)

        at_t = jnp.transpose(take(a))
        key = take(dk)
        value = take(dv)
        g_acc[:, width : 2 * width] += dot(at_t, key)
        g_acc[:, 2 * width :] += dot(at_t, value)
        column_sums(width, key)
        column_sums(2 * width, value)
        total = dot_nt(key, w[:, width : 2 * width]) + dot_nt(value, w[:, 2 * width :])
        if query is not None:
            g_acc[:, :width] += dot(at_t[:, : query.shape[0]], query)
            column_sums(0, query)
            first = total[: query.shape[0]] + dot_nt(query, w[:, :width])
            return first, total[query.shape[0] :]
        return total

    own, near = section(((own_at, rows), (halo_at, HALO)), dq[0])
    da_own[0] = own
    da_win[0, win:, :] = near.astype(BF16)

    @pl.when(noisy)
    def _():
        da_main[0] = section(((win, rows),), None).astype(BF16)

    @pl.when(second)
    def _():
        da_win[0, :win, :] = section(((0, win),), None).astype(BF16)

    @pl.when(pl.program_id(0) == pl.num_programs(0) - 1)
    def _():
        g_w[...] = g_acc[...].astype(BF16)


def final_kernel(x, da, extra, dx2, gain, grad_in, g_vec):
    value = x[...].astype(F32)
    normed, inverse = norm_stats(value)
    grad = da[...] + extra[...].astype(F32)
    grad_in[...] = dx2[...] + norm_back(grad, normed, inverse, gain[...])

    @pl.when(pl.program_id(0) == 0)
    def _():
        g_vec[...] = jnp.zeros_like(g_vec)

    g_vec[0:1, :] += jnp.sum(grad * normed, axis=0, keepdims=True)
    g_vec[1:2, :] += jnp.sum(grad, axis=0, keepdims=True)


def add_to(ref, at, value):
    ref[at] = (ref[at].astype(F32) + value.astype(F32)).astype(BF16)


def for_all(bits, body):
    if bits == 0:
        body(())
        return

    def step(n, carry):
        body(tuple((n // (1 << b)) % 2 for b in range(bits - 1, -1, -1)))
        return carry

    lax.fori_loop(0, 1 << bits, step, 0)


BACK_ORDER = (
    "S s S s",
    "u0 d0 S s",
    "d0 S s u1",
    "u0 d1 S s",
    "d1 S s d2",
    "d0 u0 u2 E",
    "o u2 d0 u1",
    "e d2 d1 u0",
    "o X e A",
    "A A u2 u0",
    "d2 A d1 P0",
    "u1 A o A",
    "u2 T e d2",
    "P1 G0 i0 o",
    "G1 i1 Y0 i0",
    "e d2 i1 G2",
    "i2 N i0 d0",
    "o d1 i2 i1",
    "Y1 N e N",
    "d2 N l i0",
    "i2 l l",
)
BACK_BITS = {
    "u0": ((0, 1, 2), True),
    "u1": ((1, 2, 0), False),
    "u2": ((0, 1, 2), False),
    "d0": ((0, 1, 2), False),
    "d1": ((0, 2, 1), False),
    "d2": ((0, 1, 2), False),
    "o": ((0, 1, 2), False),
    "i0": ((1, 2, 0), False),
    "i1": ((0, 1, 2), False),
    "i2": ((0, 1, 2), False),
}


class Reduce:
    def __init__(self, net, acc, recvs, out, rows, cols, order, over_x):
        bits, self.net, self.at, self.sent = net.bits, net, 0, False
        pair, across = {"seq": other(net.me, 0)}, {"seq": other(net.me, 1)}
        recvs = list(recvs)
        part = (slice(None), slice(None))
        begin, size = rows
        tail = tail_half = (pl.ds(begin, size), cols)
        self.acc, self.steps = acc, [None]
        if over_x:
            piece = size // 2
            part = (pl.ds(pl.multiple_of(net.x * piece, HALO), piece), slice(None))
            away = (pl.ds(pl.multiple_of((1 - net.x) * piece, HALO), piece), slice(None))
            tail = (pl.ds(pl.multiple_of(begin + net.x * piece, HALO), piece), cols)
            got_x = recvs.pop(0)

            def add_x():
                for_all(bits, lambda at: add_to(acc, at + part, got_x[at]))

            self.steps.append((net.copy(acc.at[(slice(None),) * bits + away], got_x, across), add_x))
        done = []
        for b in order if len(order) == bits else range(bits):
            got = recvs.pop(0)

            def index(mine, rest, b=b, done=tuple(done)):
                rest = iter(rest)
                return tuple(
                    mine if p == b else bit_of(net.f, p) if p in done else next(rest) for p in range(bits - 1, -1, -1)
                )

            left = bits - 1 - len(done)

            def add_bit(got=got, b=b, index=index, left=left):
                for_all(left, lambda at: add_to(acc, index(bit_of(net.f, b), at) + part, got[at]))

            src = acc.at[index(1 - bit_of(net.f, b), (slice(None),) * left) + part]
            self.steps.append((net.copy(src, got, {"fsdp": other(net.f, b)}), add_bit))
            done.append(b)
        own = tuple(bit_of(net.f, n) for n in range(bits - 1, -1, -1))
        if over_x:
            before = self.steps[-1][1]

            def keep():
                before()
                out[tail] = acc[own + part]

            self.steps[-1] = (self.steps[-1][0], keep)
            self.steps.append((net.copy(out.at[tail], out.at[tail], across), lambda: None))
        else:
            got_last = recvs.pop(0)

            def last():
                out[tail] = (acc[own].astype(F32) + got_last[...].astype(F32)).astype(BF16)

            self.steps.append((net.copy(acc.at[own], got_last, across), last))
        self.steps.append((net.copy(out.at[tail_half], out.at[tail_half], pair), lambda: None))

    def feed(self, theirs, get):
        def mine():
            for_all(self.net.bits, lambda at: add_to(self.acc, at, get(at)))

        self.steps[0] = (self.net.copy(theirs, self.acc, {"seq": other(self.net.me, 0)}), mine)

    def open(self):
        return self.at <= len(self.steps)

    def advance(self):
        if not self.open():
            return
        if self.at > 0:
            copy, then = self.steps[self.at - 1]
            copy.wait_recv()
            then()
        if self.at < len(self.steps):
            self.steps[self.at][0].start()
        self.at += 1

    def finish(self):
        while self.open():
            self.advance()
        for copy, _ in self.steps[1 if self.sent else 0 :]:
            copy.wait_send()


class SumAll:
    def __init__(self, net, value, recvs):
        self.value, self.recvs, self.at = value, recvs, 0
        devices = [{"seq": other(net.me, b)} for b in range(2)]
        devices += [{"fsdp": other(net.f, b)} for b in range(net.bits)]
        self.copies = []
        for n, device in enumerate(devices):
            src = value if n == 0 else recvs.at[len(devices) + n - 1]
            self.copies.append(net.copy(src, recvs.at[n], device))

    def open(self):
        return self.at <= len(self.copies)

    def advance(self):
        count = len(self.copies)
        if not self.open():
            return
        if self.at > 0:
            n = self.at - 1
            self.copies[n].wait_recv()
            held = self.value[...] if n == 0 else self.recvs[count + n - 1]
            self.recvs[count + n] = held + self.recvs[n]
        if self.at < count:
            self.copies[self.at].start()
        self.at += 1

    def finish(self):
        while self.open():
            self.advance()
        for copy in self.copies:
            copy.wait_send()
        return self.recvs[2 * len(self.copies) - 1]


def back_kernel(
    lay, bits, codes, queries, lse, cos, sin, vec, x, o,
    dy, q, k, v, a, w_in, w_out, w_up, w_down,
    out_rows, grad_in, f_in_out, f_out_out, f_up_out, f_down_out, sums_out, late_out,
    do, recv_parts, rwin,
    acc_in, acc_out, acc_up, acc_down, r_in, r_out, r_up, r_down, f_in, f_out, f_up, f_down,
    sums, sums_recv, late, late_recv, send, recv, sems, *biases,
):
    rows, win, keys = lay["rows"], lay["win"], lay["keys"]
    micro, width = x.shape[0], x.shape[2]
    total = micro * rows
    hidden = vec.shape[1]
    qw = QUAD * HD
    quads = width // qw
    net = Net(bits, send, recv, sems)
    where_am = noisy, second, own_at, halo_at = places(lay, (net.x, net.core))
    first, clean = jnp.logical_not(second), jnp.logical_not(noisy)
    gain = vec[0:1, :width]
    net.barrier()
    every = list(itertools.product(range(2), repeat=bits))
    count = len(every)
    pair, across = {"seq": other(net.me, 0)}, {"seq": other(net.me, 1)}
    slab_down = f_down.shape[0]
    steps = slab_down // 128
    share = count // 2
    wide = share * 128
    whole_index = (slice(None),) * bits
    here, there = net.core, 1 - net.core

    def columns(begin, size):
        return (slice(None), pl.ds(pl.multiple_of(begin, 128), size))

    @pl.when(noisy)
    def _():
        recv_parts[...] = jnp.zeros_like(recv_parts)

    sums[...] = jnp.zeros_like(sums)

    def feed_forward(dyv, wu, wd, w_ov, mid, a2, a2t, inv, acc_y, acc_da, gv, duv, gd, gu, gu_out, sem_w, sem_m):
        block = total // 4

        def loads(index):
            j, h = index // 2, index % 2
            slot = index % 2
            copies = []
            for n in range(share):
                at = pl.multiple_of((h * share + n) * slab_down + j * 128, 128)
                part = pl.ds(n * 128, 128)
                copies.append(pltpu.make_async_copy(w_up.at[:, pl.ds(at, 128)], wu.at[slot, :, part], sem_w.at[slot, 2 * n]))
                copies.append(pltpu.make_async_copy(w_down.at[pl.ds(at, 128), :], wd.at[slot, part, :], sem_w.at[slot, 2 * n + 1]))
            return copies

        first_loads = [pltpu.make_async_copy(w_out, w_ov, sem_m.at[0]), pltpu.make_async_copy(dy, dyv, sem_m.at[1])]
        for load in first_loads + loads(0):
            load.start()
        flat = lambda ref: ref[...].reshape(total, width)
        b_out, gain2, shift2, b_down = (vec[r : r + 1, :width] for r in (3, 4, 5, 7))
        first_loads[0].wait()
        def part_rows(n):
            per = rows // block
            return n // per, pl.ds(pl.multiple_of((n % per) * block, block), block)

        def open_step(n, carry):
            span = pl.ds(pl.multiple_of(n * block, block), block)
            m, sub = part_rows(n)
            value = x[m, sub, :].astype(F32) + dot(o[m, sub, :], w_ov[...]) + b_out
            mid[span, :] = value
            normed, inverse = norm_stats(value)
            inv[span, :] = inverse
            act = (normed * gain2 + shift2).astype(BF16)
            a2[span, :] = act
            a2t[:, span] = jnp.transpose(act)
            return carry

        lax.fori_loop(0, total // block, open_step, 0)
        acc_y[...] = jnp.zeros_like(acc_y)
        acc_da[...] = jnp.zeros_like(acc_da)
        first_loads[1].wait()

        away = columns(there * (width // 2), width // 2)
        near = columns(here * (width // 2), width // 2)
        for j in range(steps):
            chunks["u%d" % j].feed(gu.at[j, there], lambda at, j=j: gu[(j, here) + at])
            chunks["d%d" % j].feed(gd.at[(j,) + whole_index + away], lambda at, j=j: gd[(j,) + at + near])

        def serve_all(index, part):
            for at, tokens in enumerate(in_feed):
                if tokens[part]:

                    @pl.when(index == at)
                    def _(tokens=tokens[part]):
                        for token in tokens:
                            chunks[token].advance()

        def step(index, carry):
            j, h = index // 2, index % 2
            slot = index % 2

            @pl.when(index + 1 < 2 * steps)
            def _():
                for load in loads(index + 1):
                    load.start()

            for load in loads(index):
                load.wait()
            at = [pl.ds(pl.multiple_of((h * share + n) * slab_down + j * 128, 128), 128) for n in range(share)]
            bias = jnp.concatenate([vec[6:7, here_at] for here_at in at], axis=1)
            w_u, w_d = wu[slot], wd[slot]

            def rows_step(r, row):
                for sub in range(2):
                    span = pl.ds(pl.multiple_of((2 * r + sub) * block, block), block)
                    g, slope = gelu_both(dot(a2[span, :], w_u) + bias)
                    gv[span, :] = g
                    acc_y[span, :] += dot(g, w_d)
                    du = (dot_nt(dyv[span, :], w_d) * slope).astype(BF16)
                    duv[span, :] = du
                    row += jnp.sum(du.astype(F32), axis=0, keepdims=True)
                    acc_da[span, :] += dot_nt(du, w_u)
                return row

            row = lax.fori_loop(0, total // (2 * block), rows_step, jnp.zeros((1, wide), F32))
            for n in range(share):
                sums[6:7, at[n]] = row[:, n * 128 : n * 128 + 128]
            serve_all(index, 0)
            slab = width // count

            def half_step(m, carry):
                part = pl.ds(pl.multiple_of(m * (wide // 2), 128), wide // 2)
                g_d = dot_tn(gv[:, part], dyv[...]).astype(BF16)
                for n, low in enumerate(itertools.product(range(2), repeat=bits - 2)):
                    gd[(j, h, m) + low] = g_d[n * 128 : n * 128 + 128]
                g_u = dot(a2t[pl.ds(pl.multiple_of(m * (width // 2), 128), width // 2), :], duv[...]).astype(BF16)
                for n, low in enumerate(itertools.product(range(2), repeat=bits - 1)):
                    gu[(j, h, m) + low] = g_u[n * slab : n * slab + slab]
                return carry

            lax.fori_loop(0, 2, half_step, 0)
            serve_all(index, 1)
            return carry

        lax.fori_loop(0, 2 * steps, step, 0)
        def close_step(n, carry):
            span = pl.ds(pl.multiple_of(n * block, block), block)
            m, sub = part_rows(n)
            dyf = dyv[span, :].astype(F32)
            value = mid[span, :]
            a2[span, :] = (value + acc_y[span, :] + b_down).astype(BF16)
            normed = (value - jnp.mean(value, axis=-1, keepdims=True)) * inv[span, :]
            da = acc_da[span, :]
            dx2 = dyf + norm_back(da, normed, inv[span, :], gain2)
            acc_da[span, :] = dx2
            dp = dx2.astype(BF16)
            dyv[span, :] = dp
            do[m, sub, :] = dot_nt(dp, w_ov[...]).astype(BF16)
            for r, part in ((7, dyf), (4, da * normed), (5, da), (3, dp.astype(F32))):
                sums[r : r + 1, :width] += jnp.sum(part, axis=0, keepdims=True)
            return carry

        lax.fori_loop(0, total // block, close_step, 0)
        puts = []
        for n in range(micro):
            part = pl.ds(n * rows, rows)
            puts.append(pltpu.make_async_copy(acc_da.at[part, :], grad_in.at[n], sem_m.at[2 + 2 * n]))
            puts.append(pltpu.make_async_copy(a2.at[part, :], out_rows.at[n], sem_m.at[3 + 2 * n]))
        for put in puts:
            put.start()
        g_o = dot_tn(flat(o), dyv[...]).astype(BF16)
        slab = width // count
        for n, idx in enumerate(every):
            for c in range(2):
                gu_out[(c,) + idx] = g_o[n * slab : n * slab + slab, c * (width // 2) : (c + 1) * (width // 2)]
        chunks["o"].feed(gu_out.at[there], lambda at: gu_out[(here,) + at])
        for token in after_feed:
            chunks[token].advance()
        for name, chunk in chunks.items():
            if name[0] in "udo":
                assert chunk.at >= 2
                chunk.steps[0][0].wait_send()
                chunk.sent = True
        for put in puts:
            put.wait()

    half_out = width // 2
    slab = width // count
    chunks = {}
    for j in range(steps):
        chunks["u%d" % j] = Reduce(net, acc_up[j], r_up[j], f_up.at[j], (0, slab),
                                   columns(here * wide, wide)[1], *BACK_BITS["u%d" % j])
        chunks["d%d" % j] = Reduce(net, acc_down[j], r_down[j], f_down, (j * 128, 128),
                                   columns(here * half_out, half_out)[1], *BACK_BITS["d%d" % j])
    chunks["o"] = Reduce(net, acc_out, r_out, f_out, (0, slab), columns(here * half_out, half_out)[1], *BACK_BITS["o"])
    chunks["e"] = SumAll(net, sums, sums_recv)
    chunks["l"] = SumAll(net, late, late_recv)
    edge_at = pl.multiple_of((1 - net.core) * (rows - HALO), HALO)
    tokens = " ".join(BACK_ORDER).split()
    feed_end, free, turn = tokens.index("E"), tokens.index("X"), tokens.index("T")
    halves = lambda text, outer, inner: [[half.split() for half in part.split(inner)] for part in text.split(outer)]
    (_,), *in_feed = halves(" ".join(tokens[:feed_end]), "S", "s")
    after_feed = tokens[feed_end + 1 : free]
    early_tokens, *in_attention = [part.split() for part in " ".join(tokens[free + 1 : turn]).split("A")]
    after_attention = tokens[turn + 1 :]
    assert len(in_feed) == 2 * steps and len(in_attention) == micro * quads

    pl.run_scoped(
        feed_forward,
        pltpu.VMEM((total, width), BF16), pltpu.VMEM((2, width, wide), BF16), pltpu.VMEM((2, wide, width), BF16),
        pltpu.VMEM((width, width), BF16), pltpu.VMEM((total, width), F32), pltpu.VMEM((total, width), BF16),
        pltpu.VMEM((width, total), BF16), pltpu.VMEM((total, 1), F32), pltpu.VMEM((total, width), F32),
        pltpu.VMEM((total, width), F32), pltpu.VMEM((total, wide), BF16), pltpu.VMEM((total, wide), BF16),
        pltpu.VMEM((steps,) + (2,) * bits + (128, width), BF16),
        pltpu.VMEM((steps, 2) + (2,) * bits + (width // count, wide), BF16),
        pltpu.VMEM((2,) + (2,) * bits + (width // count, half_out), BF16),
        pltpu.SemaphoreType.DMA((2, 2 * share)), pltpu.SemaphoreType.DMA((2 + 2 * micro,)),
    )

    def backward(dq, dk, dv, w_vm, gin, parts, dwin, sem_l):
        load_w = pltpu.make_async_copy(w_in, w_vm, sem_l.at[0])
        load_w.start()
        p1 = [net.copy(dwin.at[n], rwin.at[n], pair) for n in range(micro)]
        p2 = [net.copy(parts.at[n], recv_parts.at[n], across) for n in range(micro)]
        third = 3 * width // 6
        slab_in = width // count
        for j in range(3):
            chunks["i%d" % j] = Reduce(net, acc_in[j], r_in[j], f_in, (0, slab_in),
                                       columns(here * 3 * third + j * third, third)[1], *BACK_BITS["i%d" % j])
            chunks["i%d" % j].feed(gin.at[j, there], lambda at, j=j: gin[(j, here) + at])

        def pass_on(n):
            p1[n].wait_recv()

            @pl.when(noisy)
            def _():
                @pl.when(first)
                def _():
                    add_to(parts, (n, slice(rows - win, rows), slice(None)), rwin[n, :win, :])

                p2[n].start()

        def attention(qb, kb, vb, dk_acc, dv_acc, load_sems):
            blocks = ((q, qb), (k, kb), (v, vb))

            def loads(index):
                n, h = index // quads, index % quads
                cols = pl.ds(pl.multiple_of(h * qw, qw), qw)
                slot = index % 2
                return [
                    pltpu.make_async_copy(src.at[n, :, cols], dst.at[slot], load_sems.at[slot, m])
                    for m, (src, dst) in enumerate(blocks)
                ]

            for load in loads(0):
                load.start()
            load_w.wait()

            def partial(n):
                key = jnp.concatenate([dk[n, :win, :], dk[n, pl.ds(halo_at, HALO), :]], axis=0)
                value = jnp.concatenate([dv[n, :win, :], dv[n, pl.ds(halo_at, HALO), :]], axis=0)
                w_key, w_value = w_vm[:, width : 2 * width], w_vm[:, 2 * width :]
                dwin[n] = (dot_nt(key, w_key) + dot_nt(value, w_value)).astype(BF16)
                for m in range(micro):

                    @pl.when(n == m)
                    def _(m=m):
                        p1[m].start()

                @pl.when(noisy)
                def _():
                    main = slice(win, win + rows)
                    parts[n] = (dot_nt(dk[n, main, :], w_key) + dot_nt(dv[n, main, :], w_value)).astype(BF16)

            def serve(token):
                if token[0] == "P":
                    pass_on(int(token[1]))
                else:
                    chunks[token].advance()

            for token in early_tokens:
                serve(token)

            def serve_all(index):
                for at, tokens in enumerate(in_attention):
                    if tokens:

                        @pl.when(index == at)
                        def _(tokens=tokens):
                            for token in tokens:
                                serve(token)

            def step(index, carry):
                n, h = index // quads, index % quads
                slot = index % 2

                @pl.when(index + 1 < micro * quads)
                def _():
                    for load in loads(index + 1):
                        load.start()

                @pl.when(h == 0)
                def _():
                    make_bias(lay, n, codes, queries, biases)

                for load in loads(index):
                    load.wait()
                cols = pl.ds(pl.multiple_of(h * qw, qw), qw)
                attend_back(
                    lay, slot, slice(None), qb, kb, vb, n, cols, o, do, lse, index, cos, sin,
                    n, h * qw, dq, dk, dv, dk_acc, dv_acc, biases,
                )
                @pl.when(h == quads - 1)
                def _():
                    partial(n)

                serve_all(index)
                return carry

            lax.fori_loop(0, micro * quads, step, 0)

        pl.run_scoped(
            attention,
            pltpu.VMEM((2, rows, qw), BF16), pltpu.VMEM((2, keys, qw), BF16), pltpu.VMEM((2, keys, qw), BF16),
            pltpu.VMEM((keys, qw), F32), pltpu.VMEM((keys, qw), F32),
            pltpu.SemaphoreType.DMA((2, 3)),
        )

        def projection(av, at_all, at_own, dxv, sem_a, sem_x):
            load_x = pltpu.make_async_copy(grad_in, dxv, sem_x.at[0])
            pltpu.make_async_copy(a.at[0], av, sem_a.at[0]).start()
            load_x.start()
            def turn_step(n, carry):
                pltpu.make_async_copy(a.at[n], av, sem_a.at[n]).wait()
                at_all[n] = jnp.transpose(av[...])
                at_own[n] = jnp.transpose(av[pl.ds(own_at, rows), :])

                @pl.when(n + 1 < micro)
                def _():
                    pltpu.make_async_copy(a.at[n + 1], av, sem_a.at[n + 1]).start()

                return carry

            lax.fori_loop(0, micro, turn_step, 0)
            late[...] = jnp.zeros_like(late)
            def gradient(j):
                for block in range(2):
                    col = block * 3 * third + j * third
                    source, lhs = ((dq, at_own), (dk, at_all), (dv, at_all))[col // width]
                    inside = slice(col % width, col % width + third)
                    part = width // 2

                    def rows_step(m, carry):
                        grad = jnp.zeros((part, third), F32)
                        for n in range(micro):
                            grad += dot(lhs[n, pl.ds(pl.multiple_of(m * part, 128), part), :], source[n, :, inside])
                        for low, at in enumerate(itertools.product(range(2), repeat=bits - 1)):
                            gin[(j, block, m) + at] = grad[low * slab_in : low * slab_in + slab_in].astype(BF16)
                        return carry

                    lax.fori_loop(0, 2, rows_step, 0)
                    ones = jnp.zeros((8, third), F32)
                    for n in range(micro):
                        rhs = source[n, :, inside]
                        ones += dot(jnp.ones((8, rhs.shape[0]), BF16), rhs)
                    row = 2 + col // width
                    late[row : row + 1, inside] = ones[0:1]

            def settle(n):
                @pl.when(clean)
                def _():
                    p2[n].wait_recv()

                    @pl.when(first)
                    def _():
                        add_to(recv_parts, (n, slice(rows - win, rows), slice(None)), rwin[n, :win, :])

                add_to(recv_parts, (n, pl.ds(edge_at, HALO), slice(None)), rwin[n, win:, :])

            def store(m):
                span = pl.ds(pl.multiple_of((m % 2) * (rows // 2), TILE), rows // 2)
                return pltpu.make_async_copy(dxv.at[m // 2, span, :], grad_in.at[m // 2, span, :], sem_x.at[1 + m])

            def norm_part(m):
                n, part = m // 2, m % 2
                size = rows // 2
                span = pl.ds(pl.multiple_of(part * size, TILE), size)
                mine_rows = pl.ds(pl.multiple_of(own_at + part * size, HALO), size)
                da = dot_nt(dq[n, span, :], w_vm[:, :width])
                da += dot_nt(dk[n, mine_rows, :], w_vm[:, width : 2 * width])
                da += dot_nt(dv[n, mine_rows, :], w_vm[:, 2 * width :])
                da += recv_parts[n, span, :].astype(F32)
                normed, inverse = norm_stats(x[n, span, :].astype(F32))
                dxv[n, span, :] += norm_back(da, normed, inverse, gain)
                late[0:1, :] += jnp.sum(da * normed, axis=0, keepdims=True)
                late[1:2, :] += jnp.sum(da, axis=0, keepdims=True)
                store(m).start()

            def serve(token):
                if token in chunks:
                    chunks[token].advance()
                else:
                    {"P": pass_on, "Y": settle, "G": gradient}[token[0]](int(token[1]))

            groups = [part.split() for part in " ".join(after_attention).split("N")]
            assert len(groups) == 1 + 2 * micro
            for token in groups[0]:
                serve(token)
            load_x.wait()

            def norm_step(m, carry):
                norm_part(m)
                for at, tokens in enumerate(groups[1:-1]):
                    if tokens:

                        @pl.when(m == at)
                        def _(tokens=tokens):
                            for token in tokens:
                                serve(token)

                return carry

            lax.fori_loop(0, 2 * micro, norm_step, 0)
            for token in groups[-1]:
                serve(token)
            while any(chunk.open() for chunk in chunks.values()):
                for chunk in chunks.values():
                    chunk.advance()
            sums_out[...] = chunks["e"].finish()
            late_out[...] = chunks["l"].finish()
            for name, chunk in chunks.items():
                if name not in "el":
                    chunk.finish()
            puts = [net.local(src, dst) for src, dst in ((f_in, f_in_out), (f_out, f_out_out), (f_down, f_down_out))]
            for j in range(steps):
                for n in range(count):
                    puts.append(net.local(
                        f_up.at[j, :, pl.ds(n * 128, 128)], f_up_out.at[:, pl.ds(n * slab_down + j * 128, 128)]
                    ))
            for put in puts:
                put.start()
            for put in puts:
                put.wait()
            for m in range(2 * micro):
                store(m).wait()
            for copy in p1:
                copy.wait_send()

            @pl.when(noisy)
            def _():
                for copy in p2:
                    copy.wait_send()

        pl.run_scoped(
            projection,
            pltpu.VMEM((keys, width), BF16), pltpu.VMEM((micro, width, keys), BF16),
            pltpu.VMEM((micro, width, rows), BF16), pltpu.VMEM((micro, rows, width), F32),
            pltpu.SemaphoreType.DMA((micro,)), pltpu.SemaphoreType.DMA((1 + 2 * micro,)),
        )

    third = 3 * width // 6
    pl.run_scoped(
        backward,
        pltpu.VMEM((micro, rows, width), BF16), pltpu.VMEM((micro, keys, width), BF16),
        pltpu.VMEM((micro, keys, width), BF16), pltpu.VMEM((width, 3 * width), BF16),
        pltpu.VMEM((3, 2) + (2,) * bits + (width // count, third), BF16),
        pltpu.VMEM((micro, rows, width), BF16), pltpu.VMEM((micro, win + HALO, width), BF16),
        pltpu.SemaphoreType.DMA((1,)),
    )


def finish_kernel(sizes, sums, late, g_in, g_out, g_up, g_down, o_in, o_out, o_up, o_down, *vectors):
    for src, dst in ((g_in, o_in), (g_out, o_out), (g_up, o_up), (g_down, o_down)):
        dst[...] = src[...].astype(F32)
    f = lax.axis_index("fsdp")
    width = late.shape[1]
    for r, (size, out) in enumerate(zip(sizes, vectors)):
        if r < 2:
            row = late[r : r + 1, :]
        elif r == 2:
            row = jnp.concatenate([late[m : m + 1, :] for m in range(2, 5)], axis=1)
        else:
            row = sums[r : r + 1, :] if sums.shape[1] == size * (width // sizes[0]) else sums[r : r + 1, :width]
        whole_size = row.shape[1]
        row = jnp.broadcast_to(row, (8, whole_size))
        turned = pltpu.roll(row, lax.rem(whole_size - f * size, whole_size), 1)
        out[...] = turned[0, :size]


def front_remote(
    lay, role, sizes, inputs, segment_ids, block_ids, small, weights, freqs, lse_shape, bias_scratch, spans, attn_flops
):
    micro, rows, width = inputs.shape
    keys, win = lay["keys"], lay["win"]
    bits = lax.axis_size("fsdp").bit_length() - 1
    lanes = -(-max(sizes) // 128) * 128
    full = [like((2,) * bits + p.shape, BF16) for p in weights]
    longest = max(sizes) << bits
    table_rows = win + rows + HALO
    shapes = full + [
        like((micro, rows, width), BF16), like((micro, keys, width), BF16), like((micro, keys, width), BF16),
        like((micro, keys, width), BF16), like((micro, rows, width), BF16), like(lse_shape, F32),
        like((8, longest), F32), like((table_rows, 128), F32), like((table_rows, 128), F32),
        like((micro, keys, 1), F32), like((micro, 8, rows), F32),
    ]
    remote = 3 * micro + 1 + (bits + 2) * 9
    outs = pl.pallas_call(
        functools.partial(front_kernel, lay, bits, sizes),
        in_specs=[VMEM] * 16,
        out_specs=[ANY] * 10 + [VMEM] * 5,
        out_shape=shapes,
        scratch_shapes=[
            pltpu.VMEM((micro, rows, width), BF16), pltpu.VMEM((micro, win + HALO, width), BF16),
            pltpu.VMEM((width, 3 * width), BF16), pltpu.VMEM((micro, rows, width), BF16),
            pltpu.VMEM((micro, keys, width), BF16), pltpu.VMEM((micro, keys, width), BF16),
            pltpu.VMEM((micro, keys, width), BF16), pltpu.VMEM((micro, rows, width), BF16),
            pltpu.VMEM(lse_shape, F32), pltpu.VMEM((2,) * bits + (8, lanes), F32), pltpu.VMEM((8, lanes), F32),
            pltpu.SemaphoreType.DMA((remote,)), pltpu.SemaphoreType.DMA((remote,)),
            pltpu.SemaphoreType.DMA((96,)),
        ] + bias_scratch,
        compiler_params=pltpu.CompilerParams(
            vmem_limit_bytes=VMEM_BYTES, collective_id=0, has_side_effects=True
        ),
        cost_estimate=pl.CostEstimate(flops=2 * attn_flops, bytes_accessed=40 << 20, transcendentals=0),
        name="front",
    )(inputs, segment_ids, block_ids, freqs, *weights, *small)
    joined = [w.reshape((-1, w.shape[-1])) for w in outs[:4]]
    return tuple(joined) + tuple(outs[4:])


def front_native(
    lay, role, sizes, inputs, segment_ids, block_ids, small, weights, freqs, lse_shape, bias_scratch, spans, attn_flops
):
    micro, rows, width = inputs.shape
    keys, win, length = lay["keys"], lay["win"], lay["length"]
    clean, half = role[0], role[1]
    pairs = [(0, 1), (1, 0), (2, 3), (3, 2)]
    xb = lax.ppermute(inputs, "seq", [(2, 0), (3, 1)])
    xmain = jnp.where(clean == 1, inputs, xb)
    edge = jnp.where(half == 0, inputs[:, rows - HALO :], inputs[:, :HALO])
    xc = lax.ppermute(jnp.concatenate([xmain[:, rows - win :], edge], axis=1), "seq", pairs)
    start = half * rows
    edge_at = jnp.where(half == 0, rows, -HALO)
    positions = start + jnp.concatenate([jnp.arange(-win, rows), edge_at + jnp.arange(HALO)])
    turned = positions.astype(F32)[:, None] * freqs
    sine = jnp.sin(turned)
    cos = jnp.cos(turned)
    sin = jnp.where(jnp.arange(128)[None] % HD < HD // 2, -sine, sine)
    code = segment_ids * SEG_STEP + block_ids
    padded = jnp.pad(code, ((0, 0), (win, 0)), constant_values=-1)
    key_codes = lax.dynamic_slice_in_dim(padded, start, win + rows, 1)
    own_code = lax.dynamic_slice_in_dim(code, start, rows, 1)
    own_seg = lax.dynamic_slice_in_dim(segment_ids, start, rows, 1)
    before, after = code[:, rows - HALO : rows], code[:, rows : rows + HALO]
    codes = jnp.concatenate(
        [
            key_codes,
            jnp.where((clean == 1) & (half == 0), after, -1),
            jnp.where((clean == 0) & (half == 1), before, -2),
            jnp.where(clean == 0, own_code, -2),
            jnp.where((clean == 0) & (half == 0), after, -2),
            jnp.full((micro, keys - lay["used"]), -2, jnp.int32),
        ],
        axis=1,
    )[:, :, None].astype(F32)
    queries = jnp.stack([own_seg * SEG_STEP, own_code - (1 - clean), own_code], axis=1)
    queries = jnp.concatenate([queries, jnp.zeros((micro, 5, rows), jnp.int32)], axis=1).astype(F32)
    packed = lax.all_gather(jnp.concatenate(small)[None], "fsdp", axis=0, tiled=True)
    vectors, at = [], 0
    longest = max(sizes) * packed.shape[0]
    for size in sizes:
        one = packed[:, at : at + size].reshape(-1).astype(F32)
        vectors.append(jnp.pad(one, (0, longest - one.shape[0])))
        at += size
    vec = jnp.stack(vectors)
    w_in, w_out, w_up, w_down = (lax.all_gather(p, "fsdp", axis=0, tiled=True) for p in weights)
    per_seq = lambda n, d: pl.BlockSpec((1, n, d), lambda s: (s, 0, 0))
    table_rows = win + rows + HALO
    q, k, v, a = call(
        functools.partial(qkv_kernel, lay), (micro,),
        [SMEM(), per_seq(rows, width), per_seq(rows, width), per_seq(win + HALO, width),
         whole((width, 3 * width)), whole(vec.shape), whole((table_rows, 128)), whole((table_rows, 128))],
        [per_seq(rows, width), per_seq(keys, width), per_seq(keys, width), per_seq(keys, width)],
        [like((micro, rows, width), BF16)] + [like((micro, keys, width), BF16)] * 3,
        [], 2 * micro * rows * width * 3 * width * 2, 20 << 20, "qkv",
    )(role, inputs, xb, xc, w_in, vec, cos, sin)
    qw = QUAD * HD
    quads = width // qw
    quad_block = lambda n: pl.BlockSpec((1, n, qw), lambda s, h: (s, 0, h))
    o, lse = call(
        functools.partial(attend_kernel, lay), (micro, quads),
        [pl.BlockSpec((1, keys, 1), lambda s, h: (s, 0, 0)), pl.BlockSpec((1, 8, rows), lambda s, h: (s, 0, 0)),
         quad_block(rows), quad_block(keys), quad_block(keys)],
        [quad_block(rows), pl.BlockSpec((1,) + lse_shape[1:], lambda s, h: (s * quads + h, 0, 0))],
        [like((micro, rows, width), BF16), like(lse_shape, F32)],
        bias_scratch, 2 * attn_flops, 12 << 20, "attend",
    )(codes, queries, q, k, v)
    return w_in, w_out, w_up, w_down, q, k, v, a, o, lse, vec, cos, sin, codes, queries


def back_remote(
    lay, role, sizes, inputs, cotangent, codes, queries, lse, cos, sin, vec,
    q, k, v, o, a, w_in, w_out, w_up, w_down, bias_scratch, attn_flops,
):
    micro, rows, width = inputs.shape
    keys, win = lay["keys"], lay["win"]
    bits = lax.axis_size("fsdp").bit_length() - 1
    lead = (2,) * bits
    count = 1 << bits
    hidden = w_up.shape[1]
    slab, slab_down = width // count, hidden // count
    third = width // 2
    steps, wide = slab_down // 128, count // 2 * 128

    def bank(name, r, c):
        over_x = BACK_BITS[name][1]
        kept = r // 2 if over_x else r
        over = [pltpu.VMEM(lead[: bits - 1 - b] + (kept, c), BF16) for b in range(bits)]
        ends = [pltpu.VMEM(lead + (kept, c), BF16)] if over_x else []
        return pltpu.VMEM(lead + (r, c), BF16), tuple(ends + over + ([] if over_x else [pltpu.VMEM((r, c), BF16)]))

    acc_in, r_in = zip(*[bank("i%d" % j, slab, third) for j in range(3)])
    acc_out, r_out = bank("o", slab, width // 2)
    acc_up, r_up = zip(*[bank("u%d" % j, slab, wide) for j in range(steps)])
    acc_down, r_down = zip(*[bank("d%d" % j, 128, width // 2) for j in range(steps)])
    stages = 2 + bits
    remote = (7 + 2 * steps) * (bits + 5) + 2 * stages + 4 * micro
    scratch = [
        pltpu.VMEM((micro, rows, width), BF16), pltpu.VMEM((micro, rows, width), BF16),
        pltpu.VMEM((micro, win + HALO, width), BF16),
        acc_in, acc_out, acc_up, acc_down, r_in, r_out, r_up, r_down,
        pltpu.VMEM((slab, 3 * width), BF16), pltpu.VMEM((slab, width), BF16),
        pltpu.VMEM((steps, slab, count * 128), BF16), pltpu.VMEM((slab_down, width), BF16),
        pltpu.VMEM((8, hidden), F32), pltpu.VMEM((2 * stages, 8, hidden), F32),
        pltpu.VMEM((8, width), F32), pltpu.VMEM((2 * stages, 8, width), F32),
        pltpu.SemaphoreType.DMA((remote,)), pltpu.SemaphoreType.DMA((remote,)),
        pltpu.SemaphoreType.DMA((8 + steps * count,)),
    ] + bias_scratch
    out_rows, grad_in, f_in, f_out, f_up, f_down, sums, late = pl.pallas_call(
        functools.partial(back_kernel, lay, bits),
        in_specs=[VMEM] * 8 + [ANY] * 9,
        out_specs=[ANY] * 6 + [VMEM] * 2,
        out_shape=[
            like((micro, rows, width), BF16), like((micro, rows, width), F32), like((slab, 3 * width), BF16),
            like((slab, width), BF16), like((slab, hidden), BF16), like((slab_down, width), BF16),
            like((8, hidden), F32), like((8, width), F32),
        ],
        scratch_shapes=scratch,
        compiler_params=pltpu.CompilerParams(
            vmem_limit_bytes=67043328, collective_id=1, has_side_effects=True
        ),
        cost_estimate=pl.CostEstimate(flops=6 * attn_flops, bytes_accessed=60 << 20, transcendentals=0),
        name="back",
    )(codes, queries, lse, cos, sin, vec, inputs, o, cotangent.reshape(micro * rows, width),
      q, k, v, a, w_in, w_out, w_up, w_down)
    big_shapes = [like(g.shape, F32) for g in (f_in, f_out, f_up, f_down)]
    done = pl.pallas_call(
        functools.partial(finish_kernel, sizes),
        in_specs=[VMEM] * 6,
        out_specs=[VMEM] * 12,
        out_shape=big_shapes + [like((size,), F32) for size in sizes],
        compiler_params=pltpu.CompilerParams(vmem_limit_bytes=VMEM_BYTES),
        cost_estimate=pl.CostEstimate(flops=0, bytes_accessed=6 << 20, transcendentals=0),
        name="finish",
    )(sums, late, f_in, f_out, f_up, f_down)
    return out_rows, grad_in, list(done[:4]), list(done[4:])


def back_native(
    lay, role, sizes, inputs, cotangent, codes, queries, lse, cos, sin, vec,
    q, k, v, o, a, w_in, w_out, w_up, w_down, bias_scratch, attn_flops,
):
    micro, rows, width = inputs.shape
    keys, win = lay["keys"], lay["win"]
    clean, half = role[0], role[1]
    pairs = [(0, 1), (1, 0), (2, 3), (3, 2)]
    fsdp_n = lax.axis_size("fsdp")
    hidden = w_up.shape[1]
    qw = QUAD * HD
    quads = width // qw
    total = micro * rows
    flat = lambda z: z.reshape(total, width)
    chunk = min(512, hidden)
    rows_spec = whole((total, width))
    out_rows, dx2, do, g_w_out, g_w_up, g_b_up, g_w_down, g_mlp = call(
        mlp_kernel, (hidden // chunk,),
        [rows_spec, rows_spec, rows_spec, whole((width, width)), whole(vec.shape),
         pl.BlockSpec((width, chunk), lambda j: (0, j)), pl.BlockSpec((8, chunk), lambda j: (0, j)),
         pl.BlockSpec((chunk, width), lambda j: (j, 0))],
        [rows_spec, rows_spec, rows_spec, whole((width, width)),
         pl.BlockSpec((width, chunk), lambda j: (0, j)), pl.BlockSpec((8, chunk), lambda j: (0, j)),
         pl.BlockSpec((chunk, width), lambda j: (j, 0)), whole((8, width))],
        [like((total, width), BF16), like((total, width), F32), like((total, width), BF16),
         like((width, width), BF16), like((width, hidden), BF16), like((8, hidden), F32),
         like((hidden, width), BF16), like((8, width), F32)],
        [pltpu.VMEM((total, width), F32), pltpu.VMEM((total, width), BF16), pltpu.VMEM((width, total), BF16),
         pltpu.VMEM((total, 1), F32), pltpu.VMEM((total, width), F32), pltpu.VMEM((total, width), F32)],
        2 * total * width * (6 * hidden + 3 * width), 40 << 20, "mlp",
    )(flat(o), flat(inputs), flat(cotangent), w_out, vec, w_up, vec, w_down)

    do = do.reshape(micro, rows, width)
    per_seq = lambda n, d: pl.BlockSpec((1, n, d), lambda s: (s, 0, 0))
    role_spec = SMEM()
    quad_block = lambda n: pl.BlockSpec((1, n, qw), lambda s, h: (s, 0, h))
    code_spec = pl.BlockSpec((1, keys, 1), lambda s, h: (s, 0, 0))
    query_spec = pl.BlockSpec((1, 8, rows), lambda s, h: (s, 0, 0))
    lse_spec = pl.BlockSpec((1,) + lse.shape[1:], lambda s, h: (s * quads + h, 0, 0))
    table = pl.BlockSpec((win + rows + HALO, 128), lambda s, h: (0, 0), pipeline_mode=pl.Buffered(1))
    dq, dk, dv = call(
        functools.partial(attend_back_kernel, lay), (micro, quads),
        [code_spec, query_spec, quad_block(rows), quad_block(keys), quad_block(keys),
         quad_block(rows), quad_block(rows), lse_spec, table, table],
        [quad_block(rows), quad_block(keys), quad_block(keys)],
        [like((micro, rows, width), BF16), like((micro, keys, width), BF16), like((micro, keys, width), BF16)],
        [pltpu.VMEM((keys, qw), F32), pltpu.VMEM((keys, qw), F32)] + bias_scratch,
        5 * attn_flops, 24 << 20, "attend_back",
    )(codes, queries, q, k, v, o, do, lse, cos, sin)

    da_own, da_main, da_win, g_w_in, g_b_in = call(
        functools.partial(qkv_back_kernel, lay), (micro,),
        [role_spec, per_seq(keys, width), per_seq(rows, width), per_seq(keys, width), per_seq(keys, width),
         whole((width, 3 * width))],
        [per_seq(rows, width), per_seq(rows, width), per_seq(win + HALO, width),
         whole((width, 3 * width)), whole((8, 3 * width))],
        [like((micro, rows, width), F32), like((micro, rows, width), BF16), like((micro, win + HALO, width), BF16),
         like((width, 3 * width), BF16), like((8, 3 * width), F32)],
        [pltpu.VMEM((width, 3 * width), F32)], 2 * 2 * micro * rows * width * 3 * width * 2, 40 << 20, "qkv_back",
    )(role, a, dq, dk, dv, w_in)

    from_pair = lax.ppermute(da_win, "seq", pairs).astype(F32)
    from_second = jnp.where(half == 0, from_pair[:, :win], 0.0)
    edge = from_pair[:, win:]
    gap = jnp.zeros((micro, rows - HALO, width), F32)
    edges = jnp.where(
        half == 0, jnp.concatenate([gap, edge], axis=1), jnp.concatenate([edge, gap], axis=1)
    )
    added = jnp.pad(from_second, ((0, 0), (rows - win, 0), (0, 0)))
    to_clean = (jnp.where(clean == 0, da_main.astype(F32), 0.0) + added).astype(BF16)
    from_noisy = lax.ppermute(to_clean, "seq", [(0, 2), (1, 3)])
    extra = jnp.where(clean == 1, from_noisy.astype(F32) + added, 0.0) + edges

    grad_in, g_attn = call(
        final_kernel, (2,),
        [pl.BlockSpec((total // 2, width), lambda i: (i, 0))] * 4 + [whole((1, width))],
        [pl.BlockSpec((total // 2, width), lambda i: (i, 0)), whole((8, width))],
        [like((total, width), F32), like((8, width), F32)], [], 0, 16 << 20, "norm_back",
    )(flat(inputs), flat(da_own), flat(extra), flat(dx2), vec[0:1, :width])

    def scatter(g):
        return lax.psum(lax.psum_scatter(g, "fsdp", scatter_dimension=0, tiled=True), "seq")

    big = [scatter(g).astype(F32) for g in (g_w_in, g_w_out, g_w_up, g_w_down)]
    smalls = [g_attn[0], g_attn[1], g_b_in[0], g_mlp[3], g_mlp[1], g_mlp[2], g_b_up[0], g_mlp[0]]
    pack = jnp.concatenate([g.reshape(fsdp_n, -1) for g in smalls], axis=1)
    pack = lax.psum(pack, ("seq", "fsdp"))
    mine = lax.dynamic_slice_in_dim(pack, lax.axis_index("fsdp"), 1, 0)[0]
    outs, at = [], 0
    for size in sizes:
        outs.append(mine[at : at + size])
        at += size
    return out_rows.reshape(micro, rows, width), grad_in.reshape(micro, rows, width), big, outs


def per_device(
    inputs, segment_ids, block_ids, attn_gain, attn_shift, proj_in, bias_in, proj_out, bias_out,
    mlp_gain, mlp_shift, weight_up, bias_up, weight_down, bias_down, cotangent,
):
    micro, rows, width = inputs.shape
    length = segment_ids.shape[1]
    hidden = weight_up.shape[1]
    seq_n = lax.axis_size("seq")
    fsdp_n = lax.axis_size("fsdp")
    assert seq_n == 4 and seq_n * rows == 2 * length
    lay = layout(rows, length)
    win, keys = lay["win"], lay["keys"]
    me = lax.axis_index("seq")
    clean = me // 2
    half = me % 2
    role = jnp.stack([clean, half]).astype(jnp.int32)
    pairs = [(0, 1), (1, 0), (2, 3), (3, 2)]
    small = (attn_gain, attn_shift, bias_in, bias_out, mlp_gain, mlp_shift, bias_up, bias_down)
    sizes = [p.shape[0] for p in small]
    weights = (proj_in, proj_out, weight_up, weight_down)
    half_dim = HD // 2
    freqs = (10000.0 ** (-(np.arange(half_dim, dtype=np.float32) / half_dim))).astype(np.float32)
    freqs = np.tile(freqs, 4)[None]
    quads = width // (QUAD * HD)
    qw = QUAD * HD
    spans = [hi - lo + NEAR for lo, hi in windows(lay)]
    bias_scratch = [pltpu.VMEM((rows // TILE, max(spans), TILE), F32)]
    per_seq = lambda n, d: pl.BlockSpec((1, n, d), lambda s: (s, 0, 0))
    role_spec = SMEM()
    attn_flops = micro * quads * sum(spans) * QUAD * TILE * qw * 2
    lse_shape = (micro * quads, rows // TILE, QUAD * TILE)
    table_rows = win + rows + HALO
    aligned = fsdp_n & (fsdp_n - 1) == 0 and all(p.shape[0] % (4 * HALO) in (0, 32) for p in weights)
    front = front_remote if aligned else front_native
    (w_in, w_out, w_up, w_down, q, k, v, a, o, lse, vec, cos, sin, codes, queries) = front(
        lay, role, sizes, inputs, segment_ids, block_ids, small, weights, freqs,
        lse_shape, bias_scratch, spans, attn_flops,
    )
    back = back_remote if aligned else back_native
    out_rows, grad_in, big, vectors = back(
        lay, role, sizes, inputs, cotangent, codes, queries, lse, cos, sin, vec,
        q, k, v, o, a, w_in, w_out, w_up, w_down, bias_scratch, attn_flops,
    )
    g_gain1, g_shift1, g_bin, g_bout, g_gain2, g_shift2, g_bup, g_bdown = vectors
    return (
        out_rows, grad_in, g_gain1, g_shift1, big[0], g_bin, big[1], g_bout,
        g_gain2, g_shift2, big[2], g_bup, big[3], g_bdown,
    )


def solution(mesh):
    rows = P("fsdp", "seq", None)
    one, two = P("fsdp"), P("fsdp", None)
    params = (one, one, two, one, two, one, one, one, two, one, two, one)
    return jax.shard_map(
        per_device,
        mesh=mesh,
        in_specs=(rows, two, two) + params + (rows,),
        out_specs=(rows, rows) + params,
        check_vma=False,
    )
```

```python
import functools
import itertools

import jax
import jax.numpy as jnp
import numpy as np
from jax import lax
from jax.experimental import pallas as pl
from jax.experimental.pallas import tpu as pltpu
from jax.sharding import PartitionSpec as P

HD = 64
QUAD = 4
TILE = 128
HALO = 16
NEAR = TILE + 2 * HALO
EPS = 1e-05
MASKED = -1e30
SEG_STEP = 4096
F32 = jnp.float32
BF16 = jnp.bfloat16
VMEM_BYTES = 62 * 1024 * 1024
MESH = pl.DeviceIdType.MESH
ANY = pl.BlockSpec(memory_space=pl.ANY)
VMEM = pl.BlockSpec(memory_space=pltpu.VMEM)


def dot(a, b):
    return jnp.dot(a, b, preferred_element_type=F32)


def dot_nt(a, b):
    return lax.dot_general(a, b, (((1,), (1,)), ((), ())), preferred_element_type=F32)


def dot_tn(a, b):
    return lax.dot_general(a, b, (((0,), (0,)), ((), ())), preferred_element_type=F32)


def norm_stats(x):
    center = jnp.mean(x, axis=-1, keepdims=True)
    centered = x - center
    inverse = lax.rsqrt(jnp.mean(centered * centered, axis=-1, keepdims=True) + EPS)
    return centered * inverse, inverse


def norm_back(grad, normed, inverse, gain):
    scaled = grad * gain
    first = jnp.mean(scaled, axis=-1, keepdims=True)
    second = jnp.mean(scaled * normed, axis=-1, keepdims=True)
    return inverse * (scaled - first - normed * second)


def partner(u):
    lane = lax.broadcasted_iota(jnp.int32, u.shape, 1)
    half = HD // 2
    return jnp.where(
        lane % HD < half, pltpu.roll(u, u.shape[1] - half, 1), pltpu.roll(u, half, 1)
    )


def whole(shape):
    return pl.BlockSpec(shape, lambda *_: (0,) * len(shape), pipeline_mode=pl.Buffered(1))


def call(kernel, grid, in_specs, out_specs, out_shape, scratch, flops, nbytes, name):
    return pl.pallas_call(
        kernel,
        grid=grid,
        in_specs=in_specs,
        out_specs=out_specs,
        out_shape=out_shape,
        scratch_shapes=scratch,
        compiler_params=pltpu.CompilerParams(vmem_limit_bytes=VMEM_BYTES),
        cost_estimate=pl.CostEstimate(flops=flops, bytes_accessed=nbytes, transcendentals=0),
        name=name,
    )


def like(shape, dtype):
    return jax.ShapeDtypeStruct(shape, dtype)


SMEM = functools.partial(pl.BlockSpec, memory_space=pltpu.SMEM)


def layout(rows, length):
    win = rows - length // 8
    noisy = win + rows + HALO
    used = noisy + rows + 2 * HALO
    return dict(rows=rows, win=win, length=length, noisy=noisy, used=used, keys=-(-used // 256) * 256)


def places(lay, role):
    noisy = role[0] == 0
    second = role[1] == 1
    own_at = jnp.where(noisy, lay["noisy"] + HALO, lay["win"])
    halo_at = jnp.where(
        second,
        lay["noisy"],
        jnp.where(noisy, lay["noisy"] + HALO + lay["rows"], lay["win"] + lay["rows"]),
    )
    return noisy, second, pl.multiple_of(own_at, HALO), pl.multiple_of(halo_at, HALO)


def qkv_rows(lay, where_am, n, x, xb, xc, w, b, gain, shift, cos, sin, q_out, k_out, v_out, a_out):
    width = x.shape[2]
    rows, win = lay["rows"], lay["win"]
    noisy, second, own_at, halo_at = where_am

    def norm(v):
        normed, _ = norm_stats(v.astype(F32))
        return (normed * gain + shift).astype(BF16)

    def zeros(at, count):
        for ref in (k_out, v_out, a_out):
            ref[n, at : at + count, :] = jnp.zeros((count, width), BF16)

    def section(a, parts, table, want_q):
        def put(ref, col, value):
            for begin, count, at in parts:
                ref[n, pl.ds(at, count), col : col + value.shape[1]] = value[begin : begin + count]

        put(a_out, 0, a)
        c = cos[table : table + a.shape[0], :]
        s = sin[table : table + a.shape[0], :]
        first = 0 if want_q else width
        for col in range(first, 3 * width, 256):
            part = dot(a, w[:, col : col + 256]) + b[:, col : col + 256]
            for piece in range(2):
                u = part[:, piece * 128 : piece * 128 + 128]
                at_col = col + piece * 128
                if at_col < 2 * width:
                    u = u * c + partner(u) * s
                if at_col < width:
                    q_out[n, :, at_col : at_col + 128] = (u[:rows] * (HD**-0.5)).astype(BF16)
                elif at_col < 2 * width:
                    put(k_out, at_col - width, u.astype(BF16))
                else:
                    put(v_out, at_col - 2 * width, u.astype(BF16))

    zeros(win + rows, 2 * HALO)
    zeros(lay["used"] - HALO, lay["keys"] - lay["used"] + HALO)
    own = jnp.concatenate([norm(x[n]), norm(xc[n, win:, :])], axis=0)
    section(own, ((0, rows, own_at), (rows, HALO, halo_at)), win, True)

    @pl.when(noisy)
    def _():
        section(norm(xb[n]), ((0, rows, win),), win, False)

    @pl.when(jnp.logical_not(noisy))
    def _():
        zeros(lay["noisy"] + HALO, rows)

    @pl.when(second)
    def _():
        section(norm(xc[n, :win, :]), ((0, win, 0),), 0, False)

    @pl.when(jnp.logical_not(second))
    def _():
        zeros(0, win)


def qkv_columns(lay, n, act, at_parts, table, col, count, w, b, cos, sin, q, k, v):
    width, rows = q.shape[2], lay["rows"]

    def put(ref, at_col, value):
        for begin, size, at in at_parts:
            ref[n, pl.ds(at, size), at_col : at_col + 128] = value[begin : begin + size].astype(BF16)

    c = cos[table : table + act.shape[0], :]
    s = sin[table : table + act.shape[0], :]
    part = dot(act, w[:, col : col + count]) + b[:, col : col + count]
    for at_col in range(col, col + count, 128):
        u = part[:, at_col - col : at_col - col + 128]
        if at_col < 2 * width:
            u = u * c + partner(u) * s
        if at_col < width:
            q[n, :, at_col : at_col + 128] = (u[:rows] * (HD**-0.5)).astype(BF16)
        elif at_col < 2 * width:
            put(k, at_col - width, u)
        else:
            put(v, at_col - 2 * width, u)


def qkv_kernel(lay, role, x, xb, xc, w, vec, cos, sin, *outs):
    width = x.shape[2]
    gain, shift, b = vec[0:1, :width], vec[1:2, :width], vec[2:3, : 3 * width]
    qkv_rows(lay, places(lay, role), 0, x, xb, xc, w, b, gain, shift, cos, sin, *outs)


def windows(lay):
    rows, win, length = lay["rows"], lay["win"], lay["length"]
    longest, earliest, latest = length // 2, length // 8, 3 * length // 8
    found = []
    for at in range(0, rows, TILE):
        begin = win + rows
        for origin in range(0, length, rows):
            pos = origin + at
            low = max(pos - longest, 0)
            if origin > 0:
                low = max(low, earliest)
            if pos >= latest + longest:
                low = max(low, earliest + longest)
            begin = min(begin, low - origin + win)
        found.append((begin // TILE * TILE, win + at + TILE + HALO))
    return found


def tile_loop(lay, body):
    for t, (lo, hi) in enumerate(windows(lay)):
        near = lay["noisy"] + t * TILE
        body(t, slice(t * TILE, t * TILE + TILE), slice(lo, hi), slice(near, near + NEAR), hi - lo)


def make_bias(lay, n, codes, queries, biases):
    (bias,) = biases
    groups = {}
    for t, (lo, hi) in enumerate(windows(lay)):
        groups.setdefault(hi - lo, []).append((t, lo))
    for size, tiles in groups.items():
        (t0, lo0), (t1, lo1), number = tiles[0], tiles[-1], len(tiles)
        apart = max(number - 1, 1)
        assert all(tile == (t0 + k * (t1 - t0) // apart, lo0 + k * (lo1 - lo0) // apart) for k, tile in enumerate(tiles))

        def step(k, carry, size=size, t0=t0, lo0=lo0, dt=(t1 - t0) // apart, dlo=(lo1 - lo0) // apart):
            t = t0 + k * dt
            here = pl.ds(pl.multiple_of(t * TILE, TILE), TILE)
            low, high, same = (queries[n, r : r + 1, here] for r in range(3))
            kc = codes[n, pl.ds(pl.multiple_of(lo0 + k * dlo, HALO), size), :]
            ok = jnp.logical_and(kc >= low, kc <= high)
            bias[t, :size, :] = jnp.where(ok, 0.0, MASKED)
            kn = codes[n, pl.ds(pl.multiple_of(lay["noisy"] + t * TILE, HALO), NEAR), :]
            bias[t, size : size + NEAR, :] = jnp.where(kn == same, 0.0, MASKED)
            return carry

        lax.fori_loop(0, number, step, 0)


def stacked(tile):
    lane = lax.broadcasted_iota(jnp.int32, tile.shape, 1)
    zero = jnp.zeros_like(tile)
    return jnp.concatenate(
        [jnp.where(lane // HD == h, tile, zero) for h in range(QUAD)], axis=0
    )


def own_heads(wide):
    return jnp.concatenate(
        [wide[h * HD : h * HD + HD, h * TILE : h * TILE + TILE] for h in range(QUAD)], axis=0
    )


def keys_of(ref, n, cols, lo, near):
    return jnp.concatenate([ref[n, lo, cols], ref[n, near, cols]], axis=0)


def attend(lay, n, cols, q, k, v, o_out, lse_out, lse_at, biases):
    (bias,) = biases

    def body(t, here, lo, near, size):
        qm = stacked(q[n, here, cols])
        kk = keys_of(k, n, cols, lo, near)
        vv = keys_of(v, n, cols, lo, near)
        s = dot_nt(kk, qm) + jnp.concatenate([bias[t, : size + NEAR, :]] * QUAD, axis=1)
        peak = jnp.max(s, axis=0, keepdims=True)
        p = jnp.exp(s - peak)
        total = jnp.sum(p, axis=0, keepdims=True)
        wide = dot_tn(vv, p.astype(BF16)) * (1.0 / total)
        o_out[n, here, cols] = jnp.transpose(own_heads(wide)).astype(BF16)
        lse_out[lse_at, t : t + 1, :] = peak + jnp.log(total)

    tile_loop(lay, body)


def attend_kernel(lay, codes, queries, q, k, v, o_out, lse_out, *biases):
    @pl.when(pl.program_id(1) == 0)
    def _():
        make_bias(lay, 0, codes, queries, biases)

    attend(lay, 0, slice(None), q, k, v, o_out, lse_out, 0, biases)


def attend_back(
    lay, n, cols, q, k, v, m, cols_m, o, do, lse, lse_at, cos, sin, to, col, dq_out, dk_out, dv_out, dk_acc, dv_acc, biases,
):
    rows, win = lay["rows"], lay["win"]
    qw = QUAD * HD

    def lanes(piece):
        return pl.ds(pl.multiple_of(col + piece * 128, 128), 128)

    dk_acc[...] = jnp.zeros_like(dk_acc)
    dv_acc[...] = jnp.zeros_like(dv_acc)
    (bias,) = biases

    def body(t, here, lo, near, size):
        qm = stacked(q[n, here, cols])
        dom = stacked(do[m, here, cols_m])
        kk = keys_of(k, n, cols, lo, near)
        vv = keys_of(v, n, cols, lo, near)
        both = jnp.transpose(do[m, here, cols_m].astype(F32) * o[m, here, cols_m].astype(F32))
        delta = jnp.concatenate(
            [jnp.sum(both[h * HD : h * HD + HD, :], axis=0, keepdims=True) for h in range(QUAD)],
            axis=1,
        )
        s = dot_nt(kk, qm) + jnp.concatenate([bias[t, : size + NEAR, :]] * QUAD, axis=1)
        p = jnp.exp(s - lse[lse_at, t : t + 1, :])
        dp = dot_nt(vv, dom)
        ds = (p * (dp - delta)).astype(BF16)
        pb = p.astype(BF16)
        dv = dot(pb, dom)
        dk = dot(ds, qm)
        dv_acc[lo, :] += dv[:size]
        dk_acc[lo, :] += dk[:size]
        dv_acc[near, :] += dv[size:]
        dk_acc[near, :] += dk[size:]
        wide = dot_tn(kk, ds)
        dq = jnp.transpose(own_heads(wide)) * (HD**-0.5)
        turn = slice(win + t * TILE, win + t * TILE + TILE)
        c, sn = cos[turn, :], sin[turn, :]
        for piece in range(2):
            u = dq[:, piece * 128 : piece * 128 + 128]
            dq_out[to, here, lanes(piece)] = (u * c - partner(u) * sn).astype(BF16)

    tile_loop(lay, body)
    for piece in range(2):
        dv_out[to, :, lanes(piece)] = dv_acc[:, piece * 128 : piece * 128 + 128].astype(BF16)
    half = (cos[win + rows :, :], sin[win + rows :, :])
    own = (cos[win : win + rows, :], sin[win : win + rows, :])
    tables = (
        (0, (cos[: win + rows, :], sin[: win + rows, :])),
        (win + rows, half),
        (lay["noisy"], half),
        (lay["noisy"] + HALO, own),
        (lay["used"] - HALO, half),
    )
    for at, (c, sn) in tables:
        here = slice(at, at + c.shape[0])
        for piece in range(2):
            u = dk_acc[here, piece * 128 : piece * 128 + 128]
            dk_out[to, here, lanes(piece)] = (u * c - partner(u) * sn).astype(BF16)
    spare = lay["keys"] - lay["used"]
    for piece in range(2):
        dk_out[to, lay["used"] :, lanes(piece)] = jnp.zeros((spare, 128), BF16)


def attend_back_kernel(
    lay, codes, queries, q, k, v, o, do, lse, cos, sin, dq_out, dk_out, dv_out, dk_acc, dv_acc, *biases
):
    @pl.when(pl.program_id(1) == 0)
    def _():
        make_bias(lay, 0, codes, queries, biases)

    attend_back(
        lay, 0, slice(None), q, k, v, 0, slice(None), o, do, lse, 0, cos, sin, 0, 0, dq_out, dk_out, dv_out, dk_acc, dv_acc, biases
    )


def bit_of(index, b):
    return (index // (1 << b)) % 2


def other(index, b):
    return index + (1 << b) * (1 - 2 * bit_of(index, b))


class Net:
    def __init__(self, bits, send, recv, sems):
        self.me, self.f, self.bits = lax.axis_index("seq"), lax.axis_index("fsdp"), bits
        self.core, self.x = self.me % 2, self.me // 2
        self.send, self.recv, self.sems = send, recv, sems
        self.used, self.local_used = 0, 0
        self.started = []

    def partners(self):
        return [{"seq": other(self.me, 0)}, {"seq": other(self.me, 1)}] + [
            {"fsdp": other(self.f, b)} for b in range(self.bits)
        ]

    def barrier(self):
        barrier = pltpu.get_barrier_semaphore()
        for device in self.partners():
            pl.semaphore_signal(barrier, inc=1, device_id=device, device_id_type=MESH)
        pl.semaphore_wait(barrier, 2 + self.bits)

    def copy(self, src, dst, device):
        n = self.used
        self.used += 1
        return pltpu.make_async_remote_copy(
            src_ref=src, dst_ref=dst, send_sem=self.send.at[n], recv_sem=self.recv.at[n],
            device_id=device, device_id_type=MESH,
        )

    def local(self, src, dst):
        n = self.local_used
        self.local_used += 1
        return pltpu.make_async_copy(src, dst, self.sems.at[n])

    def fsdp_index(self, done):
        return tuple(slice(None) if b in done else bit_of(self.f, b) for b in range(self.bits - 1, -1, -1))


FRONT_ORDER = (
    "E s i0 i1",
    "T s i2 R0",
    "i0 i1 i2 i0",
    "u0 s i1 u1",
    "i2 s o i1",
    "i1 V u0 i0",
    "R1 u1 i2 o",
    "i0 d0 L0 W",
    "P0 i2 L2 u0",
    "L1 H u1 d1",
    "O0 O1 O2 u0",
    "o d0 d1 A",
    "P1 u1 A d0",
    "A d1 u0 A",
    "u0 d0 u1 o",
    "A d1 A o",
    "u1 d0",
)
FRONT_BITS = {
    "i0": ((2, 0, 1), False),
    "i1": ((2, 1, 0), False),
    "i2": ((2, 1, 0), False),
    "o": ((2, 1, 0), False),
    "u0": ((2, 1, 0), True),
    "u1": ((2, 0, 1), True),
    "d0": ((2, 1, 0), False),
    "d1": ((0, 2, 1), False),
}


class Gather:
    def __init__(self, net, own, full, tail, tail_x=None, tail_core=None, order=None):
        self.net, self.at = net, 0
        mine = net.fsdp_index(())
        self.own = net.local(own.at[tail], full.at[mine + tail])
        self.stages = []
        done = []
        for b in order if order is not None and len(order) == net.bits else range(net.bits - 1, -1, -1):
            here = full.at[net.fsdp_index(done) + tail]
            src = here if done else own.at[tail]
            self.stages.append(net.copy(src, here, {"fsdp": other(net.f, b)}))
            done.append(b)
        everything = (slice(None),) * net.bits
        for region, b in ((tail_x, 1), (tail_core, 0)):
            if region is not None:
                here = full.at[everything + region]
                self.stages.append(net.copy(here, here, {"seq": other(net.me, b)}))

    def advance(self):
        if self.at > len(self.stages):
            return
        if self.at == 0:
            self.own.start()
        else:
            self.stages[self.at - 1].wait_recv()
        if self.at == 1:
            self.own.wait()
        if self.at < len(self.stages):
            self.stages[self.at].start()
        self.at += 1

    def finish(self):
        for stage in self.stages:
            stage.wait_send()


def front_kernel(
    lay, bits, sizes, x, seg, blk, freqs, w_in_s, w_out_s, w_up_s, w_down_s,
    small0, small1, small2, small3, small4, small5, small6, small7,
    w_in, w_out, w_up, w_down, q_out, k_out, v_out, a_out, o_out, lse_out, vec, cos, sin, codes, queries,
    xb, xc, w_vm, q, k, v, a, o, lse, packs, pack, send, recv, sems, *biases,
):
    rows, win, length = lay["rows"], lay["win"], lay["length"]
    width = x.shape[2]
    hidden = w_up_s.shape[1]
    micro = x.shape[0]
    net = Net(bits, send, recv, sems)
    role = (net.x, net.core)
    noisy, second, own_at, halo_at = places(lay, role)
    first = jnp.logical_not(second)
    clean = jnp.logical_not(noisy)
    net.barrier()

    pair, across = {"seq": other(net.me, 0)}, {"seq": other(net.me, 1)}
    rows_across = [net.copy(x.at[n], xb.at[n], across) for n in range(micro)]
    window = (pl.ds(rows - win, win), slice(None))
    target = (pl.ds(0, win), slice(None))
    rows_pair, rows_pair_b = [], []
    for n in range(micro):
        at = net.used
        rows_pair.append(net.copy(x.at[(n,) + window], xc.at[(n,) + target], pair))
        net.used = at
        rows_pair_b.append(net.copy(xb.at[(n,) + window], xc.at[(n,) + target], pair))
    edge_at = pl.multiple_of((1 - net.core) * (rows - HALO), HALO)
    edge = net.copy(x.at[:, pl.ds(edge_at, HALO), :], xc.at[:, pl.ds(win, HALO), :], pair)

    def columns(begin, size):
        return (slice(None), pl.ds(pl.multiple_of(begin, 128), size))

    pack[...] = jnp.zeros_like(pack)
    smalls = (small0, small1, small2, small3, small4, small5, small6, small7)
    for r, (ref, size) in enumerate(zip(smalls, sizes)):
        pack[r : r + 1, :size] = ref[...].astype(F32).reshape(1, size)
    chunks = {"s": Gather(net, pack, packs, (slice(None), slice(None)))}
    half_in, half_out, half_up = 3 * width // 2, width // 2, hidden // 2
    third = half_in // 3
    for n in range(3):
        region = columns(net.core * half_in + n * third, third)
        chunks["i%d" % n] = Gather(net, w_in_s, w_in, region, None, region, FRONT_BITS["i%d" % n][0])
    region = columns(net.core * half_out, half_out)
    chunks["o"] = Gather(net, w_out_s, w_out, region, None, region, FRONT_BITS["o"][0])
    quarter = half_up // 2
    slab = w_down_s.shape[0]
    for n in range(2):
        order, over_x = FRONT_BITS["u%d" % n]
        region = columns(net.core * half_up + n * quarter, quarter)
        part = columns(net.core * half_up + n * quarter + net.x * (quarter // 2), quarter // 2) if over_x else region
        chunks["u%d" % n] = Gather(net, w_up_s, w_up, part, part if over_x else None, region, order)
        order, over_x = FRONT_BITS["d%d" % n]
        begin = net.core * (slab // 2) + n * (slab // 4)
        region = (pl.ds(pl.multiple_of(begin, HALO), slab // 4), slice(None))
        half_region = (pl.ds(pl.multiple_of(begin + net.x * (slab // 8), HALO), slab // 8), slice(None))
        part = half_region if over_x else region
        chunks["d%d" % n] = Gather(net, w_down_s, w_down, part, part if over_x else None, region, order)

    def rows_start(n):
        @pl.when(clean)
        def _():
            rows_across[n].start()

    count = 1 << bits

    def tables():
        block = 48
        assert (win + rows + HALO) % block == 0

        def table_step(n, carry):
            span = pl.ds(pl.multiple_of(n * block, HALO), block)
            position = lax.broadcasted_iota(jnp.int32, (block, 128), 0) + n * block
            shifted = jnp.where(
                position < win + rows, position - win, position - win - rows + jnp.where(second, -HALO, rows)
            )
            turned = (shifted + jnp.where(second, rows, 0)).astype(F32) * freqs[...]
            lane = lax.broadcasted_iota(jnp.int32, (block, 128), 1)
            cos[span, :] = jnp.cos(turned)
            sine = jnp.sin(turned)
            sin[span, :] = jnp.where(lane % HD < HD // 2, -sine, sine)
            return carry

        lax.fori_loop(0, (win + rows + HALO) // block, table_step, 0)
        code = (seg[...] * SEG_STEP + blk[...]).astype(F32)
        base = (seg[...] * SEG_STEP).astype(F32)
        turned_code = jnp.transpose(jnp.concatenate([code, jnp.zeros((8 - micro, length), F32)], axis=0))
        lay_noisy = lay["noisy"]
        for n in range(micro):
            col = turned_code[:, n : n + 1]
            none = lambda count, value: jnp.full((count, 1), value, F32)
            codes[n, :win, :] = jnp.where(second, col[rows - win : rows], -1.0)
            codes[n, win : win + rows, :] = jnp.where(second, col[rows:], col[:rows])
            after, before = col[rows : rows + HALO], col[rows - HALO : rows]
            codes[n, win + rows : lay_noisy, :] = jnp.where(jnp.logical_and(clean, first), after, -1.0)
            codes[n, lay_noisy : lay_noisy + HALO, :] = jnp.where(jnp.logical_and(noisy, second), before, -2.0)
            codes[n, lay_noisy + HALO : lay_noisy + HALO + rows, :] = jnp.where(
                noisy, jnp.where(second, col[rows:], col[:rows]), -2.0
            )
            codes[n, lay["used"] - HALO : lay["used"], :] = jnp.where(jnp.logical_and(noisy, first), after, -2.0)
            codes[n, lay["used"] :, :] = none(lay["keys"] - lay["used"], -2.0)
            own_code = jnp.where(second, code[n : n + 1, rows:], code[n : n + 1, :rows])
            own_base = jnp.where(second, base[n : n + 1, rows:], base[n : n + 1, :rows])
            high = own_code - jnp.where(noisy, 1.0, 0.0)
            queries[n] = jnp.concatenate([own_base, high, own_code, jnp.zeros((5, rows), F32)], axis=0)

    def vectors():
        kinds = sorted(set(sizes))

        def spread_step(n, totals):
            piece = packs[tuple((n // (1 << b)) % 2 for b in range(bits - 1, -1, -1))]
            added = []
            for size, total in zip(kinds, totals):
                wide = size * count - piece.shape[1]
                padded = jnp.concatenate([piece, jnp.zeros((8, wide), F32)], axis=1) if wide > 0 else piece
                lanes = lax.broadcasted_iota(jnp.int32, padded.shape, 1)
                added.append(total + pltpu.roll(jnp.where(lanes < size, padded, 0.0), n * size, 1))
            return tuple(added)

        zero = tuple(jnp.zeros((8, size * count), F32) for size in kinds)
        spread = dict(zip(kinds, lax.fori_loop(0, count, spread_step, zero)))
        for r, size in enumerate(sizes):
            vec[r : r + 1, : size * count] = spread[size][r : r + 1]
            if size * count < vec.shape[1]:
                vec[r : r + 1, size * count :] = jnp.zeros((1, vec.shape[1] - size * count), F32)

    def pass_on(n):
        @pl.when(noisy)
        def _():
            rows_across[n].wait_recv()

        @pl.when(jnp.logical_and(first, noisy))
        def _():
            rows_pair_b[n].start()

        @pl.when(jnp.logical_and(first, clean))
        def _():
            rows_pair[n].start()

    loads = {}

    def load_weights(j):
        slab_in = w_in_s.shape[0]
        for n in range(count):
            at = tuple((n >> b) & 1 for b in range(bits - 1, -1, -1))
            for block in range(2):
                cols = slice(block * half_in + j * third, block * half_in + (j + 1) * third)
                copy = net.local(w_in.at[at + (slice(None), cols)], w_vm.at[n * slab_in : (n + 1) * slab_in, cols])
                copy.start()
                loads.setdefault(j, []).append(copy)

    def norm(value):
        normed, _ = norm_stats(value.astype(F32))
        return (normed * vec[0:1, :width] + vec[1:2, :width]).astype(BF16)

    def zeros(n, at, size):
        for ref in (k, v, a):
            ref[n, at : at + size, :] = jnp.zeros((size, width), BF16)

    def norms():
        def step(n, carry):
            zeros(n, win + rows, 2 * HALO)
            zeros(n, lay["used"] - HALO, lay["keys"] - lay["used"] + HALO)

            @pl.when(clean)
            def _():
                zeros(n, lay["noisy"] + HALO, rows)

            @pl.when(first)
            def _():
                zeros(n, 0, win)

            a[n, pl.ds(own_at, rows), :] = norm(x[n])
            a[n, pl.ds(halo_at, HALO), :] = norm(xc[n, win:, :])
            return carry

        lax.fori_loop(0, micro, step, 0)

    def own_rows(j):
        for load in loads[j]:
            load.wait()

        def step(n, carry):
            act = jnp.concatenate([a[n, pl.ds(own_at, rows), :], a[n, pl.ds(halo_at, HALO), :]], axis=0)
            for block in range(2):
                qkv_columns(
                    lay, n, act, ((0, rows, own_at), (rows, HALO, halo_at)), win, block * half_in + j * third, third,
                    w_vm, vec[2:3, : 3 * width], cos, sin, q, k, v,
                )
            return carry

        lax.fori_loop(0, micro, step, 0)

    def key_rows(n):
        def section(value, at):
            a[n, at : at + value.shape[0], :] = act = norm(value)
            for col in range(width, 3 * width, 384):
                qkv_columns(
                    lay, n, act, ((0, value.shape[0], at),), at, col, 384, w_vm, vec[2:3, : 3 * width], cos, sin, q, k, v
                )

        @pl.when(noisy)
        def _():
            section(xb[n], win)

        @pl.when(second)
        def _():
            for m in range(micro):

                @pl.when(n == m)
                def _(m=m):
                    rows_pair[m].wait_recv()

            section(xc[n, :win, :], 0)

        for store in stores_of(n):
            store.start()

    first_store = net.local_used
    net.local_used += 4 * micro

    def stores_of(n):
        return [
            pltpu.make_async_copy(here.at[n], there.at[n], sems.at[first_store + 4 * n + m])
            for m, (here, there) in enumerate(((q, q_out), (k, k_out), (v, v_out), (a, a_out)))
        ]

    def serve(token):
        if token in chunks:
            chunks[token].advance()
        elif len(token) == 2:
            {"R": rows_start, "P": pass_on, "L": load_weights, "O": own_rows}[token[0]](int(token[1]))
        else:
            {"E": edge.start, "W": edge.wait_recv, "T": tables, "V": vectors, "H": norms}[token]()

    ahead, *after = [part.split() for part in " ".join(FRONT_ORDER).split("A")]
    for token in ahead:
        serve(token)

    quads = width // (QUAD * HD)
    assert micro * quads == len(after)

    def step(index, carry):
        n, h = index // quads, index % quads

        @pl.when(h == 0)
        def _():
            key_rows(n)
            make_bias(lay, n, codes, queries, biases)

        cols = pl.ds(pl.multiple_of(h * QUAD * HD, QUAD * HD), QUAD * HD)
        def serve_all():
            for at, tokens in enumerate(after):
                if tokens:

                    @pl.when(index == at)
                    def _(tokens=tokens):
                        for token in tokens:
                            serve(token)

        attend(lay, n, cols, q, k, v, o, lse, index, biases)
        serve_all()
        return carry

    lax.fori_loop(0, micro * quads, step, 0)
    last = [net.local(o, o_out), net.local(lse, lse_out)]
    for store in last:
        store.start()
    while any(chunk.at <= len(chunk.stages) for chunk in chunks.values()):
        for chunk in chunks.values():
            chunk.advance()
    for chunk in chunks.values():
        chunk.finish()
    for store in stores_of(0) + stores_of(1) + last:
        store.wait()
    edge.wait_send()

    @pl.when(clean)
    def _():
        for n in range(micro):
            rows_across[n].wait_send()

    @pl.when(first)
    def _():
        for n in range(micro):
            rows_pair[n].wait_send()


def gelu_both(u):
    scale = 0.7978845608028654
    square = u * u
    inner = scale * u * (1.0 + 0.044715 * square)
    th = jnp.tanh(inner)
    plus = 0.5 * (1.0 + th)
    slope = plus + 0.5 * u * (1.0 - th * th) * (scale * (1.0 + 3 * 0.044715 * square))
    return (u * plus).astype(BF16), slope


def mlp_kernel(
    o, x, dy, w_out, vec, w_up, b_up, w_down,
    out_rows, dx2_out, do_out, g_w_out, g_w_up, g_b_up, g_w_down, g_vec,
    mid, a2, a2t, inv, acc_out, acc_da,
):
    step = pl.program_id(0)
    last = pl.num_programs(0) - 1
    width = x.shape[1]
    b_out, gain, shift, b_down = (vec[r : r + 1, :width] for r in (3, 4, 5, 7))

    @pl.when(step == 0)
    def _():
        value = x[...].astype(F32) + dot(o[...], w_out[...]) + b_out
        mid[...] = value
        normed, inverse = norm_stats(value)
        inv[...] = inverse
        a = (normed * gain + shift).astype(BF16)
        a2[...] = a
        a2t[...] = jnp.transpose(a)
        acc_out[...] = jnp.zeros_like(acc_out)
        acc_da[...] = jnp.zeros_like(acc_da)

    g, slope = gelu_both(dot(a2[...], w_up[...]) + b_up[6:7, :])
    acc_out[...] += dot(g, w_down[...])
    du32 = dot_nt(dy[...], w_down[...]) * slope
    du = du32.astype(BF16)
    g_b_up[...] = jnp.broadcast_to(jnp.sum(du.astype(F32), axis=0, keepdims=True), g_b_up.shape)
    acc_da[...] += dot_nt(du, w_up[...])
    g_w_down[...] = dot_tn(g, dy[...]).astype(BF16)
    g_w_up[...] = dot(a2t[...], du).astype(BF16)

    @pl.when(step == last)
    def _():
        dyf = dy[...].astype(F32)
        out_rows[...] = (mid[...] + acc_out[...] + b_down).astype(BF16)
        inverse = inv[...]
        value = mid[...]
        normed = (value - jnp.mean(value, axis=-1, keepdims=True)) * inverse
        da = acc_da[...]
        dx2 = dyf + norm_back(da, normed, inverse, gain)
        dx2_out[...] = dx2
        dp = dx2.astype(BF16)
        do_out[...] = dot_nt(dp, w_out[...]).astype(BF16)
        g_w_out[...] = dot_tn(o[...], dp).astype(BF16)
        g_vec[...] = jnp.concatenate(
            [
                jnp.sum(dyf, axis=0, keepdims=True),
                jnp.sum(da * normed, axis=0, keepdims=True),
                jnp.sum(da, axis=0, keepdims=True),
                jnp.sum(dp.astype(F32), axis=0, keepdims=True),
                jnp.zeros((4, dyf.shape[1]), F32),
            ],
            axis=0,
        )


def qkv_back_kernel(lay, role, a, dq, dk, dv, w, da_own, da_main, da_win, g_w, g_b, g_acc):
    width = dq.shape[2]
    rows, win = lay["rows"], lay["win"]
    noisy, second, own_at, halo_at = places(lay, role)

    @pl.when(pl.program_id(0) == 0)
    def _():
        g_acc[...] = jnp.zeros_like(g_acc)
        g_b[...] = jnp.zeros_like(g_b)

    def column_sums(col, value):
        g_b[0:1, col : col + width] += jnp.sum(value.astype(F32), axis=0, keepdims=True)

    def section(parts, query):
        def take(ref):
            return jnp.concatenate([ref[0, pl.ds(at, count), :] for at, count in parts], axis=0)

        at_t = jnp.transpose(take(a))
        key = take(dk)
        value = take(dv)
        g_acc[:, width : 2 * width] += dot(at_t, key)
        g_acc[:, 2 * width :] += dot(at_t, value)
        column_sums(width, key)
        column_sums(2 * width, value)
        total = dot_nt(key, w[:, width : 2 * width]) + dot_nt(value, w[:, 2 * width :])
        if query is not None:
            g_acc[:, :width] += dot(at_t[:, : query.shape[0]], query)
            column_sums(0, query)
            first = total[: query.shape[0]] + dot_nt(query, w[:, :width])
            return first, total[query.shape[0] :]
        return total

    own, near = section(((own_at, rows), (halo_at, HALO)), dq[0])
    da_own[0] = own
    da_win[0, win:, :] = near.astype(BF16)

    @pl.when(noisy)
    def _():
        da_main[0] = section(((win, rows),), None).astype(BF16)

    @pl.when(second)
    def _():
        da_win[0, :win, :] = section(((0, win),), None).astype(BF16)

    @pl.when(pl.program_id(0) == pl.num_programs(0) - 1)
    def _():
        g_w[...] = g_acc[...].astype(BF16)


def final_kernel(x, da, extra, dx2, gain, grad_in, g_vec):
    value = x[...].astype(F32)
    normed, inverse = norm_stats(value)
    grad = da[...] + extra[...].astype(F32)
    grad_in[...] = dx2[...] + norm_back(grad, normed, inverse, gain[...])

    @pl.when(pl.program_id(0) == 0)
    def _():
        g_vec[...] = jnp.zeros_like(g_vec)

    g_vec[0:1, :] += jnp.sum(grad * normed, axis=0, keepdims=True)
    g_vec[1:2, :] += jnp.sum(grad, axis=0, keepdims=True)


def add_to(ref, at, value):
    ref[at] = (ref[at].astype(F32) + value.astype(F32)).astype(BF16)


def for_all(bits, body):
    if bits == 0:
        body(())
        return

    def step(n, carry):
        body(tuple((n // (1 << b)) % 2 for b in range(bits - 1, -1, -1)))
        return carry

    lax.fori_loop(0, 1 << bits, step, 0)


BACK_ORDER = (
    "S s S s",
    "u0 d0 S s",
    "d0 S s u1",
    "u0 d1 S s",
    "d1 S s d2",
    "d0 u0 u2 E",
    "o u2 d0 u1",
    "e d2 d1 u0",
    "o X e A",
    "A A u2 u0",
    "d2 A d1 P0",
    "u1 A o A",
    "u2 T e d2",
    "P1 G0 i0 o",
    "G1 i1 Y0 i0",
    "e d2 i1 G2",
    "i2 N i0 d0",
    "o d1 i2 i1",
    "Y1 N e N",
    "d2 N l i0",
    "i2 l l",
)
BACK_BITS = {
    "u0": ((0, 1, 2), True),
    "u1": ((1, 2, 0), False),
    "u2": ((0, 1, 2), False),
    "d0": ((0, 1, 2), False),
    "d1": ((0, 2, 1), False),
    "d2": ((0, 1, 2), False),
    "o": ((0, 1, 2), False),
    "i0": ((1, 2, 0), False),
    "i1": ((0, 1, 2), False),
    "i2": ((0, 1, 2), False),
}


class Reduce:
    def __init__(self, net, acc, recvs, out, rows, cols, order, over_x):
        bits, self.net, self.at, self.sent = net.bits, net, 0, False
        pair, across = {"seq": other(net.me, 0)}, {"seq": other(net.me, 1)}
        recvs = list(recvs)
        part = (slice(None), slice(None))
        begin, size = rows
        tail = tail_half = (pl.ds(begin, size), cols)
        self.acc, self.steps = acc, [None]
        if over_x:
            piece = size // 2
            part = (pl.ds(pl.multiple_of(net.x * piece, HALO), piece), slice(None))
            away = (pl.ds(pl.multiple_of((1 - net.x) * piece, HALO), piece), slice(None))
            tail = (pl.ds(pl.multiple_of(begin + net.x * piece, HALO), piece), cols)
            got_x = recvs.pop(0)

            def add_x():
                for_all(bits, lambda at: add_to(acc, at + part, got_x[at]))

            self.steps.append((net.copy(acc.at[(slice(None),) * bits + away], got_x, across), add_x))
        done = []
        for b in order if len(order) == bits else range(bits):
            got = recvs.pop(0)

            def index(mine, rest, b=b, done=tuple(done)):
                rest = iter(rest)
                return tuple(
                    mine if p == b else bit_of(net.f, p) if p in done else next(rest) for p in range(bits - 1, -1, -1)
                )

            left = bits - 1 - len(done)

            def add_bit(got=got, b=b, index=index, left=left):
                for_all(left, lambda at: add_to(acc, index(bit_of(net.f, b), at) + part, got[at]))

            src = acc.at[index(1 - bit_of(net.f, b), (slice(None),) * left) + part]
            self.steps.append((net.copy(src, got, {"fsdp": other(net.f, b)}), add_bit))
            done.append(b)
        own = tuple(bit_of(net.f, n) for n in range(bits - 1, -1, -1))
        if over_x:
            before = self.steps[-1][1]

            def keep():
                before()
                out[tail] = acc[own + part]

            self.steps[-1] = (self.steps[-1][0], keep)
            self.steps.append((net.copy(out.at[tail], out.at[tail], across), lambda: None))
        else:
            got_last = recvs.pop(0)

            def last():
                out[tail] = (acc[own].astype(F32) + got_last[...].astype(F32)).astype(BF16)

            self.steps.append((net.copy(acc.at[own], got_last, across), last))
        self.steps.append((net.copy(out.at[tail_half], out.at[tail_half], pair), lambda: None))

    def feed(self, theirs, get):
        def mine():
            for_all(self.net.bits, lambda at: add_to(self.acc, at, get(at)))

        self.steps[0] = (self.net.copy(theirs, self.acc, {"seq": other(self.net.me, 0)}), mine)

    def open(self):
        return self.at <= len(self.steps)

    def advance(self):
        if not self.open():
            return
        if self.at > 0:
            copy, then = self.steps[self.at - 1]
            copy.wait_recv()
            then()
        if self.at < len(self.steps):
            self.steps[self.at][0].start()
        self.at += 1

    def finish(self):
        while self.open():
            self.advance()
        for copy, _ in self.steps[1 if self.sent else 0 :]:
            copy.wait_send()


class SumAll:
    def __init__(self, net, value, recvs):
        self.value, self.recvs, self.at = value, recvs, 0
        devices = [{"seq": other(net.me, b)} for b in range(2)]
        devices += [{"fsdp": other(net.f, b)} for b in range(net.bits)]
        self.copies = []
        for n, device in enumerate(devices):
            src = value if n == 0 else recvs.at[len(devices) + n - 1]
            self.copies.append(net.copy(src, recvs.at[n], device))

    def open(self):
        return self.at <= len(self.copies)

    def advance(self):
        count = len(self.copies)
        if not self.open():
            return
        if self.at > 0:
            n = self.at - 1
            self.copies[n].wait_recv()
            held = self.value[...] if n == 0 else self.recvs[count + n - 1]
            self.recvs[count + n] = held + self.recvs[n]
        if self.at < count:
            self.copies[self.at].start()
        self.at += 1

    def finish(self):
        while self.open():
            self.advance()
        for copy in self.copies:
            copy.wait_send()
        return self.recvs[2 * len(self.copies) - 1]


def back_kernel(
    lay, bits, codes, queries, lse, cos, sin, vec, x, o,
    dy, q, k, v, a, w_in, w_out, w_up, w_down,
    out_rows, grad_in, f_in_out, f_out_out, f_up_out, f_down_out, sums_out, late_out,
    do, recv_parts, rwin,
    acc_in, acc_out, acc_up, acc_down, r_in, r_out, r_up, r_down, f_in, f_out, f_up, f_down,
    sums, sums_recv, late, late_recv, send, recv, sems, *biases,
):
    rows, win, keys = lay["rows"], lay["win"], lay["keys"]
    micro, width = x.shape[0], x.shape[2]
    total = micro * rows
    hidden = vec.shape[1]
    qw = QUAD * HD
    quads = width // qw
    net = Net(bits, send, recv, sems)
    where_am = noisy, second, own_at, halo_at = places(lay, (net.x, net.core))
    first, clean = jnp.logical_not(second), jnp.logical_not(noisy)
    gain = vec[0:1, :width]
    net.barrier()
    every = list(itertools.product(range(2), repeat=bits))
    count = len(every)
    pair, across = {"seq": other(net.me, 0)}, {"seq": other(net.me, 1)}
    slab_down = f_down.shape[0]
    steps = slab_down // 128
    share = count // 2
    wide = share * 128
    whole_index = (slice(None),) * bits
    here, there = net.core, 1 - net.core

    def columns(begin, size):
        return (slice(None), pl.ds(pl.multiple_of(begin, 128), size))

    @pl.when(noisy)
    def _():
        recv_parts[...] = jnp.zeros_like(recv_parts)

    sums[...] = jnp.zeros_like(sums)

    def feed_forward(dyv, wu, wd, w_ov, mid, a2, a2t, inv, acc_y, acc_da, gv, duv, gd, gu, gu_out, sem_w, sem_m):
        block = total // 4

        def loads(index):
            j, h = index // 2, index % 2
            slot = index % 2
            copies = []
            for n in range(share):
                at = pl.multiple_of((h * share + n) * slab_down + j * 128, 128)
                part = pl.ds(n * 128, 128)
                copies.append(pltpu.make_async_copy(w_up.at[:, pl.ds(at, 128)], wu.at[slot, :, part], sem_w.at[slot, 2 * n]))
                copies.append(pltpu.make_async_copy(w_down.at[pl.ds(at, 128), :], wd.at[slot, part, :], sem_w.at[slot, 2 * n + 1]))
            return copies

        first_loads = [pltpu.make_async_copy(w_out, w_ov, sem_m.at[0]), pltpu.make_async_copy(dy, dyv, sem_m.at[1])]
        for load in first_loads + loads(0):
            load.start()
        flat = lambda ref: ref[...].reshape(total, width)
        b_out, gain2, shift2, b_down = (vec[r : r + 1, :width] for r in (3, 4, 5, 7))
        first_loads[0].wait()
        def part_rows(n):
            per = rows // block
            return n // per, pl.ds(pl.multiple_of((n % per) * block, block), block)

        def open_step(n, carry):
            span = pl.ds(pl.multiple_of(n * block, block), block)
            m, sub = part_rows(n)
            value = x[m, sub, :].astype(F32) + dot(o[m, sub, :], w_ov[...]) + b_out
            mid[span, :] = value
            normed, inverse = norm_stats(value)
            inv[span, :] = inverse
            act = (normed * gain2 + shift2).astype(BF16)
            a2[span, :] = act
            a2t[:, span] = jnp.transpose(act)
            return carry

        lax.fori_loop(0, total // block, open_step, 0)
        acc_y[...] = jnp.zeros_like(acc_y)
        acc_da[...] = jnp.zeros_like(acc_da)
        first_loads[1].wait()

        away = columns(there * (width // 2), width // 2)
        near = columns(here * (width // 2), width // 2)
        for j in range(steps):
            chunks["u%d" % j].feed(gu.at[j, there], lambda at, j=j: gu[(j, here) + at])
            chunks["d%d" % j].feed(gd.at[(j,) + whole_index + away], lambda at, j=j: gd[(j,) + at + near])

        def serve_all(index, part):
            for at, tokens in enumerate(in_feed):
                if tokens[part]:

                    @pl.when(index == at)
                    def _(tokens=tokens[part]):
                        for token in tokens:
                            chunks[token].advance()

        def step(index, carry):
            j, h = index // 2, index % 2
            slot = index % 2

            @pl.when(index + 1 < 2 * steps)
            def _():
                for load in loads(index + 1):
                    load.start()

            for load in loads(index):
                load.wait()
            at = [pl.ds(pl.multiple_of((h * share + n) * slab_down + j * 128, 128), 128) for n in range(share)]
            bias = jnp.concatenate([vec[6:7, here_at] for here_at in at], axis=1)
            w_u, w_d = wu[slot], wd[slot]

            def rows_step(r, row):
                for sub in range(2):
                    span = pl.ds(pl.multiple_of((2 * r + sub) * block, block), block)
                    g, slope = gelu_both(dot(a2[span, :], w_u) + bias)
                    gv[span, :] = g
                    acc_y[span, :] += dot(g, w_d)
                    du = (dot_nt(dyv[span, :], w_d) * slope).astype(BF16)
                    duv[span, :] = du
                    row += jnp.sum(du.astype(F32), axis=0, keepdims=True)
                    acc_da[span, :] += dot_nt(du, w_u)
                return row

            row = lax.fori_loop(0, total // (2 * block), rows_step, jnp.zeros((1, wide), F32))
            for n in range(share):
                sums[6:7, at[n]] = row[:, n * 128 : n * 128 + 128]
            serve_all(index, 0)
            slab = width // count

            def half_step(m, carry):
                part = pl.ds(pl.multiple_of(m * (wide // 2), 128), wide // 2)
                g_d = dot_tn(gv[:, part], dyv[...]).astype(BF16)
                for n, low in enumerate(itertools.product(range(2), repeat=bits - 2)):
                    gd[(j, h, m) + low] = g_d[n * 128 : n * 128 + 128]
                g_u = dot(a2t[pl.ds(pl.multiple_of(m * (width // 2), 128), width // 2), :], duv[...]).astype(BF16)
                for n, low in enumerate(itertools.product(range(2), repeat=bits - 1)):
                    gu[(j, h, m) + low] = g_u[n * slab : n * slab + slab]
                return carry

            lax.fori_loop(0, 2, half_step, 0)
            serve_all(index, 1)
            return carry

        lax.fori_loop(0, 2 * steps, step, 0)
        def close_step(n, carry):
            span = pl.ds(pl.multiple_of(n * block, block), block)
            m, sub = part_rows(n)
            dyf = dyv[span, :].astype(F32)
            value = mid[span, :]
            a2[span, :] = (value + acc_y[span, :] + b_down).astype(BF16)
            normed = (value - jnp.mean(value, axis=-1, keepdims=True)) * inv[span, :]
            da = acc_da[span, :]
            dx2 = dyf + norm_back(da, normed, inv[span, :], gain2)
            acc_da[span, :] = dx2
            dp = dx2.astype(BF16)
            dyv[span, :] = dp
            do[m, sub, :] = dot_nt(dp, w_ov[...]).astype(BF16)
            for r, part in ((7, dyf), (4, da * normed), (5, da), (3, dp.astype(F32))):
                sums[r : r + 1, :width] += jnp.sum(part, axis=0, keepdims=True)
            return carry

        lax.fori_loop(0, total // block, close_step, 0)
        puts = []
        for n in range(micro):
            part = pl.ds(n * rows, rows)
            puts.append(pltpu.make_async_copy(acc_da.at[part, :], grad_in.at[n], sem_m.at[2 + 2 * n]))
            puts.append(pltpu.make_async_copy(a2.at[part, :], out_rows.at[n], sem_m.at[3 + 2 * n]))
        for put in puts:
            put.start()
        g_o = dot_tn(flat(o), dyv[...]).astype(BF16)
        slab = width // count
        for n, idx in enumerate(every):
            for c in range(2):
                gu_out[(c,) + idx] = g_o[n * slab : n * slab + slab, c * (width // 2) : (c + 1) * (width // 2)]
        chunks["o"].feed(gu_out.at[there], lambda at: gu_out[(here,) + at])
        for token in after_feed:
            chunks[token].advance()
        for name, chunk in chunks.items():
            if name[0] in "udo":
                assert chunk.at >= 2
                chunk.steps[0][0].wait_send()
                chunk.sent = True
        for put in puts:
            put.wait()

    half_out = width // 2
    slab = width // count
    chunks = {}
    for j in range(steps):
        chunks["u%d" % j] = Reduce(net, acc_up[j], r_up[j], f_up.at[j], (0, slab),
                                   columns(here * wide, wide)[1], *BACK_BITS["u%d" % j])
        chunks["d%d" % j] = Reduce(net, acc_down[j], r_down[j], f_down, (j * 128, 128),
                                   columns(here * half_out, half_out)[1], *BACK_BITS["d%d" % j])
    chunks["o"] = Reduce(net, acc_out, r_out, f_out, (0, slab), columns(here * half_out, half_out)[1], *BACK_BITS["o"])
    chunks["e"] = SumAll(net, sums, sums_recv)
    chunks["l"] = SumAll(net, late, late_recv)
    edge_at = pl.multiple_of((1 - net.core) * (rows - HALO), HALO)
    tokens = " ".join(BACK_ORDER).split()
    feed_end, free, turn = tokens.index("E"), tokens.index("X"), tokens.index("T")
    halves = lambda text, outer, inner: [[half.split() for half in part.split(inner)] for part in text.split(outer)]
    (_,), *in_feed = halves(" ".join(tokens[:feed_end]), "S", "s")
    after_feed = tokens[feed_end + 1 : free]
    early_tokens, *in_attention = [part.split() for part in " ".join(tokens[free + 1 : turn]).split("A")]
    after_attention = tokens[turn + 1 :]
    assert len(in_feed) == 2 * steps and len(in_attention) == micro * quads

    pl.run_scoped(
        feed_forward,
        pltpu.VMEM((total, width), BF16), pltpu.VMEM((2, width, wide), BF16), pltpu.VMEM((2, wide, width), BF16),
        pltpu.VMEM((width, width), BF16), pltpu.VMEM((total, width), F32), pltpu.VMEM((total, width), BF16),
        pltpu.VMEM((width, total), BF16), pltpu.VMEM((total, 1), F32), pltpu.VMEM((total, width), F32),
        pltpu.VMEM((total, width), F32), pltpu.VMEM((total, wide), BF16), pltpu.VMEM((total, wide), BF16),
        pltpu.VMEM((steps,) + (2,) * bits + (128, width), BF16),
        pltpu.VMEM((steps, 2) + (2,) * bits + (width // count, wide), BF16),
        pltpu.VMEM((2,) + (2,) * bits + (width // count, half_out), BF16),
        pltpu.SemaphoreType.DMA((2, 2 * share)), pltpu.SemaphoreType.DMA((2 + 2 * micro,)),
    )

    def backward(dq, dk, dv, w_vm, gin, parts, dwin, sem_l):
        load_w = pltpu.make_async_copy(w_in, w_vm, sem_l.at[0])
        load_w.start()
        p1 = [net.copy(dwin.at[n], rwin.at[n], pair) for n in range(micro)]
        p2 = [net.copy(parts.at[n], recv_parts.at[n], across) for n in range(micro)]
        third = 3 * width // 6
        slab_in = width // count
        for j in range(3):
            chunks["i%d" % j] = Reduce(net, acc_in[j], r_in[j], f_in, (0, slab_in),
                                       columns(here * 3 * third + j * third, third)[1], *BACK_BITS["i%d" % j])
            chunks["i%d" % j].feed(gin.at[j, there], lambda at, j=j: gin[(j, here) + at])

        def pass_on(n):
            p1[n].wait_recv()

            @pl.when(noisy)
            def _():
                @pl.when(first)
                def _():
                    add_to(parts, (n, slice(rows - win, rows), slice(None)), rwin[n, :win, :])

                p2[n].start()

        def attention(qb, kb, vb, dk_acc, dv_acc, load_sems):
            blocks = ((q, qb), (k, kb), (v, vb))

            def loads(index):
                n, h = index // quads, index % quads
                cols = pl.ds(pl.multiple_of(h * qw, qw), qw)
                slot = index % 2
                return [
                    pltpu.make_async_copy(src.at[n, :, cols], dst.at[slot], load_sems.at[slot, m])
                    for m, (src, dst) in enumerate(blocks)
                ]

            for load in loads(0):
                load.start()
            load_w.wait()

            def partial(n):
                key = jnp.concatenate([dk[n, :win, :], dk[n, pl.ds(halo_at, HALO), :]], axis=0)
                value = jnp.concatenate([dv[n, :win, :], dv[n, pl.ds(halo_at, HALO), :]], axis=0)
                w_key, w_value = w_vm[:, width : 2 * width], w_vm[:, 2 * width :]
                dwin[n] = (dot_nt(key, w_key) + dot_nt(value, w_value)).astype(BF16)
                for m in range(micro):

                    @pl.when(n == m)
                    def _(m=m):
                        p1[m].start()

                @pl.when(noisy)
                def _():
                    main = slice(win, win + rows)
                    parts[n] = (dot_nt(dk[n, main, :], w_key) + dot_nt(dv[n, main, :], w_value)).astype(BF16)

            def serve(token):
                if token[0] == "P":
                    pass_on(int(token[1]))
                else:
                    chunks[token].advance()

            for token in early_tokens:
                serve(token)

            def serve_all(index):
                for at, tokens in enumerate(in_attention):
                    if tokens:

                        @pl.when(index == at)
                        def _(tokens=tokens):
                            for token in tokens:
                                serve(token)

            def step(index, carry):
                n, h = index // quads, index % quads
                slot = index % 2

                @pl.when(index + 1 < micro * quads)
                def _():
                    for load in loads(index + 1):
                        load.start()

                @pl.when(h == 0)
                def _():
                    make_bias(lay, n, codes, queries, biases)

                for load in loads(index):
                    load.wait()
                cols = pl.ds(pl.multiple_of(h * qw, qw), qw)
                attend_back(
                    lay, slot, slice(None), qb, kb, vb, n, cols, o, do, lse, index, cos, sin,
                    n, h * qw, dq, dk, dv, dk_acc, dv_acc, biases,
                )
                @pl.when(h == quads - 1)
                def _():
                    partial(n)

                serve_all(index)
                return carry

            lax.fori_loop(0, micro * quads, step, 0)

        pl.run_scoped(
            attention,
            pltpu.VMEM((2, rows, qw), BF16), pltpu.VMEM((2, keys, qw), BF16), pltpu.VMEM((2, keys, qw), BF16),
            pltpu.VMEM((keys, qw), F32), pltpu.VMEM((keys, qw), F32),
            pltpu.SemaphoreType.DMA((2, 3)),
        )

        def projection(av, at_all, at_own, dxv, sem_a, sem_x):
            load_x = pltpu.make_async_copy(grad_in, dxv, sem_x.at[0])
            pltpu.make_async_copy(a.at[0], av, sem_a.at[0]).start()
            load_x.start()
            def turn_step(n, carry):
                pltpu.make_async_copy(a.at[n], av, sem_a.at[n]).wait()
                at_all[n] = jnp.transpose(av[...])
                at_own[n] = jnp.transpose(av[pl.ds(own_at, rows), :])

                @pl.when(n + 1 < micro)
                def _():
                    pltpu.make_async_copy(a.at[n + 1], av, sem_a.at[n + 1]).start()

                return carry

            lax.fori_loop(0, micro, turn_step, 0)
            late[...] = jnp.zeros_like(late)
            def gradient(j):
                for block in range(2):
                    col = block * 3 * third + j * third
                    source, lhs = ((dq, at_own), (dk, at_all), (dv, at_all))[col // width]
                    inside = slice(col % width, col % width + third)
                    part = width // 2

                    def rows_step(m, carry):
                        grad = jnp.zeros((part, third), F32)
                        for n in range(micro):
                            grad += dot(lhs[n, pl.ds(pl.multiple_of(m * part, 128), part), :], source[n, :, inside])
                        for low, at in enumerate(itertools.product(range(2), repeat=bits - 1)):
                            gin[(j, block, m) + at] = grad[low * slab_in : low * slab_in + slab_in].astype(BF16)
                        return carry

                    lax.fori_loop(0, 2, rows_step, 0)
                    ones = jnp.zeros((8, third), F32)
                    for n in range(micro):
                        rhs = source[n, :, inside]
                        ones += dot(jnp.ones((8, rhs.shape[0]), BF16), rhs)
                    row = 2 + col // width
                    late[row : row + 1, inside] = ones[0:1]

            def settle(n):
                @pl.when(clean)
                def _():
                    p2[n].wait_recv()

                    @pl.when(first)
                    def _():
                        add_to(recv_parts, (n, slice(rows - win, rows), slice(None)), rwin[n, :win, :])

                add_to(recv_parts, (n, pl.ds(edge_at, HALO), slice(None)), rwin[n, win:, :])

            def store(m):
                span = pl.ds(pl.multiple_of((m % 2) * (rows // 2), TILE), rows // 2)
                return pltpu.make_async_copy(dxv.at[m // 2, span, :], grad_in.at[m // 2, span, :], sem_x.at[1 + m])

            def norm_part(m):
                n, part = m // 2, m % 2
                size = rows // 2
                span = pl.ds(pl.multiple_of(part * size, TILE), size)
                mine_rows = pl.ds(pl.multiple_of(own_at + part * size, HALO), size)
                da = dot_nt(dq[n, span, :], w_vm[:, :width])
                da += dot_nt(dk[n, mine_rows, :], w_vm[:, width : 2 * width])
                da += dot_nt(dv[n, mine_rows, :], w_vm[:, 2 * width :])
                da += recv_parts[n, span, :].astype(F32)
                normed, inverse = norm_stats(x[n, span, :].astype(F32))
                dxv[n, span, :] += norm_back(da, normed, inverse, gain)
                late[0:1, :] += jnp.sum(da * normed, axis=0, keepdims=True)
                late[1:2, :] += jnp.sum(da, axis=0, keepdims=True)
                store(m).start()

            def serve(token):
                if token in chunks:
                    chunks[token].advance()
                else:
                    {"P": pass_on, "Y": settle, "G": gradient}[token[0]](int(token[1]))

            groups = [part.split() for part in " ".join(after_attention).split("N")]
            assert len(groups) == 1 + 2 * micro
            for token in groups[0]:
                serve(token)
            load_x.wait()

            def norm_step(m, carry):
                norm_part(m)
                for at, tokens in enumerate(groups[1:-1]):
                    if tokens:

                        @pl.when(m == at)
                        def _(tokens=tokens):
                            for token in tokens:
                                serve(token)

                return carry

            lax.fori_loop(0, 2 * micro, norm_step, 0)
            for token in groups[-1]:
                serve(token)
            while any(chunk.open() for chunk in chunks.values()):
                for chunk in chunks.values():
                    chunk.advance()
            sums_out[...] = chunks["e"].finish()
            late_out[...] = chunks["l"].finish()
            for name, chunk in chunks.items():
                if name not in "el":
                    chunk.finish()
            puts = [net.local(src, dst) for src, dst in ((f_in, f_in_out), (f_out, f_out_out), (f_down, f_down_out))]
            for j in range(steps):
                for n in range(count):
                    puts.append(net.local(
                        f_up.at[j, :, pl.ds(n * 128, 128)], f_up_out.at[:, pl.ds(n * slab_down + j * 128, 128)]
                    ))
            for put in puts:
                put.start()
            for put in puts:
                put.wait()
            for m in range(2 * micro):
                store(m).wait()
            for copy in p1:
                copy.wait_send()

            @pl.when(noisy)
            def _():
                for copy in p2:
                    copy.wait_send()

        pl.run_scoped(
            projection,
            pltpu.VMEM((keys, width), BF16), pltpu.VMEM((micro, width, keys), BF16),
            pltpu.VMEM((micro, width, rows), BF16), pltpu.VMEM((micro, rows, width), F32),
            pltpu.SemaphoreType.DMA((micro,)), pltpu.SemaphoreType.DMA((1 + 2 * micro,)),
        )

    third = 3 * width // 6
    pl.run_scoped(
        backward,
        pltpu.VMEM((micro, rows, width), BF16), pltpu.VMEM((micro, keys, width), BF16),
        pltpu.VMEM((micro, keys, width), BF16), pltpu.VMEM((width, 3 * width), BF16),
        pltpu.VMEM((3, 2) + (2,) * bits + (width // count, third), BF16),
        pltpu.VMEM((micro, rows, width), BF16), pltpu.VMEM((micro, win + HALO, width), BF16),
        pltpu.SemaphoreType.DMA((1,)),
    )


def finish_kernel(sizes, sums, late, *refs):
    given, results, vectors, rest = refs[:6], refs[6:12], refs[12:20], refs[20:]
    held, wide, sem_in, sem_out = rest[:6], rest[6:10], rest[10], rest[11]
    loads = [pltpu.make_async_copy(src, dst, sem_in.at[n]) for n, (src, dst) in enumerate(zip(given, held))]
    stores = [
        pltpu.make_async_copy(src, dst, sem_out.at[n]) for n, (src, dst) in enumerate(zip(held[:2] + wide, results))
    ]
    for load in loads:
        load.start()
    for n in range(2):
        loads[n].wait()
        stores[n].start()
    for n in range(4):
        loads[2 + n].wait()
        wide[n][...] = held[2 + n][...].astype(F32)
        stores[2 + n].start()
    f = lax.axis_index("fsdp")
    width = late.shape[1]
    for r, (size, out) in enumerate(zip(sizes, vectors)):
        if r < 2:
            row = late[r : r + 1, :]
        elif r == 2:
            row = jnp.concatenate([late[m : m + 1, :] for m in range(2, 5)], axis=1)
        else:
            row = sums[r : r + 1, :] if sums.shape[1] == size * (width // sizes[0]) else sums[r : r + 1, :width]
        whole_size = row.shape[1]
        row = jnp.broadcast_to(row, (8, whole_size))
        turned = pltpu.roll(row, lax.rem(whole_size - f * size, whole_size), 1)
        out[...] = turned[0, :size]
    for store in stores:
        store.wait()


def front_remote(
    lay, role, sizes, inputs, segment_ids, block_ids, small, weights, freqs, lse_shape, bias_scratch, spans, attn_flops
):
    micro, rows, width = inputs.shape
    keys, win = lay["keys"], lay["win"]
    bits = lax.axis_size("fsdp").bit_length() - 1
    lanes = -(-max(sizes) // 128) * 128
    full = [like((2,) * bits + p.shape, BF16) for p in weights]
    longest = max(sizes) << bits
    table_rows = win + rows + HALO
    shapes = full + [
        like((micro, rows, width), BF16), like((micro, keys, width), BF16), like((micro, keys, width), BF16),
        like((micro, keys, width), BF16), like((micro, rows, width), BF16), like(lse_shape, F32),
        like((8, longest), F32), like((table_rows, 128), F32), like((table_rows, 128), F32),
        like((micro, keys, 1), F32), like((micro, 8, rows), F32),
    ]
    remote = 3 * micro + 1 + (bits + 2) * 9
    outs = pl.pallas_call(
        functools.partial(front_kernel, lay, bits, sizes),
        in_specs=[VMEM] * 16,
        out_specs=[ANY] * 10 + [VMEM] * 5,
        out_shape=shapes,
        scratch_shapes=[
            pltpu.VMEM((micro, rows, width), BF16), pltpu.VMEM((micro, win + HALO, width), BF16),
            pltpu.VMEM((width, 3 * width), BF16), pltpu.VMEM((micro, rows, width), BF16),
            pltpu.VMEM((micro, keys, width), BF16), pltpu.VMEM((micro, keys, width), BF16),
            pltpu.VMEM((micro, keys, width), BF16), pltpu.VMEM((micro, rows, width), BF16),
            pltpu.VMEM(lse_shape, F32), pltpu.VMEM((2,) * bits + (8, lanes), F32), pltpu.VMEM((8, lanes), F32),
            pltpu.SemaphoreType.DMA((remote,)), pltpu.SemaphoreType.DMA((remote,)),
            pltpu.SemaphoreType.DMA((96,)),
        ] + bias_scratch,
        compiler_params=pltpu.CompilerParams(
            vmem_limit_bytes=VMEM_BYTES, collective_id=0, has_side_effects=True
        ),
        cost_estimate=pl.CostEstimate(flops=2 * attn_flops, bytes_accessed=40 << 20, transcendentals=0),
        name="front",
    )(inputs, segment_ids, block_ids, freqs, *weights, *small)
    joined = [w.reshape((-1, w.shape[-1])) for w in outs[:4]]
    return tuple(joined) + tuple(outs[4:])


def front_native(
    lay, role, sizes, inputs, segment_ids, block_ids, small, weights, freqs, lse_shape, bias_scratch, spans, attn_flops
):
    micro, rows, width = inputs.shape
    keys, win, length = lay["keys"], lay["win"], lay["length"]
    clean, half = role[0], role[1]
    pairs = [(0, 1), (1, 0), (2, 3), (3, 2)]
    xb = lax.ppermute(inputs, "seq", [(2, 0), (3, 1)])
    xmain = jnp.where(clean == 1, inputs, xb)
    edge = jnp.where(half == 0, inputs[:, rows - HALO :], inputs[:, :HALO])
    xc = lax.ppermute(jnp.concatenate([xmain[:, rows - win :], edge], axis=1), "seq", pairs)
    start = half * rows
    edge_at = jnp.where(half == 0, rows, -HALO)
    positions = start + jnp.concatenate([jnp.arange(-win, rows), edge_at + jnp.arange(HALO)])
    turned = positions.astype(F32)[:, None] * freqs
    sine = jnp.sin(turned)
    cos = jnp.cos(turned)
    sin = jnp.where(jnp.arange(128)[None] % HD < HD // 2, -sine, sine)
    code = segment_ids * SEG_STEP + block_ids
    padded = jnp.pad(code, ((0, 0), (win, 0)), constant_values=-1)
    key_codes = lax.dynamic_slice_in_dim(padded, start, win + rows, 1)
    own_code = lax.dynamic_slice_in_dim(code, start, rows, 1)
    own_seg = lax.dynamic_slice_in_dim(segment_ids, start, rows, 1)
    before, after = code[:, rows - HALO : rows], code[:, rows : rows + HALO]
    codes = jnp.concatenate(
        [
            key_codes,
            jnp.where((clean == 1) & (half == 0), after, -1),
            jnp.where((clean == 0) & (half == 1), before, -2),
            jnp.where(clean == 0, own_code, -2),
            jnp.where((clean == 0) & (half == 0), after, -2),
            jnp.full((micro, keys - lay["used"]), -2, jnp.int32),
        ],
        axis=1,
    )[:, :, None].astype(F32)
    queries = jnp.stack([own_seg * SEG_STEP, own_code - (1 - clean), own_code], axis=1)
    queries = jnp.concatenate([queries, jnp.zeros((micro, 5, rows), jnp.int32)], axis=1).astype(F32)
    packed = lax.all_gather(jnp.concatenate(small)[None], "fsdp", axis=0, tiled=True)
    vectors, at = [], 0
    longest = max(sizes) * packed.shape[0]
    for size in sizes:
        one = packed[:, at : at + size].reshape(-1).astype(F32)
        vectors.append(jnp.pad(one, (0, longest - one.shape[0])))
        at += size
    vec = jnp.stack(vectors)
    w_in, w_out, w_up, w_down = (lax.all_gather(p, "fsdp", axis=0, tiled=True) for p in weights)
    per_seq = lambda n, d: pl.BlockSpec((1, n, d), lambda s: (s, 0, 0))
    table_rows = win + rows + HALO
    q, k, v, a = call(
        functools.partial(qkv_kernel, lay), (micro,),
        [SMEM(), per_seq(rows, width), per_seq(rows, width), per_seq(win + HALO, width),
         whole((width, 3 * width)), whole(vec.shape), whole((table_rows, 128)), whole((table_rows, 128))],
        [per_seq(rows, width), per_seq(keys, width), per_seq(keys, width), per_seq(keys, width)],
        [like((micro, rows, width), BF16)] + [like((micro, keys, width), BF16)] * 3,
        [], 2 * micro * rows * width * 3 * width * 2, 20 << 20, "qkv",
    )(role, inputs, xb, xc, w_in, vec, cos, sin)
    qw = QUAD * HD
    quads = width // qw
    quad_block = lambda n: pl.BlockSpec((1, n, qw), lambda s, h: (s, 0, h))
    o, lse = call(
        functools.partial(attend_kernel, lay), (micro, quads),
        [pl.BlockSpec((1, keys, 1), lambda s, h: (s, 0, 0)), pl.BlockSpec((1, 8, rows), lambda s, h: (s, 0, 0)),
         quad_block(rows), quad_block(keys), quad_block(keys)],
        [quad_block(rows), pl.BlockSpec((1,) + lse_shape[1:], lambda s, h: (s * quads + h, 0, 0))],
        [like((micro, rows, width), BF16), like(lse_shape, F32)],
        bias_scratch, 2 * attn_flops, 12 << 20, "attend",
    )(codes, queries, q, k, v)
    return w_in, w_out, w_up, w_down, q, k, v, a, o, lse, vec, cos, sin, codes, queries


def back_remote(
    lay, role, sizes, inputs, cotangent, codes, queries, lse, cos, sin, vec,
    q, k, v, o, a, w_in, w_out, w_up, w_down, bias_scratch, attn_flops,
):
    micro, rows, width = inputs.shape
    keys, win = lay["keys"], lay["win"]
    bits = lax.axis_size("fsdp").bit_length() - 1
    lead = (2,) * bits
    count = 1 << bits
    hidden = w_up.shape[1]
    slab, slab_down = width // count, hidden // count
    third = width // 2
    steps, wide = slab_down // 128, count // 2 * 128

    def bank(name, r, c):
        over_x = BACK_BITS[name][1]
        kept = r // 2 if over_x else r
        over = [pltpu.VMEM(lead[: bits - 1 - b] + (kept, c), BF16) for b in range(bits)]
        ends = [pltpu.VMEM(lead + (kept, c), BF16)] if over_x else []
        return pltpu.VMEM(lead + (r, c), BF16), tuple(ends + over + ([] if over_x else [pltpu.VMEM((r, c), BF16)]))

    acc_in, r_in = zip(*[bank("i%d" % j, slab, third) for j in range(3)])
    acc_out, r_out = bank("o", slab, width // 2)
    acc_up, r_up = zip(*[bank("u%d" % j, slab, wide) for j in range(steps)])
    acc_down, r_down = zip(*[bank("d%d" % j, 128, width // 2) for j in range(steps)])
    stages = 2 + bits
    remote = (7 + 2 * steps) * (bits + 5) + 2 * stages + 4 * micro
    scratch = [
        pltpu.VMEM((micro, rows, width), BF16), pltpu.VMEM((micro, rows, width), BF16),
        pltpu.VMEM((micro, win + HALO, width), BF16),
        acc_in, acc_out, acc_up, acc_down, r_in, r_out, r_up, r_down,
        pltpu.VMEM((slab, 3 * width), BF16), pltpu.VMEM((slab, width), BF16),
        pltpu.VMEM((steps, slab, count * 128), BF16), pltpu.VMEM((slab_down, width), BF16),
        pltpu.VMEM((8, hidden), F32), pltpu.VMEM((2 * stages, 8, hidden), F32),
        pltpu.VMEM((8, width), F32), pltpu.VMEM((2 * stages, 8, width), F32),
        pltpu.SemaphoreType.DMA((remote,)), pltpu.SemaphoreType.DMA((remote,)),
        pltpu.SemaphoreType.DMA((8 + steps * count,)),
    ] + bias_scratch
    out_rows, grad_in, f_in, f_out, f_up, f_down, sums, late = pl.pallas_call(
        functools.partial(back_kernel, lay, bits),
        in_specs=[VMEM] * 8 + [ANY] * 9,
        out_specs=[ANY] * 6 + [VMEM] * 2,
        out_shape=[
            like((micro, rows, width), BF16), like((micro, rows, width), F32), like((slab, 3 * width), BF16),
            like((slab, width), BF16), like((slab, hidden), BF16), like((slab_down, width), BF16),
            like((8, hidden), F32), like((8, width), F32),
        ],
        scratch_shapes=scratch,
        compiler_params=pltpu.CompilerParams(
            vmem_limit_bytes=67043328, collective_id=1, has_side_effects=True
        ),
        cost_estimate=pl.CostEstimate(flops=6 * attn_flops, bytes_accessed=60 << 20, transcendentals=0),
        name="back",
    )(codes, queries, lse, cos, sin, vec, inputs, o, cotangent.reshape(micro * rows, width),
      q, k, v, a, w_in, w_out, w_up, w_down)
    shards = (f_in, f_out, f_up, f_down)
    given = (out_rows, grad_in) + shards
    done = pl.pallas_call(
        functools.partial(finish_kernel, sizes),
        in_specs=[VMEM] * 2 + [ANY] * 6,
        out_specs=[ANY] * 6 + [VMEM] * 8,
        out_shape=[like(out_rows.shape, BF16), like(grad_in.shape, F32)]
        + [like(g.shape, F32) for g in shards] + [like((size,), F32) for size in sizes],
        scratch_shapes=[pltpu.VMEM(g.shape, g.dtype) for g in given] + [pltpu.VMEM(g.shape, F32) for g in shards]
        + [pltpu.SemaphoreType.DMA((6,)), pltpu.SemaphoreType.DMA((6,))],
        compiler_params=pltpu.CompilerParams(vmem_limit_bytes=VMEM_BYTES),
        cost_estimate=pl.CostEstimate(flops=0, bytes_accessed=16 << 20, transcendentals=0),
        name="finish",
    )(sums, late, *given)
    return done[0], done[1], list(done[2:6]), list(done[6:])


def back_native(
    lay, role, sizes, inputs, cotangent, codes, queries, lse, cos, sin, vec,
    q, k, v, o, a, w_in, w_out, w_up, w_down, bias_scratch, attn_flops,
):
    micro, rows, width = inputs.shape
    keys, win = lay["keys"], lay["win"]
    clean, half = role[0], role[1]
    pairs = [(0, 1), (1, 0), (2, 3), (3, 2)]
    fsdp_n = lax.axis_size("fsdp")
    hidden = w_up.shape[1]
    qw = QUAD * HD
    quads = width // qw
    total = micro * rows
    flat = lambda z: z.reshape(total, width)
    chunk = min(512, hidden)
    rows_spec = whole((total, width))
    out_rows, dx2, do, g_w_out, g_w_up, g_b_up, g_w_down, g_mlp = call(
        mlp_kernel, (hidden // chunk,),
        [rows_spec, rows_spec, rows_spec, whole((width, width)), whole(vec.shape),
         pl.BlockSpec((width, chunk), lambda j: (0, j)), pl.BlockSpec((8, chunk), lambda j: (0, j)),
         pl.BlockSpec((chunk, width), lambda j: (j, 0))],
        [rows_spec, rows_spec, rows_spec, whole((width, width)),
         pl.BlockSpec((width, chunk), lambda j: (0, j)), pl.BlockSpec((8, chunk), lambda j: (0, j)),
         pl.BlockSpec((chunk, width), lambda j: (j, 0)), whole((8, width))],
        [like((total, width), BF16), like((total, width), F32), like((total, width), BF16),
         like((width, width), BF16), like((width, hidden), BF16), like((8, hidden), F32),
         like((hidden, width), BF16), like((8, width), F32)],
        [pltpu.VMEM((total, width), F32), pltpu.VMEM((total, width), BF16), pltpu.VMEM((width, total), BF16),
         pltpu.VMEM((total, 1), F32), pltpu.VMEM((total, width), F32), pltpu.VMEM((total, width), F32)],
        2 * total * width * (6 * hidden + 3 * width), 40 << 20, "mlp",
    )(flat(o), flat(inputs), flat(cotangent), w_out, vec, w_up, vec, w_down)

    do = do.reshape(micro, rows, width)
    per_seq = lambda n, d: pl.BlockSpec((1, n, d), lambda s: (s, 0, 0))
    role_spec = SMEM()
    quad_block = lambda n: pl.BlockSpec((1, n, qw), lambda s, h: (s, 0, h))
    code_spec = pl.BlockSpec((1, keys, 1), lambda s, h: (s, 0, 0))
    query_spec = pl.BlockSpec((1, 8, rows), lambda s, h: (s, 0, 0))
    lse_spec = pl.BlockSpec((1,) + lse.shape[1:], lambda s, h: (s * quads + h, 0, 0))
    table = pl.BlockSpec((win + rows + HALO, 128), lambda s, h: (0, 0), pipeline_mode=pl.Buffered(1))
    dq, dk, dv = call(
        functools.partial(attend_back_kernel, lay), (micro, quads),
        [code_spec, query_spec, quad_block(rows), quad_block(keys), quad_block(keys),
         quad_block(rows), quad_block(rows), lse_spec, table, table],
        [quad_block(rows), quad_block(keys), quad_block(keys)],
        [like((micro, rows, width), BF16), like((micro, keys, width), BF16), like((micro, keys, width), BF16)],
        [pltpu.VMEM((keys, qw), F32), pltpu.VMEM((keys, qw), F32)] + bias_scratch,
        5 * attn_flops, 24 << 20, "attend_back",
    )(codes, queries, q, k, v, o, do, lse, cos, sin)

    da_own, da_main, da_win, g_w_in, g_b_in = call(
        functools.partial(qkv_back_kernel, lay), (micro,),
        [role_spec, per_seq(keys, width), per_seq(rows, width), per_seq(keys, width), per_seq(keys, width),
         whole((width, 3 * width))],
        [per_seq(rows, width), per_seq(rows, width), per_seq(win + HALO, width),
         whole((width, 3 * width)), whole((8, 3 * width))],
        [like((micro, rows, width), F32), like((micro, rows, width), BF16), like((micro, win + HALO, width), BF16),
         like((width, 3 * width), BF16), like((8, 3 * width), F32)],
        [pltpu.VMEM((width, 3 * width), F32)], 2 * 2 * micro * rows * width * 3 * width * 2, 40 << 20, "qkv_back",
    )(role, a, dq, dk, dv, w_in)

    from_pair = lax.ppermute(da_win, "seq", pairs).astype(F32)
    from_second = jnp.where(half == 0, from_pair[:, :win], 0.0)
    edge = from_pair[:, win:]
    gap = jnp.zeros((micro, rows - HALO, width), F32)
    edges = jnp.where(
        half == 0, jnp.concatenate([gap, edge], axis=1), jnp.concatenate([edge, gap], axis=1)
    )
    added = jnp.pad(from_second, ((0, 0), (rows - win, 0), (0, 0)))
    to_clean = (jnp.where(clean == 0, da_main.astype(F32), 0.0) + added).astype(BF16)
    from_noisy = lax.ppermute(to_clean, "seq", [(0, 2), (1, 3)])
    extra = jnp.where(clean == 1, from_noisy.astype(F32) + added, 0.0) + edges

    grad_in, g_attn = call(
        final_kernel, (2,),
        [pl.BlockSpec((total // 2, width), lambda i: (i, 0))] * 4 + [whole((1, width))],
        [pl.BlockSpec((total // 2, width), lambda i: (i, 0)), whole((8, width))],
        [like((total, width), F32), like((8, width), F32)], [], 0, 16 << 20, "norm_back",
    )(flat(inputs), flat(da_own), flat(extra), flat(dx2), vec[0:1, :width])

    def scatter(g):
        return lax.psum(lax.psum_scatter(g, "fsdp", scatter_dimension=0, tiled=True), "seq")

    big = [scatter(g).astype(F32) for g in (g_w_in, g_w_out, g_w_up, g_w_down)]
    smalls = [g_attn[0], g_attn[1], g_b_in[0], g_mlp[3], g_mlp[1], g_mlp[2], g_b_up[0], g_mlp[0]]
    pack = jnp.concatenate([g.reshape(fsdp_n, -1) for g in smalls], axis=1)
    pack = lax.psum(pack, ("seq", "fsdp"))
    mine = lax.dynamic_slice_in_dim(pack, lax.axis_index("fsdp"), 1, 0)[0]
    outs, at = [], 0
    for size in sizes:
        outs.append(mine[at : at + size])
        at += size
    return out_rows.reshape(micro, rows, width), grad_in.reshape(micro, rows, width), big, outs


def per_device(
    inputs, segment_ids, block_ids, attn_gain, attn_shift, proj_in, bias_in, proj_out, bias_out,
    mlp_gain, mlp_shift, weight_up, bias_up, weight_down, bias_down, cotangent,
):
    micro, rows, width = inputs.shape
    length = segment_ids.shape[1]
    hidden = weight_up.shape[1]
    seq_n = lax.axis_size("seq")
    fsdp_n = lax.axis_size("fsdp")
    assert seq_n == 4 and seq_n * rows == 2 * length
    lay = layout(rows, length)
    win, keys = lay["win"], lay["keys"]
    me = lax.axis_index("seq")
    clean = me // 2
    half = me % 2
    role = jnp.stack([clean, half]).astype(jnp.int32)
    pairs = [(0, 1), (1, 0), (2, 3), (3, 2)]
    small = (attn_gain, attn_shift, bias_in, bias_out, mlp_gain, mlp_shift, bias_up, bias_down)
    sizes = [p.shape[0] for p in small]
    weights = (proj_in, proj_out, weight_up, weight_down)
    half_dim = HD // 2
    freqs = (10000.0 ** (-(np.arange(half_dim, dtype=np.float32) / half_dim))).astype(np.float32)
    freqs = np.tile(freqs, 4)[None]
    quads = width // (QUAD * HD)
    qw = QUAD * HD
    spans = [hi - lo + NEAR for lo, hi in windows(lay)]
    bias_scratch = [pltpu.VMEM((rows // TILE, max(spans), TILE), F32)]
    per_seq = lambda n, d: pl.BlockSpec((1, n, d), lambda s: (s, 0, 0))
    role_spec = SMEM()
    attn_flops = micro * quads * sum(spans) * QUAD * TILE * qw * 2
    lse_shape = (micro * quads, rows // TILE, QUAD * TILE)
    table_rows = win + rows + HALO
    aligned = fsdp_n & (fsdp_n - 1) == 0 and all(p.shape[0] % (4 * HALO) in (0, 32) for p in weights)
    front = front_remote if aligned else front_native
    (w_in, w_out, w_up, w_down, q, k, v, a, o, lse, vec, cos, sin, codes, queries) = front(
        lay, role, sizes, inputs, segment_ids, block_ids, small, weights, freqs,
        lse_shape, bias_scratch, spans, attn_flops,
    )
    back = back_remote if aligned else back_native
    out_rows, grad_in, big, vectors = back(
        lay, role, sizes, inputs, cotangent, codes, queries, lse, cos, sin, vec,
        q, k, v, o, a, w_in, w_out, w_up, w_down, bias_scratch, attn_flops,
    )
    g_gain1, g_shift1, g_bin, g_bout, g_gain2, g_shift2, g_bup, g_bdown = vectors
    return (
        out_rows, grad_in, g_gain1, g_shift1, big[0], g_bin, big[1], g_bout,
        g_gain2, g_shift2, big[2], g_bup, big[3], g_bdown,
    )


def solution(mesh):
    rows = P("fsdp", "seq", None)
    one, two = P("fsdp"), P("fsdp", None)
    params = (one, one, two, one, two, one, one, one, two, one, two, one)
    return jax.shard_map(
        per_device,
        mesh=mesh,
        in_specs=(rows, two, two) + params + (rows,),
        out_specs=(rows, rows) + params,
        check_vma=False,
    )
```

```python
import functools
import itertools

import jax
import jax.numpy as jnp
import numpy as np
from jax import lax
from jax.experimental import pallas as pl
from jax.experimental.pallas import tpu as pltpu
from jax.sharding import PartitionSpec as P

HD = 64
QUAD = 4
TILE = 128
HALO = 16
NEAR = TILE + 2 * HALO
EPS = 1e-05
MASKED = -1e30
SEG_STEP = 4096
F32 = jnp.float32
BF16 = jnp.bfloat16
VMEM_BYTES = 62 * 1024 * 1024
MESH = pl.DeviceIdType.MESH
ANY = pl.BlockSpec(memory_space=pl.ANY)
VMEM = pl.BlockSpec(memory_space=pltpu.VMEM)


def dot(a, b):
    return jnp.dot(a, b, preferred_element_type=F32)


def dot_nt(a, b):
    return lax.dot_general(a, b, (((1,), (1,)), ((), ())), preferred_element_type=F32)


def dot_tn(a, b):
    return lax.dot_general(a, b, (((0,), (0,)), ((), ())), preferred_element_type=F32)


def norm_stats(x):
    center = jnp.mean(x, axis=-1, keepdims=True)
    centered = x - center
    inverse = lax.rsqrt(jnp.mean(centered * centered, axis=-1, keepdims=True) + EPS)
    return centered * inverse, inverse


def norm_back(grad, normed, inverse, gain):
    scaled = grad * gain
    first = jnp.mean(scaled, axis=-1, keepdims=True)
    second = jnp.mean(scaled * normed, axis=-1, keepdims=True)
    return inverse * (scaled - first - normed * second)


def partner(u):
    lane = lax.broadcasted_iota(jnp.int32, u.shape, 1)
    half = HD // 2
    return jnp.where(
        lane % HD < half, pltpu.roll(u, u.shape[1] - half, 1), pltpu.roll(u, half, 1)
    )


def whole(shape):
    return pl.BlockSpec(shape, lambda *_: (0,) * len(shape), pipeline_mode=pl.Buffered(1))


def call(kernel, grid, in_specs, out_specs, out_shape, scratch, flops, nbytes, name):
    return pl.pallas_call(
        kernel,
        grid=grid,
        in_specs=in_specs,
        out_specs=out_specs,
        out_shape=out_shape,
        scratch_shapes=scratch,
        compiler_params=pltpu.CompilerParams(vmem_limit_bytes=VMEM_BYTES),
        cost_estimate=pl.CostEstimate(flops=flops, bytes_accessed=nbytes, transcendentals=0),
        name=name,
    )


def like(shape, dtype):
    return jax.ShapeDtypeStruct(shape, dtype)


SMEM = functools.partial(pl.BlockSpec, memory_space=pltpu.SMEM)


def layout(rows, length):
    win = rows - length // 8
    noisy = win + rows + HALO
    used = noisy + rows + 2 * HALO
    return dict(rows=rows, win=win, length=length, noisy=noisy, used=used, keys=-(-used // 256) * 256)


def places(lay, role):
    noisy = role[0] == 0
    second = role[1] == 1
    own_at = jnp.where(noisy, lay["noisy"] + HALO, lay["win"])
    halo_at = jnp.where(
        second,
        lay["noisy"],
        jnp.where(noisy, lay["noisy"] + HALO + lay["rows"], lay["win"] + lay["rows"]),
    )
    return noisy, second, pl.multiple_of(own_at, HALO), pl.multiple_of(halo_at, HALO)


def qkv_rows(lay, where_am, n, x, xb, xc, w, b, gain, shift, cos, sin, q_out, k_out, v_out, a_out):
    width = x.shape[2]
    rows, win = lay["rows"], lay["win"]
    noisy, second, own_at, halo_at = where_am

    def norm(v):
        normed, _ = norm_stats(v.astype(F32))
        return (normed * gain + shift).astype(BF16)

    def zeros(at, count):
        for ref in (k_out, v_out, a_out):
            ref[n, at : at + count, :] = jnp.zeros((count, width), BF16)

    def section(a, parts, table, want_q):
        def put(ref, col, value):
            for begin, count, at in parts:
                ref[n, pl.ds(at, count), col : col + value.shape[1]] = value[begin : begin + count]

        put(a_out, 0, a)
        c = cos[table : table + a.shape[0], :]
        s = sin[table : table + a.shape[0], :]
        first = 0 if want_q else width
        for col in range(first, 3 * width, 256):
            part = dot(a, w[:, col : col + 256]) + b[:, col : col + 256]
            for piece in range(2):
                u = part[:, piece * 128 : piece * 128 + 128]
                at_col = col + piece * 128
                if at_col < 2 * width:
                    u = u * c + partner(u) * s
                if at_col < width:
                    q_out[n, :, at_col : at_col + 128] = (u[:rows] * (HD**-0.5)).astype(BF16)
                elif at_col < 2 * width:
                    put(k_out, at_col - width, u.astype(BF16))
                else:
                    put(v_out, at_col - 2 * width, u.astype(BF16))

    zeros(win + rows, 2 * HALO)
    zeros(lay["used"] - HALO, lay["keys"] - lay["used"] + HALO)
    own = jnp.concatenate([norm(x[n]), norm(xc[n, win:, :])], axis=0)
    section(own, ((0, rows, own_at), (rows, HALO, halo_at)), win, True)

    @pl.when(noisy)
    def _():
        section(norm(xb[n]), ((0, rows, win),), win, False)

    @pl.when(jnp.logical_not(noisy))
    def _():
        zeros(lay["noisy"] + HALO, rows)

    @pl.when(second)
    def _():
        section(norm(xc[n, :win, :]), ((0, win, 0),), 0, False)

    @pl.when(jnp.logical_not(second))
    def _():
        zeros(0, win)


def qkv_columns(lay, n, act, at_parts, table, col, count, w, b, cos, sin, q, k, v):
    width, rows = q.shape[2], lay["rows"]

    def put(ref, at_col, value):
        for begin, size, at in at_parts:
            ref[n, pl.ds(at, size), at_col : at_col + 128] = value[begin : begin + size].astype(BF16)

    c = cos[table : table + act.shape[0], :]
    s = sin[table : table + act.shape[0], :]
    part = dot(act, w[:, col : col + count]) + b[:, col : col + count]
    for at_col in range(col, col + count, 128):
        u = part[:, at_col - col : at_col - col + 128]
        if at_col < 2 * width:
            u = u * c + partner(u) * s
        if at_col < width:
            q[n, :, at_col : at_col + 128] = (u[:rows] * (HD**-0.5)).astype(BF16)
        elif at_col < 2 * width:
            put(k, at_col - width, u)
        else:
            put(v, at_col - 2 * width, u)


def qkv_kernel(lay, role, x, xb, xc, w, vec, cos, sin, *outs):
    width = x.shape[2]
    gain, shift, b = vec[0:1, :width], vec[1:2, :width], vec[2:3, : 3 * width]
    qkv_rows(lay, places(lay, role), 0, x, xb, xc, w, b, gain, shift, cos, sin, *outs)


def windows(lay):
    rows, win, length = lay["rows"], lay["win"], lay["length"]
    longest, earliest, latest = length // 2, length // 8, 3 * length // 8
    found = []
    for at in range(0, rows, TILE):
        begin = win + rows
        for origin in range(0, length, rows):
            pos = origin + at
            low = max(pos - longest, 0)
            if origin > 0:
                low = max(low, earliest)
            if pos >= latest + longest:
                low = max(low, earliest + longest)
            begin = min(begin, low - origin + win)
        found.append((begin // TILE * TILE, win + at + TILE + HALO))
    return found


def tile_loop(lay, body):
    for t, (lo, hi) in enumerate(windows(lay)):
        near = lay["noisy"] + t * TILE
        body(t, slice(t * TILE, t * TILE + TILE), slice(lo, hi), slice(near, near + NEAR), hi - lo)


def make_bias(lay, n, codes, queries, biases):
    (bias,) = biases
    groups = {}
    for t, (lo, hi) in enumerate(windows(lay)):
        groups.setdefault(hi - lo, []).append((t, lo))
    for size, tiles in groups.items():
        (t0, lo0), (t1, lo1), number = tiles[0], tiles[-1], len(tiles)
        apart = max(number - 1, 1)
        assert all(tile == (t0 + k * (t1 - t0) // apart, lo0 + k * (lo1 - lo0) // apart) for k, tile in enumerate(tiles))

        def step(k, carry, size=size, t0=t0, lo0=lo0, dt=(t1 - t0) // apart, dlo=(lo1 - lo0) // apart):
            t = t0 + k * dt
            here = pl.ds(pl.multiple_of(t * TILE, TILE), TILE)
            low, high, same = (queries[n, r : r + 1, here] for r in range(3))
            kc = codes[n, pl.ds(pl.multiple_of(lo0 + k * dlo, HALO), size), :]
            ok = jnp.logical_and(kc >= low, kc <= high)
            bias[t, :size, :] = jnp.where(ok, 0.0, MASKED)
            kn = codes[n, pl.ds(pl.multiple_of(lay["noisy"] + t * TILE, HALO), NEAR), :]
            bias[t, size : size + NEAR, :] = jnp.where(kn == same, 0.0, MASKED)
            return carry

        lax.fori_loop(0, number, step, 0)


def stacked(tile):
    lane = lax.broadcasted_iota(jnp.int32, tile.shape, 1)
    zero = jnp.zeros_like(tile)
    return jnp.concatenate(
        [jnp.where(lane // HD == h, tile, zero) for h in range(QUAD)], axis=0
    )


def own_heads(wide):
    return jnp.concatenate(
        [wide[h * HD : h * HD + HD, h * TILE : h * TILE + TILE] for h in range(QUAD)], axis=0
    )


def keys_of(ref, n, cols, lo, near):
    return jnp.concatenate([ref[n, lo, cols], ref[n, near, cols]], axis=0)


def attend(lay, n, cols, q, k, v, o_out, lse_out, lse_at, biases):
    (bias,) = biases

    def body(t, here, lo, near, size):
        qm = stacked(q[n, here, cols])
        kk = keys_of(k, n, cols, lo, near)
        vv = keys_of(v, n, cols, lo, near)
        s = dot_nt(kk, qm) + jnp.concatenate([bias[t, : size + NEAR, :]] * QUAD, axis=1)
        peak = jnp.max(s, axis=0, keepdims=True)
        p = jnp.exp(s - peak)
        total = jnp.sum(p, axis=0, keepdims=True)
        wide = dot_tn(vv, p.astype(BF16)) * (1.0 / total)
        o_out[n, here, cols] = jnp.transpose(own_heads(wide)).astype(BF16)
        lse_out[lse_at, t : t + 1, :] = peak + jnp.log(total)

    tile_loop(lay, body)


def attend_kernel(lay, codes, queries, q, k, v, o_out, lse_out, *biases):
    @pl.when(pl.program_id(1) == 0)
    def _():
        make_bias(lay, 0, codes, queries, biases)

    attend(lay, 0, slice(None), q, k, v, o_out, lse_out, 0, biases)


def attend_back(
    lay, n, cols, q, k, v, m, cols_m, o, do, lse, lse_at, cos, sin, to, col, dq_out, dk_out, dv_out, dk_acc, dv_acc, biases,
):
    rows, win = lay["rows"], lay["win"]
    qw = QUAD * HD

    def lanes(piece):
        return pl.ds(pl.multiple_of(col + piece * 128, 128), 128)

    dk_acc[...] = jnp.zeros_like(dk_acc)
    dv_acc[...] = jnp.zeros_like(dv_acc)
    (bias,) = biases

    def body(t, here, lo, near, size):
        qm = stacked(q[n, here, cols])
        dom = stacked(do[m, here, cols_m])
        kk = keys_of(k, n, cols, lo, near)
        vv = keys_of(v, n, cols, lo, near)
        both = jnp.transpose(do[m, here, cols_m].astype(F32) * o[m, here, cols_m].astype(F32))
        delta = jnp.concatenate(
            [jnp.sum(both[h * HD : h * HD + HD, :], axis=0, keepdims=True) for h in range(QUAD)],
            axis=1,
        )
        s = dot_nt(kk, qm) + jnp.concatenate([bias[t, : size + NEAR, :]] * QUAD, axis=1)
        p = jnp.exp(s - lse[lse_at, t : t + 1, :])
        dp = dot_nt(vv, dom)
        ds = (p * (dp - delta)).astype(BF16)
        pb = p.astype(BF16)
        dv = dot(pb, dom)
        dk = dot(ds, qm)
        dv_acc[lo, :] += dv[:size]
        dk_acc[lo, :] += dk[:size]
        dv_acc[near, :] += dv[size:]
        dk_acc[near, :] += dk[size:]
        wide = dot_tn(kk, ds)
        dq = jnp.transpose(own_heads(wide)) * (HD**-0.5)
        turn = slice(win + t * TILE, win + t * TILE + TILE)
        c, sn = cos[turn, :], sin[turn, :]
        for piece in range(2):
            u = dq[:, piece * 128 : piece * 128 + 128]
            dq_out[to, here, lanes(piece)] = (u * c - partner(u) * sn).astype(BF16)

    tile_loop(lay, body)
    for piece in range(2):
        dv_out[to, :, lanes(piece)] = dv_acc[:, piece * 128 : piece * 128 + 128].astype(BF16)
    half = (cos[win + rows :, :], sin[win + rows :, :])
    own = (cos[win : win + rows, :], sin[win : win + rows, :])
    tables = (
        (0, (cos[: win + rows, :], sin[: win + rows, :])),
        (win + rows, half),
        (lay["noisy"], half),
        (lay["noisy"] + HALO, own),
        (lay["used"] - HALO, half),
    )
    for at, (c, sn) in tables:
        here = slice(at, at + c.shape[0])
        for piece in range(2):
            u = dk_acc[here, piece * 128 : piece * 128 + 128]
            dk_out[to, here, lanes(piece)] = (u * c - partner(u) * sn).astype(BF16)
    spare = lay["keys"] - lay["used"]
    for piece in range(2):
        dk_out[to, lay["used"] :, lanes(piece)] = jnp.zeros((spare, 128), BF16)


def attend_back_kernel(
    lay, codes, queries, q, k, v, o, do, lse, cos, sin, dq_out, dk_out, dv_out, dk_acc, dv_acc, *biases
):
    @pl.when(pl.program_id(1) == 0)
    def _():
        make_bias(lay, 0, codes, queries, biases)

    attend_back(
        lay, 0, slice(None), q, k, v, 0, slice(None), o, do, lse, 0, cos, sin, 0, 0, dq_out, dk_out, dv_out, dk_acc, dv_acc, biases
    )


def bit_of(index, b):
    return (index // (1 << b)) % 2


def other(index, b):
    return index + (1 << b) * (1 - 2 * bit_of(index, b))


class Net:
    def __init__(self, bits, send, recv, sems):
        self.me, self.f, self.bits = lax.axis_index("seq"), lax.axis_index("fsdp"), bits
        self.core, self.x = self.me % 2, self.me // 2
        self.send, self.recv, self.sems = send, recv, sems
        self.used, self.local_used = 0, 0
        self.started = []

    def partners(self):
        return [{"seq": other(self.me, 0)}, {"seq": other(self.me, 1)}] + [
            {"fsdp": other(self.f, b)} for b in range(self.bits)
        ]

    def barrier(self):
        barrier = pltpu.get_barrier_semaphore()
        for device in self.partners():
            pl.semaphore_signal(barrier, inc=1, device_id=device, device_id_type=MESH)
        pl.semaphore_wait(barrier, 2 + self.bits)

    def copy(self, src, dst, device):
        n = self.used
        self.used += 1
        return pltpu.make_async_remote_copy(
            src_ref=src, dst_ref=dst, send_sem=self.send.at[n], recv_sem=self.recv.at[n],
            device_id=device, device_id_type=MESH,
        )

    def local(self, src, dst):
        n = self.local_used
        self.local_used += 1
        return pltpu.make_async_copy(src, dst, self.sems.at[n])

    def fsdp_index(self, done):
        return tuple(slice(None) if b in done else bit_of(self.f, b) for b in range(self.bits - 1, -1, -1))


FRONT_ORDER = (
    "E s i0 i1",
    "T s i2 R0",
    "i0 i1 i2 i0",
    "u0 s i1 u1",
    "i2 s o i1",
    "i1 V u0 i0",
    "R1 u1 i2 o",
    "i0 d0 L0 W",
    "P0 i2 L2 u0",
    "L1 H u1 d1",
    "O0 O1 O2 u0",
    "o d0 d1 A",
    "P1 u1 A d0",
    "A d1 u0 A",
    "u0 d0 u1 o",
    "A d1 A o",
    "u1 d0",
)
FRONT_BITS = {
    "i0": ((2, 0, 1), False),
    "i1": ((2, 1, 0), False),
    "i2": ((2, 1, 0), False),
    "o": ((2, 1, 0), False),
    "u0": ((2, 1, 0), True),
    "u1": ((2, 0, 1), True),
    "d0": ((2, 1, 0), False),
    "d1": ((0, 2, 1), False),
}


class Gather:
    def __init__(self, net, own, full, tail, tail_x=None, tail_core=None, order=None):
        self.net, self.at = net, 0
        mine = net.fsdp_index(())
        self.own = net.local(own.at[tail], full.at[mine + tail])
        self.stages = []
        done = []
        for b in order if order is not None and len(order) == net.bits else range(net.bits - 1, -1, -1):
            here = full.at[net.fsdp_index(done) + tail]
            src = here if done else own.at[tail]
            self.stages.append(net.copy(src, here, {"fsdp": other(net.f, b)}))
            done.append(b)
        everything = (slice(None),) * net.bits
        for region, b in ((tail_x, 1), (tail_core, 0)):
            if region is not None:
                here = full.at[everything + region]
                self.stages.append(net.copy(here, here, {"seq": other(net.me, b)}))

    def advance(self):
        if self.at > len(self.stages):
            return
        if self.at == 0:
            self.own.start()
        else:
            self.stages[self.at - 1].wait_recv()
        if self.at == 1:
            self.own.wait()
        if self.at < len(self.stages):
            self.stages[self.at].start()
        self.at += 1

    def finish(self):
        for stage in self.stages:
            stage.wait_send()


def front_kernel(
    lay, bits, sizes, x, seg, blk, freqs, w_in_s, w_out_s, w_up_s, w_down_s,
    small0, small1, small2, small3, small4, small5, small6, small7,
    w_in, w_out, w_up, w_down, q_out, k_out, v_out, a_out, o_out, lse_out, vec, cos, sin, codes, queries,
    xb, xc, w_vm, q, k, v, a, o, lse, packs, pack, coarse, send, recv, sems, *biases,
):
    rows, win, length = lay["rows"], lay["win"], lay["length"]
    width = x.shape[2]
    hidden = w_up_s.shape[1]
    micro = x.shape[0]
    net = Net(bits, send, recv, sems)
    role = (net.x, net.core)
    noisy, second, own_at, halo_at = places(lay, role)
    first = jnp.logical_not(second)
    clean = jnp.logical_not(noisy)
    net.barrier()

    pair, across = {"seq": other(net.me, 0)}, {"seq": other(net.me, 1)}
    rows_across = [net.copy(x.at[n], xb.at[n], across) for n in range(micro)]
    window = (pl.ds(rows - win, win), slice(None))
    target = (pl.ds(0, win), slice(None))
    rows_pair, rows_pair_b = [], []
    for n in range(micro):
        at = net.used
        rows_pair.append(net.copy(x.at[(n,) + window], xc.at[(n,) + target], pair))
        net.used = at
        rows_pair_b.append(net.copy(xb.at[(n,) + window], xc.at[(n,) + target], pair))
    edge_at = pl.multiple_of((1 - net.core) * (rows - HALO), HALO)
    edge = net.copy(x.at[:, pl.ds(edge_at, HALO), :], xc.at[:, pl.ds(win, HALO), :], pair)

    def columns(begin, size):
        return (slice(None), pl.ds(pl.multiple_of(begin, 128), size))

    pack[...] = jnp.zeros_like(pack)
    smalls = (small0, small1, small2, small3, small4, small5, small6, small7)
    for r, (ref, size) in enumerate(zip(smalls, sizes)):
        pack[r : r + 1, :size] = ref[...].astype(F32).reshape(1, size)
    chunks = {"s": Gather(net, pack, packs, (slice(None), slice(None)))}
    half_in, half_out, half_up = 3 * width // 2, width // 2, hidden // 2
    third = half_in // 3
    for n in range(3):
        region = columns(net.core * half_in + n * third, third)
        chunks["i%d" % n] = Gather(net, w_in_s, w_in, region, None, region, FRONT_BITS["i%d" % n][0])
    region = columns(net.core * half_out, half_out)
    chunks["o"] = Gather(net, w_out_s, w_out, region, None, region, FRONT_BITS["o"][0])
    quarter = half_up // 2
    slab = w_down_s.shape[0]
    for n in range(2):
        order, over_x = FRONT_BITS["u%d" % n]
        region = columns(net.core * half_up + n * quarter, quarter)
        part = columns(net.core * half_up + n * quarter + net.x * (quarter // 2), quarter // 2) if over_x else region
        chunks["u%d" % n] = Gather(net, w_up_s, w_up, part, part if over_x else None, region, order)
        order, over_x = FRONT_BITS["d%d" % n]
        begin = net.core * (slab // 2) + n * (slab // 4)
        region = (pl.ds(pl.multiple_of(begin, HALO), slab // 4), slice(None))
        half_region = (pl.ds(pl.multiple_of(begin + net.x * (slab // 8), HALO), slab // 8), slice(None))
        part = half_region if over_x else region
        chunks["d%d" % n] = Gather(net, w_down_s, w_down, part, part if over_x else None, region, order)

    def rows_start(n):
        @pl.when(clean)
        def _():
            rows_across[n].start()

    count = 1 << bits

    def tables():
        blocks = (win + rows) // HALO
        number = lax.broadcasted_iota(jnp.int32, (-(-(blocks + 1) // 8) * 8, 128), 0)
        begin = jnp.where(number < blocks, number * HALO - win, jnp.where(second, -HALO, rows))
        turned = (begin + jnp.where(second, rows, 0)).astype(F32) * freqs[...]
        coarse[0] = jnp.cos(turned)
        coarse[1] = jnp.sin(turned)
        inside = lax.broadcasted_iota(jnp.int32, (HALO, 128), 0).astype(F32) * freqs[...]
        fine_cos, fine_sin = jnp.cos(inside), jnp.sin(inside)
        lane = lax.broadcasted_iota(jnp.int32, (HALO, 128), 1)
        sign = jnp.where(lane % HD < HD // 2, -1.0, 1.0)

        def table_step(n, carry):
            span = pl.ds(pl.multiple_of(n * HALO, HALO), HALO)
            c, sn = coarse[0, pl.ds(n, 1), :], coarse[1, pl.ds(n, 1), :]
            cos[span, :] = c * fine_cos - sn * fine_sin
            sin[span, :] = (sn * fine_cos + c * fine_sin) * sign
            return carry

        lax.fori_loop(0, blocks + 1, table_step, 0)
        code = (seg[...] * SEG_STEP + blk[...]).astype(F32)
        base = (seg[...] * SEG_STEP).astype(F32)
        turned_code = jnp.transpose(jnp.concatenate([code, jnp.zeros((8 - micro, length), F32)], axis=0))
        lay_noisy = lay["noisy"]
        for n in range(micro):
            col = turned_code[:, n : n + 1]
            none = lambda count, value: jnp.full((count, 1), value, F32)
            codes[n, :win, :] = jnp.where(second, col[rows - win : rows], -1.0)
            codes[n, win : win + rows, :] = jnp.where(second, col[rows:], col[:rows])
            after, before = col[rows : rows + HALO], col[rows - HALO : rows]
            codes[n, win + rows : lay_noisy, :] = jnp.where(jnp.logical_and(clean, first), after, -1.0)
            codes[n, lay_noisy : lay_noisy + HALO, :] = jnp.where(jnp.logical_and(noisy, second), before, -2.0)
            codes[n, lay_noisy + HALO : lay_noisy + HALO + rows, :] = jnp.where(
                noisy, jnp.where(second, col[rows:], col[:rows]), -2.0
            )
            codes[n, lay["used"] - HALO : lay["used"], :] = jnp.where(jnp.logical_and(noisy, first), after, -2.0)
            codes[n, lay["used"] :, :] = none(lay["keys"] - lay["used"], -2.0)
            own_code = jnp.where(second, code[n : n + 1, rows:], code[n : n + 1, :rows])
            own_base = jnp.where(second, base[n : n + 1, rows:], base[n : n + 1, :rows])
            high = own_code - jnp.where(noisy, 1.0, 0.0)
            queries[n] = jnp.concatenate([own_base, high, own_code, jnp.zeros((5, rows), F32)], axis=0)

    def vectors():
        kinds = sorted(set(sizes))

        def spread_step(n, totals):
            piece = packs[tuple((n // (1 << b)) % 2 for b in range(bits - 1, -1, -1))]
            added = []
            for size, total in zip(kinds, totals):
                wide = size * count - piece.shape[1]
                padded = jnp.concatenate([piece, jnp.zeros((8, wide), F32)], axis=1) if wide > 0 else piece
                lanes = lax.broadcasted_iota(jnp.int32, padded.shape, 1)
                added.append(total + pltpu.roll(jnp.where(lanes < size, padded, 0.0), n * size, 1))
            return tuple(added)

        zero = tuple(jnp.zeros((8, size * count), F32) for size in kinds)
        spread = dict(zip(kinds, lax.fori_loop(0, count, spread_step, zero)))
        for r, size in enumerate(sizes):
            vec[r : r + 1, : size * count] = spread[size][r : r + 1]
            if size * count < vec.shape[1]:
                vec[r : r + 1, size * count :] = jnp.zeros((1, vec.shape[1] - size * count), F32)

    def pass_on(n):
        @pl.when(noisy)
        def _():
            rows_across[n].wait_recv()

        @pl.when(jnp.logical_and(first, noisy))
        def _():
            rows_pair_b[n].start()

        @pl.when(jnp.logical_and(first, clean))
        def _():
            rows_pair[n].start()

    loads = {}

    def load_weights(j):
        slab_in = w_in_s.shape[0]
        for n in range(count):
            at = tuple((n >> b) & 1 for b in range(bits - 1, -1, -1))
            for block in range(2):
                cols = slice(block * half_in + j * third, block * half_in + (j + 1) * third)
                copy = net.local(w_in.at[at + (slice(None), cols)], w_vm.at[n * slab_in : (n + 1) * slab_in, cols])
                copy.start()
                loads.setdefault(j, []).append(copy)

    def norm(value):
        normed, _ = norm_stats(value.astype(F32))
        return (normed * vec[0:1, :width] + vec[1:2, :width]).astype(BF16)

    def zeros(n, at, size):
        for ref in (k, v, a):
            ref[n, at : at + size, :] = jnp.zeros((size, width), BF16)

    def norms():
        def step(n, carry):
            zeros(n, win + rows, 2 * HALO)
            zeros(n, lay["used"] - HALO, lay["keys"] - lay["used"] + HALO)

            @pl.when(clean)
            def _():
                zeros(n, lay["noisy"] + HALO, rows)

            @pl.when(first)
            def _():
                zeros(n, 0, win)

            a[n, pl.ds(own_at, rows), :] = norm(x[n])
            a[n, pl.ds(halo_at, HALO), :] = norm(xc[n, win:, :])
            return carry

        lax.fori_loop(0, micro, step, 0)

    def own_rows(j):
        for load in loads[j]:
            load.wait()

        def step(n, carry):
            act = jnp.concatenate([a[n, pl.ds(own_at, rows), :], a[n, pl.ds(halo_at, HALO), :]], axis=0)
            for block in range(2):
                qkv_columns(
                    lay, n, act, ((0, rows, own_at), (rows, HALO, halo_at)), win, block * half_in + j * third, third,
                    w_vm, vec[2:3, : 3 * width], cos, sin, q, k, v,
                )
            return carry

        lax.fori_loop(0, micro, step, 0)

    def key_rows(n):
        def section(value, at):
            a[n, at : at + value.shape[0], :] = act = norm(value)
            for col in range(width, 3 * width, 384):
                qkv_columns(
                    lay, n, act, ((0, value.shape[0], at),), at, col, 384, w_vm, vec[2:3, : 3 * width], cos, sin, q, k, v
                )

        @pl.when(noisy)
        def _():
            section(xb[n], win)

        @pl.when(second)
        def _():
            for m in range(micro):

                @pl.when(n == m)
                def _(m=m):
                    rows_pair[m].wait_recv()

            section(xc[n, :win, :], 0)

        for store in stores_of(n):
            store.start()

    first_store = net.local_used
    net.local_used += 4 * micro

    def stores_of(n):
        return [
            pltpu.make_async_copy(here.at[n], there.at[n], sems.at[first_store + 4 * n + m])
            for m, (here, there) in enumerate(((q, q_out), (k, k_out), (v, v_out), (a, a_out)))
        ]

    def serve(token):
        if token in chunks:
            chunks[token].advance()
        elif len(token) == 2:
            {"R": rows_start, "P": pass_on, "L": load_weights, "O": own_rows}[token[0]](int(token[1]))
        else:
            {"E": edge.start, "W": edge.wait_recv, "T": tables, "V": vectors, "H": norms}[token]()

    ahead, *after = [part.split() for part in " ".join(FRONT_ORDER).split("A")]
    for token in ahead:
        serve(token)

    quads = width // (QUAD * HD)
    assert micro * quads == len(after)

    def step(index, carry):
        n, h = index // quads, index % quads

        @pl.when(h == 0)
        def _():
            key_rows(n)
            make_bias(lay, n, codes, queries, biases)

        cols = pl.ds(pl.multiple_of(h * QUAD * HD, QUAD * HD), QUAD * HD)
        def serve_all():
            for at, tokens in enumerate(after):
                if tokens:

                    @pl.when(index == at)
                    def _(tokens=tokens):
                        for token in tokens:
                            serve(token)

        attend(lay, n, cols, q, k, v, o, lse, index, biases)
        serve_all()
        return carry

    lax.fori_loop(0, micro * quads, step, 0)
    last = [net.local(o, o_out), net.local(lse, lse_out)]
    for store in last:
        store.start()
    while any(chunk.at <= len(chunk.stages) for chunk in chunks.values()):
        for chunk in chunks.values():
            chunk.advance()
    for chunk in chunks.values():
        chunk.finish()
    for store in stores_of(0) + stores_of(1) + last:
        store.wait()
    edge.wait_send()

    @pl.when(clean)
    def _():
        for n in range(micro):
            rows_across[n].wait_send()

    @pl.when(first)
    def _():
        for n in range(micro):
            rows_pair[n].wait_send()


def gelu_both(u):
    scale = 0.7978845608028654
    square = u * u
    inner = scale * u * (1.0 + 0.044715 * square)
    th = jnp.tanh(inner)
    plus = 0.5 * (1.0 + th)
    slope = plus + 0.5 * u * (1.0 - th * th) * (scale * (1.0 + 3 * 0.044715 * square))
    return (u * plus).astype(BF16), slope


def mlp_kernel(
    o, x, dy, w_out, vec, w_up, b_up, w_down,
    out_rows, dx2_out, do_out, g_w_out, g_w_up, g_b_up, g_w_down, g_vec,
    mid, a2, a2t, inv, acc_out, acc_da,
):
    step = pl.program_id(0)
    last = pl.num_programs(0) - 1
    width = x.shape[1]
    b_out, gain, shift, b_down = (vec[r : r + 1, :width] for r in (3, 4, 5, 7))

    @pl.when(step == 0)
    def _():
        value = x[...].astype(F32) + dot(o[...], w_out[...]) + b_out
        mid[...] = value
        normed, inverse = norm_stats(value)
        inv[...] = inverse
        a = (normed * gain + shift).astype(BF16)
        a2[...] = a
        a2t[...] = jnp.transpose(a)
        acc_out[...] = jnp.zeros_like(acc_out)
        acc_da[...] = jnp.zeros_like(acc_da)

    g, slope = gelu_both(dot(a2[...], w_up[...]) + b_up[6:7, :])
    acc_out[...] += dot(g, w_down[...])
    du32 = dot_nt(dy[...], w_down[...]) * slope
    du = du32.astype(BF16)
    g_b_up[...] = jnp.broadcast_to(jnp.sum(du.astype(F32), axis=0, keepdims=True), g_b_up.shape)
    acc_da[...] += dot_nt(du, w_up[...])
    g_w_down[...] = dot_tn(g, dy[...]).astype(BF16)
    g_w_up[...] = dot(a2t[...], du).astype(BF16)

    @pl.when(step == last)
    def _():
        dyf = dy[...].astype(F32)
        out_rows[...] = (mid[...] + acc_out[...] + b_down).astype(BF16)
        inverse = inv[...]
        value = mid[...]
        normed = (value - jnp.mean(value, axis=-1, keepdims=True)) * inverse
        da = acc_da[...]
        dx2 = dyf + norm_back(da, normed, inverse, gain)
        dx2_out[...] = dx2
        dp = dx2.astype(BF16)
        do_out[...] = dot_nt(dp, w_out[...]).astype(BF16)
        g_w_out[...] = dot_tn(o[...], dp).astype(BF16)
        g_vec[...] = jnp.concatenate(
            [
                jnp.sum(dyf, axis=0, keepdims=True),
                jnp.sum(da * normed, axis=0, keepdims=True),
                jnp.sum(da, axis=0, keepdims=True),
                jnp.sum(dp.astype(F32), axis=0, keepdims=True),
                jnp.zeros((4, dyf.shape[1]), F32),
            ],
            axis=0,
        )


def qkv_back_kernel(lay, role, a, dq, dk, dv, w, da_own, da_main, da_win, g_w, g_b, g_acc):
    width = dq.shape[2]
    rows, win = lay["rows"], lay["win"]
    noisy, second, own_at, halo_at = places(lay, role)

    @pl.when(pl.program_id(0) == 0)
    def _():
        g_acc[...] = jnp.zeros_like(g_acc)
        g_b[...] = jnp.zeros_like(g_b)

    def column_sums(col, value):
        g_b[0:1, col : col + width] += jnp.sum(value.astype(F32), axis=0, keepdims=True)

    def section(parts, query):
        def take(ref):
            return jnp.concatenate([ref[0, pl.ds(at, count), :] for at, count in parts], axis=0)

        at_t = jnp.transpose(take(a))
        key = take(dk)
        value = take(dv)
        g_acc[:, width : 2 * width] += dot(at_t, key)
        g_acc[:, 2 * width :] += dot(at_t, value)
        column_sums(width, key)
        column_sums(2 * width, value)
        total = dot_nt(key, w[:, width : 2 * width]) + dot_nt(value, w[:, 2 * width :])
        if query is not None:
            g_acc[:, :width] += dot(at_t[:, : query.shape[0]], query)
            column_sums(0, query)
            first = total[: query.shape[0]] + dot_nt(query, w[:, :width])
            return first, total[query.shape[0] :]
        return total

    own, near = section(((own_at, rows), (halo_at, HALO)), dq[0])
    da_own[0] = own
    da_win[0, win:, :] = near.astype(BF16)

    @pl.when(noisy)
    def _():
        da_main[0] = section(((win, rows),), None).astype(BF16)

    @pl.when(second)
    def _():
        da_win[0, :win, :] = section(((0, win),), None).astype(BF16)

    @pl.when(pl.program_id(0) == pl.num_programs(0) - 1)
    def _():
        g_w[...] = g_acc[...].astype(BF16)


def final_kernel(x, da, extra, dx2, gain, grad_in, g_vec):
    value = x[...].astype(F32)
    normed, inverse = norm_stats(value)
    grad = da[...] + extra[...].astype(F32)
    grad_in[...] = dx2[...] + norm_back(grad, normed, inverse, gain[...])

    @pl.when(pl.program_id(0) == 0)
    def _():
        g_vec[...] = jnp.zeros_like(g_vec)

    g_vec[0:1, :] += jnp.sum(grad * normed, axis=0, keepdims=True)
    g_vec[1:2, :] += jnp.sum(grad, axis=0, keepdims=True)


def add_to(ref, at, value):
    ref[at] = (ref[at].astype(F32) + value.astype(F32)).astype(BF16)


def for_all(bits, body):
    if bits == 0:
        body(())
        return

    def step(n, carry):
        body(tuple((n // (1 << b)) % 2 for b in range(bits - 1, -1, -1)))
        return carry

    lax.fori_loop(0, 1 << bits, step, 0)


BACK_ORDER = (
    "S s S s",
    "u0 d0 S s",
    "d0 S s u1",
    "u0 d1 S s",
    "d1 S s d2",
    "d0 u0 u2 E",
    "o u2 d0 u1",
    "e d2 d1 u0",
    "o X e A",
    "A A u2 u0",
    "d2 A d1 P0",
    "u1 A o A",
    "u2 T e d2",
    "P1 G0 i0 o",
    "G1 i1 Y0 i0",
    "e d2 i1 G2",
    "i2 N i0 d0",
    "o d1 i2 i1",
    "Y1 N e N",
    "d2 N l i0",
    "i2 l l",
)
BACK_BITS = {
    "u0": ((0, 1, 2), True),
    "u1": ((1, 2, 0), False),
    "u2": ((0, 1, 2), False),
    "d0": ((0, 1, 2), False),
    "d1": ((0, 2, 1), False),
    "d2": ((0, 1, 2), False),
    "o": ((0, 1, 2), False),
    "i0": ((1, 2, 0), False),
    "i1": ((0, 1, 2), False),
    "i2": ((0, 1, 2), False),
}


class Reduce:
    def __init__(self, net, acc, recvs, out, rows, cols, order, over_x):
        bits, self.net, self.at, self.sent = net.bits, net, 0, False
        pair, across = {"seq": other(net.me, 0)}, {"seq": other(net.me, 1)}
        recvs = list(recvs)
        part = (slice(None), slice(None))
        begin, size = rows
        tail = tail_half = (pl.ds(begin, size), cols)
        self.acc, self.steps = acc, [None]
        if over_x:
            piece = size // 2
            part = (pl.ds(pl.multiple_of(net.x * piece, HALO), piece), slice(None))
            away = (pl.ds(pl.multiple_of((1 - net.x) * piece, HALO), piece), slice(None))
            tail = (pl.ds(pl.multiple_of(begin + net.x * piece, HALO), piece), cols)
            got_x = recvs.pop(0)

            def add_x():
                for_all(bits, lambda at: add_to(acc, at + part, got_x[at]))

            self.steps.append((net.copy(acc.at[(slice(None),) * bits + away], got_x, across), add_x))
        done = []
        for b in order if len(order) == bits else range(bits):
            got = recvs.pop(0)

            def index(mine, rest, b=b, done=tuple(done)):
                rest = iter(rest)
                return tuple(
                    mine if p == b else bit_of(net.f, p) if p in done else next(rest) for p in range(bits - 1, -1, -1)
                )

            left = bits - 1 - len(done)

            def add_bit(got=got, b=b, index=index, left=left):
                for_all(left, lambda at: add_to(acc, index(bit_of(net.f, b), at) + part, got[at]))

            src = acc.at[index(1 - bit_of(net.f, b), (slice(None),) * left) + part]
            self.steps.append((net.copy(src, got, {"fsdp": other(net.f, b)}), add_bit))
            done.append(b)
        own = tuple(bit_of(net.f, n) for n in range(bits - 1, -1, -1))
        if over_x:
            before = self.steps[-1][1]

            def keep():
                before()
                out[tail] = acc[own + part]

            self.steps[-1] = (self.steps[-1][0], keep)
            self.steps.append((net.copy(out.at[tail], out.at[tail], across), lambda: None))
        else:
            got_last = recvs.pop(0)

            def last():
                out[tail] = (acc[own].astype(F32) + got_last[...].astype(F32)).astype(BF16)

            self.steps.append((net.copy(acc.at[own], got_last, across), last))
        self.steps.append((net.copy(out.at[tail_half], out.at[tail_half], pair), lambda: None))

    def feed(self, theirs, get):
        def mine():
            for_all(self.net.bits, lambda at: add_to(self.acc, at, get(at)))

        self.steps[0] = (self.net.copy(theirs, self.acc, {"seq": other(self.net.me, 0)}), mine)

    def open(self):
        return self.at <= len(self.steps)

    def advance(self):
        if not self.open():
            return
        if self.at > 0:
            copy, then = self.steps[self.at - 1]
            copy.wait_recv()
            then()
        if self.at < len(self.steps):
            self.steps[self.at][0].start()
        self.at += 1

    def finish(self):
        while self.open():
            self.advance()
        for copy, _ in self.steps[1 if self.sent else 0 :]:
            copy.wait_send()


class SumAll:
    def __init__(self, net, value, recvs):
        self.value, self.recvs, self.at = value, recvs, 0
        devices = [{"seq": other(net.me, b)} for b in range(2)]
        devices += [{"fsdp": other(net.f, b)} for b in range(net.bits)]
        self.copies = []
        for n, device in enumerate(devices):
            src = value if n == 0 else recvs.at[len(devices) + n - 1]
            self.copies.append(net.copy(src, recvs.at[n], device))

    def open(self):
        return self.at <= len(self.copies)

    def advance(self):
        count = len(self.copies)
        if not self.open():
            return
        if self.at > 0:
            n = self.at - 1
            self.copies[n].wait_recv()
            held = self.value[...] if n == 0 else self.recvs[count + n - 1]
            self.recvs[count + n] = held + self.recvs[n]
        if self.at < count:
            self.copies[self.at].start()
        self.at += 1

    def finish(self):
        while self.open():
            self.advance()
        for copy in self.copies:
            copy.wait_send()
        return self.recvs[2 * len(self.copies) - 1]


def back_kernel(
    lay, bits, codes, queries, lse, cos, sin, vec, x, o,
    dy, q, k, v, a, w_in, w_out, w_up, w_down,
    out_rows, grad_in, f_in_out, f_out_out, f_up_out, f_down_out, sums_out, late_out,
    do, recv_parts, rwin,
    acc_in, acc_out, acc_up, acc_down, r_in, r_out, r_up, r_down, f_in, f_out, f_up, f_down,
    sums, sums_recv, late, late_recv, send, recv, sems, *biases,
):
    rows, win, keys = lay["rows"], lay["win"], lay["keys"]
    micro, width = x.shape[0], x.shape[2]
    total = micro * rows
    hidden = vec.shape[1]
    qw = QUAD * HD
    quads = width // qw
    net = Net(bits, send, recv, sems)
    where_am = noisy, second, own_at, halo_at = places(lay, (net.x, net.core))
    first, clean = jnp.logical_not(second), jnp.logical_not(noisy)
    gain = vec[0:1, :width]
    net.barrier()
    every = list(itertools.product(range(2), repeat=bits))
    count = len(every)
    pair, across = {"seq": other(net.me, 0)}, {"seq": other(net.me, 1)}
    slab_down = f_down.shape[0]
    steps = slab_down // 128
    share = count // 2
    wide = share * 128
    whole_index = (slice(None),) * bits
    here, there = net.core, 1 - net.core

    def columns(begin, size):
        return (slice(None), pl.ds(pl.multiple_of(begin, 128), size))

    @pl.when(noisy)
    def _():
        recv_parts[...] = jnp.zeros_like(recv_parts)

    sums[...] = jnp.zeros_like(sums)

    def feed_forward(dyv, wu, wd, w_ov, mid, a2, a2t, inv, acc_y, acc_da, gv, duv, gd, gu, gu_out, sem_w, sem_m):
        block = total // 4

        def loads(index):
            j, h = index // 2, index % 2
            slot = index % 2
            copies = []
            for n in range(share):
                at = pl.multiple_of((h * share + n) * slab_down + j * 128, 128)
                part = pl.ds(n * 128, 128)
                copies.append(pltpu.make_async_copy(w_up.at[:, pl.ds(at, 128)], wu.at[slot, :, part], sem_w.at[slot, 2 * n]))
                copies.append(pltpu.make_async_copy(w_down.at[pl.ds(at, 128), :], wd.at[slot, part, :], sem_w.at[slot, 2 * n + 1]))
            return copies

        first_loads = [pltpu.make_async_copy(w_out, w_ov, sem_m.at[0]), pltpu.make_async_copy(dy, dyv, sem_m.at[1])]
        for load in first_loads + loads(0):
            load.start()
        flat = lambda ref: ref[...].reshape(total, width)
        b_out, gain2, shift2, b_down = (vec[r : r + 1, :width] for r in (3, 4, 5, 7))
        first_loads[0].wait()
        def part_rows(n):
            per = rows // block
            return n // per, pl.ds(pl.multiple_of((n % per) * block, block), block)

        def open_step(n, carry):
            span = pl.ds(pl.multiple_of(n * block, block), block)
            m, sub = part_rows(n)
            value = x[m, sub, :].astype(F32) + dot(o[m, sub, :], w_ov[...]) + b_out
            mid[span, :] = value
            normed, inverse = norm_stats(value)
            inv[span, :] = inverse
            act = (normed * gain2 + shift2).astype(BF16)
            a2[span, :] = act
            a2t[:, span] = jnp.transpose(act)
            return carry

        lax.fori_loop(0, total // block, open_step, 0)
        acc_y[...] = jnp.zeros_like(acc_y)
        acc_da[...] = jnp.zeros_like(acc_da)
        first_loads[1].wait()

        away = columns(there * (width // 2), width // 2)
        near = columns(here * (width // 2), width // 2)
        for j in range(steps):
            chunks["u%d" % j].feed(gu.at[j, there], lambda at, j=j: gu[(j, here) + at])
            chunks["d%d" % j].feed(gd.at[(j,) + whole_index + away], lambda at, j=j: gd[(j,) + at + near])

        def serve_all(index, part):
            for at, tokens in enumerate(in_feed):
                if tokens[part]:

                    @pl.when(index == at)
                    def _(tokens=tokens[part]):
                        for token in tokens:
                            chunks[token].advance()

        def step(index, carry):
            j, h = index // 2, index % 2
            slot = index % 2

            @pl.when(index + 1 < 2 * steps)
            def _():
                for load in loads(index + 1):
                    load.start()

            for load in loads(index):
                load.wait()
            at = [pl.ds(pl.multiple_of((h * share + n) * slab_down + j * 128, 128), 128) for n in range(share)]
            bias = jnp.concatenate([vec[6:7, here_at] for here_at in at], axis=1)
            w_u, w_d = wu[slot], wd[slot]

            def rows_step(r, row):
                for sub in range(2):
                    span = pl.ds(pl.multiple_of((2 * r + sub) * block, block), block)
                    g, slope = gelu_both(dot(a2[span, :], w_u) + bias)
                    gv[span, :] = g
                    acc_y[span, :] += dot(g, w_d)
                    du = (dot_nt(dyv[span, :], w_d) * slope).astype(BF16)
                    duv[span, :] = du
                    row += jnp.sum(du.astype(F32), axis=0, keepdims=True)
                    acc_da[span, :] += dot_nt(du, w_u)
                return row

            row = lax.fori_loop(0, total // (2 * block), rows_step, jnp.zeros((1, wide), F32))
            for n in range(share):
                sums[6:7, at[n]] = row[:, n * 128 : n * 128 + 128]
            serve_all(index, 0)
            slab = width // count

            def half_step(m, carry):
                part = pl.ds(pl.multiple_of(m * (wide // 2), 128), wide // 2)
                g_d = dot_tn(gv[:, part], dyv[...]).astype(BF16)
                for n, low in enumerate(itertools.product(range(2), repeat=bits - 2)):
                    gd[(j, h, m) + low] = g_d[n * 128 : n * 128 + 128]
                g_u = dot(a2t[pl.ds(pl.multiple_of(m * (width // 2), 128), width // 2), :], duv[...]).astype(BF16)
                for n, low in enumerate(itertools.product(range(2), repeat=bits - 1)):
                    gu[(j, h, m) + low] = g_u[n * slab : n * slab + slab]
                return carry

            lax.fori_loop(0, 2, half_step, 0)
            serve_all(index, 1)
            return carry

        lax.fori_loop(0, 2 * steps, step, 0)
        def close_step(n, carry):
            span = pl.ds(pl.multiple_of(n * block, block), block)
            m, sub = part_rows(n)
            dyf = dyv[span, :].astype(F32)
            value = mid[span, :]
            a2[span, :] = (value + acc_y[span, :] + b_down).astype(BF16)
            normed = (value - jnp.mean(value, axis=-1, keepdims=True)) * inv[span, :]
            da = acc_da[span, :]
            dx2 = dyf + norm_back(da, normed, inv[span, :], gain2)
            acc_da[span, :] = dx2
            dp = dx2.astype(BF16)
            dyv[span, :] = dp
            do[m, sub, :] = dot_nt(dp, w_ov[...]).astype(BF16)
            for r, part in ((7, dyf), (4, da * normed), (5, da), (3, dp.astype(F32))):
                sums[r : r + 1, :width] += jnp.sum(part, axis=0, keepdims=True)
            return carry

        lax.fori_loop(0, total // block, close_step, 0)
        puts = []
        for n in range(micro):
            part = pl.ds(n * rows, rows)
            puts.append(pltpu.make_async_copy(acc_da.at[part, :], grad_in.at[n], sem_m.at[2 + 2 * n]))
            puts.append(pltpu.make_async_copy(a2.at[part, :], out_rows.at[n], sem_m.at[3 + 2 * n]))
        for put in puts:
            put.start()
        g_o = dot_tn(flat(o), dyv[...]).astype(BF16)
        slab = width // count
        for n, idx in enumerate(every):
            for c in range(2):
                gu_out[(c,) + idx] = g_o[n * slab : n * slab + slab, c * (width // 2) : (c + 1) * (width // 2)]
        chunks["o"].feed(gu_out.at[there], lambda at: gu_out[(here,) + at])
        for token in after_feed:
            chunks[token].advance()
        for name, chunk in chunks.items():
            if name[0] in "udo":
                assert chunk.at >= 2
                chunk.steps[0][0].wait_send()
                chunk.sent = True
        for put in puts:
            put.wait()

    half_out = width // 2
    slab = width // count
    chunks = {}
    for j in range(steps):
        chunks["u%d" % j] = Reduce(net, acc_up[j], r_up[j], f_up.at[j], (0, slab),
                                   columns(here * wide, wide)[1], *BACK_BITS["u%d" % j])
        chunks["d%d" % j] = Reduce(net, acc_down[j], r_down[j], f_down, (j * 128, 128),
                                   columns(here * half_out, half_out)[1], *BACK_BITS["d%d" % j])
    chunks["o"] = Reduce(net, acc_out, r_out, f_out, (0, slab), columns(here * half_out, half_out)[1], *BACK_BITS["o"])
    chunks["e"] = SumAll(net, sums, sums_recv)
    chunks["l"] = SumAll(net, late, late_recv)
    edge_at = pl.multiple_of((1 - net.core) * (rows - HALO), HALO)
    tokens = " ".join(BACK_ORDER).split()
    feed_end, free, turn = tokens.index("E"), tokens.index("X"), tokens.index("T")
    halves = lambda text, outer, inner: [[half.split() for half in part.split(inner)] for part in text.split(outer)]
    (_,), *in_feed = halves(" ".join(tokens[:feed_end]), "S", "s")
    after_feed = tokens[feed_end + 1 : free]
    early_tokens, *in_attention = [part.split() for part in " ".join(tokens[free + 1 : turn]).split("A")]
    after_attention = tokens[turn + 1 :]
    assert len(in_feed) == 2 * steps and len(in_attention) == micro * quads

    pl.run_scoped(
        feed_forward,
        pltpu.VMEM((total, width), BF16), pltpu.VMEM((2, width, wide), BF16), pltpu.VMEM((2, wide, width), BF16),
        pltpu.VMEM((width, width), BF16), pltpu.VMEM((total, width), F32), pltpu.VMEM((total, width), BF16),
        pltpu.VMEM((width, total), BF16), pltpu.VMEM((total, 1), F32), pltpu.VMEM((total, width), F32),
        pltpu.VMEM((total, width), F32), pltpu.VMEM((total, wide), BF16), pltpu.VMEM((total, wide), BF16),
        pltpu.VMEM((steps,) + (2,) * bits + (128, width), BF16),
        pltpu.VMEM((steps, 2) + (2,) * bits + (width // count, wide), BF16),
        pltpu.VMEM((2,) + (2,) * bits + (width // count, half_out), BF16),
        pltpu.SemaphoreType.DMA((2, 2 * share)), pltpu.SemaphoreType.DMA((2 + 2 * micro,)),
    )

    def backward(dq, dk, dv, w_vm, gin, parts, dwin, sem_l):
        load_w = pltpu.make_async_copy(w_in, w_vm, sem_l.at[0])
        load_w.start()
        p1 = [net.copy(dwin.at[n], rwin.at[n], pair) for n in range(micro)]
        p2 = [net.copy(parts.at[n], recv_parts.at[n], across) for n in range(micro)]
        third = 3 * width // 6
        slab_in = width // count
        for j in range(3):
            chunks["i%d" % j] = Reduce(net, acc_in[j], r_in[j], f_in, (0, slab_in),
                                       columns(here * 3 * third + j * third, third)[1], *BACK_BITS["i%d" % j])
            chunks["i%d" % j].feed(gin.at[j, there], lambda at, j=j: gin[(j, here) + at])

        def pass_on(n):
            p1[n].wait_recv()

            @pl.when(noisy)
            def _():
                @pl.when(first)
                def _():
                    add_to(parts, (n, slice(rows - win, rows), slice(None)), rwin[n, :win, :])

                p2[n].start()

        def attention(qb, kb, vb, dk_acc, dv_acc, load_sems):
            blocks = ((q, qb), (k, kb), (v, vb))

            def loads(index):
                n, h = index // quads, index % quads
                cols = pl.ds(pl.multiple_of(h * qw, qw), qw)
                slot = index % 2
                return [
                    pltpu.make_async_copy(src.at[n, :, cols], dst.at[slot], load_sems.at[slot, m])
                    for m, (src, dst) in enumerate(blocks)
                ]

            for load in loads(0):
                load.start()
            load_w.wait()

            def partial(n):
                key = jnp.concatenate([dk[n, :win, :], dk[n, pl.ds(halo_at, HALO), :]], axis=0)
                value = jnp.concatenate([dv[n, :win, :], dv[n, pl.ds(halo_at, HALO), :]], axis=0)
                w_key, w_value = w_vm[:, width : 2 * width], w_vm[:, 2 * width :]
                dwin[n] = (dot_nt(key, w_key) + dot_nt(value, w_value)).astype(BF16)
                for m in range(micro):

                    @pl.when(n == m)
                    def _(m=m):
                        p1[m].start()

                @pl.when(noisy)
                def _():
                    main = slice(win, win + rows)
                    parts[n] = (dot_nt(dk[n, main, :], w_key) + dot_nt(dv[n, main, :], w_value)).astype(BF16)

            def serve(token):
                if token[0] == "P":
                    pass_on(int(token[1]))
                else:
                    chunks[token].advance()

            for token in early_tokens:
                serve(token)

            def serve_all(index):
                for at, tokens in enumerate(in_attention):
                    if tokens:

                        @pl.when(index == at)
                        def _(tokens=tokens):
                            for token in tokens:
                                serve(token)

            def step(index, carry):
                n, h = index // quads, index % quads
                slot = index % 2

                @pl.when(index + 1 < micro * quads)
                def _():
                    for load in loads(index + 1):
                        load.start()

                @pl.when(h == 0)
                def _():
                    make_bias(lay, n, codes, queries, biases)

                for load in loads(index):
                    load.wait()
                cols = pl.ds(pl.multiple_of(h * qw, qw), qw)
                attend_back(
                    lay, slot, slice(None), qb, kb, vb, n, cols, o, do, lse, index, cos, sin,
                    n, h * qw, dq, dk, dv, dk_acc, dv_acc, biases,
                )
                @pl.when(h == quads - 1)
                def _():
                    partial(n)

                serve_all(index)
                return carry

            lax.fori_loop(0, micro * quads, step, 0)

        pl.run_scoped(
            attention,
            pltpu.VMEM((2, rows, qw), BF16), pltpu.VMEM((2, keys, qw), BF16), pltpu.VMEM((2, keys, qw), BF16),
            pltpu.VMEM((keys, qw), F32), pltpu.VMEM((keys, qw), F32),
            pltpu.SemaphoreType.DMA((2, 3)),
        )

        def projection(av, at_all, at_own, dxv, sem_a, sem_x):
            load_x = pltpu.make_async_copy(grad_in, dxv, sem_x.at[0])
            pltpu.make_async_copy(a.at[0], av, sem_a.at[0]).start()
            load_x.start()
            def turn_step(n, carry):
                pltpu.make_async_copy(a.at[n], av, sem_a.at[n]).wait()
                at_all[n] = jnp.transpose(av[...])
                at_own[n] = jnp.transpose(av[pl.ds(own_at, rows), :])

                @pl.when(n + 1 < micro)
                def _():
                    pltpu.make_async_copy(a.at[n + 1], av, sem_a.at[n + 1]).start()

                return carry

            lax.fori_loop(0, micro, turn_step, 0)
            late[...] = jnp.zeros_like(late)
            def gradient(j):
                for block in range(2):
                    col = block * 3 * third + j * third
                    source, lhs = ((dq, at_own), (dk, at_all), (dv, at_all))[col // width]
                    inside = slice(col % width, col % width + third)
                    part = width // 2

                    def rows_step(m, carry):
                        grad = jnp.zeros((part, third), F32)
                        for n in range(micro):
                            grad += dot(lhs[n, pl.ds(pl.multiple_of(m * part, 128), part), :], source[n, :, inside])
                        for low, at in enumerate(itertools.product(range(2), repeat=bits - 1)):
                            gin[(j, block, m) + at] = grad[low * slab_in : low * slab_in + slab_in].astype(BF16)
                        return carry

                    lax.fori_loop(0, 2, rows_step, 0)
                    ones = jnp.zeros((8, third), F32)
                    for n in range(micro):
                        rhs = source[n, :, inside]
                        ones += dot(jnp.ones((8, rhs.shape[0]), BF16), rhs)
                    row = 2 + col // width
                    late[row : row + 1, inside] = ones[0:1]

            def settle(n):
                @pl.when(clean)
                def _():
                    p2[n].wait_recv()

                    @pl.when(first)
                    def _():
                        add_to(recv_parts, (n, slice(rows - win, rows), slice(None)), rwin[n, :win, :])

                add_to(recv_parts, (n, pl.ds(edge_at, HALO), slice(None)), rwin[n, win:, :])

            def store(m):
                span = pl.ds(pl.multiple_of((m % 2) * (rows // 2), TILE), rows // 2)
                return pltpu.make_async_copy(dxv.at[m // 2, span, :], grad_in.at[m // 2, span, :], sem_x.at[1 + m])

            def norm_part(m):
                n, part = m // 2, m % 2
                size = rows // 2
                span = pl.ds(pl.multiple_of(part * size, TILE), size)
                mine_rows = pl.ds(pl.multiple_of(own_at + part * size, HALO), size)
                da = dot_nt(dq[n, span, :], w_vm[:, :width])
                da += dot_nt(dk[n, mine_rows, :], w_vm[:, width : 2 * width])
                da += dot_nt(dv[n, mine_rows, :], w_vm[:, 2 * width :])
                da += recv_parts[n, span, :].astype(F32)
                normed, inverse = norm_stats(x[n, span, :].astype(F32))
                dxv[n, span, :] += norm_back(da, normed, inverse, gain)
                late[0:1, :] += jnp.sum(da * normed, axis=0, keepdims=True)
                late[1:2, :] += jnp.sum(da, axis=0, keepdims=True)
                store(m).start()

            def serve(token):
                if token in chunks:
                    chunks[token].advance()
                else:
                    {"P": pass_on, "Y": settle, "G": gradient}[token[0]](int(token[1]))

            groups = [part.split() for part in " ".join(after_attention).split("N")]
            assert len(groups) == 1 + 2 * micro
            for token in groups[0]:
                serve(token)
            load_x.wait()

            def norm_step(m, carry):
                norm_part(m)
                for at, tokens in enumerate(groups[1:-1]):
                    if tokens:

                        @pl.when(m == at)
                        def _(tokens=tokens):
                            for token in tokens:
                                serve(token)

                return carry

            lax.fori_loop(0, 2 * micro, norm_step, 0)
            for token in groups[-1]:
                serve(token)
            while any(chunk.open() for chunk in chunks.values()):
                for chunk in chunks.values():
                    chunk.advance()
            sums_out[...] = chunks["e"].finish()
            late_out[...] = chunks["l"].finish()
            for name, chunk in chunks.items():
                if name not in "el":
                    chunk.finish()
            puts = [net.local(src, dst) for src, dst in ((f_in, f_in_out), (f_out, f_out_out), (f_down, f_down_out))]
            for j in range(steps):
                for n in range(count):
                    puts.append(net.local(
                        f_up.at[j, :, pl.ds(n * 128, 128)], f_up_out.at[:, pl.ds(n * slab_down + j * 128, 128)]
                    ))
            for put in puts:
                put.start()
            for put in puts:
                put.wait()
            for m in range(2 * micro):
                store(m).wait()
            for copy in p1:
                copy.wait_send()

            @pl.when(noisy)
            def _():
                for copy in p2:
                    copy.wait_send()

        pl.run_scoped(
            projection,
            pltpu.VMEM((keys, width), BF16), pltpu.VMEM((micro, width, keys), BF16),
            pltpu.VMEM((micro, width, rows), BF16), pltpu.VMEM((micro, rows, width), F32),
            pltpu.SemaphoreType.DMA((micro,)), pltpu.SemaphoreType.DMA((1 + 2 * micro,)),
        )

    third = 3 * width // 6
    pl.run_scoped(
        backward,
        pltpu.VMEM((micro, rows, width), BF16), pltpu.VMEM((micro, keys, width), BF16),
        pltpu.VMEM((micro, keys, width), BF16), pltpu.VMEM((width, 3 * width), BF16),
        pltpu.VMEM((3, 2) + (2,) * bits + (width // count, third), BF16),
        pltpu.VMEM((micro, rows, width), BF16), pltpu.VMEM((micro, win + HALO, width), BF16),
        pltpu.SemaphoreType.DMA((1,)),
    )


def finish_kernel(sizes, sums, late, *refs):
    given, results, vectors, rest = refs[:6], refs[6:12], refs[12:20], refs[20:]
    held, wide, sem_in, sem_out = rest[:6], rest[6:10], rest[10], rest[11]
    loads = [pltpu.make_async_copy(src, dst, sem_in.at[n]) for n, (src, dst) in enumerate(zip(given, held))]
    stores = [
        pltpu.make_async_copy(src, dst, sem_out.at[n]) for n, (src, dst) in enumerate(zip(held[:2] + wide, results))
    ]
    for load in loads:
        load.start()
    for n in range(2):
        loads[n].wait()
        stores[n].start()
    for n in range(4):
        loads[2 + n].wait()
        wide[n][...] = held[2 + n][...].astype(F32)
        stores[2 + n].start()
    f = lax.axis_index("fsdp")
    width = late.shape[1]
    for r, (size, out) in enumerate(zip(sizes, vectors)):
        if r < 2:
            row = late[r : r + 1, :]
        elif r == 2:
            row = jnp.concatenate([late[m : m + 1, :] for m in range(2, 5)], axis=1)
        else:
            row = sums[r : r + 1, :] if sums.shape[1] == size * (width // sizes[0]) else sums[r : r + 1, :width]
        whole_size = row.shape[1]
        row = jnp.broadcast_to(row, (8, whole_size))
        turned = pltpu.roll(row, lax.rem(whole_size - f * size, whole_size), 1)
        out[...] = turned[0, :size]
    for store in stores:
        store.wait()


def front_remote(
    lay, role, sizes, inputs, segment_ids, block_ids, small, weights, freqs, lse_shape, bias_scratch, spans, attn_flops
):
    micro, rows, width = inputs.shape
    keys, win = lay["keys"], lay["win"]
    bits = lax.axis_size("fsdp").bit_length() - 1
    lanes = -(-max(sizes) // 128) * 128
    full = [like((2,) * bits + p.shape, BF16) for p in weights]
    longest = max(sizes) << bits
    table_rows = win + rows + HALO
    shapes = full + [
        like((micro, rows, width), BF16), like((micro, keys, width), BF16), like((micro, keys, width), BF16),
        like((micro, keys, width), BF16), like((micro, rows, width), BF16), like(lse_shape, F32),
        like((8, longest), F32), like((table_rows, 128), F32), like((table_rows, 128), F32),
        like((micro, keys, 1), F32), like((micro, 8, rows), F32),
    ]
    remote = 3 * micro + 1 + (bits + 2) * 9
    outs = pl.pallas_call(
        functools.partial(front_kernel, lay, bits, sizes),
        in_specs=[VMEM] * 16,
        out_specs=[ANY] * 10 + [VMEM] * 5,
        out_shape=shapes,
        scratch_shapes=[
            pltpu.VMEM((micro, rows, width), BF16), pltpu.VMEM((micro, win + HALO, width), BF16),
            pltpu.VMEM((width, 3 * width), BF16), pltpu.VMEM((micro, rows, width), BF16),
            pltpu.VMEM((micro, keys, width), BF16), pltpu.VMEM((micro, keys, width), BF16),
            pltpu.VMEM((micro, keys, width), BF16), pltpu.VMEM((micro, rows, width), BF16),
            pltpu.VMEM(lse_shape, F32), pltpu.VMEM((2,) * bits + (8, lanes), F32), pltpu.VMEM((8, lanes), F32),
            pltpu.VMEM((2, -(-(table_rows // HALO) // 8) * 8, 128), F32),
            pltpu.SemaphoreType.DMA((remote,)), pltpu.SemaphoreType.DMA((remote,)),
            pltpu.SemaphoreType.DMA((96,)),
        ] + bias_scratch,
        compiler_params=pltpu.CompilerParams(
            vmem_limit_bytes=VMEM_BYTES, collective_id=0, has_side_effects=True
        ),
        cost_estimate=pl.CostEstimate(flops=2 * attn_flops, bytes_accessed=40 << 20, transcendentals=0),
        name="front",
    )(inputs, segment_ids, block_ids, freqs, *weights, *small)
    joined = [w.reshape((-1, w.shape[-1])) for w in outs[:4]]
    return tuple(joined) + tuple(outs[4:])


def front_native(
    lay, role, sizes, inputs, segment_ids, block_ids, small, weights, freqs, lse_shape, bias_scratch, spans, attn_flops
):
    micro, rows, width = inputs.shape
    keys, win, length = lay["keys"], lay["win"], lay["length"]
    clean, half = role[0], role[1]
    pairs = [(0, 1), (1, 0), (2, 3), (3, 2)]
    xb = lax.ppermute(inputs, "seq", [(2, 0), (3, 1)])
    xmain = jnp.where(clean == 1, inputs, xb)
    edge = jnp.where(half == 0, inputs[:, rows - HALO :], inputs[:, :HALO])
    xc = lax.ppermute(jnp.concatenate([xmain[:, rows - win :], edge], axis=1), "seq", pairs)
    start = half * rows
    edge_at = jnp.where(half == 0, rows, -HALO)
    positions = start + jnp.concatenate([jnp.arange(-win, rows), edge_at + jnp.arange(HALO)])
    turned = positions.astype(F32)[:, None] * freqs
    sine = jnp.sin(turned)
    cos = jnp.cos(turned)
    sin = jnp.where(jnp.arange(128)[None] % HD < HD // 2, -sine, sine)
    code = segment_ids * SEG_STEP + block_ids
    padded = jnp.pad(code, ((0, 0), (win, 0)), constant_values=-1)
    key_codes = lax.dynamic_slice_in_dim(padded, start, win + rows, 1)
    own_code = lax.dynamic_slice_in_dim(code, start, rows, 1)
    own_seg = lax.dynamic_slice_in_dim(segment_ids, start, rows, 1)
    before, after = code[:, rows - HALO : rows], code[:, rows : rows + HALO]
    codes = jnp.concatenate(
        [
            key_codes,
            jnp.where((clean == 1) & (half == 0), after, -1),
            jnp.where((clean == 0) & (half == 1), before, -2),
            jnp.where(clean == 0, own_code, -2),
            jnp.where((clean == 0) & (half == 0), after, -2),
            jnp.full((micro, keys - lay["used"]), -2, jnp.int32),
        ],
        axis=1,
    )[:, :, None].astype(F32)
    queries = jnp.stack([own_seg * SEG_STEP, own_code - (1 - clean), own_code], axis=1)
    queries = jnp.concatenate([queries, jnp.zeros((micro, 5, rows), jnp.int32)], axis=1).astype(F32)
    packed = lax.all_gather(jnp.concatenate(small)[None], "fsdp", axis=0, tiled=True)
    vectors, at = [], 0
    longest = max(sizes) * packed.shape[0]
    for size in sizes:
        one = packed[:, at : at + size].reshape(-1).astype(F32)
        vectors.append(jnp.pad(one, (0, longest - one.shape[0])))
        at += size
    vec = jnp.stack(vectors)
    w_in, w_out, w_up, w_down = (lax.all_gather(p, "fsdp", axis=0, tiled=True) for p in weights)
    per_seq = lambda n, d: pl.BlockSpec((1, n, d), lambda s: (s, 0, 0))
    table_rows = win + rows + HALO
    q, k, v, a = call(
        functools.partial(qkv_kernel, lay), (micro,),
        [SMEM(), per_seq(rows, width), per_seq(rows, width), per_seq(win + HALO, width),
         whole((width, 3 * width)), whole(vec.shape), whole((table_rows, 128)), whole((table_rows, 128))],
        [per_seq(rows, width), per_seq(keys, width), per_seq(keys, width), per_seq(keys, width)],
        [like((micro, rows, width), BF16)] + [like((micro, keys, width), BF16)] * 3,
        [], 2 * micro * rows * width * 3 * width * 2, 20 << 20, "qkv",
    )(role, inputs, xb, xc, w_in, vec, cos, sin)
    qw = QUAD * HD
    quads = width // qw
    quad_block = lambda n: pl.BlockSpec((1, n, qw), lambda s, h: (s, 0, h))
    o, lse = call(
        functools.partial(attend_kernel, lay), (micro, quads),
        [pl.BlockSpec((1, keys, 1), lambda s, h: (s, 0, 0)), pl.BlockSpec((1, 8, rows), lambda s, h: (s, 0, 0)),
         quad_block(rows), quad_block(keys), quad_block(keys)],
        [quad_block(rows), pl.BlockSpec((1,) + lse_shape[1:], lambda s, h: (s * quads + h, 0, 0))],
        [like((micro, rows, width), BF16), like(lse_shape, F32)],
        bias_scratch, 2 * attn_flops, 12 << 20, "attend",
    )(codes, queries, q, k, v)
    return w_in, w_out, w_up, w_down, q, k, v, a, o, lse, vec, cos, sin, codes, queries


def back_remote(
    lay, role, sizes, inputs, cotangent, codes, queries, lse, cos, sin, vec,
    q, k, v, o, a, w_in, w_out, w_up, w_down, bias_scratch, attn_flops,
):
    micro, rows, width = inputs.shape
    keys, win = lay["keys"], lay["win"]
    bits = lax.axis_size("fsdp").bit_length() - 1
    lead = (2,) * bits
    count = 1 << bits
    hidden = w_up.shape[1]
    slab, slab_down = width // count, hidden // count
    third = width // 2
    steps, wide = slab_down // 128, count // 2 * 128

    def bank(name, r, c):
        over_x = BACK_BITS[name][1]
        kept = r // 2 if over_x else r
        over = [pltpu.VMEM(lead[: bits - 1 - b] + (kept, c), BF16) for b in range(bits)]
        ends = [pltpu.VMEM(lead + (kept, c), BF16)] if over_x else []
        return pltpu.VMEM(lead + (r, c), BF16), tuple(ends + over + ([] if over_x else [pltpu.VMEM((r, c), BF16)]))

    acc_in, r_in = zip(*[bank("i%d" % j, slab, third) for j in range(3)])
    acc_out, r_out = bank("o", slab, width // 2)
    acc_up, r_up = zip(*[bank("u%d" % j, slab, wide) for j in range(steps)])
    acc_down, r_down = zip(*[bank("d%d" % j, 128, width // 2) for j in range(steps)])
    stages = 2 + bits
    remote = (7 + 2 * steps) * (bits + 5) + 2 * stages + 4 * micro
    scratch = [
        pltpu.VMEM((micro, rows, width), BF16), pltpu.VMEM((micro, rows, width), BF16),
        pltpu.VMEM((micro, win + HALO, width), BF16),
        acc_in, acc_out, acc_up, acc_down, r_in, r_out, r_up, r_down,
        pltpu.VMEM((slab, 3 * width), BF16), pltpu.VMEM((slab, width), BF16),
        pltpu.VMEM((steps, slab, count * 128), BF16), pltpu.VMEM((slab_down, width), BF16),
        pltpu.VMEM((8, hidden), F32), pltpu.VMEM((2 * stages, 8, hidden), F32),
        pltpu.VMEM((8, width), F32), pltpu.VMEM((2 * stages, 8, width), F32),
        pltpu.SemaphoreType.DMA((remote,)), pltpu.SemaphoreType.DMA((remote,)),
        pltpu.SemaphoreType.DMA((8 + steps * count,)),
    ] + bias_scratch
    out_rows, grad_in, f_in, f_out, f_up, f_down, sums, late = pl.pallas_call(
        functools.partial(back_kernel, lay, bits),
        in_specs=[VMEM] * 8 + [ANY] * 9,
        out_specs=[ANY] * 6 + [VMEM] * 2,
        out_shape=[
            like((micro, rows, width), BF16), like((micro, rows, width), F32), like((slab, 3 * width), BF16),
            like((slab, width), BF16), like((slab, hidden), BF16), like((slab_down, width), BF16),
            like((8, hidden), F32), like((8, width), F32),
        ],
        scratch_shapes=scratch,
        compiler_params=pltpu.CompilerParams(
            vmem_limit_bytes=67043328, collective_id=1, has_side_effects=True
        ),
        cost_estimate=pl.CostEstimate(flops=6 * attn_flops, bytes_accessed=60 << 20, transcendentals=0),
        name="back",
    )(codes, queries, lse, cos, sin, vec, inputs, o, cotangent.reshape(micro * rows, width),
      q, k, v, a, w_in, w_out, w_up, w_down)
    shards = (f_in, f_out, f_up, f_down)
    given = (out_rows, grad_in) + shards
    done = pl.pallas_call(
        functools.partial(finish_kernel, sizes),
        in_specs=[VMEM] * 2 + [ANY] * 6,
        out_specs=[ANY] * 6 + [VMEM] * 8,
        out_shape=[like(out_rows.shape, BF16), like(grad_in.shape, F32)]
        + [like(g.shape, F32) for g in shards] + [like((size,), F32) for size in sizes],
        scratch_shapes=[pltpu.VMEM(g.shape, g.dtype) for g in given] + [pltpu.VMEM(g.shape, F32) for g in shards]
        + [pltpu.SemaphoreType.DMA((6,)), pltpu.SemaphoreType.DMA((6,))],
        compiler_params=pltpu.CompilerParams(vmem_limit_bytes=VMEM_BYTES),
        cost_estimate=pl.CostEstimate(flops=0, bytes_accessed=16 << 20, transcendentals=0),
        name="finish",
    )(sums, late, *given)
    return done[0], done[1], list(done[2:6]), list(done[6:])


def back_native(
    lay, role, sizes, inputs, cotangent, codes, queries, lse, cos, sin, vec,
    q, k, v, o, a, w_in, w_out, w_up, w_down, bias_scratch, attn_flops,
):
    micro, rows, width = inputs.shape
    keys, win = lay["keys"], lay["win"]
    clean, half = role[0], role[1]
    pairs = [(0, 1), (1, 0), (2, 3), (3, 2)]
    fsdp_n = lax.axis_size("fsdp")
    hidden = w_up.shape[1]
    qw = QUAD * HD
    quads = width // qw
    total = micro * rows
    flat = lambda z: z.reshape(total, width)
    chunk = min(512, hidden)
    rows_spec = whole((total, width))
    out_rows, dx2, do, g_w_out, g_w_up, g_b_up, g_w_down, g_mlp = call(
        mlp_kernel, (hidden // chunk,),
        [rows_spec, rows_spec, rows_spec, whole((width, width)), whole(vec.shape),
         pl.BlockSpec((width, chunk), lambda j: (0, j)), pl.BlockSpec((8, chunk), lambda j: (0, j)),
         pl.BlockSpec((chunk, width), lambda j: (j, 0))],
        [rows_spec, rows_spec, rows_spec, whole((width, width)),
         pl.BlockSpec((width, chunk), lambda j: (0, j)), pl.BlockSpec((8, chunk), lambda j: (0, j)),
         pl.BlockSpec((chunk, width), lambda j: (j, 0)), whole((8, width))],
        [like((total, width), BF16), like((total, width), F32), like((total, width), BF16),
         like((width, width), BF16), like((width, hidden), BF16), like((8, hidden), F32),
         like((hidden, width), BF16), like((8, width), F32)],
        [pltpu.VMEM((total, width), F32), pltpu.VMEM((total, width), BF16), pltpu.VMEM((width, total), BF16),
         pltpu.VMEM((total, 1), F32), pltpu.VMEM((total, width), F32), pltpu.VMEM((total, width), F32)],
        2 * total * width * (6 * hidden + 3 * width), 40 << 20, "mlp",
    )(flat(o), flat(inputs), flat(cotangent), w_out, vec, w_up, vec, w_down)

    do = do.reshape(micro, rows, width)
    per_seq = lambda n, d: pl.BlockSpec((1, n, d), lambda s: (s, 0, 0))
    role_spec = SMEM()
    quad_block = lambda n: pl.BlockSpec((1, n, qw), lambda s, h: (s, 0, h))
    code_spec = pl.BlockSpec((1, keys, 1), lambda s, h: (s, 0, 0))
    query_spec = pl.BlockSpec((1, 8, rows), lambda s, h: (s, 0, 0))
    lse_spec = pl.BlockSpec((1,) + lse.shape[1:], lambda s, h: (s * quads + h, 0, 0))
    table = pl.BlockSpec((win + rows + HALO, 128), lambda s, h: (0, 0), pipeline_mode=pl.Buffered(1))
    dq, dk, dv = call(
        functools.partial(attend_back_kernel, lay), (micro, quads),
        [code_spec, query_spec, quad_block(rows), quad_block(keys), quad_block(keys),
         quad_block(rows), quad_block(rows), lse_spec, table, table],
        [quad_block(rows), quad_block(keys), quad_block(keys)],
        [like((micro, rows, width), BF16), like((micro, keys, width), BF16), like((micro, keys, width), BF16)],
        [pltpu.VMEM((keys, qw), F32), pltpu.VMEM((keys, qw), F32)] + bias_scratch,
        5 * attn_flops, 24 << 20, "attend_back",
    )(codes, queries, q, k, v, o, do, lse, cos, sin)

    da_own, da_main, da_win, g_w_in, g_b_in = call(
        functools.partial(qkv_back_kernel, lay), (micro,),
        [role_spec, per_seq(keys, width), per_seq(rows, width), per_seq(keys, width), per_seq(keys, width),
         whole((width, 3 * width))],
        [per_seq(rows, width), per_seq(rows, width), per_seq(win + HALO, width),
         whole((width, 3 * width)), whole((8, 3 * width))],
        [like((micro, rows, width), F32), like((micro, rows, width), BF16), like((micro, win + HALO, width), BF16),
         like((width, 3 * width), BF16), like((8, 3 * width), F32)],
        [pltpu.VMEM((width, 3 * width), F32)], 2 * 2 * micro * rows * width * 3 * width * 2, 40 << 20, "qkv_back",
    )(role, a, dq, dk, dv, w_in)

    from_pair = lax.ppermute(da_win, "seq", pairs).astype(F32)
    from_second = jnp.where(half == 0, from_pair[:, :win], 0.0)
    edge = from_pair[:, win:]
    gap = jnp.zeros((micro, rows - HALO, width), F32)
    edges = jnp.where(
        half == 0, jnp.concatenate([gap, edge], axis=1), jnp.concatenate([edge, gap], axis=1)
    )
    added = jnp.pad(from_second, ((0, 0), (rows - win, 0), (0, 0)))
    to_clean = (jnp.where(clean == 0, da_main.astype(F32), 0.0) + added).astype(BF16)
    from_noisy = lax.ppermute(to_clean, "seq", [(0, 2), (1, 3)])
    extra = jnp.where(clean == 1, from_noisy.astype(F32) + added, 0.0) + edges

    grad_in, g_attn = call(
        final_kernel, (2,),
        [pl.BlockSpec((total // 2, width), lambda i: (i, 0))] * 4 + [whole((1, width))],
        [pl.BlockSpec((total // 2, width), lambda i: (i, 0)), whole((8, width))],
        [like((total, width), F32), like((8, width), F32)], [], 0, 16 << 20, "norm_back",
    )(flat(inputs), flat(da_own), flat(extra), flat(dx2), vec[0:1, :width])

    def scatter(g):
        return lax.psum(lax.psum_scatter(g, "fsdp", scatter_dimension=0, tiled=True), "seq")

    big = [scatter(g).astype(F32) for g in (g_w_in, g_w_out, g_w_up, g_w_down)]
    smalls = [g_attn[0], g_attn[1], g_b_in[0], g_mlp[3], g_mlp[1], g_mlp[2], g_b_up[0], g_mlp[0]]
    pack = jnp.concatenate([g.reshape(fsdp_n, -1) for g in smalls], axis=1)
    pack = lax.psum(pack, ("seq", "fsdp"))
    mine = lax.dynamic_slice_in_dim(pack, lax.axis_index("fsdp"), 1, 0)[0]
    outs, at = [], 0
    for size in sizes:
        outs.append(mine[at : at + size])
        at += size
    return out_rows.reshape(micro, rows, width), grad_in.reshape(micro, rows, width), big, outs


def per_device(
    inputs, segment_ids, block_ids, attn_gain, attn_shift, proj_in, bias_in, proj_out, bias_out,
    mlp_gain, mlp_shift, weight_up, bias_up, weight_down, bias_down, cotangent,
):
    micro, rows, width = inputs.shape
    length = segment_ids.shape[1]
    hidden = weight_up.shape[1]
    seq_n = lax.axis_size("seq")
    fsdp_n = lax.axis_size("fsdp")
    assert seq_n == 4 and seq_n * rows == 2 * length
    lay = layout(rows, length)
    win, keys = lay["win"], lay["keys"]
    me = lax.axis_index("seq")
    clean = me // 2
    half = me % 2
    role = jnp.stack([clean, half]).astype(jnp.int32)
    pairs = [(0, 1), (1, 0), (2, 3), (3, 2)]
    small = (attn_gain, attn_shift, bias_in, bias_out, mlp_gain, mlp_shift, bias_up, bias_down)
    sizes = [p.shape[0] for p in small]
    weights = (proj_in, proj_out, weight_up, weight_down)
    half_dim = HD // 2
    freqs = (10000.0 ** (-(np.arange(half_dim, dtype=np.float32) / half_dim))).astype(np.float32)
    freqs = np.tile(freqs, 4)[None]
    quads = width // (QUAD * HD)
    qw = QUAD * HD
    spans = [hi - lo + NEAR for lo, hi in windows(lay)]
    bias_scratch = [pltpu.VMEM((rows // TILE, max(spans), TILE), F32)]
    per_seq = lambda n, d: pl.BlockSpec((1, n, d), lambda s: (s, 0, 0))
    role_spec = SMEM()
    attn_flops = micro * quads * sum(spans) * QUAD * TILE * qw * 2
    lse_shape = (micro * quads, rows // TILE, QUAD * TILE)
    table_rows = win + rows + HALO
    aligned = fsdp_n & (fsdp_n - 1) == 0 and all(p.shape[0] % (4 * HALO) in (0, 32) for p in weights)
    front = front_remote if aligned else front_native
    (w_in, w_out, w_up, w_down, q, k, v, a, o, lse, vec, cos, sin, codes, queries) = front(
        lay, role, sizes, inputs, segment_ids, block_ids, small, weights, freqs,
        lse_shape, bias_scratch, spans, attn_flops,
    )
    back = back_remote if aligned else back_native
    out_rows, grad_in, big, vectors = back(
        lay, role, sizes, inputs, cotangent, codes, queries, lse, cos, sin, vec,
        q, k, v, o, a, w_in, w_out, w_up, w_down, bias_scratch, attn_flops,
    )
    g_gain1, g_shift1, g_bin, g_bout, g_gain2, g_shift2, g_bup, g_bdown = vectors
    return (
        out_rows, grad_in, g_gain1, g_shift1, big[0], g_bin, big[1], g_bout,
        g_gain2, g_shift2, big[2], g_bup, big[3], g_bdown,
    )


def solution(mesh):
    rows = P("fsdp", "seq", None)
    one, two = P("fsdp"), P("fsdp", None)
    params = (one, one, two, one, two, one, one, one, two, one, two, one)
    return jax.shard_map(
        per_device,
        mesh=mesh,
        in_specs=(rows, two, two) + params + (rows,),
        out_specs=(rows, rows) + params,
        check_vma=False,
    )
```
